32 devices in a mesh: wide: 8 (over z, y), narrow: 4 (over x, core).
Axes of the slice: x: 2, y: 2, z: 4, core: 2. Of those that a mesh axis runs over, the one named last changes fastest.
Arguments:
- passage_ids: int32 [64, 384], P(('wide', 'narrow')), may hold values from 0 to 17999
- query_ids: int32 [8, 32], P('wide'), may hold values from 0 to 17999
- passage_query: int32 [64], replicated, may hold values from -1 to 7, as said below
- kept_mask: int32 [64], replicated, may hold values 0 or 1
- neg_count: int32 [8], P('wide'), may hold values from 1 to 7, as said below
- step_count: int32 [1], replicated, may hold values from 2 to 20
- embed_table: float32 [18384, 768], P(None, ('wide', 'narrow')), may hold values from -6 to 6
- attend_in: float32 [2, 768, 2304], P(None, ('wide', 'narrow')), may hold values from -0.3125 to 0.3125
- attend_out: float32 [2, 768, 768], P(None, ('wide', 'narrow')), may hold values from -0.625 to 0.625
- expand_weight: float32 [2, 768, 3072], P(None, ('wide', 'narrow')), may hold values from -0.21875 to 0.21875
- shrink_weight: float32 [2, 3072, 768], P(None, ('wide', 'narrow')), may hold values from -0.109375 to 0.109375
- norm_gains: float32 [2, 3, 768], P(None, None, ('wide', 'narrow')), may hold values from 0.5 to 1.5
- bias_terms: float32 [2, 8448], P(None, ('wide', 'narrow')), may hold values from -0.6 to 0.6
- embed_first: float32 [18384, 768], P(None, ('wide', 'narrow')), may hold values from -3.7598107e-05 to 3.7598107e-05
- embed_second: float32 [18384, 768], P(None, ('wide', 'narrow')), may hold values from 1.59032e-12 to 2.544512e-11
- attend_in_first: float32 [2, 768, 2304], P(None, ('wide', 'narrow')), may hold values from -0.0001252017 to 0.0001252017
- attend_in_second: float32 [2, 768, 2304], P(None, ('wide', 'narrow')), may hold values from 1.7670223e-11 to 2.8272357e-10
- attend_out_first: float32 [2, 768, 768], P(None, ('wide', 'narrow')), may hold values from -0.0001252017 to 0.0001252017
- attend_out_second: float32 [2, 768, 768], P(None, ('wide', 'narrow')), may hold values from 1.7670223e-11 to 2.8272357e-10
- expand_first: float32 [2, 768, 3072], P(None, ('wide', 'narrow')), may hold values from -0.0001252017 to 0.0001252017
- expand_second: float32 [2, 768, 3072], P(None, ('wide', 'narrow')), may hold values from 1.7670223e-11 to 2.8272357e-10
- shrink_first: float32 [2, 3072, 768], P(None, ('wide', 'narrow')), may hold values from -0.0001252017 to 0.0001252017
- shrink_second: float32 [2, 3072, 768], P(None, ('wide', 'narrow')), may hold values from 1.7670223e-11 to 2.8272357e-10
- gains_first: float32 [2, 3, 768], P(None, None, ('wide', 'narrow')), may hold values from -0.0003759811 to 0.0003759811
- gains_second: float32 [2, 3, 768], P(None, None, ('wide', 'narrow')), may hold values from 1.59032e-10 to 2.544512e-09
- bias_first: float32 [2, 8448], P(None, ('wide', 'narrow')), may hold values from -0.0003759811 to 0.0003759811
- bias_second: float32 [2, 8448], P(None, ('wide', 'narrow')), may hold values from 1.59032e-10 to 2.544512e-09
Outputs:
- loss: float32 [], replicated
- grad_norm: float32 [], replicated
- embed_table_new: float32 [18384, 768], P(None, ('wide', 'narrow'))
- embed_first_new: float32 [18384, 768], P(None, ('wide', 'narrow'))
- embed_second_new: float32 [18384, 768], P(None, ('wide', 'narrow'))
- attend_in_new: float32 [2, 768, 2304], P(None, ('wide', 'narrow'))
- attend_in_first_new: float32 [2, 768, 2304], P(None, ('wide', 'narrow'))
- attend_in_second_new: float32 [2, 768, 2304], P(None, ('wide', 'narrow'))
- attend_out_new: float32 [2, 768, 768], P(None, ('wide', 'narrow'))
- attend_out_first_new: float32 [2, 768, 768], P(None, ('wide', 'narrow'))
- attend_out_second_new: float32 [2, 768, 768], P(None, ('wide', 'narrow'))
- expand_new: float32 [2, 768, 3072], P(None, ('wide', 'narrow'))
- expand_first_new: float32 [2, 768, 3072], P(None, ('wide', 'narrow'))
- expand_second_new: float32 [2, 768, 3072], P(None, ('wide', 'narrow'))
- shrink_new: float32 [2, 3072, 768], P(None, ('wide', 'narrow'))
- shrink_first_new: float32 [2, 3072, 768], P(None, ('wide', 'narrow'))
- shrink_second_new: float32 [2, 3072, 768], P(None, ('wide', 'narrow'))
- norm_gains_new: float32 [2, 3, 768], P(None, None, ('wide', 'narrow'))
- gains_first_new: float32 [2, 3, 768], P(None, None, ('wide', 'narrow'))
- gains_second_new: float32 [2, 3, 768], P(None, None, ('wide', 'narrow'))
- bias_terms_new: float32 [2, 8448], P(None, ('wide', 'narrow'))
- bias_first_new: float32 [2, 8448], P(None, ('wide', 'narrow'))
- bias_second_new: float32 [2, 8448], P(None, ('wide', 'narrow'))
The draws below stay inside these ranges and needn't reach their ends.
Inputs may be any that keep to these rules, and one draw needn't show every extreme that they name: `passage_query`: slots from 0 hold the passages of query 0, then of query 1 and so on, each query 2 to 8 consecutive slots (the first is its positive), one query exactly 8, 40 slots in all; the remaining slots hold -1. `neg_count`: one less than the number of slots of that query in passage_query.
All inputs are finite; a program needn't handle non-finite values.
Results may differ from the reference program's by a relative error of at most 0.022.
The reference program's roundings to bfloat16 on the way count: a program that leaves them out, or rounds other values in their place, can miss the bound.
Values may be sent and summed in bfloat16 or wider, within the bound.
A program may use at most 448 MiB of HBM per device.

```python
import math
import jax
import jax.numpy as jnp
from jax import lax

D = 768
H = 12
HD = 64
FF = 3072
V = 18000
LP = 384
LQ = 32
NQ = 8
PASS = 64
NPARAM = 28296192


def query_counts(key):
    draw_key = jax.random.fold_in(key, 7)
    pick_key = jax.random.fold_in(key, 11)
    halves = jax.random.randint(draw_key, (NQ // 2,), 0, 7)
    chosen = jax.random.randint(pick_key, (), 0, NQ // 2)
    halves = jnp.where(jnp.arange(NQ // 2) == chosen, 6, halves)
    extra = jnp.stack([halves, 6 - halves], axis=1).reshape(NQ)
    return (2 + extra).astype(jnp.int32)


def draw_neg_count(key, part):
    return (query_counts(key) - 1).astype(jnp.int32)


def draw_passage_query(key, part):
    counts = query_counts(key)
    ends = jnp.cumsum(counts)
    slots = jnp.arange(PASS, dtype=jnp.int32)
    owner = jnp.sum((ends[None, :] <= slots[:, None]).astype(jnp.int32), axis=1)
    return jnp.where(slots < ends[NQ - 1], owner, -1).astype(jnp.int32)


def plant(result, key, low, top_value):
    shape = result.shape
    index_at = [jax.random.randint(jax.random.fold_in(key, axis), (), 0, shape[axis]) for axis in range(len(shape))]
    result = result.at[tuple(index_at)].set(low)
    longest = shape.index(max(shape))
    index_at[longest] = (index_at[longest] + 1) % shape[longest]
    return result.at[tuple(index_at)].set(top_value)


def block_scale(rng, dims, split, least, largest):
    def one(dim, shards_of):
        steps = jax.random.uniform(jax.random.fold_in(jax.random.fold_in(rng, 6), dim), (shards_of,), jnp.float32, least / len(split), largest / len(split))
        return jnp.repeat(jnp.exp(steps), dims[dim] // shards_of).reshape((-1,) + (1,) * (len(dims) - dim - 1))

    level = one(*split[0])
    for cut in split[1:]:
        level = level * one(*cut)
    return level


def noise(own_key, dims, scale, reach, split=(), kind=jnp.bfloat16):
    drawn = jax.random.normal(own_key, dims, jnp.float32) * scale
    if len(split) > 0:
        drawn = block_scale(own_key, dims, split, -0.22, 0.18) * drawn
    return jnp.clip(drawn, min=-reach, max=reach).astype(kind)


def setup_inputs(seed: int = 0) -> dict:
    seeds = jax.random.split(jax.random.key(seed), 28)
    passage_ids = plant(jax.random.randint(seeds[0], (PASS, LP), 0, V), jax.random.fold_in(seeds[0], 1), 0, V - 1).astype(jnp.int32)
    query_ids = plant(jax.random.randint(seeds[1], (NQ, LQ), 0, V), jax.random.fold_in(seeds[1], 1), 0, V - 1).astype(jnp.int32)
    passage_query = draw_passage_query(jax.random.fold_in(seeds[27], 71), 0)
    kept_mask = plant((jax.random.randint(seeds[3], (PASS,), 0, 2) < 1).astype(jnp.int32), jax.random.fold_in(seeds[3], 1), 0, 1)
    neg_count = draw_neg_count(jax.random.fold_in(seeds[27], 71), 0)
    step_count = jax.random.randint(seeds[5], (1,), 2, 21).astype(jnp.int32)
    embed_table = noise(seeds[6], (V + LP, D), 1.0, 6.0, ((1, 32),), jnp.float32)
    attend_in = noise(seeds[7], (2, D, 3 * D), (D // 2) ** -0.5, 0.3125, ((1, 32),), jnp.float32)
    attend_out = noise(seeds[8], (2, D, D), (D // 8) ** -0.5, 0.625, ((1, 32),), jnp.float32)
    expand_weight = noise(seeds[9], (2, D, FF), D ** -0.5, 0.21875, ((1, 32),), jnp.float32)
    shrink_weight = noise(seeds[10], (2, FF, D), FF ** -0.5, 0.109375, ((1, 32),), jnp.float32)
    norm_gains = jnp.clip(1.0 + 0.1 * jax.random.normal(seeds[11], (2, 3, D), jnp.float32), 0.5, 1.5)
    bias_terms = noise(seeds[12], (2, 7 * D + FF), 0.1, 0.6, ((1, 32),), jnp.float32)
    embed_first = noise(seeds[13], (V + LP, D), (0.0333 / NPARAM ** 0.5), 3.7598107155645266e-05, ((1, 32),), jnp.float32)
    embed_second = jnp.clip(jnp.exp(math.log(2.5445119969380592e-11) - 2.7725887 * jax.random.uniform(seeds[14], (V + LP, D), jnp.float32) ** block_scale(seeds[14], (V + LP, D), ((1, 32),), -0.2, 0.2)), 1.590319998086287e-12, 2.5445119969380592e-11)
    attend_in_first = noise(seeds[15], (2, D, 3 * D), (0.111 / NPARAM ** 0.5), 0.0001252017, ((1, 32),), jnp.float32)
    attend_in_second = jnp.clip(jnp.exp(math.log(2.827235667801631e-10) - 2.7725887 * jax.random.uniform(seeds[16], (2, D, 3 * D), jnp.float32) ** block_scale(seeds[16], (2, D, 3 * D), ((1, 32),), -0.2, 0.2)), 1.7670222923760193e-11, 2.827235667801631e-10)
    attend_out_first = noise(seeds[17], (2, D, D), (0.111 / NPARAM ** 0.5), 0.0001252017, ((1, 32),), jnp.float32)
    attend_out_second = jnp.clip(jnp.exp(math.log(2.827235667801631e-10) - 2.7725887 * jax.random.uniform(seeds[18], (2, D, D), jnp.float32) ** block_scale(seeds[18], (2, D, D), ((1, 32),), -0.2, 0.2)), 1.7670222923760193e-11, 2.827235667801631e-10)
    expand_first = noise(seeds[19], (2, D, FF), (0.111 / NPARAM ** 0.5), 0.0001252017, ((1, 32),), jnp.float32)
    expand_second = jnp.clip(jnp.exp(math.log(2.827235667801631e-10) - 2.7725887 * jax.random.uniform(seeds[20], (2, D, FF), jnp.float32) ** block_scale(seeds[20], (2, D, FF), ((1, 32),), -0.2, 0.2)), 1.7670222923760193e-11, 2.827235667801631e-10)
    shrink_first = noise(seeds[21], (2, FF, D), (0.111 / NPARAM ** 0.5), 0.0001252017, ((1, 32),), jnp.float32)
    shrink_second = jnp.clip(jnp.exp(math.log(2.827235667801631e-10) - 2.7725887 * jax.random.uniform(seeds[22], (2, FF, D), jnp.float32) ** block_scale(seeds[22], (2, FF, D), ((1, 32),), -0.2, 0.2)), 1.7670222923760193e-11, 2.827235667801631e-10)
    gains_first = noise(seeds[23], (2, 3, D), (0.333 / NPARAM ** 0.5), 0.0003759811, ((2, 32),), jnp.float32)
    gains_second = jnp.clip(jnp.exp(math.log(2.544511934488014e-09) - 2.7725887 * jax.random.uniform(seeds[24], (2, 3, D), jnp.float32) ** block_scale(seeds[24], (2, 3, D), ((2, 32),), -0.2, 0.2)), 1.5903199590550088e-10, 2.544511934488014e-09)
    bias_first = noise(seeds[25], (2, 7 * D + FF), (0.333 / NPARAM ** 0.5), 0.0003759811, ((1, 32),), jnp.float32)
    bias_second = jnp.clip(jnp.exp(math.log(2.544511934488014e-09) - 2.7725887 * jax.random.uniform(seeds[26], (2, 7 * D + FF), jnp.float32) ** block_scale(seeds[26], (2, 7 * D + FF), ((1, 32),), -0.2, 0.2)), 1.5903199590550088e-10, 2.544511934488014e-09)
    return dict(passage_ids=passage_ids, query_ids=query_ids, passage_query=passage_query, kept_mask=kept_mask, neg_count=neg_count, step_count=step_count, embed_table=embed_table, attend_in=attend_in, attend_out=attend_out, expand_weight=expand_weight, shrink_weight=shrink_weight, norm_gains=norm_gains, bias_terms=bias_terms, embed_first=embed_first, embed_second=embed_second, attend_in_first=attend_in_first, attend_in_second=attend_in_second, attend_out_first=attend_out_first, attend_out_second=attend_out_second, expand_first=expand_first, expand_second=expand_second, shrink_first=shrink_first, shrink_second=shrink_second, gains_first=gains_first, gains_second=gains_second, bias_first=bias_first, bias_second=bias_second)


@jax.custom_vjp
def low(v):
    return lax.optimization_barrier(v.astype(jnp.bfloat16)).astype(jnp.float32)

@jax.custom_vjp
def low_back(v):
    return v

def low_keep(v):
    return (low(v), None)

def low_pass(kept, grad):
    return (grad,)

def back_keep(v):
    return (v, None)

def back_low(kept, grad):
    return (low(grad),)
low.defvjp(low_keep, low_pass)
low_back.defvjp(back_keep, back_low)
HIGHEST = lax.Precision.HIGHEST
MARGIN = 1.0
CLIP = 1.0
BETA_ONE = 0.9
BETA_TWO = 0.999
LEARN_RATES = (1.0, 0.02, 0.08, 0.02, 0.02, 1.0, 0.1)
WEIGHT_DECAY = 0.01
ADAM_EPS = 1e-08
NORM_EPS = 1e-05
group_rows = 8

def norm_layer(values, gain, shift):
    center = values - lax.optimization_barrier(jnp.mean(values, axis=-1, keepdims=True))
    spread = lax.optimization_barrier(jnp.mean(center * center, axis=-1, keepdims=True))
    return center * lax.rsqrt(spread + NORM_EPS) * gain + shift

def project(values, weight):
    return jnp.einsum('...i,ij->...j', values, weight, precision=HIGHEST)

def encode(token_ids, table, attend_in, attend_out, expand, shrink, gain, bias):
    batch, length = token_ids.shape
    embedded = jnp.take(table, token_ids, axis=0) + table[V:V + length][None]
    normed = norm_layer(embedded, gain[0], bias[6 * D + FF:7 * D + FF])
    qkv_bias = jnp.concatenate([bias[0:D], jnp.zeros((D,), jnp.float32), bias[D:2 * D]])
    packed = low(low_back(project(low(normed), attend_in) + qkv_bias))
    heads = packed.reshape(batch, length, 3, H, HD)
    scores = jnp.einsum('bqhd,bkhd->bhqk', heads[:, :, 0], heads[:, :, 1], precision=HIGHEST) * 0.125
    scores = low_back(scores)
    probs = low(jax.nn.softmax(scores, axis=-1))
    mixed = jnp.einsum('bhqk,bkhd->bqhd', probs, heads[:, :, 2], precision=HIGHEST).reshape(batch, length, D)
    mixed = low(low_back(mixed))
    branch = low_back(project(mixed, attend_out) + bias[2 * D:3 * D])
    middle = norm_layer(normed + branch, gain[1], bias[3 * D:4 * D])
    upper = low_back(project(low(middle), expand) + bias[4 * D:4 * D + FF])
    active = low(jax.nn.gelu(upper, approximate=False))
    lower = low_back(project(active, shrink) + bias[4 * D + FF:5 * D + FF])
    output = norm_layer(middle + lower, gain[2], bias[5 * D + FF:6 * D + FF])
    return low(low_back(output[:, 0]))

def total_loss(weights, passage_ids, query_ids, passage_query, kept_mask, neg_count):
    table, attend_in, attend_out, expand, shrink, gains, biases = [low(item) for item in weights]
    query_vecs = encode(query_ids, table, attend_in[0], attend_out[0], expand[0], shrink[0], gains[0], biases[0])

    def encode_group(group_ids):
        return encode(group_ids, table, attend_in[1], attend_out[1], expand[1], shrink[1], gains[1], biases[1])
    groups = passage_ids.reshape(PASS // group_rows, group_rows, LP)
    passage_vecs = lax.map(jax.checkpoint(encode_group), groups).reshape(PASS, D)
    scores = jnp.dot(query_vecs, passage_vecs.T, precision=HIGHEST) * (2.0 * D ** (-0.5))
    scores = low_back(scores)
    owner = passage_query
    valid = owner >= 0
    earlier = jnp.concatenate([jnp.full((1,), -1, jnp.int32), owner[:-1]])
    first = valid & (owner != earlier)
    queries = jnp.arange(NQ, dtype=jnp.int32)
    member = owner[None, :] == queries[:, None]
    positive = member & first[None, :]
    negative = member & jnp.logical_not(first)[None, :] & (kept_mask == 1)[None, :]
    masked = jnp.where(valid[None, :], scores, -1e+30)
    peak = lax.optimization_barrier(jnp.max(masked, axis=1, keepdims=True))
    summed = lax.optimization_barrier(jnp.sum(jnp.where(valid[None, :], jnp.exp(masked - peak), 0.0), axis=1))
    logsum = peak[:, 0] + jnp.log(summed)
    pos_score = lax.optimization_barrier(jnp.sum(jnp.where(positive, scores, 0.0), axis=1))
    margins = MARGIN - pos_score[:, None] + scores
    hinge = lax.optimization_barrier(jnp.sum(jnp.where(negative & (margins > 0), margins, 0.0), axis=1)) / neg_count.astype(jnp.float32)
    return jnp.sum(logsum - pos_score + hinge)

def adam_update(weight, grad, first, second, step, rate):
    first_new = BETA_ONE * first + (1.0 - BETA_ONE) * grad
    second_new = BETA_TWO * second + (1.0 - BETA_TWO) * grad * grad
    first_hat = first_new / (1.0 - BETA_ONE ** step)
    second_hat = second_new / (1.0 - BETA_TWO ** step)
    weight_new = weight - rate * (first_hat / (jnp.sqrt(second_hat) + ADAM_EPS) + WEIGHT_DECAY * weight)
    return (weight_new, first_new, second_new)

def reference(passage_ids, query_ids, passage_query, kept_mask, neg_count, step_count, embed_table, attend_in, attend_out, expand_weight, shrink_weight, norm_gains, bias_terms, embed_first, embed_second, attend_in_first, attend_in_second, attend_out_first, attend_out_second, expand_first, expand_second, shrink_first, shrink_second, gains_first, gains_second, bias_first, bias_second):
    weights = (embed_table, attend_in, attend_out, expand_weight, shrink_weight, norm_gains, bias_terms)

    def loss_of(params):
        return total_loss(params, passage_ids, query_ids, passage_query, kept_mask, neg_count)
    loss, pullback = jax.vjp(loss_of, weights)
    grads = pullback(jnp.ones_like(loss))[0]
    squares = jnp.zeros((), jnp.float32)
    for grad in grads:
        squares = squares + jnp.sum(grad * grad)
    grad_norm = jnp.sqrt(squares)
    factor = CLIP / jnp.maximum(grad_norm, CLIP)
    step = step_count[0].astype(jnp.float32)
    firsts = (embed_first, attend_in_first, attend_out_first, expand_first, shrink_first, gains_first, bias_first)
    seconds = (embed_second, attend_in_second, attend_out_second, expand_second, shrink_second, gains_second, bias_second)
    updated = [adam_update(weights[index], grads[index] * factor, firsts[index], seconds[index], step, LEARN_RATES[index]) for index in range(7)]
    return (loss, grad_norm, updated[0][0], updated[0][1], updated[0][2], updated[1][0], updated[1][1], updated[1][2], updated[2][0], updated[2][1], updated[2][2], updated[3][0], updated[3][1], updated[3][2], updated[4][0], updated[4][1], updated[4][2], updated[5][0], updated[5][1], updated[5][2], updated[6][0], updated[6][1], updated[6][2])
```

```python
import jax
import jax.numpy as jnp
from jax import lax
from jax.sharding import PartitionSpec as P

D = 768
H = 12
HD = 64
FF = 3072
V = 18000
LP = 384
LQ = 32
LANE = 128
VALID_PER_QUERY = 5

MARGIN = 1.0
CLIP = 1.0
BETA_ONE = 0.9
BETA_TWO = 0.999
LEARN_RATES = (1.0, 0.02, 0.08, 0.02, 0.02, 1.0, 0.1)
WEIGHT_DECAY = 0.01
ADAM_EPS = 1e-08
NORM_EPS = 1e-05
AXES = ("wide", "narrow")
F32 = jnp.float32
BF16 = jnp.bfloat16
O_Q, O_V, O_O, O_1, O_IN, O_OUT, O_2, O_EMB = (
    0, D, 2 * D, 3 * D, 4 * D, 4 * D + FF, 5 * D + FF, 6 * D + FF
)


def dot(left, right, dims):
    return lax.dot_general(left, right, (dims, ((), ())), preferred_element_type=F32)


def norm_rows(values, gain, shift):
    center = values - jnp.mean(values, axis=-1, keepdims=True)
    spread = jnp.mean(center * center, axis=-1, keepdims=True)
    scale = lax.rsqrt(spread + NORM_EPS)
    hat = center * scale
    return hat * gain + shift, hat, scale


def norm_rows_back(grad, gain, hat, scale):
    scaled = grad * gain
    mean_one = jnp.mean(scaled, axis=-1, keepdims=True)
    mean_two = jnp.mean(scaled * hat, axis=-1, keepdims=True)
    return scale * (scaled - mean_one - hat * mean_two)


def gelu_both(upper):
    cdf = 0.5 * (1.0 + lax.erf(upper * 0.7071067811865476))
    pdf = jnp.exp(-0.5 * upper * upper) * 0.3989422804014327
    return upper * cdf, cdf + upper * pdf


def adam_update(weight, grad, first, second, step, rate):
    first_new = BETA_ONE * first + (1.0 - BETA_ONE) * grad
    second_new = BETA_TWO * second + (1.0 - BETA_TWO) * grad * grad
    first_hat = first_new / (1.0 - BETA_ONE**step)
    second_hat = second_new / (1.0 - BETA_TWO**step)
    weight_new = weight - rate * (
        first_hat / (jnp.sqrt(second_hat) + ADAM_EPS) + WEIGHT_DECAY * weight
    )
    return (weight_new, first_new, second_new)


def gather_axes(value, axis=0):
    return lax.all_gather(value, AXES, axis=axis, tiled=False)


def exchange(blocks):
    return lax.all_to_all(blocks, AXES, 0, 0, tiled=False)


def head_mask(dtype):
    rows = lax.broadcasted_iota(jnp.int32, (H, D), 0)
    cols = lax.broadcasted_iota(jnp.int32, (H, D), 1)
    return (cols // HD == rows).astype(dtype)


def spread_heads(row):
    return row[None, :] * head_mask(row.dtype)


def table_rows(table_t, ids):
    return jnp.take(table_t, ids, axis=1)


def table_sums(values_t, ids, size):
    return jax.ops.segment_sum(values_t.T.astype(F32), ids, num_segments=size).T


def encode_front(emb_t, w_in, w_out, gain, bias, length):
    width = emb_t.shape[1]
    center = emb_t - jnp.mean(emb_t, axis=0, keepdims=True)
    spread = jnp.mean(center * center, axis=0, keepdims=True)
    scale = lax.rsqrt(spread + NORM_EPS)
    hat = center * scale
    x0 = hat * gain[0][:, None] + bias[O_EMB : O_EMB + D][:, None]
    x_low = x0.astype(BF16)
    first_low = x_low[:, 0]
    q = (dot(first_low[None], w_in[:, :D], ((1,), (0,)))[0] + bias[O_Q : O_Q + D]).astype(BF16)
    k = dot(w_in[:, D : 2 * D], x_low, ((0,), (0,))).astype(BF16)
    v = (
        dot(w_in[:, 2 * D :], x_low, ((0,), (0,))) + bias[O_V : O_V + D][:, None]
    ).astype(BF16)
    q_heads = spread_heads(q)
    s = dot(q_heads, k, ((1,), (0,))) * 0.125
    if length < width:
        live = lax.broadcasted_iota(jnp.int32, (1, width), 1) < length
        s = jnp.where(live, s, -1e30)
    peak = jnp.max(s, axis=1, keepdims=True)
    e = jnp.exp(s - peak)
    p = e / jnp.sum(e, axis=1, keepdims=True)
    p_low = p.astype(BF16)
    mixed = dot(p_low, v, ((1,), (1,)))
    a = jnp.sum(mixed * head_mask(F32), axis=0).astype(BF16)
    o = dot(a[None], w_out, ((1,), (0,)))[0] + bias[O_O : O_O + D]
    return x0[:, 0] + o, (hat, scale, x_low, q, k, v, p, p_low, a)


def encode_back(kept, row_grad, w_in, w_out, gain):
    hat, scale, x_low, q, k, v, p, p_low, a = kept
    do = row_grad.astype(BF16)
    da = dot(do[None], w_out, ((1,), (1,)))[0].astype(BF16)
    da_heads = spread_heads(da)
    q_heads = spread_heads(q)
    dp = dot(da_heads, v, ((1,), (0,)))
    ds = (p * (dp - jnp.sum(dp * p, axis=1, keepdims=True))).astype(BF16)
    dq_heads = dot(ds, k, ((1,), (1,)))
    dq = (jnp.sum(dq_heads * head_mask(F32), axis=0) * 0.125).astype(BF16)
    t = dot(ds, x_low, ((1,), (1,))) * 0.125
    w = dot(p_low, x_low, ((1,), (1,)))
    gk = (dot(q_heads, w_in[:, D : 2 * D], ((1,), (1,))) * 0.125).astype(BF16)
    ev = dot(da_heads, w_in[:, 2 * D :], ((1,), (1,))).astype(BF16)
    gx = dot(gk, ds, ((0,), (0,))) + dot(ev, p_low, ((0,), (0,)))
    first = row_grad + dot(dq[None], w_in[:, :D], ((1,), (1,)))[0]
    is_first = lax.broadcasted_iota(jnp.int32, (1, gx.shape[1]), 1) == 0
    gx = gx + jnp.where(is_first, first[:, None], 0.0)
    p_sum = jnp.sum(p_low.astype(F32), axis=1)
    dbv = jnp.repeat(p_sum, HD) * da.astype(F32)
    g_gain = jnp.sum(gx * hat, axis=1)
    g_shift = jnp.sum(gx, axis=1)
    scaled = gx * gain[0][:, None]
    mean_one = jnp.mean(scaled, axis=0, keepdims=True)
    mean_two = jnp.mean(scaled * hat, axis=0, keepdims=True)
    g_emb = scale * (scaled - mean_one - hat * mean_two)
    return g_emb, (t.astype(BF16), w.astype(BF16), q, da, dq, dbv, g_gain, g_shift)


def on_device(
    passage_ids, query_ids, passage_query, kept_mask, neg_count, step_count,
    embed_table, attend_in, attend_out, expand_weight, shrink_weight, norm_gains, bias_terms,
    embed_first, embed_second, attend_in_first, attend_in_second,
    attend_out_first, attend_out_second, expand_first, expand_second,
    shrink_first, shrink_second, gains_first, gains_second, bias_first, bias_second,
):
    narrow = lax.axis_size("narrow")
    nd = lax.axis_size("wide") * narrow
    me = lax.axis_index("wide") * narrow + lax.axis_index("narrow")
    cols = embed_table.shape[1]
    n_slots = passage_query.shape[0]
    nq = query_ids.shape[0] * lax.axis_size("wide")
    n_valid = VALID_PER_QUERY * nq
    cap = -(-n_valid // nd)
    rows_p = cap * nd
    ff_cols = FF // nd

    pid = lax.all_gather(passage_ids, AXES, axis=0, tiled=True)[:n_valid]
    qid = lax.all_gather(query_ids, "wide", axis=0, tiled=True)
    qid_pad = jnp.pad(qid, ((0, 0), (0, LANE - LQ)))
    all_ids = jnp.concatenate([pid.reshape(-1), qid_pad.reshape(-1)])

    table_t = embed_table.T
    table_low = table_t.astype(BF16)
    got = table_rows(table_low, all_ids)
    got_p = got[:, : n_valid * LP].reshape(cols, n_valid, LP)
    got_p = jnp.pad(got_p, ((0, 0), (0, rows_p - n_valid), (0, 0)))
    got_p = got_p.reshape(cols, cap, nd, LP).transpose(2, 0, 1, 3).reshape(nd, cols, cap * LP)
    got_q = got[:, n_valid * LP :].reshape(cols, nq, LANE).transpose(1, 0, 2)
    got_q = jnp.pad(got_q, ((nd - nq, 0), (0, 0), (0, 0)))
    mine = exchange(jnp.concatenate([got_p, got_q], axis=2)).reshape(D, cap * LP + LANE)
    pos = lax.all_gather(table_low[:, V : V + LP], AXES, axis=0, tiled=True).astype(F32)

    w_in = lax.all_gather(attend_in.astype(BF16), AXES, axis=1, tiled=True)
    w_out = lax.all_gather(attend_out.astype(BF16), AXES, axis=1, tiled=True)
    gains = lax.all_gather(norm_gains.astype(BF16), AXES, axis=2, tiled=True).astype(F32)
    bias = lax.all_gather(bias_terms.astype(BF16), AXES, axis=1, tiled=True).astype(F32)
    w_up = exchange(
        expand_weight.astype(BF16).reshape(2, cols, nd, ff_cols).transpose(2, 0, 1, 3)
    )
    w_up = w_up.transpose(1, 0, 2, 3).reshape(2, D, ff_cols)
    w_down = shrink_weight.astype(BF16)

    fronts = []
    for c in range(cap):
        emb = mine[:, c * LP : (c + 1) * LP].astype(F32) + pos
        fronts.append(encode_front(emb, w_in[1], w_out[1], gains[1], bias[1], LP))
    emb = mine[:, cap * LP :].astype(F32) + pos[:, :LANE]
    fronts.append(encode_front(emb, w_in[0], w_out[0], gains[0], bias[0], LQ))
    rows = gather_axes(jnp.stack([f[0] for f in fronts]))
    row_in = (rows[nd - nq :, cap], rows[:, :cap].transpose(1, 0, 2).reshape(rows_p, D))

    mids, ups = [], []
    partial_y = []
    b_in_all = bias[:, O_IN : O_IN + FF].reshape(2, nd, ff_cols)
    b_in = lax.dynamic_index_in_dim(b_in_all, me, 1, False)
    for e in range(2):
        h, hat1, scale1 = norm_rows(row_in[e], gains[e, 1], bias[e, O_1 : O_1 + D])
        h_low = h.astype(BF16)
        upper = dot(h_low, w_up[e], ((1,), (0,))) + b_in[e]
        active, slope = gelu_both(upper)
        f_low = active.astype(BF16)
        partial_y.append(dot(f_low, w_down[e], ((1,), (0,))))
        mids.append((h, hat1, scale1, h_low))
        ups.append((f_low, slope))
    y_all = lax.psum(jnp.concatenate(partial_y), AXES)
    y = (y_all[:nq], y_all[nq:])
    tops = []
    vecs = []
    for e in range(2):
        z, hat2, scale2 = norm_rows(
            mids[e][0] + y[e] + bias[e, O_OUT : O_OUT + D], gains[e, 2], bias[e, O_2 : O_2 + D]
        )
        tops.append((hat2, scale2))
        vecs.append(z.astype(BF16))
    qvec, pvec = vecs

    owner = passage_query[:rows_p]
    kept = kept_mask[:rows_p] == 1
    earlier = jnp.concatenate([jnp.full((1,), -1, jnp.int32), owner[:-1]])
    valid = owner >= 0
    first = valid & (owner != earlier)
    member = owner[None, :] == jnp.arange(nq, dtype=jnp.int32)[:, None]
    positive = member & first[None, :]
    negative = member & jnp.logical_not(first)[None, :] & kept[None, :]
    counts = jnp.sum(member.astype(F32), axis=1) - 1.0
    score_scale = 2.0 * D ** (-0.5)
    scores = dot(qvec, pvec, ((1,), (1,))) * score_scale
    masked = jnp.where(valid[None, :], scores, -1e30)
    peak = jnp.max(masked, axis=1)
    summed = jnp.sum(jnp.where(valid[None, :], jnp.exp(masked - peak[:, None]), 0.0), axis=1)
    logsum = peak + jnp.log(summed)
    pos_score = jnp.sum(jnp.where(positive, scores, 0.0), axis=1)
    margins = MARGIN - pos_score[:, None] + scores
    active_neg = negative & (margins > 0)
    hinge = jnp.sum(jnp.where(active_neg, margins, 0.0), axis=1) / counts
    active_total = jnp.sum(active_neg.astype(F32), axis=1)
    loss = jnp.sum(logsum - pos_score + hinge)
    score_grad = (
        jnp.where(valid[None, :], jnp.exp(scores - logsum[:, None]), 0.0)
        - positive.astype(F32) * (1.0 + active_total / counts)[:, None]
        + active_neg.astype(F32) / counts[:, None]
    )
    score_low = score_grad.astype(BF16)
    vec_grads = (
        (dot(score_low, pvec, ((1,), (0,))) * score_scale).astype(BF16).astype(F32),
        (dot(score_low, qvec, ((0,), (0,))) * score_scale).astype(BF16).astype(F32),
    )

    partial_h = []
    gain_grads = [[None] * 3 for _ in range(2)]
    shifts = [dict() for _ in range(2)]
    top_grads, shrink_grads, du_parts = [], [], []
    for e in range(2):
        hat2, scale2 = tops[e]
        gain_grads[e][2] = jnp.sum(vec_grads[e] * hat2, axis=0)
        shifts[e]["2"] = jnp.sum(vec_grads[e], axis=0)
        g_top = norm_rows_back(vec_grads[e], gains[e, 2], hat2, scale2)
        dy = g_top.astype(BF16)
        shifts[e]["out"] = jnp.sum(dy.astype(F32), axis=0)
        f_low, slope = ups[e]
        shrink_grads.append(dot(f_low, dy, ((0,), (0,))))
        df = dot(dy, w_down[e], ((1,), (1,)))
        du = (slope * df).astype(BF16)
        du_parts.append(du)
        partial_h.append(dot(du, w_up[e], ((1,), (1,))))
        top_grads.append(g_top)
    h_all = lax.psum(jnp.concatenate(partial_h), AXES)
    h_back = (h_all[:nq], h_all[nq:])
    du_all = gather_axes(jnp.concatenate(du_parts))
    du_all = du_all.transpose(1, 0, 2).reshape(nq + rows_p, FF)
    do_rows, expand_grads, mid_grads = [], [], []
    for e in range(2):
        h, hat1, scale1, h_low = mids[e]
        du_full = du_all[:nq] if e == 0 else du_all[nq:]
        shifts[e]["in"] = jnp.sum(du_full.astype(F32), axis=0)
        h_cols = lax.dynamic_slice_in_dim(h_low, me * cols, cols, 1)
        expand_grads.append(dot(h_cols, du_full, ((0,), (0,))))
        g_h = top_grads[e] + h_back[e]
        gain_grads[e][1] = jnp.sum(g_h * hat1, axis=0)
        shifts[e]["1"] = jnp.sum(g_h, axis=0)
        g_mid = norm_rows_back(g_h, gains[e, 1], hat1, scale1)
        mid_grads.append(g_mid)
        do_low = g_mid.astype(BF16)
        do_rows.append(do_low)
        shifts[e]["o"] = jnp.sum(do_low.astype(F32), axis=0)

    mine_p = lax.dynamic_index_in_dim(mid_grads[1].reshape(cap, nd, D), me, 1, False)
    q_at = jnp.clip(me - (nd - nq), 0, nq - 1)
    q_live = (me >= nd - nq).astype(F32)
    mine_q = lax.dynamic_index_in_dim(mid_grads[0], q_at, 0, False) * q_live
    backs = [
        encode_back(fronts[c][1], mine_p[c], w_in[1], w_out[1], gains[1]) for c in range(cap)
    ]
    backs.append(encode_back(fronts[cap][1], mine_q, w_in[0], w_out[0], gains[0]))

    send = jnp.concatenate([b[0] for b in backs], axis=1).astype(BF16).reshape(nd, cols, -1)
    came = exchange(send)
    came_p = came[:, :, : cap * LP].reshape(nd, cols, cap, LP).transpose(1, 2, 0, 3)
    came_p = came_p.reshape(cols, rows_p, LP)[:, :n_valid]
    came_q = came[nd - nq :, :, cap * LP :].transpose(1, 0, 2)
    token_grads = jnp.concatenate(
        [came_p.reshape(cols, n_valid * LP), came_q.reshape(cols, nq * LANE)], axis=1
    )
    table_grad = table_sums(token_grads, all_ids, V + LP)
    pos_grad = jnp.sum(came_p.astype(F32), axis=1)
    pos_grad = pos_grad.at[:, :LANE].add(jnp.sum(came_q.astype(F32), axis=1))
    table_grad = table_grad.at[:, V:].add(pos_grad)

    def by_columns(pick):
        stacked = jnp.stack([pick(i) for i in range(cap + 1)])
        r = stacked.shape[1]
        return exchange(stacked.reshape(cap + 1, r, nd, cols).transpose(2, 0, 1, 3))

    t_all = by_columns(lambda i: backs[i][1][0])
    w_all = by_columns(lambda i: backs[i][1][1])
    x_all = by_columns(lambda i: fronts[i][1][2][:, 0][None])[:, :, 0]
    a_all = by_columns(lambda i: fronts[i][1][8][None])[:, :, 0]
    q_all = gather_axes(jnp.stack([b[1][2] for b in backs]))
    da_all = gather_axes(jnp.stack([b[1][3] for b in backs]))
    dq_all = gather_axes(jnp.stack([b[1][4] for b in backs]))

    def of_encoder(value, e):
        if e == 0:
            return value[nd - nq :, cap]
        return value[:, :cap].reshape((nd * cap,) + value.shape[2:])

    in_grads, out_grads = [], []
    for e in range(2):
        t, w, x, a = (of_encoder(u, e) for u in (t_all, w_all, x_all, a_all))
        q, da, dq = (of_encoder(u, e) for u in (q_all, da_all, dq_all))
        rows_e = q.shape[0]
        qh = q.reshape(rows_e, H, HD)
        dah = da.reshape(rows_e, H, HD)
        g_q = dot(x, dq, ((0,), (0,)))
        g_k = jnp.einsum("phi,phd->ihd", t, qh, preferred_element_type=F32).reshape(cols, D)
        g_v = jnp.einsum("phi,phd->ihd", w, dah, preferred_element_type=F32).reshape(cols, D)
        in_grads.append(jnp.concatenate([g_q, g_k, g_v], axis=1))
        do_e = do_rows[e] if e == 0 else do_rows[e].reshape(cap, nd, D).transpose(1, 0, 2).reshape(nd * cap, D)
        out_grads.append(dot(a, do_e, ((0,), (0,))))
        shifts[e]["q"] = jnp.sum(dq.astype(F32), axis=0)
    small = jnp.stack(
        [
            jnp.stack([backs[cap][1][j] for j in (5, 6, 7)]),
            jnp.stack([sum(backs[c][1][j] for c in range(cap)) for j in (5, 6, 7)]),
        ]
    )
    small = lax.psum(small, AXES)
    gain_grad = jnp.stack([jnp.stack([small[e, 1], gain_grads[e][1], gain_grads[e][2]]) for e in range(2)])
    bias_grad = jnp.stack(
        [
            jnp.concatenate(
                [shifts[e]["q"], small[e, 0], shifts[e]["o"], shifts[e]["1"], shifts[e]["in"],
                 shifts[e]["out"], shifts[e]["2"], small[e, 2]]
            )
            for e in range(2)
        ]
    )
    grads = (
        table_grad.T,
        jnp.stack(in_grads),
        jnp.stack(out_grads),
        jnp.stack(expand_grads),
        jnp.stack(shrink_grads),
        lax.dynamic_slice_in_dim(gain_grad, me * cols, cols, 2),
        lax.dynamic_slice_in_dim(bias_grad, me * bias_terms.shape[1], bias_terms.shape[1], 1),
    )
    local_squares = sum(jnp.sum(g * g) for g in grads)
    grad_norm = jnp.sqrt(lax.psum(local_squares, AXES))
    factor = CLIP / jnp.maximum(grad_norm, CLIP)
    step = step_count[0].astype(F32)
    masters = (embed_table, attend_in, attend_out, expand_weight, shrink_weight, norm_gains, bias_terms)
    firsts = (embed_first, attend_in_first, attend_out_first, expand_first, shrink_first, gains_first, bias_first)
    seconds = (embed_second, attend_in_second, attend_out_second, expand_second, shrink_second, gains_second, bias_second)
    results = [loss, grad_norm]
    for index in range(7):
        results.extend(
            adam_update(masters[index], grads[index] * factor, firsts[index], seconds[index], step, LEARN_RATES[index])
        )
    return tuple(results)


def solution(mesh):
    both = ("wide", "narrow")
    weight_specs = (P(None, both),) + (P(None, both, None),) * 4 + (P(None, None, both), P(None, both))
    pairs = tuple(s for spec in weight_specs for s in (spec, spec))
    in_specs = (P(both, None), P("wide", None), P(), P(), P("wide"), P()) + weight_specs + pairs
    out_specs = (P(), P()) + tuple(s for spec in weight_specs for s in (spec, spec, spec))
    return jax.shard_map(on_device, mesh=mesh, in_specs=in_specs, out_specs=out_specs, check_vma=False)
```

```python
import functools

import jax
import jax.numpy as jnp
from jax import lax
from jax.experimental import pallas as pl
from jax.experimental.pallas import tpu as pltpu
from jax.sharding import PartitionSpec as P

D = 768
H = 12
HD = 64
FF = 3072
V = 18000
LP = 384
LQ = 32
LANE = 128
VALID_PER_QUERY = 5

MARGIN = 1.0
CLIP = 1.0
BETA_ONE = 0.9
BETA_TWO = 0.999
LEARN_RATES = (1.0, 0.02, 0.08, 0.02, 0.02, 1.0, 0.1)
WEIGHT_DECAY = 0.01
ADAM_EPS = 1e-08
NORM_EPS = 1e-05
AXES = ("wide", "narrow")
F32 = jnp.float32
BF16 = jnp.bfloat16
O_Q, O_V, O_O, O_1, O_IN, O_OUT, O_2, O_EMB = (
    0, D, 2 * D, 3 * D, 4 * D, 4 * D + FF, 5 * D + FF, 6 * D + FF
)


def dot(left, right, dims):
    return lax.dot_general(left, right, (dims, ((), ())), preferred_element_type=F32)


def norm_rows(values, gain, shift):
    center = values - jnp.mean(values, axis=-1, keepdims=True)
    spread = jnp.mean(center * center, axis=-1, keepdims=True)
    scale = lax.rsqrt(spread + NORM_EPS)
    hat = center * scale
    return hat * gain + shift, hat, scale


def norm_rows_back(grad, gain, hat, scale):
    scaled = grad * gain
    mean_one = jnp.mean(scaled, axis=-1, keepdims=True)
    mean_two = jnp.mean(scaled * hat, axis=-1, keepdims=True)
    return scale * (scaled - mean_one - hat * mean_two)


def gelu_both(upper):
    cdf = 0.5 * (1.0 + lax.erf(upper * 0.7071067811865476))
    pdf = jnp.exp(-0.5 * upper * upper) * 0.3989422804014327
    return upper * cdf, cdf + upper * pdf


def adam_update(weight, grad, first, second, step, rate):
    first_new = BETA_ONE * first + (1.0 - BETA_ONE) * grad
    second_new = BETA_TWO * second + (1.0 - BETA_TWO) * grad * grad
    first_hat = first_new / (1.0 - BETA_ONE**step)
    second_hat = second_new / (1.0 - BETA_TWO**step)
    weight_new = weight - rate * (
        first_hat / (jnp.sqrt(second_hat) + ADAM_EPS) + WEIGHT_DECAY * weight
    )
    return (weight_new, first_new, second_new)


MESH = pl.DeviceIdType.MESH
HASH = 512


class Send:
    def __init__(self, src, dst, take, put, many_src, many_dst, sources, targets):
        self.src, self.dst, self.take, self.put = src, dst, take, put
        self.many_src, self.many_dst = many_src, many_dst
        self.sources, self.targets = sources, targets


def inside(index, span):
    return jnp.logical_and(index >= span[0], index < span[1])


def comm_body(sends, n_in, n_out, nd, narrow, *refs):
    ins, outs = refs[:n_in], refs[n_in : n_in + n_out]
    send_sem, recv_sem, own_sem = refs[n_in + n_out :]
    me = lax.axis_index("wide") * narrow + lax.axis_index("narrow")
    barrier = pltpu.get_barrier_semaphore()

    def greet(k, carry):
        t = lax.rem(me + k, nd)
        pl.semaphore_signal(
            barrier, inc=1, device_id=(t // narrow, lax.rem(t, narrow)), device_id_type=MESH
        )
        return carry

    lax.fori_loop(1, nd, greet, 0)
    pl.semaphore_wait(barrier, nd - 1)

    def push(k, carry):
        t = lax.rem(me + k, nd)
        for i, s in enumerate(sends):

            @pl.when(jnp.logical_and(inside(me, s.sources), inside(t, s.targets)))
            def _():
                pltpu.make_async_remote_copy(
                    src_ref=s.take(ins[s.src], me, t),
                    dst_ref=s.put(outs[s.dst], me, t),
                    send_sem=send_sem.at[i],
                    recv_sem=recv_sem.at[i],
                    device_id=(t // narrow, lax.rem(t, narrow)),
                    device_id_type=MESH,
                ).start()

        return carry

    lax.fori_loop(1, nd, push, 0)
    for i, s in enumerate(sends):
        both = jnp.logical_and(inside(me, s.sources), inside(me, s.targets))

        @pl.when(both)
        def _():
            own = pltpu.make_async_copy(
                s.take(ins[s.src], me, me), s.put(outs[s.dst], me, me), own_sem.at[i]
            )
            own.start()
            own.wait()

    for i, s in enumerate(sends):
        n_t = s.targets[1] - s.targets[0]
        n_s = s.sources[1] - s.sources[0]
        is_s, is_t = inside(me, s.sources), inside(me, s.targets)
        for own in (0, 1):
            mine = is_t if own else jnp.logical_not(is_t)
            if n_t - own > 0:

                @pl.when(jnp.logical_and(is_s, mine))
                def _():
                    view = s.many_src(ins[s.src], n_t - own) if s.many_src(ins[s.src], 1) is not None else outs[s.dst].at[pl.ds(0, n_t - own)]
                    pltpu.make_async_copy(view, view, send_sem.at[i]).wait()

            mine = is_s if own else jnp.logical_not(is_s)
            if n_s - own > 0:

                @pl.when(jnp.logical_and(is_t, mine))
                def _():
                    view = s.many_dst(outs[s.dst], n_s - own)
                    pltpu.make_async_copy(view, view, recv_sem.at[i]).wait()


def comm(collective, arrays, out_shapes, sends, nd, narrow):
    vmem = pl.BlockSpec(memory_space=pltpu.VMEM)
    n = len(sends)
    return pl.pallas_call(
        functools.partial(comm_body, sends, len(arrays), len(out_shapes), nd, narrow),
        out_shape=[jax.ShapeDtypeStruct(s, d) for s, d in out_shapes],
        in_specs=[vmem] * len(arrays),
        out_specs=[vmem] * len(out_shapes),
        scratch_shapes=[
            pltpu.SemaphoreType.DMA((n,)),
            pltpu.SemaphoreType.DMA((n,)),
            pltpu.SemaphoreType.DMA((n,)),
        ],
        compiler_params=pltpu.CompilerParams(collective_id=collective, has_side_effects=True),
    )(*arrays)


def send_all(src, dst, nd):
    return Send(
        src, dst,
        lambda ref, s, t: ref,
        lambda ref, s, t: ref.at[s],
        lambda ref, n: None, lambda ref, n: ref.at[pl.ds(0, n)],
        (0, nd), (0, nd),
    )


def send_blocks(src, dst, nd):
    return Send(
        src, dst,
        lambda ref, s, t: ref.at[t],
        lambda ref, s, t: ref.at[s],
        lambda ref, n: ref.at[pl.ds(0, n)], lambda ref, n: ref.at[pl.ds(0, n)],
        (0, nd), (0, nd),
    )


def stack_pairs(pieces, store):
    rows = pieces[0].shape[0]
    for i in range(0, len(pieces), 2):
        store(i * rows, jnp.concatenate(pieces[i : i + 2], axis=0))


def gather_body(rows, blocks, table_ref, ids_ref, out_ref, stacked):
    @pl.when(pl.program_id(0) == 0)
    def _():
        pieces = [
            table_ref[:, b * HASH : (b + 1) * HASH].astype(F32) for b in range(blocks)
        ]

        def store(row, value):
            stacked[row : row + value.shape[0], :] = value.astype(BF16)

        stack_pairs(pieces, store)

    ids = ids_ref[0]
    low = ids & (HASH - 1)
    high = ids >> (HASH.bit_length() - 1)
    width = ids.shape[1]
    hot = (lax.broadcasted_iota(jnp.int32, (HASH, width), 0) == low).astype(F32).astype(BF16)
    picked = jnp.dot(stacked[...], hot, preferred_element_type=F32)
    value = jnp.zeros((rows, width), F32)
    for b in range(blocks):
        value = jnp.where(high == b, picked[b * rows : (b + 1) * rows], value)
    out_ref[...] = value.astype(BF16)


def table_rows(table, ids):
    rows, total = table.shape
    tokens = ids.shape[0]
    tile = 512
    blocks = total // HASH
    return pl.pallas_call(
        functools.partial(gather_body, rows, blocks),
        grid=(tokens // tile,),
        out_shape=jax.ShapeDtypeStruct((rows, tokens), BF16),
        in_specs=[
            pl.BlockSpec((rows, total), lambda i: (0, 0)),
            pl.BlockSpec((1, 1, tile), lambda i: (i, 0, 0)),
        ],
        out_specs=pl.BlockSpec((rows, tile), lambda i: (0, i)),
        scratch_shapes=[pltpu.VMEM((blocks * rows, HASH), BF16)],
        name="table_rows",
    )(table, ids.reshape(tokens // tile, 1, tile))


def scatter_body(rows, blocks, values_ref, ids_ref, out_ref, spread, acc):
    step = pl.program_id(0)
    ids = ids_ref[0]
    low = ids & (HASH - 1)
    high = ids >> (HASH.bit_length() - 1)
    width = ids.shape[1]
    values = values_ref[...].astype(F32)
    pieces = [jnp.where(high == b, values, 0.0) for b in range(blocks)]

    def store(row, value):
        spread[row : row + value.shape[0], :] = value.astype(BF16)

    stack_pairs(pieces, store)
    hot = (lax.broadcasted_iota(jnp.int32, (HASH, width), 0) == low).astype(F32).astype(BF16)
    part = lax.dot_general(
        spread[...], hot, (((1,), (1,)), ((), ())), preferred_element_type=F32
    )

    @pl.when(step == 0)
    def _():
        acc[...] = part

    @pl.when(step > 0)
    def _():
        acc[...] += part

    @pl.when(step == pl.num_programs(0) - 1)
    def _():
        for b in range(blocks):
            out_ref[:, b * HASH : (b + 1) * HASH] = acc[b * rows : (b + 1) * rows, :]


def table_sums(values, ids, total):
    rows, tokens = values.shape
    tile = 1024
    blocks = total // HASH
    return pl.pallas_call(
        functools.partial(scatter_body, rows, blocks),
        grid=(tokens // tile,),
        out_shape=jax.ShapeDtypeStruct((rows, total), F32),
        in_specs=[
            pl.BlockSpec((rows, tile), lambda i: (0, i)),
            pl.BlockSpec((1, 1, tile), lambda i: (i, 0, 0)),
        ],
        out_specs=pl.BlockSpec((rows, total), lambda i: (0, 0)),
        scratch_shapes=[
            pltpu.VMEM((blocks * rows, tile), BF16),
            pltpu.VMEM((blocks * rows, HASH), F32),
        ],
        name="table_sums",
    )(values, ids.reshape(tokens // tile, 1, tile))


def head_mask(dtype):
    rows = lax.broadcasted_iota(jnp.int32, (H, D), 0)
    cols = lax.broadcasted_iota(jnp.int32, (H, D), 1)
    return (cols // HD == rows).astype(dtype)


def spread_heads(row):
    return row[None, :] * head_mask(row.dtype)


def encode_front(emb_t, w_in, w_out, gain, bias, length):
    width = emb_t.shape[1]
    center = emb_t - jnp.mean(emb_t, axis=0, keepdims=True)
    spread = jnp.mean(center * center, axis=0, keepdims=True)
    scale = lax.rsqrt(spread + NORM_EPS)
    hat = center * scale
    x0 = hat * gain[0][:, None] + bias[O_EMB : O_EMB + D][:, None]
    x_low = x0.astype(BF16)
    first_low = x_low[:, 0]
    q = (dot(first_low[None], w_in[:, :D], ((1,), (0,)))[0] + bias[O_Q : O_Q + D]).astype(BF16)
    k = dot(w_in[:, D : 2 * D], x_low, ((0,), (0,))).astype(BF16)
    v = (
        dot(w_in[:, 2 * D :], x_low, ((0,), (0,))) + bias[O_V : O_V + D][:, None]
    ).astype(BF16)
    q_heads = spread_heads(q)
    s = dot(q_heads, k, ((1,), (0,))) * 0.125
    if length < width:
        live = lax.broadcasted_iota(jnp.int32, (1, width), 1) < length
        s = jnp.where(live, s, -1e30)
    peak = jnp.max(s, axis=1, keepdims=True)
    e = jnp.exp(s - peak)
    p = e / jnp.sum(e, axis=1, keepdims=True)
    p_low = p.astype(BF16)
    mixed = dot(p_low, v, ((1,), (1,)))
    a = jnp.sum(mixed * head_mask(F32), axis=0).astype(BF16)
    o = dot(a[None], w_out, ((1,), (0,)))[0] + bias[O_O : O_O + D]
    return x0[:, 0] + o, (hat, scale, x_low, q, k, v, p, p_low, a)


def encode_back(kept, row_grad, w_in, w_out, gain):
    hat, scale, x_low, q, k, v, p, p_low, a = kept
    do = row_grad.astype(BF16)
    da = dot(do[None], w_out, ((1,), (1,)))[0].astype(BF16)
    da_heads = spread_heads(da)
    q_heads = spread_heads(q)
    dp = dot(da_heads, v, ((1,), (0,)))
    ds = (p * (dp - jnp.sum(dp * p, axis=1, keepdims=True))).astype(BF16)
    dq_heads = dot(ds, k, ((1,), (1,)))
    dq = (jnp.sum(dq_heads * head_mask(F32), axis=0) * 0.125).astype(BF16)
    t = dot(ds, x_low, ((1,), (1,))) * 0.125
    w = dot(p_low, x_low, ((1,), (1,)))
    gk = (dot(q_heads, w_in[:, D : 2 * D], ((1,), (1,))) * 0.125).astype(BF16)
    ev = dot(da_heads, w_in[:, 2 * D :], ((1,), (1,))).astype(BF16)
    gx = dot(gk, ds, ((0,), (0,))) + dot(ev, p_low, ((0,), (0,)))
    first = row_grad + dot(dq[None], w_in[:, :D], ((1,), (1,)))[0]
    is_first = lax.broadcasted_iota(jnp.int32, (1, gx.shape[1]), 1) == 0
    gx = gx + jnp.where(is_first, first[:, None], 0.0)
    p_sum = jnp.sum(p_low.astype(F32), axis=1)
    dbv = jnp.repeat(p_sum, HD) * da.astype(F32)
    g_gain = jnp.sum(gx * hat, axis=1)
    g_shift = jnp.sum(gx, axis=1)
    scaled = gx * gain[0][:, None]
    mean_one = jnp.mean(scaled, axis=0, keepdims=True)
    mean_two = jnp.mean(scaled * hat, axis=0, keepdims=True)
    g_emb = scale * (scaled - mean_one - hat * mean_two)
    return g_emb, (t.astype(BF16), w.astype(BF16), q, da, dq, dbv, g_gain, g_shift)


def on_device(
    passage_ids, query_ids, passage_query, kept_mask, neg_count, step_count,
    embed_table, attend_in, attend_out, expand_weight, shrink_weight, norm_gains, bias_terms,
    embed_first, embed_second, attend_in_first, attend_in_second,
    attend_out_first, attend_out_second, expand_first, expand_second,
    shrink_first, shrink_second, gains_first, gains_second, bias_first, bias_second,
):
    narrow = lax.axis_size("narrow")
    nd = lax.axis_size("wide") * narrow
    me = lax.axis_index("wide") * narrow + lax.axis_index("narrow")
    cols = embed_table.shape[1]
    n_slots = passage_query.shape[0]
    nq = query_ids.shape[0] * lax.axis_size("wide")
    n_valid = VALID_PER_QUERY * nq
    cap = -(-n_valid // nd)
    rows_p = cap * nd
    ff_cols = FF // nd

    exch = functools.partial(comm, nd=nd, narrow=narrow)
    rows_c = -(-cols // 8) * 8
    n_ids = passage_ids.shape[0] + query_ids.shape[0]
    small_width = max(cols, bias_terms.shape[1], 1)
    small_width = -(-small_width // LANE) * LANE

    def widen(value, width):
        return jnp.pad(value, ((0, 0), (0, width - value.shape[1])))

    ids_mine = jnp.concatenate([passage_ids, widen(query_ids, LP)])
    small_mine = jnp.concatenate(
        [widen(norm_gains.reshape(6, cols), small_width), widen(bias_terms, small_width)]
    ).astype(BF16)
    ids_got, small_got = exch(
        1,
        [ids_mine, small_mine],
        [((nd, n_ids, LP), jnp.int32), ((nd, 8, small_width), BF16)],
        [send_all(0, 0, nd), send_all(1, 1, nd)],
    )
    n_own = passage_ids.shape[0]
    pid = ids_got[:, :n_own].reshape(n_slots, LP)[:n_valid]
    qid = ids_got.reshape(-1, narrow, n_ids, LP)[:, 0, n_own:, :LANE].reshape(nq, LANE)
    all_ids = jnp.concatenate([pid.reshape(-1), qid.reshape(-1)])
    gains = small_got[:, :6, :cols].transpose(1, 0, 2).reshape(2, 3, D).astype(F32)
    bias = small_got[:, 6:, : bias_terms.shape[1]].transpose(1, 0, 2).reshape(2, -1).astype(F32)

    table_t = embed_table.T
    table_low = table_t.astype(BF16)
    vocab = V + LP
    total = -(-vocab // HASH) * HASH
    table_pad = jnp.pad(table_low, ((0, rows_c - cols), (0, total - vocab)))
    got = table_rows(table_pad, all_ids)
    pos_mine = table_pad[:, V : V + LP]
    up_mine = expand_weight.astype(BF16).reshape(2 * cols, nd, ff_cols).transpose(1, 0, 2)
    q_from = n_valid * LP
    width = cap * LP + LANE

    def passage_move(c, forward):
        span = (0, min(nd, n_valid - c * nd))
        if forward:
            return Send(
                0, 0,
                lambda ref, s, t: ref.at[:, pl.ds(pl.multiple_of((c * nd + t) * LP, LANE), LP)],
                lambda ref, s, t: ref.at[s, :, pl.ds(c * LP, LP)],
                lambda ref, n: ref.at[:, pl.ds(0, n * LP)],
                lambda ref, n: ref.at[pl.ds(0, n), :, pl.ds(0, LP)],
                (0, nd), span,
            )
        return Send(
            0, 0,
            lambda ref, s, t: ref.at[t, :, pl.ds(c * LP, LP)],
            lambda ref, s, t: ref.at[:, pl.ds(pl.multiple_of((c * nd + s) * LP, LANE), LP)],
            lambda ref, n: ref.at[pl.ds(0, n), :, pl.ds(0, LP)],
            lambda ref, n: ref.at[:, pl.ds(0, n * LP)],
            span, (0, nd),
        )

    def query_move(forward):
        span = (nd - nq, nd)
        if forward:
            return Send(
                0, 0,
                lambda ref, s, t: ref.at[
                    :, pl.ds(pl.multiple_of(q_from + (t - (nd - nq)) * LANE, LANE), LANE)
                ],
                lambda ref, s, t: ref.at[s, :, pl.ds(cap * LP, LANE)],
                lambda ref, n: ref.at[:, pl.ds(0, n * LANE)],
                lambda ref, n: ref.at[pl.ds(0, n), :, pl.ds(0, LANE)],
                (0, nd), span,
            )
        return Send(
            0, 0,
            lambda ref, s, t: ref.at[t, :, pl.ds(cap * LP, LANE)],
            lambda ref, s, t: ref.at[
                :, pl.ds(pl.multiple_of(q_from + (s - (nd - nq)) * LANE, LANE), LANE)
            ],
            lambda ref, n: ref.at[pl.ds(0, n), :, pl.ds(0, LANE)],
            lambda ref, n: ref.at[:, pl.ds(0, n * LANE)],
            span, (0, nd),
        )

    mine, pos, w_up = exch(
        2,
        [got, pos_mine, up_mine],
        [((nd, rows_c, width), BF16), ((nd, rows_c, LP), BF16), ((nd, 2 * cols, ff_cols), BF16)],
        [passage_move(c, True) for c in range(cap)]
        + [query_move(True), send_all(1, 1, nd), send_blocks(2, 2, nd)],
    )
    live = jnp.concatenate(
        [jnp.broadcast_to(c * nd + me < n_valid, (LP,)) for c in range(cap)]
        + [jnp.broadcast_to(me >= nd - nq, (LANE,))]
    )
    mine = jnp.where(live, mine[:, :cols].reshape(D, width), 0)
    pos = pos[:, :cols].reshape(D, LP).astype(F32)
    w_up = w_up.reshape(nd, 2, cols, ff_cols).transpose(1, 0, 2, 3).reshape(2, D, ff_cols)
    w_down = shrink_weight.astype(BF16)
    w_in = lax.all_gather(attend_in.astype(BF16), AXES, axis=1, tiled=True)
    w_out = lax.all_gather(attend_out.astype(BF16), AXES, axis=1, tiled=True)

    fronts = []
    for c in range(cap):
        emb = mine[:, c * LP : (c + 1) * LP].astype(F32) + pos
        fronts.append(encode_front(emb, w_in[1], w_out[1], gains[1], bias[1], LP))
    emb = mine[:, cap * LP :].astype(F32) + pos[:, :LANE]
    fronts.append(encode_front(emb, w_in[0], w_out[0], gains[0], bias[0], LQ))
    (rows,) = exch(
        3, [jnp.stack([f[0] for f in fronts])], [((nd, cap + 1, D), F32)], [send_all(0, 0, nd)]
    )
    row_in = (rows[nd - nq :, cap], rows[:, :cap].transpose(1, 0, 2).reshape(rows_p, D))

    def by_owner(queries, passages):
        q_part = jnp.pad(queries, ((nd - nq, 0), (0, 0)))[:, None]
        return jnp.concatenate([passages.reshape(cap, nd, D).transpose(1, 0, 2), q_part], axis=1)

    def to_rows(blocks):
        return (
            blocks[nd - nq :, cap],
            blocks[:, :cap].transpose(1, 0, 2).reshape(rows_p, D),
        )


    mids, ups = [], []
    partial_y = []
    b_in_all = bias[:, O_IN : O_IN + FF].reshape(2, nd, ff_cols)
    b_in = lax.dynamic_index_in_dim(b_in_all, me, 1, False)
    for e in range(2):
        h, hat1, scale1 = norm_rows(row_in[e], gains[e, 1], bias[e, O_1 : O_1 + D])
        h_low = h.astype(BF16)
        upper = dot(h_low, w_up[e], ((1,), (0,))) + b_in[e]
        active, slope = gelu_both(upper)
        f_low = active.astype(BF16)
        partial_y.append(dot(f_low, w_down[e], ((1,), (0,))))
        mids.append((h, hat1, scale1, h_low))
        ups.append((f_low, slope))
    (y_parts,) = exch(
        4, [by_owner(*partial_y)], [((nd, cap + 1, D), F32)], [send_blocks(0, 0, nd)]
    )
    (y_all,) = exch(
        5, [jnp.sum(y_parts, axis=0)], [((nd, cap + 1, D), F32)], [send_all(0, 0, nd)]
    )
    y = to_rows(y_all)
    tops = []
    vecs = []
    for e in range(2):
        z, hat2, scale2 = norm_rows(
            mids[e][0] + y[e] + bias[e, O_OUT : O_OUT + D], gains[e, 2], bias[e, O_2 : O_2 + D]
        )
        tops.append((hat2, scale2))
        vecs.append(z.astype(BF16))
    qvec, pvec = vecs

    owner = passage_query[:rows_p]
    kept = kept_mask[:rows_p] == 1
    earlier = jnp.concatenate([jnp.full((1,), -1, jnp.int32), owner[:-1]])
    valid = owner >= 0
    first = valid & (owner != earlier)
    member = owner[None, :] == jnp.arange(nq, dtype=jnp.int32)[:, None]
    positive = member & first[None, :]
    negative = member & jnp.logical_not(first)[None, :] & kept[None, :]
    counts = jnp.sum(member.astype(F32), axis=1) - 1.0
    score_scale = 2.0 * D ** (-0.5)
    scores = dot(qvec, pvec, ((1,), (1,))) * score_scale
    masked = jnp.where(valid[None, :], scores, -1e30)
    peak = jnp.max(masked, axis=1)
    summed = jnp.sum(jnp.where(valid[None, :], jnp.exp(masked - peak[:, None]), 0.0), axis=1)
    logsum = peak + jnp.log(summed)
    pos_score = jnp.sum(jnp.where(positive, scores, 0.0), axis=1)
    margins = MARGIN - pos_score[:, None] + scores
    active_neg = negative & (margins > 0)
    hinge = jnp.sum(jnp.where(active_neg, margins, 0.0), axis=1) / counts
    active_total = jnp.sum(active_neg.astype(F32), axis=1)
    loss = jnp.sum(logsum - pos_score + hinge)
    score_grad = (
        jnp.where(valid[None, :], jnp.exp(scores - logsum[:, None]), 0.0)
        - positive.astype(F32) * (1.0 + active_total / counts)[:, None]
        + active_neg.astype(F32) / counts[:, None]
    )
    score_low = score_grad.astype(BF16)
    vec_grads = (
        (dot(score_low, pvec, ((1,), (0,))) * score_scale).astype(BF16).astype(F32),
        (dot(score_low, qvec, ((0,), (0,))) * score_scale).astype(BF16).astype(F32),
    )

    partial_h = []
    gain_grads = [[None] * 3 for _ in range(2)]
    shifts = [dict() for _ in range(2)]
    top_grads, shrink_grads, du_parts = [], [], []
    for e in range(2):
        hat2, scale2 = tops[e]
        gain_grads[e][2] = jnp.sum(vec_grads[e] * hat2, axis=0)
        shifts[e]["2"] = jnp.sum(vec_grads[e], axis=0)
        g_top = norm_rows_back(vec_grads[e], gains[e, 2], hat2, scale2)
        dy = g_top.astype(BF16)
        shifts[e]["out"] = jnp.sum(dy.astype(F32), axis=0)
        f_low, slope = ups[e]
        shrink_grads.append(dot(f_low, dy, ((0,), (0,))))
        df = dot(dy, w_down[e], ((1,), (1,)))
        du = (slope * df).astype(BF16)
        du_parts.append(du)
        partial_h.append(dot(du, w_up[e], ((1,), (1,))))
        top_grads.append(g_top)
    du_mine = jnp.concatenate(du_parts)
    h_parts, du_all = exch(
        6,
        [by_owner(*partial_h), du_mine],
        [((nd, cap + 1, D), F32), ((nd, nq + rows_p, ff_cols), BF16)],
        [send_blocks(0, 0, nd), send_all(1, 1, nd)],
    )
    h_mine = jnp.sum(h_parts, axis=0)
    top_mine = lax.dynamic_index_in_dim(by_owner(*top_grads), me, 0, False)
    rows_mine = lax.dynamic_index_in_dim(rows, me, 0, False)
    is_q = (me >= nd - nq).astype(F32)
    has = jnp.stack([(c * nd + me < n_valid).astype(F32) for c in range(cap)] + [is_q])
    g_h = (top_mine + h_mine) * has[:, None]
    gain_one = jnp.stack([gains[1, 1]] * cap + [gains[0, 1]])
    shift_one = jnp.stack([bias[1, O_1 : O_1 + D]] * cap + [bias[0, O_1 : O_1 + D]])
    _, hat_mine, scale_mine = norm_rows(rows_mine, gain_one, shift_one)
    g_mid = norm_rows_back(g_h, gain_one, hat_mine, scale_mine)
    gain_mid = g_h * hat_mine
    do_mine = g_mid.astype(BF16)
    backs = [
        encode_back(
            fronts[c][1], g_mid[c], w_in[1 if c < cap else 0], w_out[1 if c < cap else 0],
            gains[1 if c < cap else 0],
        )
        for c in range(cap + 1)
    ]

    def both_encoders(pick):
        return jnp.stack([pick(cap), sum(pick(c) for c in range(cap))])

    sums = jnp.concatenate(
        [both_encoders(lambda i, j=j: backs[i][1][j]) for j in (5, 6, 7)]
        + [both_encoders(lambda i: gain_mid[i]), both_encoders(lambda i: g_h[i])]
    )
    line = jnp.concatenate(
        [jnp.stack([b[1][j] for b in backs]) for j in (2, 3, 4)] + [do_mine, sums.astype(BF16)]
    )
    n_line = 4 * (cap + 1) + 10
    factor_t = jnp.concatenate(
        [b[1][0] for b in backs] + [b[1][1] for b in backs]
        + [f[1][2][:, 0][None] for f in fronts] + [f[1][8][None] for f in fronts]
    )
    n_factor = factor_t.shape[0]
    f_pad = -(-n_factor // LANE) * LANE
    factor_cols = jnp.pad(factor_t, ((0, f_pad - n_factor), (0, 0))).T

    def pad_rows(value):
        value = value.reshape(nd, cols, value.shape[1])
        return jnp.pad(value, ((0, 0), (0, rows_c - cols), (0, 0)))

    send = pad_rows(jnp.concatenate([b[0] for b in backs], axis=1).astype(BF16))
    token_grads, factors, lines = exch(
        7,
        [send, pad_rows(factor_cols), line],
        [
            ((rows_c, n_valid * LP + nq * LANE), BF16),
            ((nd, rows_c, f_pad), BF16),
            ((nd, n_line, D), BF16),
        ],
        [passage_move(c, False) for c in range(cap)]
        + [query_move(False), send_blocks(1, 1, nd), send_all(2, 2, nd)],
    )
    table_grad = table_sums(token_grads, all_ids, total)[:cols, :vocab]
    token_grads = token_grads[:cols].astype(F32)
    pos_grad = jnp.sum(token_grads[:, :q_from].reshape(cols, n_valid, LP), axis=1)
    pos_grad = pos_grad.at[:, :LANE].add(
        jnp.sum(token_grads[:, q_from:].reshape(cols, nq, LANE), axis=1)
    )
    table_grad = table_grad.at[:, V:].add(pos_grad)

    step_h = (cap + 1) * H
    factors = factors[:, :cols].transpose(0, 2, 1)
    t_all = factors[:, :step_h].reshape(nd, cap + 1, H, cols)
    w_all = factors[:, step_h : 2 * step_h].reshape(nd, cap + 1, H, cols)
    x_all = factors[:, 2 * step_h : 2 * step_h + cap + 1]
    a_all = factors[:, 2 * step_h + cap + 1 : 2 * step_h + 2 * (cap + 1)]
    q_all, da_all, dq_all, do_all = (
        lines[:, j * (cap + 1) : (j + 1) * (cap + 1)] for j in range(4)
    )
    sums = jnp.sum(lines[:, 4 * (cap + 1) :].astype(F32), axis=0).reshape(5, 2, D)

    def of_encoder(value, e):
        if e == 0:
            return value[nd - nq :, cap]
        return value[:, :cap].reshape((nd * cap,) + value.shape[2:])

    du_all = du_all.transpose(1, 0, 2).reshape(nq + rows_p, FF)
    in_grads, out_grads, expand_grads = [], [], []
    for e in range(2):
        du_full = du_all[:nq] if e == 0 else du_all[nq:]
        shifts[e]["in"] = jnp.sum(du_full.astype(F32), axis=0)
        h_cols = lax.dynamic_slice_in_dim(mids[e][3], me * cols, cols, 1)
        expand_grads.append(dot(h_cols, du_full, ((0,), (0,))))
        t, w, x, a = (of_encoder(u, e) for u in (t_all, w_all, x_all, a_all))
        q, da, dq, do = (of_encoder(u, e) for u in (q_all, da_all, dq_all, do_all))
        rows_e = q.shape[0]
        qh = q.reshape(rows_e, H, HD)
        dah = da.reshape(rows_e, H, HD)
        g_q = dot(x, dq, ((0,), (0,)))
        g_k = jnp.einsum("phi,phd->ihd", t, qh, preferred_element_type=F32).reshape(cols, D)
        g_v = jnp.einsum("phi,phd->ihd", w, dah, preferred_element_type=F32).reshape(cols, D)
        in_grads.append(jnp.concatenate([g_q, g_k, g_v], axis=1))
        out_grads.append(dot(a, do, ((0,), (0,))))
        shifts[e]["q"] = jnp.sum(dq.astype(F32), axis=0)
        shifts[e]["o"] = jnp.sum(do.astype(F32), axis=0)
    gain_grad = jnp.stack(
        [jnp.stack([sums[1, e], sums[3, e], gain_grads[e][2]]) for e in range(2)]
    )
    bias_grad = jnp.stack(
        [
            jnp.concatenate(
                [shifts[e]["q"], sums[0, e], shifts[e]["o"], sums[4, e], shifts[e]["in"],
                 shifts[e]["out"], shifts[e]["2"], sums[2, e]]
            )
            for e in range(2)
        ]
    )
    grads = (
        table_grad.T,
        jnp.stack(in_grads),
        jnp.stack(out_grads),
        jnp.stack(expand_grads),
        jnp.stack(shrink_grads),
        lax.dynamic_slice_in_dim(gain_grad, me * cols, cols, 2),
        lax.dynamic_slice_in_dim(bias_grad, me * bias_terms.shape[1], bias_terms.shape[1], 1),
    )
    local_squares = sum(jnp.sum(g * g) for g in grads)
    (squares,) = exch(
        8, [jnp.broadcast_to(local_squares, (8, LANE))], [((nd, 8, LANE), F32)],
        [send_all(0, 0, nd)],
    )
    grad_norm = jnp.sqrt(jnp.sum(squares[:, 0, 0]))
    factor = CLIP / jnp.maximum(grad_norm, CLIP)
    step = step_count[0].astype(F32)
    masters = (embed_table, attend_in, attend_out, expand_weight, shrink_weight, norm_gains, bias_terms)
    firsts = (embed_first, attend_in_first, attend_out_first, expand_first, shrink_first, gains_first, bias_first)
    seconds = (embed_second, attend_in_second, attend_out_second, expand_second, shrink_second, gains_second, bias_second)
    results = [loss, grad_norm]
    for index in range(7):
        results.extend(
            adam_update(masters[index], grads[index] * factor, firsts[index], seconds[index], step, LEARN_RATES[index])
        )
    return tuple(results)


def solution(mesh):
    both = ("wide", "narrow")
    weight_specs = (P(None, both),) + (P(None, both, None),) * 4 + (P(None, None, both), P(None, both))
    pairs = tuple(s for spec in weight_specs for s in (spec, spec))
    in_specs = (P(both, None), P("wide", None), P(), P(), P("wide"), P()) + weight_specs + pairs
    out_specs = (P(), P()) + tuple(s for spec in weight_specs for s in (spec, spec, spec))
    return jax.shard_map(on_device, mesh=mesh, in_specs=in_specs, out_specs=out_specs, check_vma=False)
```

```python
import functools

import jax
import jax.numpy as jnp
from jax import lax
from jax.experimental import pallas as pl
from jax.experimental.pallas import tpu as pltpu
from jax.sharding import PartitionSpec as P

D = 768
H = 12
HD = 64
FF = 3072
V = 18000
LP = 384
LQ = 32
LANE = 128
VALID_PER_QUERY = 5

MARGIN = 1.0
CLIP = 1.0
BETA_ONE = 0.9
BETA_TWO = 0.999
LEARN_RATES = (1.0, 0.02, 0.08, 0.02, 0.02, 1.0, 0.1)
WEIGHT_DECAY = 0.01
ADAM_EPS = 1e-08
NORM_EPS = 1e-05
AXES = ("wide", "narrow")
F32 = jnp.float32
BF16 = jnp.bfloat16
O_Q, O_V, O_O, O_1, O_IN, O_OUT, O_2, O_EMB = (
    0, D, 2 * D, 3 * D, 4 * D, 4 * D + FF, 5 * D + FF, 6 * D + FF
)


def dot(left, right, dims):
    return lax.dot_general(left, right, (dims, ((), ())), preferred_element_type=F32)


def norm_rows(values, gain, shift):
    center = values - jnp.mean(values, axis=-1, keepdims=True)
    spread = jnp.mean(center * center, axis=-1, keepdims=True)
    scale = lax.rsqrt(spread + NORM_EPS)
    hat = center * scale
    return hat * gain + shift, hat, scale


def norm_rows_back(grad, gain, hat, scale):
    scaled = grad * gain
    mean_one = jnp.mean(scaled, axis=-1, keepdims=True)
    mean_two = jnp.mean(scaled * hat, axis=-1, keepdims=True)
    return scale * (scaled - mean_one - hat * mean_two)


def gelu_both(upper):
    cdf = 0.5 * (1.0 + lax.erf(upper * 0.7071067811865476))
    pdf = jnp.exp(-0.5 * upper * upper) * 0.3989422804014327
    return upper * cdf, cdf + upper * pdf


def adam_update(weight, grad, first, second, step, rate):
    first_new = BETA_ONE * first + (1.0 - BETA_ONE) * grad
    second_new = BETA_TWO * second + (1.0 - BETA_TWO) * grad * grad
    first_hat = first_new / (1.0 - BETA_ONE**step)
    second_hat = second_new / (1.0 - BETA_TWO**step)
    weight_new = weight - rate * (
        first_hat / (jnp.sqrt(second_hat) + ADAM_EPS) + WEIGHT_DECAY * weight
    )
    return (weight_new, first_new, second_new)


MESH = pl.DeviceIdType.MESH
HASH = 512


class Send:
    def __init__(self, src, dst, take, put, many_src, many_dst, sources, targets):
        self.src, self.dst, self.take, self.put = src, dst, take, put
        self.many_src, self.many_dst = many_src, many_dst
        self.sources, self.targets = sources, targets


def inside(index, span):
    return jnp.logical_and(index >= span[0], index < span[1])


def comm_body(sends, n_in, n_out, nd, narrow, *refs):
    ins, outs = refs[:n_in], refs[n_in : n_in + n_out]
    send_sem, recv_sem, own_sem = refs[n_in + n_out :]
    me = lax.axis_index("wide") * narrow + lax.axis_index("narrow")
    barrier = pltpu.get_barrier_semaphore()

    def greet(k, carry):
        t = lax.rem(me + k, nd)
        pl.semaphore_signal(
            barrier, inc=1, device_id=(t // narrow, lax.rem(t, narrow)), device_id_type=MESH
        )
        return carry

    lax.fori_loop(1, nd, greet, 0)
    pl.semaphore_wait(barrier, nd - 1)

    def push(k, carry):
        t = lax.rem(me + k, nd)
        for i, s in enumerate(sends):

            @pl.when(jnp.logical_and(inside(me, s.sources), inside(t, s.targets)))
            def _():
                pltpu.make_async_remote_copy(
                    src_ref=s.take(ins[s.src], me, t),
                    dst_ref=s.put(outs[s.dst], me, t),
                    send_sem=send_sem.at[i],
                    recv_sem=recv_sem.at[i],
                    device_id=(t // narrow, lax.rem(t, narrow)),
                    device_id_type=MESH,
                ).start()

        return carry

    lax.fori_loop(1, nd, push, 0)
    for i, s in enumerate(sends):
        both = jnp.logical_and(inside(me, s.sources), inside(me, s.targets))

        @pl.when(both)
        def _():
            own = pltpu.make_async_copy(
                s.take(ins[s.src], me, me), s.put(outs[s.dst], me, me), own_sem.at[i]
            )
            own.start()
            own.wait()

    for i, s in enumerate(sends):
        n_t = s.targets[1] - s.targets[0]
        n_s = s.sources[1] - s.sources[0]
        is_s, is_t = inside(me, s.sources), inside(me, s.targets)
        for own in (0, 1):
            mine = is_t if own else jnp.logical_not(is_t)
            if n_t - own > 0:

                @pl.when(jnp.logical_and(is_s, mine))
                def _():
                    view = s.many_src(ins[s.src], n_t - own) if s.many_src(ins[s.src], 1) is not None else outs[s.dst].at[pl.ds(0, n_t - own)]
                    pltpu.make_async_copy(view, view, send_sem.at[i]).wait()

            mine = is_s if own else jnp.logical_not(is_s)
            if n_s - own > 0:

                @pl.when(jnp.logical_and(is_t, mine))
                def _():
                    view = s.many_dst(outs[s.dst], n_s - own)
                    pltpu.make_async_copy(view, view, recv_sem.at[i]).wait()


def comm(collective, arrays, out_shapes, sends, nd, narrow):
    vmem = pl.BlockSpec(memory_space=pltpu.VMEM)
    n = len(sends)
    return pl.pallas_call(
        functools.partial(comm_body, sends, len(arrays), len(out_shapes), nd, narrow),
        out_shape=[jax.ShapeDtypeStruct(s, d) for s, d in out_shapes],
        in_specs=[vmem] * len(arrays),
        out_specs=[vmem] * len(out_shapes),
        scratch_shapes=[
            pltpu.SemaphoreType.DMA((n,)),
            pltpu.SemaphoreType.DMA((n,)),
            pltpu.SemaphoreType.DMA((n,)),
        ],
        compiler_params=pltpu.CompilerParams(collective_id=collective, has_side_effects=True),
    )(*arrays)


def send_all(src, dst, nd):
    return Send(
        src, dst,
        lambda ref, s, t: ref,
        lambda ref, s, t: ref.at[s],
        lambda ref, n: None, lambda ref, n: ref.at[pl.ds(0, n)],
        (0, nd), (0, nd),
    )


def send_blocks(src, dst, nd):
    return Send(
        src, dst,
        lambda ref, s, t: ref.at[t],
        lambda ref, s, t: ref.at[s],
        lambda ref, n: ref.at[pl.ds(0, n)], lambda ref, n: ref.at[pl.ds(0, n)],
        (0, nd), (0, nd),
    )


def stack_pairs(pieces, store):
    rows = pieces[0].shape[0]
    for i in range(0, len(pieces), 2):
        store(i * rows, jnp.concatenate(pieces[i : i + 2], axis=0))


def gather_body(rows, blocks, table_ref, ids_ref, out_ref, stacked):
    @pl.when(pl.program_id(0) == 0)
    def _():
        pieces = [
            table_ref[:, b * HASH : (b + 1) * HASH].astype(F32) for b in range(blocks)
        ]

        def store(row, value):
            stacked[row : row + value.shape[0], :] = value.astype(BF16)

        stack_pairs(pieces, store)

    ids = ids_ref[0]
    low = ids & (HASH - 1)
    high = ids >> (HASH.bit_length() - 1)
    width = ids.shape[1]
    hot = (lax.broadcasted_iota(jnp.int32, (HASH, width), 0) == low).astype(F32).astype(BF16)
    picked = jnp.dot(stacked[...], hot, preferred_element_type=F32)
    value = jnp.zeros((rows, width), F32)
    for b in range(blocks):
        value = jnp.where(high == b, picked[b * rows : (b + 1) * rows], value)
    out_ref[...] = value.astype(BF16)


def table_rows(table, ids):
    rows, total = table.shape
    tokens = ids.shape[0]
    tile = 512
    blocks = total // HASH
    return pl.pallas_call(
        functools.partial(gather_body, rows, blocks),
        grid=(tokens // tile,),
        out_shape=jax.ShapeDtypeStruct((rows, tokens), BF16),
        in_specs=[
            pl.BlockSpec((rows, total), lambda i: (0, 0)),
            pl.BlockSpec((1, 1, tile), lambda i: (i, 0, 0)),
        ],
        out_specs=pl.BlockSpec((rows, tile), lambda i: (0, i)),
        scratch_shapes=[pltpu.VMEM((blocks * rows, HASH), BF16)],
        name="table_rows",
    )(table, ids.reshape(tokens // tile, 1, tile))


def scatter_body(rows, blocks, values_ref, ids_ref, out_ref, spread, acc):
    step = pl.program_id(0)
    ids = ids_ref[0]
    low = ids & (HASH - 1)
    high = ids >> (HASH.bit_length() - 1)
    width = ids.shape[1]
    values = values_ref[...].astype(F32)
    pieces = [jnp.where(high == b, values, 0.0) for b in range(blocks)]

    def store(row, value):
        spread[row : row + value.shape[0], :] = value.astype(BF16)

    stack_pairs(pieces, store)
    hot = (lax.broadcasted_iota(jnp.int32, (HASH, width), 0) == low).astype(F32).astype(BF16)
    part = lax.dot_general(
        spread[...], hot, (((1,), (1,)), ((), ())), preferred_element_type=F32
    )

    @pl.when(step == 0)
    def _():
        acc[...] = part

    @pl.when(step > 0)
    def _():
        acc[...] += part

    @pl.when(step == pl.num_programs(0) - 1)
    def _():
        for b in range(blocks):
            out_ref[:, b * HASH : (b + 1) * HASH] = acc[b * rows : (b + 1) * rows, :]


def table_sums(values, ids, total):
    rows, tokens = values.shape
    tile = 1024
    blocks = total // HASH
    return pl.pallas_call(
        functools.partial(scatter_body, rows, blocks),
        grid=(tokens // tile,),
        out_shape=jax.ShapeDtypeStruct((rows, total), F32),
        in_specs=[
            pl.BlockSpec((rows, tile), lambda i: (0, i)),
            pl.BlockSpec((1, 1, tile), lambda i: (i, 0, 0)),
        ],
        out_specs=pl.BlockSpec((rows, total), lambda i: (0, 0)),
        scratch_shapes=[
            pltpu.VMEM((blocks * rows, tile), BF16),
            pltpu.VMEM((blocks * rows, HASH), F32),
        ],
        name="table_sums",
    )(values, ids.reshape(tokens // tile, 1, tile))


def head_mask(dtype):
    rows = lax.broadcasted_iota(jnp.int32, (H, D), 0)
    cols = lax.broadcasted_iota(jnp.int32, (H, D), 1)
    return (cols // HD == rows).astype(dtype)


def spread_heads(row):
    return row[None, :] * head_mask(row.dtype)


def encode_front(emb_t, w_in, w_out, gain, bias, length):
    width = emb_t.shape[1]
    center = emb_t - jnp.mean(emb_t, axis=0, keepdims=True)
    spread = jnp.mean(center * center, axis=0, keepdims=True)
    scale = lax.rsqrt(spread + NORM_EPS)
    hat = center * scale
    x0 = hat * gain[0][:, None] + bias[O_EMB : O_EMB + D][:, None]
    x_low = x0.astype(BF16)
    first_low = x_low[:, 0]
    q = (dot(first_low[None], w_in[:, :D], ((1,), (0,)))[0] + bias[O_Q : O_Q + D]).astype(BF16)
    k = dot(w_in[:, D : 2 * D], x_low, ((0,), (0,))).astype(BF16)
    v = (
        dot(w_in[:, 2 * D :], x_low, ((0,), (0,))) + bias[O_V : O_V + D][:, None]
    ).astype(BF16)
    q_heads = spread_heads(q)
    s = dot(q_heads, k, ((1,), (0,))) * 0.125
    if length < width:
        live = lax.broadcasted_iota(jnp.int32, (1, width), 1) < length
        s = jnp.where(live, s, -1e30)
    peak = jnp.max(s, axis=1, keepdims=True)
    e = jnp.exp(s - peak)
    p = e / jnp.sum(e, axis=1, keepdims=True)
    p_low = p.astype(BF16)
    mixed = dot(p_low, v, ((1,), (1,)))
    a = jnp.sum(mixed * head_mask(F32), axis=0).astype(BF16)
    o = dot(a[None], w_out, ((1,), (0,)))[0] + bias[O_O : O_O + D]
    return x0[:, 0] + o, (hat, scale, x_low, q, k, v, p, p_low, a)


def encode_back(kept, row_grad, w_in, w_out, gain):
    hat, scale, x_low, q, k, v, p, p_low, a = kept
    do = row_grad.astype(BF16)
    da = dot(do[None], w_out, ((1,), (1,)))[0].astype(BF16)
    da_heads = spread_heads(da)
    q_heads = spread_heads(q)
    dp = dot(da_heads, v, ((1,), (0,)))
    ds = (p * (dp - jnp.sum(dp * p, axis=1, keepdims=True))).astype(BF16)
    dq_heads = dot(ds, k, ((1,), (1,)))
    dq = (jnp.sum(dq_heads * head_mask(F32), axis=0) * 0.125).astype(BF16)
    t = dot(ds, x_low, ((1,), (1,))) * 0.125
    w = dot(p_low, x_low, ((1,), (1,)))
    gk = (dot(q_heads, w_in[:, D : 2 * D], ((1,), (1,))) * 0.125).astype(BF16)
    ev = dot(da_heads, w_in[:, 2 * D :], ((1,), (1,))).astype(BF16)
    gx = dot(gk, ds, ((0,), (0,))) + dot(ev, p_low, ((0,), (0,)))
    first = row_grad + dot(dq[None], w_in[:, :D], ((1,), (1,)))[0]
    is_first = lax.broadcasted_iota(jnp.int32, (1, gx.shape[1]), 1) == 0
    gx = gx + jnp.where(is_first, first[:, None], 0.0)
    p_sum = jnp.sum(p_low.astype(F32), axis=1)
    dbv = jnp.repeat(p_sum, HD) * da.astype(F32)
    g_gain = jnp.sum(gx * hat, axis=1)
    g_shift = jnp.sum(gx, axis=1)
    scaled = gx * gain[0][:, None]
    mean_one = jnp.mean(scaled, axis=0, keepdims=True)
    mean_two = jnp.mean(scaled * hat, axis=0, keepdims=True)
    g_emb = scale * (scaled - mean_one - hat * mean_two)
    return g_emb, (t.astype(BF16), w.astype(BF16), q, da, dq, dbv, g_gain, g_shift)


NN = (((1,), (0,)), ((), ()))
NT = (((1,), (1,)), ((), ()))
TN = (((0,), (0,)), ((), ()))
HIGH = lax.Precision.HIGHEST


def mm(left, right, dims, precision=None):
    return lax.dot_general(
        left, right, dims, preferred_element_type=F32, precision=precision
    )


def iota(shape, dim):
    return lax.broadcasted_iota(jnp.int32, shape, dim)


def as_bf16(mask):
    return mask.astype(F32).astype(BF16)


class Flow:
    def __init__(self, take, put, many, sources, targets):
        self.take, self.put, self.many = take, put, many
        self.sources, self.targets = sources, targets


class Net:
    def __init__(self, nd, narrow, send_sem, recv_sem, own_sem):
        self.nd, self.narrow = nd, narrow
        self.send_sem, self.recv_sem, self.own_sem = send_sem, recv_sem, own_sem
        self.me = lax.axis_index("wide") * narrow + lax.axis_index("narrow")
        self.used = 0

    def where(self, t):
        return (t // self.narrow, lax.rem(t, self.narrow))

    def barrier(self):
        sem = pltpu.get_barrier_semaphore()

        def greet(k, carry):
            t = lax.rem(self.me + k, self.nd)
            pl.semaphore_signal(sem, inc=1, device_id=self.where(t), device_id_type=MESH)
            return carry

        lax.fori_loop(1, self.nd, greet, 0)
        pl.semaphore_wait(sem, self.nd - 1)

    def start(self, flows):
        me, nd = self.me, self.nd
        base = self.used
        self.used += len(flows)

        def push(k, carry):
            t = lax.rem(me + k, nd)
            for i, f in enumerate(flows):

                @pl.when(jnp.logical_and(inside(me, f.sources), inside(t, f.targets)))
                def _():
                    pltpu.make_async_remote_copy(
                        src_ref=f.take(me, t),
                        dst_ref=f.put(me, t),
                        send_sem=self.send_sem.at[base + i],
                        recv_sem=self.recv_sem.at[base + i],
                        device_id=self.where(t),
                        device_id_type=MESH,
                    ).start()

            return carry

        for i, f in enumerate(flows):

            @pl.when(jnp.logical_and(inside(me, f.sources), inside(me, f.targets)))
            def _():
                pltpu.make_async_copy(
                    f.take(me, me), f.put(me, me), self.own_sem.at[base + i]
                ).start()

        lax.fori_loop(1, nd, push, 0)
        return base

    def finish(self, flows, base):
        me = self.me
        for i, f in enumerate(flows):
            n_t = f.targets[1] - f.targets[0]
            n_s = f.sources[1] - f.sources[0]
            is_s, is_t = inside(me, f.sources), inside(me, f.targets)

            @pl.when(jnp.logical_and(is_s, is_t))
            def _():
                pltpu.make_async_copy(
                    f.take(me, me), f.put(me, me), self.own_sem.at[base + i]
                ).wait()

            for own in (0, 1):
                mine = is_s if own else jnp.logical_not(is_s)
                if n_s - own > 0:

                    @pl.when(jnp.logical_and(is_t, mine))
                    def _():
                        view = f.many(n_s - own)
                        pltpu.make_async_copy(view, view, self.recv_sem.at[base + i]).wait()

            for own in (0, 1):
                mine = is_t if own else jnp.logical_not(is_t)
                if n_t - own > 0:

                    @pl.when(jnp.logical_and(is_s, mine))
                    def _():
                        view = f.many(n_t - own)
                        pltpu.make_async_copy(view, view, self.send_sem.at[base + i]).wait()


class Unit:
    def __init__(self, count, length):
        self.count, self.length = count, length
        self.tokens = count * length
        self.bits = count.bit_length() - 1
        self.rows = max(16, H * count)
        self.seqs = max(8, count)

    def pick(self):
        lane = iota((self.seqs, self.tokens), 1)
        seq = iota((self.seqs, self.tokens), 0)
        return lane == seq * self.length

    def spread(self):
        row, seq = iota((self.rows, self.seqs), 0), iota((self.rows, self.seqs), 1)
        return as_bf16((row & (self.count - 1)) == seq)

    def collect(self):
        row, seq = iota((self.seqs, self.rows), 1), iota((self.seqs, self.rows), 0)
        return as_bf16((row & (self.count - 1)) == seq)

    def heads(self):
        row, col = iota((self.rows, D), 0), iota((self.rows, D), 1)
        return ((row >> self.bits) == (col >> 6)).astype(F32)

    def live(self):
        row, lane = iota((self.rows, self.tokens), 0), iota((self.rows, self.tokens), 1)
        return (lane >> 5) == (row & (self.count - 1))


def unit_front(unit, emb, e, w_in, w_out, cv, rv, keep):
    center = emb - jnp.mean(emb, axis=0, keepdims=True)
    spread = jnp.mean(center * center, axis=0, keepdims=True)
    scale = lax.rsqrt(spread + NORM_EPS)
    hat = center * scale
    x0 = hat * cv[:, 3 * e : 3 * e + 1] + cv[:, 3 * e + 1 : 3 * e + 2]
    x_low = x0.astype(BF16)
    pick = unit.pick()
    x_first = mm(as_bf16(pick), x_low, NT).astype(BF16)
    x0_first = mm(pick.astype(F32), x0, NT, HIGH)
    q = (mm(x_first, w_in[e, :, 0:D], NN) + rv[8 * e : 8 * e + 1, :]).astype(BF16)
    k = mm(w_in[e, :, D : 2 * D], x_low, TN).astype(BF16)
    v = (mm(w_in[e, :, 2 * D : 3 * D], x_low, TN) + cv[:, 3 * e + 2 : 3 * e + 3]).astype(BF16)
    heads = unit.heads()
    q_heads = (mm(unit.spread(), q, NN) * heads).astype(BF16)
    s = mm(q_heads, k, NN) * 0.125
    if unit.count > 1:
        s = jnp.where(unit.live(), s, -1e30)
    peak = jnp.max(s, axis=1, keepdims=True)
    ex = jnp.exp(s - peak)
    p = ex / jnp.sum(ex, axis=1, keepdims=True)
    mixed = (mm(p.astype(BF16), v, NT) * heads).astype(BF16)
    a = mm(unit.collect(), mixed, NN).astype(BF16)
    o = mm(a, w_out[e], NN) + rv[8 * e + 1 : 8 * e + 2, :]
    keep(hat, scale, x_low, x_first, q, k, v, p, a)
    return x0_first + o


def unit_back(unit, row_grad, e, w_in, w_out, cv, kept):
    hat, scale, x_low, x_first, q, k, v, p, a = kept
    heads = unit.heads()
    spread, collect = unit.spread(), unit.collect()
    p_low = p.astype(BF16)
    do = row_grad.astype(BF16)
    da = mm(do, w_out[e], NT).astype(BF16)
    q_heads = (mm(spread, q, NN) * heads).astype(BF16)
    da_heads = (mm(spread, da, NN) * heads).astype(BF16)
    dp = mm(da_heads, v, NN)
    ds = (p * (dp - jnp.sum(dp * p, axis=1, keepdims=True))).astype(BF16)
    dq_heads = (mm(ds, k, NT) * heads * 0.125).astype(BF16)
    dq = mm(collect, dq_heads, NN).astype(BF16)
    t = mm(ds, x_low, NT) * 0.125
    w = mm(p_low, x_low, NT)
    gk = (mm(q_heads, w_in[e, :, D : 2 * D], NT) * 0.125).astype(BF16)
    ev = mm(da_heads, w_in[e, :, 2 * D : 3 * D], NT).astype(BF16)
    first = row_grad + mm(dq, w_in[e, :, 0:D], NT)
    gx = mm(gk, ds, TN) + mm(ev, p_low, TN)
    gx = gx + mm(first, unit.pick().astype(F32), TN, HIGH)
    p_sum = jnp.sum(p_low.astype(F32), axis=1, keepdims=True)
    dbv = jnp.sum(p_sum * da_heads.astype(F32), axis=0, keepdims=True)
    g_gain = jnp.sum(gx * hat, axis=1, keepdims=True)
    g_shift = jnp.sum(gx, axis=1, keepdims=True)
    scaled = gx * cv[:, 3 * e : 3 * e + 1]
    mean_one = jnp.mean(scaled, axis=0, keepdims=True)
    mean_two = jnp.mean(scaled * hat, axis=0, keepdims=True)
    g_emb = scale * (scaled - mean_one - hat * mean_two)
    return g_emb, t, w, da, dq, do, dbv, g_gain, g_shift


def load_rows(ref, count):
    return jnp.concatenate(
        [ref[pl.ds(j, count, stride=8), :] for j in range(D // LANE)], axis=1
    )


def store_rows(ref, value):
    for j in range(D // LANE):
        ref[pl.ds(j, value.shape[0], stride=8), :] = value[:, j * LANE : (j + 1) * LANE]


def middle_body(
    n_valid, nq, nd, narrow, cols, query_home, token_total,
    mine, mine_q, pos, w_in, w_out, w_up, w_down, cv, rv, b_in, slots,
    o_tok, o_fac, o_facq, o_line, o_lineq, o_du, o_shrink, o_h, o_rows, o_loss,
    hat_s, scale_s, xl_s, xf_s, q_s, k_s, v_s, p_s, a_s,
    hat_q, scale_q, xl_q, xf_q, q_q, k_q, v_q, p_q, a_q,
    r1_own, r1_ownq, r1_all, y_send, y_recv, y_sum, y_all, h_send, h_recv, h_recvq,
    du_own, du_f, gtok, gtok_q, fac, fac_q, line, line_q, f_s, slope_s, hlow_s, g_top_s, sums_s,
    size48,
    send_sem, recv_sem, own_sem,
):
    cap = -(-n_valid // nd)
    rows = n_valid + nq
    net = Net(nd, narrow, send_sem, recv_sem, own_sem)
    me = net.me
    everyone = (0, nd)
    home = (query_home, query_home + 1)
    q_owner = nd - nq
    q_owners = (q_owner, nd)

    def span(c):
        return (0, min(nd, n_valid - c * nd))

    net.barrier()
    passage = Unit(1, LP)
    queries = Unit(nq, LQ)
    n_mine = jnp.where(me < n_valid - (cap - 1) * nd, cap, cap - 1)

    def front(c, carry):
        at = pl.ds(pl.multiple_of(c * LP, LANE), LP)
        emb = (mine[:, :, at].astype(F32) + pos[...].astype(F32)).reshape(D, LP)

        def keep(hat, scale, x_low, x_first, q, k, v, p, a):
            hat_s[c], scale_s[c], xl_s[c], xf_s[c] = hat, scale, x_low, x_first
            q_s[c], k_s[c], v_s[c], p_s[c], a_s[c] = q, k, v, p, a

        r1 = unit_front(passage, emb, 1, w_in, w_out, cv, rv, keep)
        for j in range(D // LANE):
            r1_own[c, j : j + 1, :] = r1[0:1, j * LANE : (j + 1) * LANE]
        return carry

    lax.fori_loop(0, n_mine, front, 0)

    @pl.when(me == query_home)
    def _():
        parts = pos[:, :, 0:LANE].astype(F32).reshape(D, LANE)[:, 0:LQ]
        emb = mine_q[...].astype(F32).reshape(D, nq * LQ) + jnp.concatenate([parts] * nq, axis=1)

        def keep(hat, scale, x_low, x_first, q, k, v, p, a):
            hat_q[...], scale_q[...], xl_q[...], xf_q[...] = hat, scale, x_low, x_first
            q_q[...], k_q[...], v_q[...], p_q[...], a_q[...] = q, k, v, p, a

        store_rows(r1_ownq, unit_front(queries, emb, 0, w_in, w_out, cv, rv, keep))

    flows = [
        Flow(
            lambda s, t, c=c: r1_own.at[c],
            lambda s, t, c=c: r1_all.at[pl.ds(pl.multiple_of(8 * (c * nd + s), 8), 8), :],
            lambda n: r1_all.at[pl.ds(0, 8 * n), :],
            span(c), everyone,
        )
        for c in range(cap)
    ] + [
        Flow(
            lambda s, t: r1_ownq,
            lambda s, t: r1_all.at[pl.ds(8 * n_valid, 8 * nq), :],
            lambda n: y_recv_q(n),
            home, everyone,
        )
    ]

    def y_recv_q(n):
        return h_recvq.at[pl.ds(0, n)]

    base = net.start(flows)
    net.finish(flows, base)

    part = {1: (0, n_valid), 0: (n_valid, nq)}
    y_parts = []
    for e in (1, 0):
        at, n = part[e]
        r1 = load_rows(r1_all.at[pl.ds(8 * at, 8 * n), :], n)
        h, hat1, scale1 = norm_rows(r1, rv[8 * e + 5 : 8 * e + 6, :], rv[8 * e + 2 : 8 * e + 3, :])
        h_low = h.astype(BF16)
        hlow_s[at : at + n, :] = h
        o_h[at : at + n, :] = h_low.astype(F32)
        upper = mm(h_low, w_up[e], NN) + b_in[e : e + 1, :]
        active, slope = gelu_both(upper)
        f_low = active.astype(BF16)
        f_s[at : at + n, :] = f_low.astype(F32)
        slope_s[at : at + n, :] = slope
        y_parts.append(mm(f_low, w_down[e], NN))
    store_rows(y_send, jnp.concatenate(y_parts, axis=0))
    flows = [
        Flow(
            lambda s, t, c=c: y_send.at[pl.ds(pl.multiple_of(8 * (c * nd + t), 8), 8), :],
            lambda s, t, c=c: y_recv.at[s, c],
            lambda n, c=c: y_recv.at[pl.ds(0, n), c],
            everyone, span(c),
        )
        for c in range(cap)
    ] + [
        Flow(
            lambda s, t: y_send.at[pl.ds(pl.multiple_of(8 * (n_valid + t - q_owner), 8), 8), :],
            lambda s, t: y_recv.at[s, cap],
            lambda n: y_recv.at[pl.ds(0, n), cap],
            everyone, q_owners,
        )
    ]
    base = net.start(flows)
    net.finish(flows, base)
    y_sum[...] = jnp.sum(y_recv[...], axis=0)
    flows = [
        Flow(
            lambda s, t, c=c: y_sum.at[c],
            lambda s, t, c=c: y_all.at[pl.ds(pl.multiple_of(8 * (c * nd + s), 8), 8), :],
            lambda n: y_all.at[pl.ds(0, 8 * n), :],
            span(c), everyone,
        )
        for c in range(cap)
    ] + [
        Flow(
            lambda s, t: y_sum.at[cap],
            lambda s, t: y_all.at[pl.ds(pl.multiple_of(8 * (n_valid + s - q_owner), 8), 8), :],
            lambda n: y_all.at[pl.ds(0, 8 * n), :],
            q_owners, everyone,
        )
    ]
    base = net.start(flows)
    net.finish(flows, base)

    tops, vecs = {}, {}
    for e in (1, 0):
        at, n = part[e]
        y = load_rows(y_all.at[pl.ds(8 * at, 8 * n), :], n)
        top = hlow_s[at : at + n, :] + y + rv[8 * e + 3 : 8 * e + 4, :]
        z, hat2, scale2 = norm_rows(
            top, rv[8 * e + 6 : 8 * e + 7, :], rv[8 * e + 4 : 8 * e + 5, :]
        )
        tops[e] = (hat2, scale2)
        vecs[e] = z.astype(BF16)
    qvec, pvec = vecs[0], vecs[1]
    owner = slots[0:1, 0:n_valid]
    is_first = slots[1:2, 0:n_valid] == 1
    kept_slot = slots[2:3, 0:n_valid] == 1
    member = owner == iota((nq, n_valid), 0)
    valid = jnp.broadcast_to(owner >= 0, (nq, n_valid))
    positive = jnp.logical_and(member, is_first)
    negative = jnp.logical_and(member, jnp.logical_and(jnp.logical_not(is_first), kept_slot))
    counts = jnp.sum(member.astype(F32), axis=1, keepdims=True) - 1.0
    score_scale = 2.0 * D ** (-0.5)
    scores = mm(qvec, pvec, NT) * score_scale
    masked = jnp.where(valid, scores, -1e30)
    peak = jnp.max(masked, axis=1, keepdims=True)
    summed = jnp.sum(jnp.where(valid, jnp.exp(masked - peak), 0.0), axis=1, keepdims=True)
    logsum = peak + jnp.log(summed)
    pos_score = jnp.sum(jnp.where(positive, scores, 0.0), axis=1, keepdims=True)
    margins = MARGIN - pos_score + scores
    active = jnp.logical_and(negative, margins > 0)
    hinge = jnp.sum(jnp.where(active, margins, 0.0), axis=1, keepdims=True) / counts
    active_total = jnp.sum(active.astype(F32), axis=1, keepdims=True)
    loss = jnp.sum(logsum - pos_score + hinge, axis=0, keepdims=True)
    o_loss[...] = jnp.broadcast_to(loss, (8, LANE))
    score_grad = (
        jnp.where(valid, jnp.exp(scores - logsum), 0.0)
        - positive.astype(F32) * (1.0 + active_total / counts)
        + active.astype(F32) / counts
    )
    score_low = score_grad.astype(BF16)
    vec_grads = {
        0: (mm(score_low, pvec, NN) * score_scale).astype(BF16).astype(F32),
        1: (mm(score_low, qvec, TN) * score_scale).astype(BF16).astype(F32),
    }
    h_parts, out_rows = [], {}
    for e in (1, 0):
        at, n = part[e]
        hat2, scale2 = tops[e]
        grad = vec_grads[e]
        g_top = norm_rows_back(grad, rv[8 * e + 6 : 8 * e + 7, :], hat2, scale2)
        dy = g_top.astype(BF16)
        g_top_s[at : at + n, :] = g_top
        out_rows[e] = [
            jnp.sum(grad * hat2, axis=0, keepdims=True),
            jnp.sum(grad, axis=0, keepdims=True),
            jnp.sum(dy.astype(F32), axis=0, keepdims=True),
        ]
        f_low = f_s[at : at + n, :].astype(BF16)
        o_shrink[e] = mm(f_low, dy, TN)
        df = mm(dy, w_down[e], NT)
        du = (slope_s[at : at + n, :] * df).astype(BF16)
        du_f[at : at + n, :] = du.astype(F32)
        h_parts.append(mm(du, w_up[e], NT))
    for e in (0, 1):
        for j in range(3):
            o_rows[3 * e + j : 3 * e + j + 1, :] = out_rows[e][j]
    du_own[...] = du_f[...].astype(BF16)
    store_rows(h_send, jnp.concatenate(h_parts, axis=0))
    flows = [
        Flow(
            lambda s, t, c=c: h_send.at[pl.ds(pl.multiple_of(8 * (c * nd + t), 8), 8), :],
            lambda s, t, c=c: h_recv.at[s, c],
            lambda n, c=c: h_recv.at[pl.ds(0, n), c],
            everyone, span(c),
        )
        for c in range(cap)
    ] + [
        Flow(
            lambda s, t: h_send.at[pl.ds(8 * n_valid, 8 * nq), :],
            lambda s, t: h_recvq.at[s],
            lambda n: h_recvq.at[pl.ds(0, n)],
            everyone, home,
        )
    ]
    du_flows = [
        Flow(
            lambda s, t: du_own,
            lambda s, t: o_du.at[s],
            lambda n: o_du.at[pl.ds(0, n)],
            everyone, everyone,
        )
    ]
    base = net.start(flows)
    du_base = net.start(du_flows)
    fac[...] = jnp.zeros_like(fac)
    line[...] = jnp.zeros_like(line)
    sums_s[...] = jnp.zeros_like(sums_s)
    o_tok[:, n_valid * LP + nq * LQ :] = jnp.zeros(
        (cols, token_total - n_valid * LP - nq * LQ), BF16
    )
    net.finish(flows, base)

    def load_rows_sum(ref, count):
        total = jnp.sum(ref[...], axis=0)
        h_send[0 : 8 * count, :] = total
        return load_rows(h_send.at[pl.ds(0, 8 * count), :], count)

    lane = iota((D, LANE), 1)

    def back(c, carry):
        slot = c * nd + me
        tile = jnp.sum(h_recv[:, c], axis=0)
        dh = jnp.concatenate([tile[j : j + 1, :] for j in range(D // LANE)], axis=1)
        top = g_top_s[pl.ds(slot, 1), :]
        g_h = top + dh
        r1 = jnp.concatenate([r1_own[c, j : j + 1, :] for j in range(D // LANE)], axis=1)
        gain1 = rv[8 + 5 : 8 + 6, :]
        _, hat1, scale1 = norm_rows(r1, gain1, gain1)
        g_mid = norm_rows_back(g_h, gain1, hat1, scale1)
        row_grad = jnp.where(iota((8, D), 0) == 0, jnp.broadcast_to(g_mid, (8, D)), 0.0)
        kept = (
            hat_s[c], scale_s[c], xl_s[c], xf_s[c], q_s[c], k_s[c], v_s[c], p_s[c], a_s[c]
        )
        g_emb, t, w, da, dq, do, dbv, g_gain, g_shift = unit_back(
            passage, row_grad, 1, w_in, w_out, cv, kept
        )
        gtok[c] = g_emb.reshape(nd, cols, LP).astype(BF16)
        tw = jnp.concatenate([t, w, xf_s[c].astype(F32), a_s[c].astype(F32)], axis=0)
        tw = jnp.concatenate([tw, jnp.zeros((LANE - 48, D), F32)], axis=0)
        tw_t = jnp.transpose(tw)
        moved = jnp.where(lane < 48, tw_t, 0.0)
        placed = pltpu.roll(moved, 64 * c, 1)
        fac[...] = (fac[...].astype(F32) + placed.reshape(nd, cols, LANE)).astype(BF16)
        which = iota((16, D), 0)
        new = jnp.zeros((16, D), F32)
        for j, row in enumerate((q_s[c], da, dq, do)):
            new = new + jnp.where(which == 2 * j + c, row.astype(F32)[0:1, :], 0.0)
        line[...] = line[...] + new
        columns = jnp.where(lane == 0, g_gain, jnp.where(lane == 1, g_shift, 0.0))
        flat = jnp.transpose(columns)[0:8, :]
        extra = (
            jnp.where(iota((8, D), 0) == 2, dbv, 0.0)
            + jnp.where(iota((8, D), 0) == 3, g_h * hat1, 0.0)
            + jnp.where(iota((8, D), 0) == 4, g_h, 0.0)
        )
        sums_s[...] = sums_s[...] + flat + extra
        return carry

    lax.fori_loop(0, n_mine, back, 0)
    line_q[0:16, :] = (line[...] + jnp.concatenate([jnp.zeros((8, D), F32), sums_s[...]], axis=0)).astype(BF16)

    @pl.when(me == query_home)
    def _():
        dh = load_rows_sum(h_recvq, nq)
        at, n = part[0]
        g_h = g_top_s[at : at + n, :] + dh
        r1 = load_rows(r1_ownq, nq)
        gain1 = rv[5:6, :]
        _, hat1, scale1 = norm_rows(r1, gain1, gain1)
        g_mid = norm_rows_back(g_h, gain1, hat1, scale1)
        kept = (
            hat_q[...], scale_q[...], xl_q[...], xf_q[...], q_q[...], k_q[...], v_q[...],
            p_q[...], a_q[...],
        )
        g_emb, t, w, da, dq, do, dbv, g_gain, g_shift = unit_back(
            queries, g_mid, 0, w_in, w_out, cv, kept
        )
        gtok_q[...] = g_emb.reshape(nd, cols, nq * LQ).astype(BF16)
        tw = jnp.concatenate([t, w, xf_q[...].astype(F32), a_q[...].astype(F32)], axis=0)
        n_tw = tw.shape[0]
        tw = jnp.concatenate([tw, jnp.zeros((fac_q.shape[2] - n_tw, D), F32)], axis=0)
        fac_q[...] = jnp.transpose(tw).reshape(nd, cols, fac_q.shape[2]).astype(BF16)
        columns = jnp.where(lane == 0, g_gain, jnp.where(lane == 1, g_shift, 0.0))
        flat = jnp.transpose(columns)[0:8, :]
        extra = (
            jnp.where(iota((8, D), 0) == 2, dbv, 0.0)
            + jnp.where(iota((8, D), 0) == 3, jnp.sum(g_h * hat1, axis=0, keepdims=True), 0.0)
            + jnp.where(iota((8, D), 0) == 4, jnp.sum(g_h, axis=0, keepdims=True), 0.0)
        )
        block = jnp.concatenate(
            [q_q[...].astype(F32), da.astype(F32), dq.astype(F32), do.astype(F32), flat + extra,
             jnp.zeros((8, D), F32)],
            axis=0,
        )
        line_q[16:64, :] = block.astype(BF16)

    flows = [
        Flow(
            lambda s, t, c=c: gtok.at[c, t],
            lambda s, t, c=c: o_tok.at[:, pl.ds(pl.multiple_of((c * nd + s) * LP, LANE), LP)],
            lambda n: o_tok.at[:, pl.ds(0, n * LP)],
            span(c), everyone,
        )
        for c in range(cap)
    ] + [
        Flow(
            lambda s, t: gtok_q.at[t],
            lambda s, t: o_tok.at[:, pl.ds(n_valid * LP, nq * LQ)],
            lambda n: o_tok.at[:, pl.ds(0, n * nq * LQ)],
            home, everyone,
        ),
        Flow(
            lambda s, t: fac.at[t],
            lambda s, t: o_fac.at[s],
            lambda n: o_fac.at[pl.ds(0, n)],
            everyone, everyone,
        ),
        Flow(
            lambda s, t: fac_q.at[t],
            lambda s, t: o_facq,
            lambda n: fac_q.at[pl.ds(0, n)],
            home, everyone,
        ),
        Flow(
            lambda s, t: line_q.at[pl.ds(0, 16), :],
            lambda s, t: o_line.at[s],
            lambda n: o_line.at[pl.ds(0, n)],
            everyone, everyone,
        ),
        Flow(
            lambda s, t: line_q.at[pl.ds(16, 48), :],
            lambda s, t: o_lineq,
            lambda n: o_line48(n),
            home, everyone,
        ),
    ]

    def o_line48(n):
        return size48.at[pl.ds(0, n)]

    base = net.start(flows)
    net.finish(flows, base)
    net.finish(du_flows, du_base)


def middle(n_valid, nq, nd, narrow, cols, query_home, token_total, arrays):
    cap = -(-n_valid // nd)
    rows = n_valid + nq
    tq = nq * LQ
    unit, unit_q = Unit(1, LP), Unit(nq, LQ)
    fac_lanes = -(-(2 * unit_q.rows + 2 * unit_q.seqs) // LANE) * LANE
    vmem = pl.BlockSpec(memory_space=pltpu.VMEM)

    def like(*shape, dtype=F32):
        return jax.ShapeDtypeStruct(shape, dtype)

    def kept(lead, u):
        return [
            pltpu.VMEM(lead + (D, u.tokens), F32),
            pltpu.VMEM(lead + (1, u.tokens), F32),
            pltpu.VMEM(lead + (D, u.tokens), BF16),
            pltpu.VMEM(lead + (u.seqs, D), BF16),
            pltpu.VMEM(lead + (u.seqs, D), BF16),
            pltpu.VMEM(lead + (D, u.tokens), BF16),
            pltpu.VMEM(lead + (D, u.tokens), BF16),
            pltpu.VMEM(lead + (u.rows, u.tokens), F32),
            pltpu.VMEM(lead + (u.seqs, D), BF16),
        ]

    flows = 5 * (cap + 1) + 5
    return pl.pallas_call(
        functools.partial(
            middle_body, n_valid, nq, nd, narrow, cols, query_home, token_total
        ),
        out_shape=[
            like(cols, token_total, dtype=BF16),
            like(nd, cols, LANE, dtype=BF16),
            like(cols, fac_lanes, dtype=BF16),
            like(nd, 16, D, dtype=BF16),
            like(48, D, dtype=BF16),
            like(nd, rows, LANE, dtype=BF16),
            like(2, LANE, D),
            like(rows, D),
            like(8, D),
            like(8, LANE),
        ],
        in_specs=[vmem] * len(arrays),
        out_specs=[vmem] * 10,
        scratch_shapes=kept((cap,), unit)
        + kept((), unit_q)
        + [
            pltpu.VMEM((cap, 8, LANE), F32),
            pltpu.VMEM((8 * nq, LANE), F32),
            pltpu.VMEM((8 * rows, LANE), F32),
            pltpu.VMEM((8 * rows, LANE), F32),
            pltpu.VMEM((nd, cap + 1, 8, LANE), F32),
            pltpu.VMEM((cap + 1, 8, LANE), F32),
            pltpu.VMEM((8 * rows, LANE), F32),
            pltpu.VMEM((8 * rows, LANE), F32),
            pltpu.VMEM((nd, cap, 8, LANE), F32),
            pltpu.VMEM((nd, 8 * nq, LANE), F32),
            pltpu.VMEM((rows, LANE), BF16),
            pltpu.VMEM((rows, LANE), F32),
            pltpu.VMEM((cap, nd, cols, LP), BF16),
            pltpu.VMEM((nd, cols, tq), BF16),
            pltpu.VMEM((nd, cols, LANE), BF16),
            pltpu.VMEM((nd, cols, fac_lanes), BF16),
            pltpu.VMEM((16, D), F32),
            pltpu.VMEM((64, D), BF16),
            pltpu.VMEM((rows, LANE), F32),
            pltpu.VMEM((rows, LANE), F32),
            pltpu.VMEM((rows, D), F32),
            pltpu.VMEM((rows, D), F32),
            pltpu.VMEM((8, D), F32),
            pltpu.VMEM((nd, 48, D), BF16),
            pltpu.SemaphoreType.DMA((flows,)),
            pltpu.SemaphoreType.DMA((flows,)),
            pltpu.SemaphoreType.DMA((flows,)),
        ],
        compiler_params=pltpu.CompilerParams(
            collective_id=3, has_side_effects=True, vmem_limit_bytes=62 * 1024 * 1024
        ),
        name="middle",
    )(*arrays)


def on_device_rows(
    passage_ids, query_ids, passage_query, kept_mask, neg_count, step_count,
    embed_table, attend_in, attend_out, expand_weight, shrink_weight, norm_gains, bias_terms,
    embed_first, embed_second, attend_in_first, attend_in_second,
    attend_out_first, attend_out_second, expand_first, expand_second,
    shrink_first, shrink_second, gains_first, gains_second, bias_first, bias_second,
):
    narrow = lax.axis_size("narrow")
    nd = lax.axis_size("wide") * narrow
    me = lax.axis_index("wide") * narrow + lax.axis_index("narrow")
    cols = embed_table.shape[1]
    n_slots = passage_query.shape[0]
    nq = query_ids.shape[0] * lax.axis_size("wide")
    n_valid = VALID_PER_QUERY * nq
    cap = -(-n_valid // nd)
    rows_p = cap * nd
    ff_cols = FF // nd

    exch = functools.partial(comm, nd=nd, narrow=narrow)
    rows_c = -(-cols // 8) * 8
    n_ids = passage_ids.shape[0] + query_ids.shape[0]
    small_width = max(cols, bias_terms.shape[1], 1)
    small_width = -(-small_width // LANE) * LANE

    def widen(value, width):
        return jnp.pad(value, ((0, 0), (0, width - value.shape[1])))

    ids_mine = jnp.concatenate([passage_ids, widen(query_ids, LP)])
    small_mine = jnp.concatenate(
        [widen(norm_gains.reshape(6, cols), small_width), widen(bias_terms, small_width)]
    ).astype(BF16)
    ids_got, small_got = exch(
        1,
        [ids_mine, small_mine],
        [((nd, n_ids, LP), jnp.int32), ((nd, 8, small_width), BF16)],
        [send_all(0, 0, nd), send_all(1, 1, nd)],
    )
    n_own = passage_ids.shape[0]
    pid = ids_got[:, :n_own].reshape(n_slots, LP)[:n_valid]
    qid = ids_got.reshape(-1, narrow, n_ids, LP)[:, 0, n_own:, :LANE].reshape(nq, LANE)
    all_ids = jnp.concatenate([pid.reshape(-1), qid.reshape(-1)])
    gains = small_got[:, :6, :cols].transpose(1, 0, 2).reshape(2, 3, D).astype(F32)
    bias = small_got[:, 6:, : bias_terms.shape[1]].transpose(1, 0, 2).reshape(2, -1).astype(F32)

    table_t = embed_table.T
    table_low = table_t.astype(BF16)
    vocab = V + LP
    total = -(-vocab // HASH) * HASH
    table_pad = jnp.pad(table_low, ((0, rows_c - cols), (0, total - vocab)))
    got = table_rows(table_pad, all_ids)
    pos_mine = table_pad[:, V : V + LP]
    up_mine = expand_weight.astype(BF16).reshape(2 * cols, nd, ff_cols).transpose(1, 0, 2)
    q_from = n_valid * LP
    width = cap * LP + LANE

    def passage_move(c, forward):
        span = (0, min(nd, n_valid - c * nd))
        if forward:
            return Send(
                0, 0,
                lambda ref, s, t: ref.at[:, pl.ds(pl.multiple_of((c * nd + t) * LP, LANE), LP)],
                lambda ref, s, t: ref.at[s, :, pl.ds(c * LP, LP)],
                lambda ref, n: ref.at[:, pl.ds(0, n * LP)],
                lambda ref, n: ref.at[pl.ds(0, n), :, pl.ds(0, LP)],
                (0, nd), span,
            )
        return Send(
            0, 0,
            lambda ref, s, t: ref.at[t, :, pl.ds(c * LP, LP)],
            lambda ref, s, t: ref.at[:, pl.ds(pl.multiple_of((c * nd + s) * LP, LANE), LP)],
            lambda ref, n: ref.at[pl.ds(0, n), :, pl.ds(0, LP)],
            lambda ref, n: ref.at[:, pl.ds(0, n * LP)],
            span, (0, nd),
        )

    def query_move(forward):
        span = (nd - nq, nd)
        if forward:
            return Send(
                0, 0,
                lambda ref, s, t: ref.at[
                    :, pl.ds(pl.multiple_of(q_from + (t - (nd - nq)) * LANE, LANE), LANE)
                ],
                lambda ref, s, t: ref.at[s, :, pl.ds(cap * LP, LANE)],
                lambda ref, n: ref.at[:, pl.ds(0, n * LANE)],
                lambda ref, n: ref.at[pl.ds(0, n), :, pl.ds(0, LANE)],
                (0, nd), span,
            )
        return Send(
            0, 0,
            lambda ref, s, t: ref.at[t, :, pl.ds(cap * LP, LANE)],
            lambda ref, s, t: ref.at[
                :, pl.ds(pl.multiple_of(q_from + (s - (nd - nq)) * LANE, LANE), LANE)
            ],
            lambda ref, n: ref.at[pl.ds(0, n), :, pl.ds(0, LANE)],
            lambda ref, n: ref.at[:, pl.ds(0, n * LANE)],
            span, (0, nd),
        )

    mine, pos, w_up = exch(
        2,
        [got, pos_mine, up_mine],
        [((nd, rows_c, width), BF16), ((nd, rows_c, LP), BF16), ((nd, 2 * cols, ff_cols), BF16)],
        [passage_move(c, True) for c in range(cap)]
        + [query_move(True), send_all(1, 1, nd), send_blocks(2, 2, nd)],
    )
    live = jnp.concatenate(
        [jnp.broadcast_to(c * nd + me < n_valid, (LP,)) for c in range(cap)]
        + [jnp.broadcast_to(me >= nd - nq, (LANE,))]
    )
    mine = jnp.where(live, mine[:, :cols].reshape(D, width), 0)
    pos = pos[:, :cols].reshape(D, LP).astype(F32)
    w_up = w_up.reshape(nd, 2, cols, ff_cols).transpose(1, 0, 2, 3).reshape(2, D, ff_cols)
    w_down = shrink_weight.astype(BF16)
    w_in = lax.all_gather(attend_in.astype(BF16), AXES, axis=1, tiled=True)
    w_out = lax.all_gather(attend_out.astype(BF16), AXES, axis=1, tiled=True)

    fronts = []
    for c in range(cap):
        emb = mine[:, c * LP : (c + 1) * LP].astype(F32) + pos
        fronts.append(encode_front(emb, w_in[1], w_out[1], gains[1], bias[1], LP))
    emb = mine[:, cap * LP :].astype(F32) + pos[:, :LANE]
    fronts.append(encode_front(emb, w_in[0], w_out[0], gains[0], bias[0], LQ))
    (rows,) = exch(
        3, [jnp.stack([f[0] for f in fronts])], [((nd, cap + 1, D), F32)], [send_all(0, 0, nd)]
    )
    row_in = (rows[nd - nq :, cap], rows[:, :cap].transpose(1, 0, 2).reshape(rows_p, D))

    def by_owner(queries, passages):
        q_part = jnp.pad(queries, ((nd - nq, 0), (0, 0)))[:, None]
        return jnp.concatenate([passages.reshape(cap, nd, D).transpose(1, 0, 2), q_part], axis=1)

    def to_rows(blocks):
        return (
            blocks[nd - nq :, cap],
            blocks[:, :cap].transpose(1, 0, 2).reshape(rows_p, D),
        )


    mids, ups = [], []
    partial_y = []
    b_in_all = bias[:, O_IN : O_IN + FF].reshape(2, nd, ff_cols)
    b_in = lax.dynamic_index_in_dim(b_in_all, me, 1, False)
    for e in range(2):
        h, hat1, scale1 = norm_rows(row_in[e], gains[e, 1], bias[e, O_1 : O_1 + D])
        h_low = h.astype(BF16)
        upper = dot(h_low, w_up[e], ((1,), (0,))) + b_in[e]
        active, slope = gelu_both(upper)
        f_low = active.astype(BF16)
        partial_y.append(dot(f_low, w_down[e], ((1,), (0,))))
        mids.append((h, hat1, scale1, h_low))
        ups.append((f_low, slope))
    (y_parts,) = exch(
        4, [by_owner(*partial_y)], [((nd, cap + 1, D), F32)], [send_blocks(0, 0, nd)]
    )
    (y_all,) = exch(
        5, [jnp.sum(y_parts, axis=0)], [((nd, cap + 1, D), F32)], [send_all(0, 0, nd)]
    )
    y = to_rows(y_all)
    tops = []
    vecs = []
    for e in range(2):
        z, hat2, scale2 = norm_rows(
            mids[e][0] + y[e] + bias[e, O_OUT : O_OUT + D], gains[e, 2], bias[e, O_2 : O_2 + D]
        )
        tops.append((hat2, scale2))
        vecs.append(z.astype(BF16))
    qvec, pvec = vecs

    owner = passage_query[:rows_p]
    kept = kept_mask[:rows_p] == 1
    earlier = jnp.concatenate([jnp.full((1,), -1, jnp.int32), owner[:-1]])
    valid = owner >= 0
    first = valid & (owner != earlier)
    member = owner[None, :] == jnp.arange(nq, dtype=jnp.int32)[:, None]
    positive = member & first[None, :]
    negative = member & jnp.logical_not(first)[None, :] & kept[None, :]
    counts = jnp.sum(member.astype(F32), axis=1) - 1.0
    score_scale = 2.0 * D ** (-0.5)
    scores = dot(qvec, pvec, ((1,), (1,))) * score_scale
    masked = jnp.where(valid[None, :], scores, -1e30)
    peak = jnp.max(masked, axis=1)
    summed = jnp.sum(jnp.where(valid[None, :], jnp.exp(masked - peak[:, None]), 0.0), axis=1)
    logsum = peak + jnp.log(summed)
    pos_score = jnp.sum(jnp.where(positive, scores, 0.0), axis=1)
    margins = MARGIN - pos_score[:, None] + scores
    active_neg = negative & (margins > 0)
    hinge = jnp.sum(jnp.where(active_neg, margins, 0.0), axis=1) / counts
    active_total = jnp.sum(active_neg.astype(F32), axis=1)
    loss = jnp.sum(logsum - pos_score + hinge)
    score_grad = (
        jnp.where(valid[None, :], jnp.exp(scores - logsum[:, None]), 0.0)
        - positive.astype(F32) * (1.0 + active_total / counts)[:, None]
        + active_neg.astype(F32) / counts[:, None]
    )
    score_low = score_grad.astype(BF16)
    vec_grads = (
        (dot(score_low, pvec, ((1,), (0,))) * score_scale).astype(BF16).astype(F32),
        (dot(score_low, qvec, ((0,), (0,))) * score_scale).astype(BF16).astype(F32),
    )

    partial_h = []
    gain_grads = [[None] * 3 for _ in range(2)]
    shifts = [dict() for _ in range(2)]
    top_grads, shrink_grads, du_parts = [], [], []
    for e in range(2):
        hat2, scale2 = tops[e]
        gain_grads[e][2] = jnp.sum(vec_grads[e] * hat2, axis=0)
        shifts[e]["2"] = jnp.sum(vec_grads[e], axis=0)
        g_top = norm_rows_back(vec_grads[e], gains[e, 2], hat2, scale2)
        dy = g_top.astype(BF16)
        shifts[e]["out"] = jnp.sum(dy.astype(F32), axis=0)
        f_low, slope = ups[e]
        shrink_grads.append(dot(f_low, dy, ((0,), (0,))))
        df = dot(dy, w_down[e], ((1,), (1,)))
        du = (slope * df).astype(BF16)
        du_parts.append(du)
        partial_h.append(dot(du, w_up[e], ((1,), (1,))))
        top_grads.append(g_top)
    du_mine = jnp.concatenate(du_parts)
    h_parts, du_all = exch(
        6,
        [by_owner(*partial_h), du_mine],
        [((nd, cap + 1, D), F32), ((nd, nq + rows_p, ff_cols), BF16)],
        [send_blocks(0, 0, nd), send_all(1, 1, nd)],
    )
    h_mine = jnp.sum(h_parts, axis=0)
    top_mine = lax.dynamic_index_in_dim(by_owner(*top_grads), me, 0, False)
    rows_mine = lax.dynamic_index_in_dim(rows, me, 0, False)
    is_q = (me >= nd - nq).astype(F32)
    has = jnp.stack([(c * nd + me < n_valid).astype(F32) for c in range(cap)] + [is_q])
    g_h = (top_mine + h_mine) * has[:, None]
    gain_one = jnp.stack([gains[1, 1]] * cap + [gains[0, 1]])
    shift_one = jnp.stack([bias[1, O_1 : O_1 + D]] * cap + [bias[0, O_1 : O_1 + D]])
    _, hat_mine, scale_mine = norm_rows(rows_mine, gain_one, shift_one)
    g_mid = norm_rows_back(g_h, gain_one, hat_mine, scale_mine)
    gain_mid = g_h * hat_mine
    do_mine = g_mid.astype(BF16)
    backs = [
        encode_back(
            fronts[c][1], g_mid[c], w_in[1 if c < cap else 0], w_out[1 if c < cap else 0],
            gains[1 if c < cap else 0],
        )
        for c in range(cap + 1)
    ]

    def both_encoders(pick):
        return jnp.stack([pick(cap), sum(pick(c) for c in range(cap))])

    sums = jnp.concatenate(
        [both_encoders(lambda i, j=j: backs[i][1][j]) for j in (5, 6, 7)]
        + [both_encoders(lambda i: gain_mid[i]), both_encoders(lambda i: g_h[i])]
    )
    line = jnp.concatenate(
        [jnp.stack([b[1][j] for b in backs]) for j in (2, 3, 4)] + [do_mine, sums.astype(BF16)]
    )
    n_line = 4 * (cap + 1) + 10
    factor_t = jnp.concatenate(
        [b[1][0] for b in backs] + [b[1][1] for b in backs]
        + [f[1][2][:, 0][None] for f in fronts] + [f[1][8][None] for f in fronts]
    )
    n_factor = factor_t.shape[0]
    f_pad = -(-n_factor // LANE) * LANE
    factor_cols = jnp.pad(factor_t, ((0, f_pad - n_factor), (0, 0))).T

    def pad_rows(value):
        value = value.reshape(nd, cols, value.shape[1])
        return jnp.pad(value, ((0, 0), (0, rows_c - cols), (0, 0)))

    send = pad_rows(jnp.concatenate([b[0] for b in backs], axis=1).astype(BF16))
    token_grads, factors, lines = exch(
        7,
        [send, pad_rows(factor_cols), line],
        [
            ((rows_c, n_valid * LP + nq * LANE), BF16),
            ((nd, rows_c, f_pad), BF16),
            ((nd, n_line, D), BF16),
        ],
        [passage_move(c, False) for c in range(cap)]
        + [query_move(False), send_blocks(1, 1, nd), send_all(2, 2, nd)],
    )
    table_grad = table_sums(token_grads, all_ids, total)[:cols, :vocab]
    token_grads = token_grads[:cols].astype(F32)
    pos_grad = jnp.sum(token_grads[:, :q_from].reshape(cols, n_valid, LP), axis=1)
    pos_grad = pos_grad.at[:, :LANE].add(
        jnp.sum(token_grads[:, q_from:].reshape(cols, nq, LANE), axis=1)
    )
    table_grad = table_grad.at[:, V:].add(pos_grad)

    step_h = (cap + 1) * H
    factors = factors[:, :cols].transpose(0, 2, 1)
    t_all = factors[:, :step_h].reshape(nd, cap + 1, H, cols)
    w_all = factors[:, step_h : 2 * step_h].reshape(nd, cap + 1, H, cols)
    x_all = factors[:, 2 * step_h : 2 * step_h + cap + 1]
    a_all = factors[:, 2 * step_h + cap + 1 : 2 * step_h + 2 * (cap + 1)]
    q_all, da_all, dq_all, do_all = (
        lines[:, j * (cap + 1) : (j + 1) * (cap + 1)] for j in range(4)
    )
    sums = jnp.sum(lines[:, 4 * (cap + 1) :].astype(F32), axis=0).reshape(5, 2, D)

    def of_encoder(value, e):
        if e == 0:
            return value[nd - nq :, cap]
        return value[:, :cap].reshape((nd * cap,) + value.shape[2:])

    du_all = du_all.transpose(1, 0, 2).reshape(nq + rows_p, FF)
    in_grads, out_grads, expand_grads = [], [], []
    for e in range(2):
        du_full = du_all[:nq] if e == 0 else du_all[nq:]
        shifts[e]["in"] = jnp.sum(du_full.astype(F32), axis=0)
        h_cols = lax.dynamic_slice_in_dim(mids[e][3], me * cols, cols, 1)
        expand_grads.append(dot(h_cols, du_full, ((0,), (0,))))
        t, w, x, a = (of_encoder(u, e) for u in (t_all, w_all, x_all, a_all))
        q, da, dq, do = (of_encoder(u, e) for u in (q_all, da_all, dq_all, do_all))
        rows_e = q.shape[0]
        qh = q.reshape(rows_e, H, HD)
        dah = da.reshape(rows_e, H, HD)
        g_q = dot(x, dq, ((0,), (0,)))
        g_k = jnp.einsum("phi,phd->ihd", t, qh, preferred_element_type=F32).reshape(cols, D)
        g_v = jnp.einsum("phi,phd->ihd", w, dah, preferred_element_type=F32).reshape(cols, D)
        in_grads.append(jnp.concatenate([g_q, g_k, g_v], axis=1))
        out_grads.append(dot(a, do, ((0,), (0,))))
        shifts[e]["q"] = jnp.sum(dq.astype(F32), axis=0)
        shifts[e]["o"] = jnp.sum(do.astype(F32), axis=0)
    gain_grad = jnp.stack(
        [jnp.stack([sums[1, e], sums[3, e], gain_grads[e][2]]) for e in range(2)]
    )
    bias_grad = jnp.stack(
        [
            jnp.concatenate(
                [shifts[e]["q"], sums[0, e], shifts[e]["o"], sums[4, e], shifts[e]["in"],
                 shifts[e]["out"], shifts[e]["2"], sums[2, e]]
            )
            for e in range(2)
        ]
    )
    grads = (
        table_grad.T,
        jnp.stack(in_grads),
        jnp.stack(out_grads),
        jnp.stack(expand_grads),
        jnp.stack(shrink_grads),
        lax.dynamic_slice_in_dim(gain_grad, me * cols, cols, 2),
        lax.dynamic_slice_in_dim(bias_grad, me * bias_terms.shape[1], bias_terms.shape[1], 1),
    )
    local_squares = sum(jnp.sum(g * g) for g in grads)
    (squares,) = exch(
        8, [jnp.broadcast_to(local_squares, (8, LANE))], [((nd, 8, LANE), F32)],
        [send_all(0, 0, nd)],
    )
    grad_norm = jnp.sqrt(jnp.sum(squares[:, 0, 0]))
    factor = CLIP / jnp.maximum(grad_norm, CLIP)
    step = step_count[0].astype(F32)
    masters = (embed_table, attend_in, attend_out, expand_weight, shrink_weight, norm_gains, bias_terms)
    firsts = (embed_first, attend_in_first, attend_out_first, expand_first, shrink_first, gains_first, bias_first)
    seconds = (embed_second, attend_in_second, attend_out_second, expand_second, shrink_second, gains_second, bias_second)
    results = [loss, grad_norm]
    for index in range(7):
        results.extend(
            adam_update(masters[index], grads[index] * factor, firsts[index], seconds[index], step, LEARN_RATES[index])
        )
    return tuple(results)


def on_device(
    passage_ids, query_ids, passage_query, kept_mask, neg_count, step_count,
    embed_table, attend_in, attend_out, expand_weight, shrink_weight, norm_gains, bias_terms,
    embed_first, embed_second, attend_in_first, attend_in_second,
    attend_out_first, attend_out_second, expand_first, expand_second,
    shrink_first, shrink_second, gains_first, gains_second, bias_first, bias_second,
):
    if embed_table.shape[1] % 8 != 0:
        return on_device_rows(
            passage_ids, query_ids, passage_query, kept_mask, neg_count, step_count,
            embed_table, attend_in, attend_out, expand_weight, shrink_weight, norm_gains,
            bias_terms, embed_first, embed_second, attend_in_first, attend_in_second,
            attend_out_first, attend_out_second, expand_first, expand_second,
            shrink_first, shrink_second, gains_first, gains_second, bias_first, bias_second,
        )
    narrow = lax.axis_size("narrow")
    nd = lax.axis_size("wide") * narrow
    me = lax.axis_index("wide") * narrow + lax.axis_index("narrow")
    cols = embed_table.shape[1]
    n_slots = passage_query.shape[0]
    per_wide = query_ids.shape[0]
    nq = per_wide * lax.axis_size("wide")
    n_valid = VALID_PER_QUERY * nq
    cap = -(-n_valid // nd)
    ff_cols = FF // nd
    rows = n_valid + nq
    tq = nq * LQ
    query_home = nd * 5 // 8 - 1
    exch = functools.partial(comm, nd=nd, narrow=narrow)
    small_width = -(-max(cols, bias_terms.shape[1]) // LANE) * LANE
    ids_width = max(LP, -(-tq // LANE) * LANE)

    def widen(value, width):
        return jnp.pad(value, ((0, 0), (0, width - value.shape[1])))

    spot = jnp.arange(tq) // (LQ * per_wide) == lax.axis_index("wide")
    spot = spot & (lax.axis_index("narrow") == 0)
    q_line = jnp.where(spot, jnp.tile(query_ids.reshape(-1), tq // (LQ * per_wide)), 0)
    ids_mine = jnp.concatenate([widen(passage_ids, ids_width), widen(q_line[None], ids_width)])
    small_mine = jnp.concatenate(
        [widen(norm_gains.reshape(6, cols), small_width), widen(bias_terms, small_width)]
    ).astype(BF16)
    n_own = passage_ids.shape[0]
    ids_got, small_got = exch(
        1,
        [ids_mine, small_mine],
        [((nd, n_own + 1, ids_width), jnp.int32), ((nd, 8, small_width), BF16)],
        [send_all(0, 0, nd), send_all(1, 1, nd)],
    )
    pid = ids_got[:, :n_own, :LP].reshape(n_slots, LP)[:n_valid]
    qid = jnp.sum(ids_got[:, n_own, :tq], axis=0)
    q_from = n_valid * LP
    token_total = -(-(q_from + tq) // 1024) * 1024
    all_ids = jnp.pad(jnp.concatenate([pid.reshape(-1), qid]), (0, token_total - q_from - tq))
    gains = small_got[:, :6, :cols].transpose(1, 0, 2).reshape(2, 3, D).astype(F32)
    bias = small_got[:, 6:, : bias_terms.shape[1]].transpose(1, 0, 2).reshape(2, -1).astype(F32)

    vocab = V + LP
    total = -(-vocab // HASH) * HASH
    table_low = jnp.pad(embed_table.T.astype(BF16), ((0, 0), (0, total - vocab)))
    got = table_rows(table_low, all_ids)
    pos_mine = table_low[:, V : V + LP]
    up_mine = expand_weight.astype(BF16).reshape(2 * cols, nd, ff_cols).transpose(1, 0, 2)

    def passage_move(c):
        return Send(
            0, 0,
            lambda ref, s, t: ref.at[:, pl.ds(pl.multiple_of((c * nd + t) * LP, LANE), LP)],
            lambda ref, s, t: ref.at[s, :, pl.ds(c * LP, LP)],
            lambda ref, n: ref.at[:, pl.ds(0, n * LP)],
            lambda ref, n: ref.at[pl.ds(0, n), :, pl.ds(0, LP)],
            (0, nd), (0, min(nd, n_valid - c * nd)),
        )

    query_move = Send(
        0, 1,
        lambda ref, s, t: ref.at[:, pl.ds(q_from, tq)],
        lambda ref, s, t: ref.at[s],
        lambda ref, n: ref.at[:, pl.ds(0, n * tq)],
        lambda ref, n: ref.at[pl.ds(0, n)],
        (0, nd), (query_home, query_home + 1),
    )
    mine, mine_q, pos, w_up = exch(
        2,
        [got, pos_mine, up_mine],
        [
            ((nd, cols, cap * LP), BF16), ((nd, cols, tq), BF16), ((nd, cols, LP), BF16),
            ((nd, 2 * cols, ff_cols), BF16),
        ],
        [passage_move(c) for c in range(cap)]
        + [query_move, send_all(1, 2, nd), send_blocks(2, 3, nd)],
    )
    w_up = w_up.reshape(nd, 2, cols, ff_cols).transpose(1, 0, 2, 3).reshape(2, D, ff_cols)
    w_up = jnp.pad(w_up, ((0, 0), (0, 0), (0, LANE - ff_cols)))
    w_down = jnp.pad(shrink_weight.astype(BF16), ((0, 0), (0, LANE - ff_cols), (0, 0)))
    w_in = lax.all_gather(attend_in.astype(BF16), AXES, axis=1, tiled=True)
    w_out = lax.all_gather(attend_out.astype(BF16), AXES, axis=1, tiled=True)
    cv = jnp.stack(
        [v for e in range(2) for v in (
            gains[e, 0], bias[e, O_EMB : O_EMB + D], bias[e, O_V : O_V + D])]
        + [jnp.zeros((D,), F32)] * 2,
        axis=1,
    )
    rv = jnp.stack(
        [v for e in range(2) for v in (
            bias[e, O_Q : O_Q + D], bias[e, O_O : O_O + D], bias[e, O_1 : O_1 + D],
            bias[e, O_OUT : O_OUT + D], bias[e, O_2 : O_2 + D], gains[e, 1], gains[e, 2],
            jnp.zeros((D,), F32))]
    )
    b_in = lax.dynamic_index_in_dim(
        bias[:, O_IN : O_IN + FF].reshape(2, nd, ff_cols), me, 1, False
    )
    b_in = jnp.pad(b_in, ((0, 6), (0, LANE - ff_cols)))
    earlier = jnp.concatenate([jnp.full((1,), -1, jnp.int32), passage_query[:-1]])
    first_slot = ((passage_query >= 0) & (passage_query != earlier)).astype(jnp.int32)
    slots = jnp.pad(
        jnp.stack([passage_query, first_slot, kept_mask])[:, :n_valid],
        ((0, 5), (0, -(-n_valid // LANE) * LANE - n_valid)),
    )
    tok, fac, fac_q, line, line_q, du_all, shrink_g, h_low, out_rows, loss = middle(
        n_valid, nq, nd, narrow, cols, query_home, token_total,
        [mine, mine_q, pos, w_in, w_out, w_up, w_down, cv, rv, b_in, slots],
    )
    loss = loss[0, 0]

    table_grad = table_sums(tok, all_ids, total)[:, :vocab]
    tok = tok.astype(F32)
    pos_grad = jnp.sum(tok[:, :q_from].reshape(cols, n_valid, LP), axis=1)
    q_pos = jnp.sum(tok[:, q_from : q_from + tq].reshape(cols, nq, LQ), axis=1)
    pos_grad = pos_grad.at[:, :LQ].add(q_pos)
    table_grad = table_grad.at[:, V:].add(pos_grad)

    by_lane = fac.transpose(0, 2, 1).reshape(nd, 2, 64, cols)[:, :cap]
    q_rows = H * nq
    q_lane = fac_q.T
    heads_q = lambda v: v.reshape(H, nq, cols).transpose(1, 0, 2)
    factors = {
        1: tuple(
            v.reshape((nd * cap,) + v.shape[2:])
            for v in (by_lane[:, :, 0:H], by_lane[:, :, 16 : 16 + H], by_lane[:, :, 32],
                      by_lane[:, :, 40])
        ),
        0: (
            heads_q(q_lane[:q_rows]), heads_q(q_lane[q_rows : 2 * q_rows]),
            q_lane[2 * q_rows : 2 * q_rows + nq], q_lane[2 * q_rows + nq : 2 * q_rows + 2 * nq],
        ),
    }
    lines = {
        1: tuple(line[:, 2 * j : 2 * j + cap].reshape(nd * cap, D) for j in range(4)),
        0: tuple(line_q[nq * j : nq * (j + 1)] for j in range(4)),
    }
    sums = {1: jnp.sum(line[:, 8:13].astype(F32), axis=0), 0: line_q[32:37].astype(F32)}
    du_rows = du_all[:, :, :ff_cols].transpose(1, 0, 2).reshape(rows, FF)
    h_cols = lax.dynamic_slice_in_dim(h_low, me * cols, cols, 1).astype(BF16)
    in_grads, out_grads, expand_grads, bias_parts, gain_parts = [], [], [], [], []
    for e in range(2):
        at, n = (n_valid, nq) if e == 0 else (0, n_valid)
        du_e = du_rows[at : at + n]
        expand_grads.append(dot(h_cols[at : at + n], du_e, ((0,), (0,))))
        t, w, x, a = factors[e]
        q, da, dq, do = lines[e]
        n_e = q.shape[0]
        g_q = dot(x, dq, ((0,), (0,)))
        g_k = jnp.einsum(
            "phi,phd->ihd", t, q.reshape(n_e, H, HD), preferred_element_type=F32
        ).reshape(cols, D)
        g_v = jnp.einsum(
            "phi,phd->ihd", w, da.reshape(n_e, H, HD), preferred_element_type=F32
        ).reshape(cols, D)
        in_grads.append(jnp.concatenate([g_q, g_k, g_v], axis=1))
        out_grads.append(dot(a, do, ((0,), (0,))))
        s = sums[e]
        gain_parts.append(jnp.stack([s[0], s[3], out_rows[3 * e]]))
        bias_parts.append(
            jnp.concatenate(
                [jnp.sum(dq.astype(F32), axis=0), s[2], jnp.sum(do.astype(F32), axis=0), s[4],
                 jnp.sum(du_e.astype(F32), axis=0), out_rows[3 * e + 2], out_rows[3 * e + 1], s[1]]
            )
        )
    grads = (
        table_grad.T,
        jnp.stack(in_grads),
        jnp.stack(out_grads),
        jnp.stack(expand_grads),
        shrink_g[:, :ff_cols],
        lax.dynamic_slice_in_dim(jnp.stack(gain_parts), me * cols, cols, 2),
        lax.dynamic_slice_in_dim(
            jnp.stack(bias_parts), me * bias_terms.shape[1], bias_terms.shape[1], 1
        ),
    )
    local_squares = sum(jnp.sum(g * g) for g in grads)
    (squares,) = exch(
        8, [jnp.broadcast_to(local_squares, (8, LANE))], [((nd, 8, LANE), F32)],
        [send_all(0, 0, nd)],
    )
    grad_norm = jnp.sqrt(jnp.sum(squares[:, 0, 0]))
    factor = CLIP / jnp.maximum(grad_norm, CLIP)
    step = step_count[0].astype(F32)
    masters = (embed_table, attend_in, attend_out, expand_weight, shrink_weight, norm_gains, bias_terms)
    firsts = (embed_first, attend_in_first, attend_out_first, expand_first, shrink_first, gains_first, bias_first)
    seconds = (embed_second, attend_in_second, attend_out_second, expand_second, shrink_second, gains_second, bias_second)
    results = [loss, grad_norm]
    for index in range(7):
        results.extend(
            adam_update(masters[index], grads[index] * factor, firsts[index], seconds[index], step, LEARN_RATES[index])
        )
    return tuple(results)


def solution(mesh):
    both = ("wide", "narrow")
    weight_specs = (P(None, both),) + (P(None, both, None),) * 4 + (P(None, None, both), P(None, both))
    pairs = tuple(s for spec in weight_specs for s in (spec, spec))
    in_specs = (P(both, None), P("wide", None), P(), P(), P("wide"), P()) + weight_specs + pairs
    out_specs = (P(), P()) + tuple(s for spec in weight_specs for s in (spec, spec, spec))
    return jax.shard_map(on_device, mesh=mesh, in_specs=in_specs, out_specs=out_specs, check_vma=False)
```

```python
import functools

import jax
import jax.numpy as jnp
from jax import lax
from jax.experimental import pallas as pl
from jax.experimental.pallas import tpu as pltpu
from jax.sharding import PartitionSpec as P

D = 768
H = 12
HD = 64
FF = 3072
V = 18000
LP = 384
LQ = 32
LANE = 128
VALID_PER_QUERY = 5

MARGIN = 1.0
CLIP = 1.0
BETA_ONE = 0.9
BETA_TWO = 0.999
LEARN_RATES = (1.0, 0.02, 0.08, 0.02, 0.02, 1.0, 0.1)
WEIGHT_DECAY = 0.01
ADAM_EPS = 1e-08
NORM_EPS = 1e-05
AXES = ("wide", "narrow")
F32 = jnp.float32
BF16 = jnp.bfloat16
O_Q, O_V, O_O, O_1, O_IN, O_OUT, O_2, O_EMB = (
    0, D, 2 * D, 3 * D, 4 * D, 4 * D + FF, 5 * D + FF, 6 * D + FF
)


def dot(left, right, dims):
    return lax.dot_general(left, right, (dims, ((), ())), preferred_element_type=F32)


def norm_rows(values, gain, shift):
    center = values - jnp.mean(values, axis=-1, keepdims=True)
    spread = jnp.mean(center * center, axis=-1, keepdims=True)
    scale = lax.rsqrt(spread + NORM_EPS)
    hat = center * scale
    return hat * gain + shift, hat, scale


def norm_rows_back(grad, gain, hat, scale):
    scaled = grad * gain
    mean_one = jnp.mean(scaled, axis=-1, keepdims=True)
    mean_two = jnp.mean(scaled * hat, axis=-1, keepdims=True)
    return scale * (scaled - mean_one - hat * mean_two)


def gelu_both(upper):
    cdf = 0.5 * (1.0 + lax.erf(upper * 0.7071067811865476))
    pdf = jnp.exp(-0.5 * upper * upper) * 0.3989422804014327
    return upper * cdf, cdf + upper * pdf


def adam_update(weight, grad, first, second, step, rate):
    first_new = BETA_ONE * first + (1.0 - BETA_ONE) * grad
    second_new = BETA_TWO * second + (1.0 - BETA_TWO) * grad * grad
    first_hat = first_new / (1.0 - BETA_ONE**step)
    second_hat = second_new / (1.0 - BETA_TWO**step)
    weight_new = weight - rate * (
        first_hat / (jnp.sqrt(second_hat) + ADAM_EPS) + WEIGHT_DECAY * weight
    )
    return (weight_new, first_new, second_new)


MESH = pl.DeviceIdType.MESH
HASH = 512


class Send:
    def __init__(self, src, dst, take, put, many_src, many_dst, sources, targets):
        self.src, self.dst, self.take, self.put = src, dst, take, put
        self.many_src, self.many_dst = many_src, many_dst
        self.sources, self.targets = sources, targets


def inside(index, span):
    return jnp.logical_and(index >= span[0], index < span[1])


def comm_body(sends, n_in, n_out, nd, narrow, *refs):
    ins, outs = refs[:n_in], refs[n_in : n_in + n_out]
    send_sem, recv_sem, own_sem = refs[n_in + n_out :]
    me = lax.axis_index("wide") * narrow + lax.axis_index("narrow")
    barrier = pltpu.get_barrier_semaphore()

    def greet(k, carry):
        t = lax.rem(me + k, nd)
        pl.semaphore_signal(
            barrier, inc=1, device_id=(t // narrow, lax.rem(t, narrow)), device_id_type=MESH
        )
        return carry

    lax.fori_loop(1, nd, greet, 0)
    pl.semaphore_wait(barrier, nd - 1)

    def push(k, carry):
        t = lax.rem(me + k, nd)
        for i, s in enumerate(sends):

            @pl.when(jnp.logical_and(inside(me, s.sources), inside(t, s.targets)))
            def _():
                pltpu.make_async_remote_copy(
                    src_ref=s.take(ins[s.src], me, t),
                    dst_ref=s.put(outs[s.dst], me, t),
                    send_sem=send_sem.at[i],
                    recv_sem=recv_sem.at[i],
                    device_id=(t // narrow, lax.rem(t, narrow)),
                    device_id_type=MESH,
                ).start()

        return carry

    lax.fori_loop(1, nd, push, 0)
    for i, s in enumerate(sends):
        both = jnp.logical_and(inside(me, s.sources), inside(me, s.targets))

        @pl.when(both)
        def _():
            own = pltpu.make_async_copy(
                s.take(ins[s.src], me, me), s.put(outs[s.dst], me, me), own_sem.at[i]
            )
            own.start()
            own.wait()

    for i, s in enumerate(sends):
        n_t = s.targets[1] - s.targets[0]
        n_s = s.sources[1] - s.sources[0]
        is_s, is_t = inside(me, s.sources), inside(me, s.targets)
        for own in (0, 1):
            mine = is_t if own else jnp.logical_not(is_t)
            if n_t - own > 0:

                @pl.when(jnp.logical_and(is_s, mine))
                def _():
                    view = s.many_src(ins[s.src], n_t - own) if s.many_src(ins[s.src], 1) is not None else outs[s.dst].at[pl.ds(0, n_t - own)]
                    pltpu.make_async_copy(view, view, send_sem.at[i]).wait()

            mine = is_s if own else jnp.logical_not(is_s)
            if n_s - own > 0:

                @pl.when(jnp.logical_and(is_t, mine))
                def _():
                    view = s.many_dst(outs[s.dst], n_s - own)
                    pltpu.make_async_copy(view, view, recv_sem.at[i]).wait()


def comm(collective, arrays, out_shapes, sends, nd, narrow):
    vmem = pl.BlockSpec(memory_space=pltpu.VMEM)
    n = len(sends)
    return pl.pallas_call(
        functools.partial(comm_body, sends, len(arrays), len(out_shapes), nd, narrow),
        out_shape=[jax.ShapeDtypeStruct(s, d) for s, d in out_shapes],
        in_specs=[vmem] * len(arrays),
        out_specs=[vmem] * len(out_shapes),
        scratch_shapes=[
            pltpu.SemaphoreType.DMA((n,)),
            pltpu.SemaphoreType.DMA((n,)),
            pltpu.SemaphoreType.DMA((n,)),
        ],
        compiler_params=pltpu.CompilerParams(collective_id=collective, has_side_effects=True),
    )(*arrays)


def send_all(src, dst, nd):
    return Send(
        src, dst,
        lambda ref, s, t: ref,
        lambda ref, s, t: ref.at[s],
        lambda ref, n: None, lambda ref, n: ref.at[pl.ds(0, n)],
        (0, nd), (0, nd),
    )


def send_blocks(src, dst, nd):
    return Send(
        src, dst,
        lambda ref, s, t: ref.at[t],
        lambda ref, s, t: ref.at[s],
        lambda ref, n: ref.at[pl.ds(0, n)], lambda ref, n: ref.at[pl.ds(0, n)],
        (0, nd), (0, nd),
    )


def stack_pairs(pieces, store):
    rows = pieces[0].shape[0]
    for i in range(0, len(pieces), 2):
        store(i * rows, jnp.concatenate(pieces[i : i + 2], axis=0))


def gather_body(rows, blocks, table_ref, ids_ref, out_ref, stacked):
    @pl.when(pl.program_id(0) == 0)
    def _():
        pieces = [
            table_ref[:, b * HASH : (b + 1) * HASH].astype(F32) for b in range(blocks)
        ]

        def store(row, value):
            stacked[row : row + value.shape[0], :] = value.astype(BF16)

        stack_pairs(pieces, store)

    ids = ids_ref[0]
    low = ids & (HASH - 1)
    high = ids >> (HASH.bit_length() - 1)
    width = ids.shape[1]
    hot = (lax.broadcasted_iota(jnp.int32, (HASH, width), 0) == low).astype(F32).astype(BF16)
    picked = jnp.dot(stacked[...], hot, preferred_element_type=F32)
    value = jnp.zeros((rows, width), F32)
    for b in range(blocks):
        value = jnp.where(high == b, picked[b * rows : (b + 1) * rows], value)
    out_ref[...] = value.astype(BF16)


def table_rows(table, ids):
    rows, total = table.shape
    tokens = ids.shape[0]
    tile = 512
    blocks = total // HASH
    return pl.pallas_call(
        functools.partial(gather_body, rows, blocks),
        grid=(tokens // tile,),
        out_shape=jax.ShapeDtypeStruct((rows, tokens), BF16),
        in_specs=[
            pl.BlockSpec((rows, total), lambda i: (0, 0)),
            pl.BlockSpec((1, 1, tile), lambda i: (i, 0, 0)),
        ],
        out_specs=pl.BlockSpec((rows, tile), lambda i: (0, i)),
        scratch_shapes=[pltpu.VMEM((blocks * rows, HASH), BF16)],
        name="table_rows",
    )(table, ids.reshape(tokens // tile, 1, tile))


def scatter_body(rows, blocks, values_ref, ids_ref, out_ref, spread, acc):
    step = pl.program_id(0)
    ids = ids_ref[0]
    low = ids & (HASH - 1)
    high = ids >> (HASH.bit_length() - 1)
    width = ids.shape[1]
    values = values_ref[...].astype(F32)
    pieces = [jnp.where(high == b, values, 0.0) for b in range(blocks)]

    def store(row, value):
        spread[row : row + value.shape[0], :] = value.astype(BF16)

    stack_pairs(pieces, store)
    hot = (lax.broadcasted_iota(jnp.int32, (HASH, width), 0) == low).astype(F32).astype(BF16)
    part = lax.dot_general(
        spread[...], hot, (((1,), (1,)), ((), ())), preferred_element_type=F32
    )

    @pl.when(step == 0)
    def _():
        acc[...] = part

    @pl.when(step > 0)
    def _():
        acc[...] += part

    @pl.when(step == pl.num_programs(0) - 1)
    def _():
        for b in range(blocks):
            out_ref[:, b * HASH : (b + 1) * HASH] = acc[b * rows : (b + 1) * rows, :]


def table_sums(values, ids, total):
    rows, tokens = values.shape
    tile = 1024
    blocks = total // HASH
    return pl.pallas_call(
        functools.partial(scatter_body, rows, blocks),
        grid=(tokens // tile,),
        out_shape=jax.ShapeDtypeStruct((rows, total), F32),
        in_specs=[
            pl.BlockSpec((rows, tile), lambda i: (0, i)),
            pl.BlockSpec((1, 1, tile), lambda i: (i, 0, 0)),
        ],
        out_specs=pl.BlockSpec((rows, total), lambda i: (0, 0)),
        scratch_shapes=[
            pltpu.VMEM((blocks * rows, tile), BF16),
            pltpu.VMEM((blocks * rows, HASH), F32),
        ],
        name="table_sums",
    )(values, ids.reshape(tokens // tile, 1, tile))


def head_mask(dtype):
    rows = lax.broadcasted_iota(jnp.int32, (H, D), 0)
    cols = lax.broadcasted_iota(jnp.int32, (H, D), 1)
    return (cols // HD == rows).astype(dtype)


def spread_heads(row):
    return row[None, :] * head_mask(row.dtype)


def encode_front(emb_t, w_in, w_out, gain, bias, length):
    width = emb_t.shape[1]
    center = emb_t - jnp.mean(emb_t, axis=0, keepdims=True)
    spread = jnp.mean(center * center, axis=0, keepdims=True)
    scale = lax.rsqrt(spread + NORM_EPS)
    hat = center * scale
    x0 = hat * gain[0][:, None] + bias[O_EMB : O_EMB + D][:, None]
    x_low = x0.astype(BF16)
    first_low = x_low[:, 0]
    q = (dot(first_low[None], w_in[:, :D], ((1,), (0,)))[0] + bias[O_Q : O_Q + D]).astype(BF16)
    k = dot(w_in[:, D : 2 * D], x_low, ((0,), (0,))).astype(BF16)
    v = (
        dot(w_in[:, 2 * D :], x_low, ((0,), (0,))) + bias[O_V : O_V + D][:, None]
    ).astype(BF16)
    q_heads = spread_heads(q)
    s = dot(q_heads, k, ((1,), (0,))) * 0.125
    if length < width:
        live = lax.broadcasted_iota(jnp.int32, (1, width), 1) < length
        s = jnp.where(live, s, -1e30)
    peak = jnp.max(s, axis=1, keepdims=True)
    e = jnp.exp(s - peak)
    p = e / jnp.sum(e, axis=1, keepdims=True)
    p_low = p.astype(BF16)
    mixed = dot(p_low, v, ((1,), (1,)))
    a = jnp.sum(mixed * head_mask(F32), axis=0).astype(BF16)
    o = dot(a[None], w_out, ((1,), (0,)))[0] + bias[O_O : O_O + D]
    return x0[:, 0] + o, (hat, scale, x_low, q, k, v, p, p_low, a)


def encode_back(kept, row_grad, w_in, w_out, gain):
    hat, scale, x_low, q, k, v, p, p_low, a = kept
    do = row_grad.astype(BF16)
    da = dot(do[None], w_out, ((1,), (1,)))[0].astype(BF16)
    da_heads = spread_heads(da)
    q_heads = spread_heads(q)
    dp = dot(da_heads, v, ((1,), (0,)))
    ds = (p * (dp - jnp.sum(dp * p, axis=1, keepdims=True))).astype(BF16)
    dq_heads = dot(ds, k, ((1,), (1,)))
    dq = (jnp.sum(dq_heads * head_mask(F32), axis=0) * 0.125).astype(BF16)
    t = dot(ds, x_low, ((1,), (1,))) * 0.125
    w = dot(p_low, x_low, ((1,), (1,)))
    gk = (dot(q_heads, w_in[:, D : 2 * D], ((1,), (1,))) * 0.125).astype(BF16)
    ev = dot(da_heads, w_in[:, 2 * D :], ((1,), (1,))).astype(BF16)
    gx = dot(gk, ds, ((0,), (0,))) + dot(ev, p_low, ((0,), (0,)))
    first = row_grad + dot(dq[None], w_in[:, :D], ((1,), (1,)))[0]
    is_first = lax.broadcasted_iota(jnp.int32, (1, gx.shape[1]), 1) == 0
    gx = gx + jnp.where(is_first, first[:, None], 0.0)
    p_sum = jnp.sum(p_low.astype(F32), axis=1)
    dbv = jnp.repeat(p_sum, HD) * da.astype(F32)
    g_gain = jnp.sum(gx * hat, axis=1)
    g_shift = jnp.sum(gx, axis=1)
    scaled = gx * gain[0][:, None]
    mean_one = jnp.mean(scaled, axis=0, keepdims=True)
    mean_two = jnp.mean(scaled * hat, axis=0, keepdims=True)
    g_emb = scale * (scaled - mean_one - hat * mean_two)
    return g_emb, (t.astype(BF16), w.astype(BF16), q, da, dq, dbv, g_gain, g_shift)


NN = (((1,), (0,)), ((), ()))
NT = (((1,), (1,)), ((), ()))
TN = (((0,), (0,)), ((), ()))
HIGH = lax.Precision.HIGHEST


def mm(left, right, dims, precision=None):
    return lax.dot_general(
        left, right, dims, preferred_element_type=F32, precision=precision
    )


def iota(shape, dim):
    return lax.broadcasted_iota(jnp.int32, shape, dim)


def as_bf16(mask):
    return mask.astype(F32).astype(BF16)


class Flow:
    def __init__(self, take, put, many, sources, targets):
        self.take, self.put, self.many = take, put, many
        self.sources, self.targets = sources, targets


class Net:
    def __init__(self, nd, narrow, send_sem, recv_sem, own_sem):
        self.nd, self.narrow = nd, narrow
        self.send_sem, self.recv_sem, self.own_sem = send_sem, recv_sem, own_sem
        self.me = lax.axis_index("wide") * narrow + lax.axis_index("narrow")
        self.used = 0

    def where(self, t):
        return (t // self.narrow, lax.rem(t, self.narrow))

    def barrier(self):
        sem = pltpu.get_barrier_semaphore()

        def greet(k, carry):
            t = lax.rem(self.me + k, self.nd)
            pl.semaphore_signal(sem, inc=1, device_id=self.where(t), device_id_type=MESH)
            return carry

        lax.fori_loop(1, self.nd, greet, 0)
        pl.semaphore_wait(sem, self.nd - 1)

    def start(self, flows):
        me, nd = self.me, self.nd
        base = self.used
        self.used += len(flows)

        def push(k, carry):
            t = lax.rem(me + k, nd)
            for i, f in enumerate(flows):

                @pl.when(jnp.logical_and(inside(me, f.sources), inside(t, f.targets)))
                def _():
                    pltpu.make_async_remote_copy(
                        src_ref=f.take(me, t),
                        dst_ref=f.put(me, t),
                        send_sem=self.send_sem.at[base + i],
                        recv_sem=self.recv_sem.at[base + i],
                        device_id=self.where(t),
                        device_id_type=MESH,
                    ).start()

            return carry

        for i, f in enumerate(flows):

            @pl.when(jnp.logical_and(inside(me, f.sources), inside(me, f.targets)))
            def _():
                pltpu.make_async_copy(
                    f.take(me, me), f.put(me, me), self.own_sem.at[base + i]
                ).start()

        lax.fori_loop(1, nd, push, 0)
        return base

    def finish(self, flows, base):
        me = self.me
        for i, f in enumerate(flows):
            n_t = f.targets[1] - f.targets[0]
            n_s = f.sources[1] - f.sources[0]
            is_s, is_t = inside(me, f.sources), inside(me, f.targets)

            @pl.when(jnp.logical_and(is_s, is_t))
            def _():
                pltpu.make_async_copy(
                    f.take(me, me), f.put(me, me), self.own_sem.at[base + i]
                ).wait()

            for own in (0, 1):
                mine = is_s if own else jnp.logical_not(is_s)
                if n_s - own > 0:

                    @pl.when(jnp.logical_and(is_t, mine))
                    def _():
                        view = f.many(n_s - own)
                        pltpu.make_async_copy(view, view, self.recv_sem.at[base + i]).wait()

            for own in (0, 1):
                mine = is_t if own else jnp.logical_not(is_t)
                if n_t - own > 0:

                    @pl.when(jnp.logical_and(is_s, mine))
                    def _():
                        view = f.many(n_t - own)
                        pltpu.make_async_copy(view, view, self.send_sem.at[base + i]).wait()


class Unit:
    def __init__(self, count, length):
        self.count, self.length = count, length
        self.tokens = count * length
        self.bits = count.bit_length() - 1
        self.rows = max(16, H * count)
        self.seqs = max(8, count)

    def pick(self):
        lane = iota((self.seqs, self.tokens), 1)
        seq = iota((self.seqs, self.tokens), 0)
        return lane == seq * self.length

    def spread(self):
        row, seq = iota((self.rows, self.seqs), 0), iota((self.rows, self.seqs), 1)
        return as_bf16((row & (self.count - 1)) == seq)

    def collect(self):
        row, seq = iota((self.seqs, self.rows), 1), iota((self.seqs, self.rows), 0)
        return as_bf16((row & (self.count - 1)) == seq)

    def heads(self):
        row, col = iota((self.rows, D), 0), iota((self.rows, D), 1)
        return ((row >> self.bits) == (col >> 6)).astype(F32)

    def live(self):
        row, lane = iota((self.rows, self.tokens), 0), iota((self.rows, self.tokens), 1)
        return (lane >> 5) == (row & (self.count - 1))


def unit_front(unit, emb, e, w, cv, rv, keep):
    center = emb - jnp.mean(emb, axis=0, keepdims=True)
    spread = jnp.mean(center * center, axis=0, keepdims=True)
    scale = lax.rsqrt(spread + NORM_EPS)
    hat = center * scale
    x0 = hat * cv[:, 3 * e : 3 * e + 1] + cv[:, 3 * e + 1 : 3 * e + 2]
    x_low = x0.astype(BF16)
    pick = unit.pick()
    x_first = mm(as_bf16(pick), x_low, NT).astype(BF16)
    x0_first = mm(pick.astype(F32), x0, NT, HIGH)
    q = (mm(x_first, w[:, 0:D], NN) + rv[8 * e : 8 * e + 1, :]).astype(BF16)
    k = mm(w[:, D : 2 * D], x_low, TN).astype(BF16)
    v = (mm(w[:, 2 * D : 3 * D], x_low, TN) + cv[:, 3 * e + 2 : 3 * e + 3]).astype(BF16)
    heads = unit.heads()
    q_heads = (mm(unit.spread(), q, NN) * heads).astype(BF16)
    s = mm(q_heads, k, NN) * 0.125
    if unit.count > 1:
        s = jnp.where(unit.live(), s, -1e30)
    peak = jnp.max(s, axis=1, keepdims=True)
    ex = jnp.exp(s - peak)
    p = ex / jnp.sum(ex, axis=1, keepdims=True)
    mixed = (mm(p.astype(BF16), v, NT) * heads).astype(BF16)
    a = mm(unit.collect(), mixed, NN).astype(BF16)
    o = mm(a, w[:, 3 * D : 4 * D], NN) + rv[8 * e + 1 : 8 * e + 2, :]
    keep(hat, scale, x_low, x_first, q, k, v, p, a)
    return x0_first + o


def unit_back(unit, row_grad, e, w, cv, kept):
    hat, scale, x_low, x_first, q, k, v, p, a = kept
    heads = unit.heads()
    spread, collect = unit.spread(), unit.collect()
    p_low = p.astype(BF16)
    do = row_grad.astype(BF16)
    da = mm(do, w[:, 3 * D : 4 * D], NT).astype(BF16)
    q_heads = (mm(spread, q, NN) * heads).astype(BF16)
    da_heads = (mm(spread, da, NN) * heads).astype(BF16)
    dp = mm(da_heads, v, NN)
    ds = (p * (dp - jnp.sum(dp * p, axis=1, keepdims=True))).astype(BF16)
    dq_heads = (mm(ds, k, NT) * heads * 0.125).astype(BF16)
    dq = mm(collect, dq_heads, NN).astype(BF16)
    t = mm(ds, x_low, NT) * 0.125
    wx = mm(p_low, x_low, NT)
    gk = (mm(q_heads, w[:, D : 2 * D], NT) * 0.125).astype(BF16)
    ev = mm(da_heads, w[:, 2 * D : 3 * D], NT).astype(BF16)
    first = row_grad + mm(dq, w[:, 0:D], NT)
    gx = mm(gk, ds, TN) + mm(ev, p_low, TN)
    gx = gx + mm(first, unit.pick().astype(F32), TN, HIGH)
    p_sum = jnp.sum(p_low.astype(F32), axis=1, keepdims=True)
    dbv = jnp.sum(p_sum * da_heads.astype(F32), axis=0, keepdims=True)
    g_gain = jnp.sum(gx * hat, axis=1, keepdims=True)
    g_shift = jnp.sum(gx, axis=1, keepdims=True)
    scaled = gx * cv[:, 3 * e : 3 * e + 1]
    mean_one = jnp.mean(scaled, axis=0, keepdims=True)
    mean_two = jnp.mean(scaled * hat, axis=0, keepdims=True)
    g_emb = scale * (scaled - mean_one - hat * mean_two)
    return g_emb, t, wx, da, dq, do, dbv, g_gain, g_shift


def load_rows(ref, count):
    return jnp.concatenate(
        [ref[pl.ds(j, count, stride=8), :] for j in range(D // LANE)], axis=1
    )


def store_rows(ref, value):
    for j in range(D // LANE):
        ref[pl.ds(j, value.shape[0], stride=8), :] = value[:, j * LANE : (j + 1) * LANE]


def middle_body(
    n_valid, nq, nd, narrow, cols, query_home, token_total,
    mine, mine_q, w_one, w_zero, w_up, w_down, cv, rv, b_in, slots,
    o_tok, o_fac, o_facq, o_line, o_lineq, o_du, o_shrink, o_h, o_rows, o_loss,
    hat_s, scale_s, xl_s, xf_s, q_s, k_s, v_s, p_s, a_s,
    hat_q, scale_q, xl_q, xf_q, q_q, k_q, v_q, p_q, a_q,
    r1_own, r1_ownq, r1_all, y_send, y_recv, y_sum, y_all, h_send, h_recv, h_recvq,
    du_own, du_f, gtok, gtok_q, fac, fac_q, line, line_q, f_s, slope_s, hlow_s, g_top_s, sums_s,
    size48,
    send_sem, recv_sem, own_sem,
):
    cap = -(-n_valid // nd)
    rows = n_valid + nq
    net = Net(nd, narrow, send_sem, recv_sem, own_sem)
    me = net.me
    everyone = (0, nd)
    home = (query_home, query_home + 1)
    q_owner = nd - nq
    q_owners = (q_owner, nd)

    def span(c):
        return (0, min(nd, n_valid - c * nd))

    net.barrier()
    passage = Unit(1, LP)
    queries = Unit(nq, LQ)
    n_mine = jnp.where(me < n_valid - (cap - 1) * nd, cap, cap - 1)

    def front(c, carry):
        at = pl.ds(pl.multiple_of(c * LP, LANE), LP)
        emb = mine[:, :, at].astype(F32).reshape(D, LP) + w_one[:, 4 * D :].astype(F32)

        def keep(hat, scale, x_low, x_first, q, k, v, p, a):
            hat_s[c], scale_s[c], xl_s[c], xf_s[c] = hat, scale, x_low, x_first
            q_s[c], k_s[c], v_s[c], p_s[c], a_s[c] = q, k, v, p, a

        r1 = unit_front(passage, emb, 1, w_one, cv, rv, keep)
        for j in range(D // LANE):
            r1_own[c, j : j + 1, :] = r1[0:1, j * LANE : (j + 1) * LANE]
        return carry

    lax.fori_loop(0, n_mine, front, 0)

    @pl.when(me == query_home)
    def _():
        parts = w_one[:, 4 * D : 4 * D + LANE].astype(F32)[:, 0:LQ]
        emb = mine_q[...].astype(F32).reshape(D, nq * LQ) + jnp.concatenate([parts] * nq, axis=1)

        def keep(hat, scale, x_low, x_first, q, k, v, p, a):
            hat_q[...], scale_q[...], xl_q[...], xf_q[...] = hat, scale, x_low, x_first
            q_q[...], k_q[...], v_q[...], p_q[...], a_q[...] = q, k, v, p, a

        store_rows(r1_ownq, unit_front(queries, emb, 0, w_zero, cv, rv, keep))

    flows = [
        Flow(
            lambda s, t, c=c: r1_own.at[c],
            lambda s, t, c=c: r1_all.at[pl.ds(pl.multiple_of(8 * (c * nd + s), 8), 8), :],
            lambda n: r1_all.at[pl.ds(0, 8 * n), :],
            span(c), everyone,
        )
        for c in range(cap)
    ] + [
        Flow(
            lambda s, t: r1_ownq,
            lambda s, t: r1_all.at[pl.ds(8 * n_valid, 8 * nq), :],
            lambda n: y_recv_q(n),
            home, everyone,
        )
    ]

    def y_recv_q(n):
        return h_recvq.at[pl.ds(0, n)]

    base = net.start(flows)
    net.finish(flows, base)

    part = {1: (0, n_valid), 0: (n_valid, nq)}
    y_parts = []
    for e in (1, 0):
        at, n = part[e]
        r1 = load_rows(r1_all.at[pl.ds(8 * at, 8 * n), :], n)
        h, hat1, scale1 = norm_rows(r1, rv[8 * e + 5 : 8 * e + 6, :], rv[8 * e + 2 : 8 * e + 3, :])
        h_low = h.astype(BF16)
        hlow_s[at : at + n, :] = h
        o_h[at : at + n, :] = h_low.astype(F32)
        upper = mm(h_low, w_up[e], NN) + b_in[e : e + 1, :]
        active, slope = gelu_both(upper)
        f_low = active.astype(BF16)
        f_s[at : at + n, :] = f_low.astype(F32)
        slope_s[at : at + n, :] = slope
        y_parts.append(mm(f_low, w_down[e], NN))
    store_rows(y_send, jnp.concatenate(y_parts, axis=0))
    flows = [
        Flow(
            lambda s, t, c=c: y_send.at[pl.ds(pl.multiple_of(8 * (c * nd + t), 8), 8), :],
            lambda s, t, c=c: y_recv.at[s, c],
            lambda n, c=c: y_recv.at[pl.ds(0, n), c],
            everyone, span(c),
        )
        for c in range(cap)
    ] + [
        Flow(
            lambda s, t: y_send.at[pl.ds(pl.multiple_of(8 * (n_valid + t - q_owner), 8), 8), :],
            lambda s, t: y_recv.at[s, cap],
            lambda n: y_recv.at[pl.ds(0, n), cap],
            everyone, q_owners,
        )
    ]
    base = net.start(flows)
    net.finish(flows, base)
    y_sum[...] = jnp.sum(y_recv[...], axis=0)
    flows = [
        Flow(
            lambda s, t, c=c: y_sum.at[c],
            lambda s, t, c=c: y_all.at[pl.ds(pl.multiple_of(8 * (c * nd + s), 8), 8), :],
            lambda n: y_all.at[pl.ds(0, 8 * n), :],
            span(c), everyone,
        )
        for c in range(cap)
    ] + [
        Flow(
            lambda s, t: y_sum.at[cap],
            lambda s, t: y_all.at[pl.ds(pl.multiple_of(8 * (n_valid + s - q_owner), 8), 8), :],
            lambda n: y_all.at[pl.ds(0, 8 * n), :],
            q_owners, everyone,
        )
    ]
    base = net.start(flows)
    net.finish(flows, base)

    tops, vecs = {}, {}
    for e in (1, 0):
        at, n = part[e]
        y = load_rows(y_all.at[pl.ds(8 * at, 8 * n), :], n)
        top = hlow_s[at : at + n, :] + y + rv[8 * e + 3 : 8 * e + 4, :]
        z, hat2, scale2 = norm_rows(
            top, rv[8 * e + 6 : 8 * e + 7, :], rv[8 * e + 4 : 8 * e + 5, :]
        )
        tops[e] = (hat2, scale2)
        vecs[e] = z.astype(BF16)
    qvec, pvec = vecs[0], vecs[1]
    owner = slots[0:1, 0:n_valid]
    is_first = slots[1:2, 0:n_valid] == 1
    kept_slot = slots[2:3, 0:n_valid] == 1
    member = owner == iota((nq, n_valid), 0)
    valid = jnp.broadcast_to(owner >= 0, (nq, n_valid))
    positive = jnp.logical_and(member, is_first)
    negative = jnp.logical_and(member, jnp.logical_and(jnp.logical_not(is_first), kept_slot))
    counts = jnp.sum(member.astype(F32), axis=1, keepdims=True) - 1.0
    score_scale = 2.0 * D ** (-0.5)
    scores = mm(qvec, pvec, NT) * score_scale
    masked = jnp.where(valid, scores, -1e30)
    peak = jnp.max(masked, axis=1, keepdims=True)
    summed = jnp.sum(jnp.where(valid, jnp.exp(masked - peak), 0.0), axis=1, keepdims=True)
    logsum = peak + jnp.log(summed)
    pos_score = jnp.sum(jnp.where(positive, scores, 0.0), axis=1, keepdims=True)
    margins = MARGIN - pos_score + scores
    active = jnp.logical_and(negative, margins > 0)
    hinge = jnp.sum(jnp.where(active, margins, 0.0), axis=1, keepdims=True) / counts
    active_total = jnp.sum(active.astype(F32), axis=1, keepdims=True)
    loss = jnp.sum(logsum - pos_score + hinge, axis=0, keepdims=True)
    o_loss[...] = jnp.broadcast_to(loss, (8, LANE))
    score_grad = (
        jnp.where(valid, jnp.exp(scores - logsum), 0.0)
        - positive.astype(F32) * (1.0 + active_total / counts)
        + active.astype(F32) / counts
    )
    score_low = score_grad.astype(BF16)
    vec_grads = {
        0: (mm(score_low, pvec, NN) * score_scale).astype(BF16).astype(F32),
        1: (mm(score_low, qvec, TN) * score_scale).astype(BF16).astype(F32),
    }
    h_parts, out_rows = [], {}
    for e in (1, 0):
        at, n = part[e]
        hat2, scale2 = tops[e]
        grad = vec_grads[e]
        g_top = norm_rows_back(grad, rv[8 * e + 6 : 8 * e + 7, :], hat2, scale2)
        dy = g_top.astype(BF16)
        g_top_s[at : at + n, :] = g_top
        out_rows[e] = [
            jnp.sum(grad * hat2, axis=0, keepdims=True),
            jnp.sum(grad, axis=0, keepdims=True),
            jnp.sum(dy.astype(F32), axis=0, keepdims=True),
        ]
        f_low = f_s[at : at + n, :].astype(BF16)
        o_shrink[e] = mm(f_low, dy, TN)
        df = mm(dy, w_down[e], NT)
        du = (slope_s[at : at + n, :] * df).astype(BF16)
        du_f[at : at + n, :] = du.astype(F32)
        h_parts.append(mm(du, w_up[e], NT))
    for e in (0, 1):
        for j in range(3):
            o_rows[3 * e + j : 3 * e + j + 1, :] = out_rows[e][j]
    du_own[...] = du_f[...].astype(BF16)
    store_rows(h_send, jnp.concatenate(h_parts, axis=0))
    flows = [
        Flow(
            lambda s, t, c=c: h_send.at[pl.ds(pl.multiple_of(8 * (c * nd + t), 8), 8), :],
            lambda s, t, c=c: h_recv.at[s, c],
            lambda n, c=c: h_recv.at[pl.ds(0, n), c],
            everyone, span(c),
        )
        for c in range(cap)
    ] + [
        Flow(
            lambda s, t: h_send.at[pl.ds(8 * n_valid, 8 * nq), :],
            lambda s, t: h_recvq.at[s],
            lambda n: h_recvq.at[pl.ds(0, n)],
            everyone, home,
        )
    ]
    du_flows = [
        Flow(
            lambda s, t: du_own,
            lambda s, t: o_du.at[s],
            lambda n: o_du.at[pl.ds(0, n)],
            everyone, everyone,
        )
    ]
    base = net.start(flows)
    du_base = net.start(du_flows)
    fac[...] = jnp.zeros_like(fac)
    line[...] = jnp.zeros_like(line)
    sums_s[...] = jnp.zeros_like(sums_s)
    o_tok[:, n_valid * LP + nq * LQ :] = jnp.zeros(
        (cols, token_total - n_valid * LP - nq * LQ), BF16
    )
    net.finish(flows, base)

    def load_rows_sum(ref, count):
        total = jnp.sum(ref[...], axis=0)
        h_send[0 : 8 * count, :] = total
        return load_rows(h_send.at[pl.ds(0, 8 * count), :], count)

    lane = iota((D, LANE), 1)

    def back(c, carry):
        slot = c * nd + me
        tile = jnp.sum(h_recv[:, c], axis=0)
        dh = jnp.concatenate([tile[j : j + 1, :] for j in range(D // LANE)], axis=1)
        top = g_top_s[pl.ds(slot, 1), :]
        g_h = top + dh
        r1 = jnp.concatenate([r1_own[c, j : j + 1, :] for j in range(D // LANE)], axis=1)
        gain1 = rv[8 + 5 : 8 + 6, :]
        _, hat1, scale1 = norm_rows(r1, gain1, gain1)
        g_mid = norm_rows_back(g_h, gain1, hat1, scale1)
        row_grad = jnp.where(iota((8, D), 0) == 0, jnp.broadcast_to(g_mid, (8, D)), 0.0)
        kept = (
            hat_s[c], scale_s[c], xl_s[c], xf_s[c], q_s[c], k_s[c], v_s[c], p_s[c], a_s[c]
        )
        g_emb, t, w, da, dq, do, dbv, g_gain, g_shift = unit_back(
            passage, row_grad, 1, w_one, cv, kept
        )
        gtok[c] = g_emb.reshape(nd, cols, LP).astype(BF16)
        tw = jnp.concatenate([t, w, xf_s[c].astype(F32), a_s[c].astype(F32)], axis=0)
        tw = jnp.concatenate([tw, jnp.zeros((LANE - 48, D), F32)], axis=0)
        tw_t = jnp.transpose(tw)
        moved = jnp.where(lane < 48, tw_t, 0.0)
        placed = pltpu.roll(moved, 64 * c, 1)
        fac[...] = (fac[...].astype(F32) + placed.reshape(nd, cols, LANE)).astype(BF16)
        which = iota((16, D), 0)
        new = jnp.zeros((16, D), F32)
        for j, row in enumerate((q_s[c], da, dq, do)):
            new = new + jnp.where(which == 2 * j + c, row.astype(F32)[0:1, :], 0.0)
        line[...] = line[...] + new
        columns = jnp.where(lane == 0, g_gain, jnp.where(lane == 1, g_shift, 0.0))
        flat = jnp.transpose(columns)[0:8, :]
        extra = (
            jnp.where(iota((8, D), 0) == 2, dbv, 0.0)
            + jnp.where(iota((8, D), 0) == 3, g_h * hat1, 0.0)
            + jnp.where(iota((8, D), 0) == 4, g_h, 0.0)
        )
        sums_s[...] = sums_s[...] + flat + extra
        return carry

    lax.fori_loop(0, n_mine, back, 0)
    line_q[0:16, :] = (line[...] + jnp.concatenate([jnp.zeros((8, D), F32), sums_s[...]], axis=0)).astype(BF16)

    @pl.when(me == query_home)
    def _():
        dh = load_rows_sum(h_recvq, nq)
        at, n = part[0]
        g_h = g_top_s[at : at + n, :] + dh
        r1 = load_rows(r1_ownq, nq)
        gain1 = rv[5:6, :]
        _, hat1, scale1 = norm_rows(r1, gain1, gain1)
        g_mid = norm_rows_back(g_h, gain1, hat1, scale1)
        kept = (
            hat_q[...], scale_q[...], xl_q[...], xf_q[...], q_q[...], k_q[...], v_q[...],
            p_q[...], a_q[...],
        )
        g_emb, t, w, da, dq, do, dbv, g_gain, g_shift = unit_back(
            queries, g_mid, 0, w_zero, cv, kept
        )
        gtok_q[...] = g_emb.reshape(nd, cols, nq * LQ).astype(BF16)
        tw = jnp.concatenate([t, w, xf_q[...].astype(F32), a_q[...].astype(F32)], axis=0)
        n_tw = tw.shape[0]
        tw = jnp.concatenate([tw, jnp.zeros((fac_q.shape[2] - n_tw, D), F32)], axis=0)
        fac_q[...] = jnp.transpose(tw).reshape(nd, cols, fac_q.shape[2]).astype(BF16)
        columns = jnp.where(lane == 0, g_gain, jnp.where(lane == 1, g_shift, 0.0))
        flat = jnp.transpose(columns)[0:8, :]
        extra = (
            jnp.where(iota((8, D), 0) == 2, dbv, 0.0)
            + jnp.where(iota((8, D), 0) == 3, jnp.sum(g_h * hat1, axis=0, keepdims=True), 0.0)
            + jnp.where(iota((8, D), 0) == 4, jnp.sum(g_h, axis=0, keepdims=True), 0.0)
        )
        block = jnp.concatenate(
            [q_q[...].astype(F32), da.astype(F32), dq.astype(F32), do.astype(F32), flat + extra,
             jnp.zeros((8, D), F32)],
            axis=0,
        )
        line_q[16:64, :] = block.astype(BF16)

    flows = [
        Flow(
            lambda s, t, c=c: gtok.at[c, t],
            lambda s, t, c=c: o_tok.at[:, pl.ds(pl.multiple_of((c * nd + s) * LP, LANE), LP)],
            lambda n: o_tok.at[:, pl.ds(0, n * LP)],
            span(c), everyone,
        )
        for c in range(cap)
    ] + [
        Flow(
            lambda s, t: gtok_q.at[t],
            lambda s, t: o_tok.at[:, pl.ds(n_valid * LP, nq * LQ)],
            lambda n: o_tok.at[:, pl.ds(0, n * nq * LQ)],
            home, everyone,
        ),
        Flow(
            lambda s, t: fac.at[t],
            lambda s, t: o_fac.at[s],
            lambda n: o_fac.at[pl.ds(0, n)],
            everyone, everyone,
        ),
        Flow(
            lambda s, t: fac_q.at[t],
            lambda s, t: o_facq,
            lambda n: fac_q.at[pl.ds(0, n)],
            home, everyone,
        ),
        Flow(
            lambda s, t: line_q.at[pl.ds(0, 16), :],
            lambda s, t: o_line.at[s],
            lambda n: o_line.at[pl.ds(0, n)],
            everyone, everyone,
        ),
        Flow(
            lambda s, t: line_q.at[pl.ds(16, 48), :],
            lambda s, t: o_lineq,
            lambda n: o_line48(n),
            home, everyone,
        ),
    ]

    def o_line48(n):
        return size48.at[pl.ds(0, n)]

    base = net.start(flows)
    net.finish(flows, base)
    net.finish(du_flows, du_base)


def middle(n_valid, nq, nd, narrow, cols, query_home, token_total, arrays):
    cap = -(-n_valid // nd)
    rows = n_valid + nq
    tq = nq * LQ
    unit, unit_q = Unit(1, LP), Unit(nq, LQ)
    fac_lanes = -(-(2 * unit_q.rows + 2 * unit_q.seqs) // LANE) * LANE
    vmem = pl.BlockSpec(memory_space=pltpu.VMEM)

    def like(*shape, dtype=F32):
        return jax.ShapeDtypeStruct(shape, dtype)

    def kept(lead, u):
        return [
            pltpu.VMEM(lead + (D, u.tokens), F32),
            pltpu.VMEM(lead + (1, u.tokens), F32),
            pltpu.VMEM(lead + (D, u.tokens), BF16),
            pltpu.VMEM(lead + (u.seqs, D), BF16),
            pltpu.VMEM(lead + (u.seqs, D), BF16),
            pltpu.VMEM(lead + (D, u.tokens), BF16),
            pltpu.VMEM(lead + (D, u.tokens), BF16),
            pltpu.VMEM(lead + (u.rows, u.tokens), F32),
            pltpu.VMEM(lead + (u.seqs, D), BF16),
        ]

    flows = 5 * (cap + 1) + 5
    return pl.pallas_call(
        functools.partial(
            middle_body, n_valid, nq, nd, narrow, cols, query_home, token_total
        ),
        out_shape=[
            like(cols, token_total, dtype=BF16),
            like(nd, cols, LANE, dtype=BF16),
            like(cols, fac_lanes, dtype=BF16),
            like(nd, 16, D, dtype=BF16),
            like(48, D, dtype=BF16),
            like(nd, rows, LANE, dtype=BF16),
            like(2, LANE, D),
            like(rows, D),
            like(8, D),
            like(8, LANE),
        ],
        in_specs=[vmem] * len(arrays),
        out_specs=[vmem] * 10,
        scratch_shapes=kept((cap,), unit)
        + kept((), unit_q)
        + [
            pltpu.VMEM((cap, 8, LANE), F32),
            pltpu.VMEM((8 * nq, LANE), F32),
            pltpu.VMEM((8 * rows, LANE), F32),
            pltpu.VMEM((8 * rows, LANE), F32),
            pltpu.VMEM((nd, cap + 1, 8, LANE), F32),
            pltpu.VMEM((cap + 1, 8, LANE), F32),
            pltpu.VMEM((8 * rows, LANE), F32),
            pltpu.VMEM((8 * rows, LANE), F32),
            pltpu.VMEM((nd, cap, 8, LANE), F32),
            pltpu.VMEM((nd, 8 * nq, LANE), F32),
            pltpu.VMEM((rows, LANE), BF16),
            pltpu.VMEM((rows, LANE), F32),
            pltpu.VMEM((cap, nd, cols, LP), BF16),
            pltpu.VMEM((nd, cols, tq), BF16),
            pltpu.VMEM((nd, cols, LANE), BF16),
            pltpu.VMEM((nd, cols, fac_lanes), BF16),
            pltpu.VMEM((16, D), F32),
            pltpu.VMEM((64, D), BF16),
            pltpu.VMEM((rows, LANE), F32),
            pltpu.VMEM((rows, LANE), F32),
            pltpu.VMEM((rows, D), F32),
            pltpu.VMEM((rows, D), F32),
            pltpu.VMEM((8, D), F32),
            pltpu.VMEM((nd, 48, D), BF16),
            pltpu.SemaphoreType.DMA((flows,)),
            pltpu.SemaphoreType.DMA((flows,)),
            pltpu.SemaphoreType.DMA((flows,)),
        ],
        compiler_params=pltpu.CompilerParams(
            collective_id=3, has_side_effects=True, vmem_limit_bytes=62 * 1024 * 1024
        ),
        name="middle",
    )(*arrays)


def stack_table(rows, blocks, table, stacked):
    last = (V - (blocks - 1) * HASH + LANE - 1) // LANE * LANE

    def piece(b):
        if b >= blocks:
            return []
        if b == blocks - 1:
            part = table[:, b * HASH : b * HASH + last].astype(F32)
            return [jnp.concatenate([part, jnp.zeros((rows, HASH - last), F32)], axis=1)]
        return [table[:, b * HASH : (b + 1) * HASH].astype(F32)]

    for b in range(0, blocks, 2):
        both = jnp.concatenate(piece(b) + piece(b + 1), axis=0)
        stacked[b * rows : b * rows + both.shape[0], :] = both.astype(BF16)


def pick_tokens(rows, blocks, stacked, ids):
    low = ids & (HASH - 1)
    high = ids >> (HASH.bit_length() - 1)
    width = ids.shape[1]
    hot = as_bf16(iota((HASH, width), 0) == low)
    picked = jnp.dot(stacked[...], hot, preferred_element_type=F32)
    value = jnp.zeros((rows, width), F32)
    for b in range(blocks):
        value = jnp.where(high == b, picked[b * rows : (b + 1) * rows], value)
    return value.astype(BF16)


def first_body(
    n_valid, nq, nd, narrow, cols, home_at, blocks, forward_from,
    ids_mine, small_mine, table, win, wout, pos_mine, up_mine,
    ids_got, small_got, mine, mine_q, wall, w0, up_got,
    stacked, tokens, tokens_q, p0,
    send_sem, recv_sem, own_sem, wide_send, wide_recv, x_send, x_recv, c_send, c_recv,
):
    cap = -(-n_valid // nd)
    wide = nd // narrow
    tq = nq * LQ
    n_own = ids_mine.shape[0] - 1
    net = Net(nd, narrow, send_sem, recv_sem, own_sem)
    me = net.me
    w_at, n_at = lax.axis_index("wide"), lax.axis_index("narrow")
    x_at, c_at = n_at ^ 2, n_at ^ 1
    everyone = (0, nd)
    home = (home_at, home_at + 1)

    wall[w_at, n_at] = jnp.concatenate([win[1], wout[1], pos_mine[...]], axis=1).astype(BF16)
    p0[...] = jnp.concatenate([win[0], wout[0]], axis=1).astype(BF16)

    net.barrier()
    small = [
        Flow(
            lambda s, t: ids_mine, lambda s, t: ids_got.at[s],
            lambda n: ids_got.at[pl.ds(0, n)], everyone, everyone,
        ),
        Flow(
            lambda s, t: small_mine, lambda s, t: small_got.at[s],
            lambda n: small_got.at[pl.ds(0, n)], everyone, everyone,
        ),
    ]
    small_base = net.start(small)

    def wide_copy(k, carry):
        t = lax.rem(w_at + k, wide)
        pltpu.make_async_remote_copy(
            src_ref=wall.at[w_at, n_at], dst_ref=wall.at[w_at, n_at],
            send_sem=wide_send, recv_sem=wide_recv.at[w_at],
            device_id=(t, n_at), device_id_type=MESH,
        ).start()
        return carry

    lax.fori_loop(1, wide, wide_copy, 0)

    def to_x(row):
        return pltpu.make_async_remote_copy(
            src_ref=wall.at[row, n_at], dst_ref=wall.at[row, n_at],
            send_sem=x_send, recv_sem=x_recv.at[row],
            device_id=(w_at, x_at), device_id_type=MESH,
        )

    def to_core(row, col, which):
        return pltpu.make_async_remote_copy(
            src_ref=wall.at[row, col], dst_ref=wall.at[row, col],
            send_sem=c_send, recv_sem=c_recv.at[which, row],
            device_id=(w_at, c_at), device_id_type=MESH,
        )

    def forward(k):
        row = lax.rem(w_at - k + wide, wide)

        @pl.when(k > 0)
        def _():
            pltpu.make_async_copy(
                wall.at[row, n_at], wall.at[row, n_at], wide_recv.at[row]
            ).wait()

        to_x(row).start()
        to_core(row, n_at, 0).start()

    stack_table(cols, blocks, table, stacked)
    net.finish(small, small_base)

    pairs = n_valid // n_own
    moves = [
        Flow(
            lambda s, t, c=c: tokens.at[(c * nd + t) // n_own, lax.rem(c * nd + t, n_own)],
            lambda s, t, c=c: mine.at[s, :, pl.ds(c * LP, LP)],
            lambda n: mine.at[pl.ds(0, n), :, pl.ds(0, LP)],
            everyone, (0, min(nd, n_valid - c * nd)),
        )
        for c in range(cap)
    ]
    base = net.used
    net.used += cap

    def send_pair(at):
        for j in range(n_own):
            slot = at * n_own + j
            c = slot // nd
            t = lax.rem(slot, nd)
            dst = mine.at[me, :, pl.ds(pl.multiple_of(c * LP, LANE), LP)]

            @pl.when(t != me)
            def _():
                pltpu.make_async_remote_copy(
                    src_ref=tokens.at[at, j], dst_ref=dst,
                    send_sem=send_sem.at[base + c], recv_sem=recv_sem.at[base + c],
                    device_id=net.where(t), device_id_type=MESH,
                ).start()

            @pl.when(t == me)
            def _():
                pltpu.make_async_copy(tokens.at[at, j], dst, own_sem.at[base + c]).start()

    def gather(i, carry):
        at = lax.rem(i + me, pairs)
        ids = jnp.concatenate([ids_got[at, j : j + 1, 0:LP] for j in range(n_own)], axis=1)
        rows = pick_tokens(cols, blocks, stacked, ids)
        for j in range(n_own):
            tokens[at, j] = rows[:, j * LP : (j + 1) * LP]

        @pl.when(i > 0)
        def _():
            send_pair(lax.rem(i - 1 + me, pairs))

        @pl.when(jnp.logical_and(i >= forward_from, i < forward_from + wide))
        def _():
            forward(i - forward_from)

        return carry

    q_ids = jnp.zeros((1, tq), jnp.int32)
    for d in range(0, nd, narrow):
        q_ids = q_ids + ids_got[d, n_own : n_own + 1, 0:tq]
    tokens_q[...] = pick_tokens(cols, blocks, stacked, q_ids)
    q_moves = [
        Flow(
            lambda s, t: tokens_q, lambda s, t: mine_q.at[s],
            lambda n: mine_q.at[pl.ds(0, n)], everyone, home,
        ),
    ]
    home_moves = [
        Flow(
            lambda s, t: p0, lambda s, t: w0.at[s],
            lambda n: w0.at[pl.ds(0, n)], everyone, home,
        ),
    ]
    q_base = net.start(q_moves)
    home_base = net.start(home_moves)
    lax.fori_loop(0, pairs, gather, 0)
    send_pair(lax.rem(pairs - 1 + me, pairs))
    up_moves = [
        Flow(
            lambda s, t: up_mine.at[t], lambda s, t: up_got.at[s],
            lambda n: up_got.at[pl.ds(0, n)], everyone, everyone,
        )
    ]
    up_base = net.start(up_moves)
    for k in range(wide):
        if forward_from + k >= pairs:
            forward(k)

    def second(k, carry):
        row = lax.rem(w_at - k + wide, wide)
        pltpu.make_async_copy(wall.at[row, x_at], wall.at[row, x_at], x_recv.at[row]).wait()
        to_core(row, x_at, 1).start()
        return carry

    lax.fori_loop(0, wide, second, 0)
    net.finish(moves, base)
    net.finish(q_moves, q_base)
    net.finish(up_moves, up_base)
    net.finish(home_moves, home_base)

    def last(row, carry):
        for which, col in ((0, c_at), (1, c_at ^ 2)):
            pltpu.make_async_copy(
                wall.at[row, col], wall.at[row, col], c_recv.at[which, row]
            ).wait()
        return carry

    lax.fori_loop(0, wide, last, 0)
    many = wall.at[pl.ds(0, wide - 1), 0]
    pltpu.make_async_copy(many, many, wide_send).wait()
    many = wall.at[:, 0]
    pltpu.make_async_copy(many, many, x_send).wait()
    many = wall.at[:, pl.ds(0, 2)]
    pltpu.make_async_copy(many, many, c_send).wait()


def first(n_valid, nq, nd, narrow, cols, home_at, arrays, forward_from):
    cap = -(-n_valid // nd)
    wide = nd // narrow
    tq = nq * LQ
    ids_mine, small_mine, up_mine = arrays[0], arrays[1], arrays[6]
    n_own = ids_mine.shape[0] - 1
    blocks = -(-V // HASH)
    vmem = pl.BlockSpec(memory_space=pltpu.VMEM)
    flows = 5 + cap

    def like(*shape, dtype=BF16):
        return jax.ShapeDtypeStruct(shape, dtype)

    dma = pltpu.SemaphoreType.DMA
    return pl.pallas_call(
        functools.partial(
            first_body, n_valid, nq, nd, narrow, cols, home_at, blocks, forward_from
        ),
        out_shape=[
            like(nd, *ids_mine.shape, dtype=jnp.int32),
            like(nd, *small_mine.shape),
            like(nd, cols, cap * LP),
            like(nd, cols, tq),
            like(wide, narrow, cols, 4 * D + LP),
            like(nd, cols, 4 * D),
            like(*up_mine.shape),
        ],
        in_specs=[vmem] * len(arrays),
        out_specs=[vmem] * 7,
        scratch_shapes=[
            pltpu.VMEM((blocks * cols, HASH), BF16),
            pltpu.VMEM((n_valid // n_own, n_own, cols, LP), BF16),
            pltpu.VMEM((cols, tq), BF16),
            pltpu.VMEM((cols, 4 * D), BF16),
            dma((flows,)), dma((flows,)), dma((flows,)),
            dma(()), dma((wide,)), dma(()), dma((wide,)), dma(()), dma((2, wide)),
        ],
        compiler_params=pltpu.CompilerParams(
            collective_id=2, has_side_effects=True, vmem_limit_bytes=62 * 1024 * 1024
        ),
        name="first",
    )(*arrays)


def on_device_rows(
    passage_ids, query_ids, passage_query, kept_mask, neg_count, step_count,
    embed_table, attend_in, attend_out, expand_weight, shrink_weight, norm_gains, bias_terms,
    embed_first, embed_second, attend_in_first, attend_in_second,
    attend_out_first, attend_out_second, expand_first, expand_second,
    shrink_first, shrink_second, gains_first, gains_second, bias_first, bias_second,
):
    narrow = lax.axis_size("narrow")
    nd = lax.axis_size("wide") * narrow
    me = lax.axis_index("wide") * narrow + lax.axis_index("narrow")
    cols = embed_table.shape[1]
    n_slots = passage_query.shape[0]
    nq = query_ids.shape[0] * lax.axis_size("wide")
    n_valid = VALID_PER_QUERY * nq
    cap = -(-n_valid // nd)
    rows_p = cap * nd
    ff_cols = FF // nd

    exch = functools.partial(comm, nd=nd, narrow=narrow)
    rows_c = -(-cols // 8) * 8
    n_ids = passage_ids.shape[0] + query_ids.shape[0]
    small_width = max(cols, bias_terms.shape[1], 1)
    small_width = -(-small_width // LANE) * LANE

    def widen(value, width):
        return jnp.pad(value, ((0, 0), (0, width - value.shape[1])))

    ids_mine = jnp.concatenate([passage_ids, widen(query_ids, LP)])
    small_mine = jnp.concatenate(
        [widen(norm_gains.reshape(6, cols), small_width), widen(bias_terms, small_width)]
    ).astype(BF16)
    ids_got, small_got = exch(
        1,
        [ids_mine, small_mine],
        [((nd, n_ids, LP), jnp.int32), ((nd, 8, small_width), BF16)],
        [send_all(0, 0, nd), send_all(1, 1, nd)],
    )
    n_own = passage_ids.shape[0]
    pid = ids_got[:, :n_own].reshape(n_slots, LP)[:n_valid]
    qid = ids_got.reshape(-1, narrow, n_ids, LP)[:, 0, n_own:, :LANE].reshape(nq, LANE)
    all_ids = jnp.concatenate([pid.reshape(-1), qid.reshape(-1)])
    gains = small_got[:, :6, :cols].transpose(1, 0, 2).reshape(2, 3, D).astype(F32)
    bias = small_got[:, 6:, : bias_terms.shape[1]].transpose(1, 0, 2).reshape(2, -1).astype(F32)

    table_t = embed_table.T
    table_low = table_t.astype(BF16)
    vocab = V + LP
    total = -(-vocab // HASH) * HASH
    table_pad = jnp.pad(table_low, ((0, rows_c - cols), (0, total - vocab)))
    got = table_rows(table_pad, all_ids)
    pos_mine = table_pad[:, V : V + LP]
    up_mine = expand_weight.astype(BF16).reshape(2 * cols, nd, ff_cols).transpose(1, 0, 2)
    q_from = n_valid * LP
    width = cap * LP + LANE

    def passage_move(c, forward):
        span = (0, min(nd, n_valid - c * nd))
        if forward:
            return Send(
                0, 0,
                lambda ref, s, t: ref.at[:, pl.ds(pl.multiple_of((c * nd + t) * LP, LANE), LP)],
                lambda ref, s, t: ref.at[s, :, pl.ds(c * LP, LP)],
                lambda ref, n: ref.at[:, pl.ds(0, n * LP)],
                lambda ref, n: ref.at[pl.ds(0, n), :, pl.ds(0, LP)],
                (0, nd), span,
            )
        return Send(
            0, 0,
            lambda ref, s, t: ref.at[t, :, pl.ds(c * LP, LP)],
            lambda ref, s, t: ref.at[:, pl.ds(pl.multiple_of((c * nd + s) * LP, LANE), LP)],
            lambda ref, n: ref.at[pl.ds(0, n), :, pl.ds(0, LP)],
            lambda ref, n: ref.at[:, pl.ds(0, n * LP)],
            span, (0, nd),
        )

    def query_move(forward):
        span = (nd - nq, nd)
        if forward:
            return Send(
                0, 0,
                lambda ref, s, t: ref.at[
                    :, pl.ds(pl.multiple_of(q_from + (t - (nd - nq)) * LANE, LANE), LANE)
                ],
                lambda ref, s, t: ref.at[s, :, pl.ds(cap * LP, LANE)],
                lambda ref, n: ref.at[:, pl.ds(0, n * LANE)],
                lambda ref, n: ref.at[pl.ds(0, n), :, pl.ds(0, LANE)],
                (0, nd), span,
            )
        return Send(
            0, 0,
            lambda ref, s, t: ref.at[t, :, pl.ds(cap * LP, LANE)],
            lambda ref, s, t: ref.at[
                :, pl.ds(pl.multiple_of(q_from + (s - (nd - nq)) * LANE, LANE), LANE)
            ],
            lambda ref, n: ref.at[pl.ds(0, n), :, pl.ds(0, LANE)],
            lambda ref, n: ref.at[:, pl.ds(0, n * LANE)],
            span, (0, nd),
        )

    mine, pos, w_up = exch(
        2,
        [got, pos_mine, up_mine],
        [((nd, rows_c, width), BF16), ((nd, rows_c, LP), BF16), ((nd, 2 * cols, ff_cols), BF16)],
        [passage_move(c, True) for c in range(cap)]
        + [query_move(True), send_all(1, 1, nd), send_blocks(2, 2, nd)],
    )
    live = jnp.concatenate(
        [jnp.broadcast_to(c * nd + me < n_valid, (LP,)) for c in range(cap)]
        + [jnp.broadcast_to(me >= nd - nq, (LANE,))]
    )
    mine = jnp.where(live, mine[:, :cols].reshape(D, width), 0)
    pos = pos[:, :cols].reshape(D, LP).astype(F32)
    w_up = w_up.reshape(nd, 2, cols, ff_cols).transpose(1, 0, 2, 3).reshape(2, D, ff_cols)
    w_down = shrink_weight.astype(BF16)
    w_in = lax.all_gather(attend_in.astype(BF16), AXES, axis=1, tiled=True)
    w_out = lax.all_gather(attend_out.astype(BF16), AXES, axis=1, tiled=True)

    fronts = []
    for c in range(cap):
        emb = mine[:, c * LP : (c + 1) * LP].astype(F32) + pos
        fronts.append(encode_front(emb, w_in[1], w_out[1], gains[1], bias[1], LP))
    emb = mine[:, cap * LP :].astype(F32) + pos[:, :LANE]
    fronts.append(encode_front(emb, w_in[0], w_out[0], gains[0], bias[0], LQ))
    (rows,) = exch(
        3, [jnp.stack([f[0] for f in fronts])], [((nd, cap + 1, D), F32)], [send_all(0, 0, nd)]
    )
    row_in = (rows[nd - nq :, cap], rows[:, :cap].transpose(1, 0, 2).reshape(rows_p, D))

    def by_owner(queries, passages):
        q_part = jnp.pad(queries, ((nd - nq, 0), (0, 0)))[:, None]
        return jnp.concatenate([passages.reshape(cap, nd, D).transpose(1, 0, 2), q_part], axis=1)

    def to_rows(blocks):
        return (
            blocks[nd - nq :, cap],
            blocks[:, :cap].transpose(1, 0, 2).reshape(rows_p, D),
        )


    mids, ups = [], []
    partial_y = []
    b_in_all = bias[:, O_IN : O_IN + FF].reshape(2, nd, ff_cols)
    b_in = lax.dynamic_index_in_dim(b_in_all, me, 1, False)
    for e in range(2):
        h, hat1, scale1 = norm_rows(row_in[e], gains[e, 1], bias[e, O_1 : O_1 + D])
        h_low = h.astype(BF16)
        upper = dot(h_low, w_up[e], ((1,), (0,))) + b_in[e]
        active, slope = gelu_both(upper)
        f_low = active.astype(BF16)
        partial_y.append(dot(f_low, w_down[e], ((1,), (0,))))
        mids.append((h, hat1, scale1, h_low))
        ups.append((f_low, slope))
    (y_parts,) = exch(
        4, [by_owner(*partial_y)], [((nd, cap + 1, D), F32)], [send_blocks(0, 0, nd)]
    )
    (y_all,) = exch(
        5, [jnp.sum(y_parts, axis=0)], [((nd, cap + 1, D), F32)], [send_all(0, 0, nd)]
    )
    y = to_rows(y_all)
    tops = []
    vecs = []
    for e in range(2):
        z, hat2, scale2 = norm_rows(
            mids[e][0] + y[e] + bias[e, O_OUT : O_OUT + D], gains[e, 2], bias[e, O_2 : O_2 + D]
        )
        tops.append((hat2, scale2))
        vecs.append(z.astype(BF16))
    qvec, pvec = vecs

    owner = passage_query[:rows_p]
    kept = kept_mask[:rows_p] == 1
    earlier = jnp.concatenate([jnp.full((1,), -1, jnp.int32), owner[:-1]])
    valid = owner >= 0
    first = valid & (owner != earlier)
    member = owner[None, :] == jnp.arange(nq, dtype=jnp.int32)[:, None]
    positive = member & first[None, :]
    negative = member & jnp.logical_not(first)[None, :] & kept[None, :]
    counts = jnp.sum(member.astype(F32), axis=1) - 1.0
    score_scale = 2.0 * D ** (-0.5)
    scores = dot(qvec, pvec, ((1,), (1,))) * score_scale
    masked = jnp.where(valid[None, :], scores, -1e30)
    peak = jnp.max(masked, axis=1)
    summed = jnp.sum(jnp.where(valid[None, :], jnp.exp(masked - peak[:, None]), 0.0), axis=1)
    logsum = peak + jnp.log(summed)
    pos_score = jnp.sum(jnp.where(positive, scores, 0.0), axis=1)
    margins = MARGIN - pos_score[:, None] + scores
    active_neg = negative & (margins > 0)
    hinge = jnp.sum(jnp.where(active_neg, margins, 0.0), axis=1) / counts
    active_total = jnp.sum(active_neg.astype(F32), axis=1)
    loss = jnp.sum(logsum - pos_score + hinge)
    score_grad = (
        jnp.where(valid[None, :], jnp.exp(scores - logsum[:, None]), 0.0)
        - positive.astype(F32) * (1.0 + active_total / counts)[:, None]
        + active_neg.astype(F32) / counts[:, None]
    )
    score_low = score_grad.astype(BF16)
    vec_grads = (
        (dot(score_low, pvec, ((1,), (0,))) * score_scale).astype(BF16).astype(F32),
        (dot(score_low, qvec, ((0,), (0,))) * score_scale).astype(BF16).astype(F32),
    )

    partial_h = []
    gain_grads = [[None] * 3 for _ in range(2)]
    shifts = [dict() for _ in range(2)]
    top_grads, shrink_grads, du_parts = [], [], []
    for e in range(2):
        hat2, scale2 = tops[e]
        gain_grads[e][2] = jnp.sum(vec_grads[e] * hat2, axis=0)
        shifts[e]["2"] = jnp.sum(vec_grads[e], axis=0)
        g_top = norm_rows_back(vec_grads[e], gains[e, 2], hat2, scale2)
        dy = g_top.astype(BF16)
        shifts[e]["out"] = jnp.sum(dy.astype(F32), axis=0)
        f_low, slope = ups[e]
        shrink_grads.append(dot(f_low, dy, ((0,), (0,))))
        df = dot(dy, w_down[e], ((1,), (1,)))
        du = (slope * df).astype(BF16)
        du_parts.append(du)
        partial_h.append(dot(du, w_up[e], ((1,), (1,))))
        top_grads.append(g_top)
    du_mine = jnp.concatenate(du_parts)
    h_parts, du_all = exch(
        6,
        [by_owner(*partial_h), du_mine],
        [((nd, cap + 1, D), F32), ((nd, nq + rows_p, ff_cols), BF16)],
        [send_blocks(0, 0, nd), send_all(1, 1, nd)],
    )
    h_mine = jnp.sum(h_parts, axis=0)
    top_mine = lax.dynamic_index_in_dim(by_owner(*top_grads), me, 0, False)
    rows_mine = lax.dynamic_index_in_dim(rows, me, 0, False)
    is_q = (me >= nd - nq).astype(F32)
    has = jnp.stack([(c * nd + me < n_valid).astype(F32) for c in range(cap)] + [is_q])
    g_h = (top_mine + h_mine) * has[:, None]
    gain_one = jnp.stack([gains[1, 1]] * cap + [gains[0, 1]])
    shift_one = jnp.stack([bias[1, O_1 : O_1 + D]] * cap + [bias[0, O_1 : O_1 + D]])
    _, hat_mine, scale_mine = norm_rows(rows_mine, gain_one, shift_one)
    g_mid = norm_rows_back(g_h, gain_one, hat_mine, scale_mine)
    gain_mid = g_h * hat_mine
    do_mine = g_mid.astype(BF16)
    backs = [
        encode_back(
            fronts[c][1], g_mid[c], w_in[1 if c < cap else 0], w_out[1 if c < cap else 0],
            gains[1 if c < cap else 0],
        )
        for c in range(cap + 1)
    ]

    def both_encoders(pick):
        return jnp.stack([pick(cap), sum(pick(c) for c in range(cap))])

    sums = jnp.concatenate(
        [both_encoders(lambda i, j=j: backs[i][1][j]) for j in (5, 6, 7)]
        + [both_encoders(lambda i: gain_mid[i]), both_encoders(lambda i: g_h[i])]
    )
    line = jnp.concatenate(
        [jnp.stack([b[1][j] for b in backs]) for j in (2, 3, 4)] + [do_mine, sums.astype(BF16)]
    )
    n_line = 4 * (cap + 1) + 10
    factor_t = jnp.concatenate(
        [b[1][0] for b in backs] + [b[1][1] for b in backs]
        + [f[1][2][:, 0][None] for f in fronts] + [f[1][8][None] for f in fronts]
    )
    n_factor = factor_t.shape[0]
    f_pad = -(-n_factor // LANE) * LANE
    factor_cols = jnp.pad(factor_t, ((0, f_pad - n_factor), (0, 0))).T

    def pad_rows(value):
        value = value.reshape(nd, cols, value.shape[1])
        return jnp.pad(value, ((0, 0), (0, rows_c - cols), (0, 0)))

    send = pad_rows(jnp.concatenate([b[0] for b in backs], axis=1).astype(BF16))
    token_grads, factors, lines = exch(
        7,
        [send, pad_rows(factor_cols), line],
        [
            ((rows_c, n_valid * LP + nq * LANE), BF16),
            ((nd, rows_c, f_pad), BF16),
            ((nd, n_line, D), BF16),
        ],
        [passage_move(c, False) for c in range(cap)]
        + [query_move(False), send_blocks(1, 1, nd), send_all(2, 2, nd)],
    )
    table_grad = table_sums(token_grads, all_ids, total)[:cols, :vocab]
    token_grads = token_grads[:cols].astype(F32)
    pos_grad = jnp.sum(token_grads[:, :q_from].reshape(cols, n_valid, LP), axis=1)
    pos_grad = pos_grad.at[:, :LANE].add(
        jnp.sum(token_grads[:, q_from:].reshape(cols, nq, LANE), axis=1)
    )
    table_grad = table_grad.at[:, V:].add(pos_grad)

    step_h = (cap + 1) * H
    factors = factors[:, :cols].transpose(0, 2, 1)
    t_all = factors[:, :step_h].reshape(nd, cap + 1, H, cols)
    w_all = factors[:, step_h : 2 * step_h].reshape(nd, cap + 1, H, cols)
    x_all = factors[:, 2 * step_h : 2 * step_h + cap + 1]
    a_all = factors[:, 2 * step_h + cap + 1 : 2 * step_h + 2 * (cap + 1)]
    q_all, da_all, dq_all, do_all = (
        lines[:, j * (cap + 1) : (j + 1) * (cap + 1)] for j in range(4)
    )
    sums = jnp.sum(lines[:, 4 * (cap + 1) :].astype(F32), axis=0).reshape(5, 2, D)

    def of_encoder(value, e):
        if e == 0:
            return value[nd - nq :, cap]
        return value[:, :cap].reshape((nd * cap,) + value.shape[2:])

    du_all = du_all.transpose(1, 0, 2).reshape(nq + rows_p, FF)
    in_grads, out_grads, expand_grads = [], [], []
    for e in range(2):
        du_full = du_all[:nq] if e == 0 else du_all[nq:]
        shifts[e]["in"] = jnp.sum(du_full.astype(F32), axis=0)
        h_cols = lax.dynamic_slice_in_dim(mids[e][3], me * cols, cols, 1)
        expand_grads.append(dot(h_cols, du_full, ((0,), (0,))))
        t, w, x, a = (of_encoder(u, e) for u in (t_all, w_all, x_all, a_all))
        q, da, dq, do = (of_encoder(u, e) for u in (q_all, da_all, dq_all, do_all))
        rows_e = q.shape[0]
        qh = q.reshape(rows_e, H, HD)
        dah = da.reshape(rows_e, H, HD)
        g_q = dot(x, dq, ((0,), (0,)))
        g_k = jnp.einsum("phi,phd->ihd", t, qh, preferred_element_type=F32).reshape(cols, D)
        g_v = jnp.einsum("phi,phd->ihd", w, dah, preferred_element_type=F32).reshape(cols, D)
        in_grads.append(jnp.concatenate([g_q, g_k, g_v], axis=1))
        out_grads.append(dot(a, do, ((0,), (0,))))
        shifts[e]["q"] = jnp.sum(dq.astype(F32), axis=0)
        shifts[e]["o"] = jnp.sum(do.astype(F32), axis=0)
    gain_grad = jnp.stack(
        [jnp.stack([sums[1, e], sums[3, e], gain_grads[e][2]]) for e in range(2)]
    )
    bias_grad = jnp.stack(
        [
            jnp.concatenate(
                [shifts[e]["q"], sums[0, e], shifts[e]["o"], sums[4, e], shifts[e]["in"],
                 shifts[e]["out"], shifts[e]["2"], sums[2, e]]
            )
            for e in range(2)
        ]
    )
    grads = (
        table_grad.T,
        jnp.stack(in_grads),
        jnp.stack(out_grads),
        jnp.stack(expand_grads),
        jnp.stack(shrink_grads),
        lax.dynamic_slice_in_dim(gain_grad, me * cols, cols, 2),
        lax.dynamic_slice_in_dim(bias_grad, me * bias_terms.shape[1], bias_terms.shape[1], 1),
    )
    local_squares = sum(jnp.sum(g * g) for g in grads)
    (squares,) = exch(
        8, [jnp.broadcast_to(local_squares, (8, LANE))], [((nd, 8, LANE), F32)],
        [send_all(0, 0, nd)],
    )
    grad_norm = jnp.sqrt(jnp.sum(squares[:, 0, 0]))
    factor = CLIP / jnp.maximum(grad_norm, CLIP)
    step = step_count[0].astype(F32)
    masters = (embed_table, attend_in, attend_out, expand_weight, shrink_weight, norm_gains, bias_terms)
    firsts = (embed_first, attend_in_first, attend_out_first, expand_first, shrink_first, gains_first, bias_first)
    seconds = (embed_second, attend_in_second, attend_out_second, expand_second, shrink_second, gains_second, bias_second)
    results = [loss, grad_norm]
    for index in range(7):
        results.extend(
            adam_update(masters[index], grads[index] * factor, firsts[index], seconds[index], step, LEARN_RATES[index])
        )
    return tuple(results)


def on_device(
    passage_ids, query_ids, passage_query, kept_mask, neg_count, step_count,
    embed_table, attend_in, attend_out, expand_weight, shrink_weight, norm_gains, bias_terms,
    embed_first, embed_second, attend_in_first, attend_in_second,
    attend_out_first, attend_out_second, expand_first, expand_second,
    shrink_first, shrink_second, gains_first, gains_second, bias_first, bias_second,
):
    if embed_table.shape[1] % 8 != 0 or lax.axis_size("narrow") != 4 or passage_ids.shape[0] != 2:
        return on_device_rows(
            passage_ids, query_ids, passage_query, kept_mask, neg_count, step_count,
            embed_table, attend_in, attend_out, expand_weight, shrink_weight, norm_gains,
            bias_terms, embed_first, embed_second, attend_in_first, attend_in_second,
            attend_out_first, attend_out_second, expand_first, expand_second,
            shrink_first, shrink_second, gains_first, gains_second, bias_first, bias_second,
        )
    narrow = lax.axis_size("narrow")
    nd = lax.axis_size("wide") * narrow
    me = lax.axis_index("wide") * narrow + lax.axis_index("narrow")
    cols = embed_table.shape[1]
    n_slots = passage_query.shape[0]
    per_wide = query_ids.shape[0]
    nq = per_wide * lax.axis_size("wide")
    n_valid = VALID_PER_QUERY * nq
    cap = -(-n_valid // nd)
    ff_cols = FF // nd
    rows = n_valid + nq
    tq = nq * LQ
    query_home = nd * 5 // 8 - 1
    exch = functools.partial(comm, nd=nd, narrow=narrow)
    small_width = -(-max(cols, bias_terms.shape[1]) // LANE) * LANE
    ids_width = max(LP, -(-tq // LANE) * LANE)

    def widen(value, width):
        return jnp.pad(value, ((0, 0), (0, width - value.shape[1])))

    spot = jnp.arange(tq) // (LQ * per_wide) == lax.axis_index("wide")
    spot = spot & (lax.axis_index("narrow") == 0)
    q_line = jnp.where(spot, jnp.tile(query_ids.reshape(-1), tq // (LQ * per_wide)), 0)
    ids_mine = jnp.concatenate([widen(passage_ids, ids_width), widen(q_line[None], ids_width)])
    small_mine = jnp.concatenate(
        [widen(norm_gains.reshape(6, cols), small_width), widen(bias_terms, small_width)]
    ).astype(BF16)
    n_own = passage_ids.shape[0]
    table_t = embed_table.T
    up_mine = expand_weight.astype(BF16).reshape(2 * cols, nd, ff_cols).transpose(1, 0, 2)
    ids_got, small_got, mine, mine_q, w_one, w_zero, w_up = first(
        n_valid, nq, nd, narrow, cols, query_home,
        [ids_mine, small_mine, table_t, attend_in, attend_out, table_t[:, V : V + LP], up_mine],
        12,
    )
    w_one = w_one.reshape(D, 4 * D + LP)
    w_zero = w_zero.reshape(D, 4 * D)
    pid = ids_got[:, :n_own, :LP].reshape(n_slots, LP)[:n_valid]
    qid = jnp.sum(ids_got[:, n_own, :tq], axis=0)
    q_from = n_valid * LP
    token_total = -(-(q_from + tq) // 1024) * 1024
    all_ids = jnp.pad(jnp.concatenate([pid.reshape(-1), qid]), (0, token_total - q_from - tq))
    gains = small_got[:, :6, :cols].transpose(1, 0, 2).reshape(2, 3, D).astype(F32)
    bias = small_got[:, 6:, : bias_terms.shape[1]].transpose(1, 0, 2).reshape(2, -1).astype(F32)

    vocab = V + LP
    total = -(-vocab // HASH) * HASH
    w_up = w_up.reshape(nd, 2, cols, ff_cols).transpose(1, 0, 2, 3).reshape(2, D, ff_cols)
    w_up = jnp.pad(w_up, ((0, 0), (0, 0), (0, LANE - ff_cols)))
    w_down = jnp.pad(shrink_weight.astype(BF16), ((0, 0), (0, LANE - ff_cols), (0, 0)))
    cv = jnp.stack(
        [v for e in range(2) for v in (
            gains[e, 0], bias[e, O_EMB : O_EMB + D], bias[e, O_V : O_V + D])]
        + [jnp.zeros((D,), F32)] * 2,
        axis=1,
    )
    rv = jnp.stack(
        [v for e in range(2) for v in (
            bias[e, O_Q : O_Q + D], bias[e, O_O : O_O + D], bias[e, O_1 : O_1 + D],
            bias[e, O_OUT : O_OUT + D], bias[e, O_2 : O_2 + D], gains[e, 1], gains[e, 2],
            jnp.zeros((D,), F32))]
    )
    b_in = lax.dynamic_index_in_dim(
        bias[:, O_IN : O_IN + FF].reshape(2, nd, ff_cols), me, 1, False
    )
    b_in = jnp.pad(b_in, ((0, 6), (0, LANE - ff_cols)))
    earlier = jnp.concatenate([jnp.full((1,), -1, jnp.int32), passage_query[:-1]])
    first_slot = ((passage_query >= 0) & (passage_query != earlier)).astype(jnp.int32)
    slots = jnp.pad(
        jnp.stack([passage_query, first_slot, kept_mask])[:, :n_valid],
        ((0, 5), (0, -(-n_valid // LANE) * LANE - n_valid)),
    )
    tok, fac, fac_q, line, line_q, du_all, shrink_g, h_low, out_rows, loss = middle(
        n_valid, nq, nd, narrow, cols, query_home, token_total,
        [mine, mine_q, w_one, w_zero, w_up, w_down, cv, rv, b_in, slots],
    )
    loss = loss[0, 0]

    table_grad = table_sums(tok, all_ids, total)[:, :vocab]
    tok = tok.astype(F32)
    pos_grad = jnp.sum(tok[:, :q_from].reshape(cols, n_valid, LP), axis=1)
    q_pos = jnp.sum(tok[:, q_from : q_from + tq].reshape(cols, nq, LQ), axis=1)
    pos_grad = pos_grad.at[:, :LQ].add(q_pos)
    table_grad = table_grad.at[:, V:].add(pos_grad)

    by_lane = fac.transpose(0, 2, 1).reshape(nd, 2, 64, cols)[:, :cap]
    q_rows = H * nq
    q_lane = fac_q.T
    heads_q = lambda v: v.reshape(H, nq, cols).transpose(1, 0, 2)
    factors = {
        1: tuple(
            v.reshape((nd * cap,) + v.shape[2:])
            for v in (by_lane[:, :, 0:H], by_lane[:, :, 16 : 16 + H], by_lane[:, :, 32],
                      by_lane[:, :, 40])
        ),
        0: (
            heads_q(q_lane[:q_rows]), heads_q(q_lane[q_rows : 2 * q_rows]),
            q_lane[2 * q_rows : 2 * q_rows + nq], q_lane[2 * q_rows + nq : 2 * q_rows + 2 * nq],
        ),
    }
    lines = {
        1: tuple(line[:, 2 * j : 2 * j + cap].reshape(nd * cap, D) for j in range(4)),
        0: tuple(line_q[nq * j : nq * (j + 1)] for j in range(4)),
    }
    sums = {1: jnp.sum(line[:, 8:13].astype(F32), axis=0), 0: line_q[32:37].astype(F32)}
    du_rows = du_all[:, :, :ff_cols].transpose(1, 0, 2).reshape(rows, FF)
    h_cols = lax.dynamic_slice_in_dim(h_low, me * cols, cols, 1).astype(BF16)
    in_grads, out_grads, expand_grads, bias_parts, gain_parts = [], [], [], [], []
    for e in range(2):
        at, n = (n_valid, nq) if e == 0 else (0, n_valid)
        du_e = du_rows[at : at + n]
        expand_grads.append(dot(h_cols[at : at + n], du_e, ((0,), (0,))))
        t, w, x, a = factors[e]
        q, da, dq, do = lines[e]
        n_e = q.shape[0]
        g_q = dot(x, dq, ((0,), (0,)))
        g_k = jnp.einsum(
            "phi,phd->ihd", t, q.reshape(n_e, H, HD), preferred_element_type=F32
        ).reshape(cols, D)
        g_v = jnp.einsum(
            "phi,phd->ihd", w, da.reshape(n_e, H, HD), preferred_element_type=F32
        ).reshape(cols, D)
        in_grads.append(jnp.concatenate([g_q, g_k, g_v], axis=1))
        out_grads.append(dot(a, do, ((0,), (0,))))
        s = sums[e]
        gain_parts.append(jnp.stack([s[0], s[3], out_rows[3 * e]]))
        bias_parts.append(
            jnp.concatenate(
                [jnp.sum(dq.astype(F32), axis=0), s[2], jnp.sum(do.astype(F32), axis=0), s[4],
                 jnp.sum(du_e.astype(F32), axis=0), out_rows[3 * e + 2], out_rows[3 * e + 1], s[1]]
            )
        )
    grads = (
        table_grad.T,
        jnp.stack(in_grads),
        jnp.stack(out_grads),
        jnp.stack(expand_grads),
        shrink_g[:, :ff_cols],
        lax.dynamic_slice_in_dim(jnp.stack(gain_parts), me * cols, cols, 2),
        lax.dynamic_slice_in_dim(
            jnp.stack(bias_parts), me * bias_terms.shape[1], bias_terms.shape[1], 1
        ),
    )
    local_squares = sum(jnp.sum(g * g) for g in grads)
    (squares,) = exch(
        8, [jnp.broadcast_to(local_squares, (8, LANE))], [((nd, 8, LANE), F32)],
        [send_all(0, 0, nd)],
    )
    grad_norm = jnp.sqrt(jnp.sum(squares[:, 0, 0]))
    factor = CLIP / jnp.maximum(grad_norm, CLIP)
    step = step_count[0].astype(F32)
    masters = (embed_table, attend_in, attend_out, expand_weight, shrink_weight, norm_gains, bias_terms)
    firsts = (embed_first, attend_in_first, attend_out_first, expand_first, shrink_first, gains_first, bias_first)
    seconds = (embed_second, attend_in_second, attend_out_second, expand_second, shrink_second, gains_second, bias_second)
    results = [loss, grad_norm]
    for index in range(7):
        results.extend(
            adam_update(masters[index], grads[index] * factor, firsts[index], seconds[index], step, LEARN_RATES[index])
        )
    return tuple(results)


def solution(mesh):
    both = ("wide", "narrow")
    weight_specs = (P(None, both),) + (P(None, both, None),) * 4 + (P(None, None, both), P(None, both))
    pairs = tuple(s for spec in weight_specs for s in (spec, spec))
    in_specs = (P(both, None), P("wide", None), P(), P(), P("wide"), P()) + weight_specs + pairs
    out_specs = (P(), P()) + tuple(s for spec in weight_specs for s in (spec, spec, spec))
    return jax.shard_map(on_device, mesh=mesh, in_specs=in_specs, out_specs=out_specs, check_vma=False)
```

```python
import functools

import jax
import jax.numpy as jnp
from jax import lax
from jax.experimental import pallas as pl
from jax.experimental.pallas import tpu as pltpu
from jax.sharding import PartitionSpec as P

D = 768
H = 12
HD = 64
FF = 3072
V = 18000
LP = 384
LQ = 32
LANE = 128
VALID_PER_QUERY = 5

MARGIN = 1.0
CLIP = 1.0
BETA_ONE = 0.9
BETA_TWO = 0.999
LEARN_RATES = (1.0, 0.02, 0.08, 0.02, 0.02, 1.0, 0.1)
WEIGHT_DECAY = 0.01
ADAM_EPS = 1e-08
NORM_EPS = 1e-05
AXES = ("wide", "narrow")
F32 = jnp.float32
BF16 = jnp.bfloat16
O_Q, O_V, O_O, O_1, O_IN, O_OUT, O_2, O_EMB = (
    0, D, 2 * D, 3 * D, 4 * D, 4 * D + FF, 5 * D + FF, 6 * D + FF
)


def dot(left, right, dims):
    return lax.dot_general(left, right, (dims, ((), ())), preferred_element_type=F32)


def norm_rows(values, gain, shift):
    center = values - jnp.mean(values, axis=-1, keepdims=True)
    spread = jnp.mean(center * center, axis=-1, keepdims=True)
    scale = lax.rsqrt(spread + NORM_EPS)
    hat = center * scale
    return hat * gain + shift, hat, scale


def norm_rows_back(grad, gain, hat, scale):
    scaled = grad * gain
    mean_one = jnp.mean(scaled, axis=-1, keepdims=True)
    mean_two = jnp.mean(scaled * hat, axis=-1, keepdims=True)
    return scale * (scaled - mean_one - hat * mean_two)


def gelu_both(upper):
    cdf = 0.5 * (1.0 + lax.erf(upper * 0.7071067811865476))
    pdf = jnp.exp(-0.5 * upper * upper) * 0.3989422804014327
    return upper * cdf, cdf + upper * pdf


def adam_update(weight, grad, first, second, step, rate):
    first_new = BETA_ONE * first + (1.0 - BETA_ONE) * grad
    second_new = BETA_TWO * second + (1.0 - BETA_TWO) * grad * grad
    first_hat = first_new / (1.0 - BETA_ONE**step)
    second_hat = second_new / (1.0 - BETA_TWO**step)
    weight_new = weight - rate * (
        first_hat / (jnp.sqrt(second_hat) + ADAM_EPS) + WEIGHT_DECAY * weight
    )
    return (weight_new, first_new, second_new)


MESH = pl.DeviceIdType.MESH
HASH = 512


class Send:
    def __init__(self, src, dst, take, put, many_src, many_dst, sources, targets):
        self.src, self.dst, self.take, self.put = src, dst, take, put
        self.many_src, self.many_dst = many_src, many_dst
        self.sources, self.targets = sources, targets


def inside(index, span):
    return jnp.logical_and(index >= span[0], index < span[1])


def comm_body(sends, n_in, n_out, nd, narrow, *refs):
    ins, outs = refs[:n_in], refs[n_in : n_in + n_out]
    send_sem, recv_sem, own_sem = refs[n_in + n_out :]
    me = lax.axis_index("wide") * narrow + lax.axis_index("narrow")
    barrier = pltpu.get_barrier_semaphore()

    def greet(k, carry):
        t = lax.rem(me + k, nd)
        pl.semaphore_signal(
            barrier, inc=1, device_id=(t // narrow, lax.rem(t, narrow)), device_id_type=MESH
        )
        return carry

    lax.fori_loop(1, nd, greet, 0)
    pl.semaphore_wait(barrier, nd - 1)

    def push(k, carry):
        t = lax.rem(me + k, nd)
        for i, s in enumerate(sends):

            @pl.when(jnp.logical_and(inside(me, s.sources), inside(t, s.targets)))
            def _():
                pltpu.make_async_remote_copy(
                    src_ref=s.take(ins[s.src], me, t),
                    dst_ref=s.put(outs[s.dst], me, t),
                    send_sem=send_sem.at[i],
                    recv_sem=recv_sem.at[i],
                    device_id=(t // narrow, lax.rem(t, narrow)),
                    device_id_type=MESH,
                ).start()

        return carry

    lax.fori_loop(1, nd, push, 0)
    for i, s in enumerate(sends):
        both = jnp.logical_and(inside(me, s.sources), inside(me, s.targets))

        @pl.when(both)
        def _():
            own = pltpu.make_async_copy(
                s.take(ins[s.src], me, me), s.put(outs[s.dst], me, me), own_sem.at[i]
            )
            own.start()
            own.wait()

    for i, s in enumerate(sends):
        n_t = s.targets[1] - s.targets[0]
        n_s = s.sources[1] - s.sources[0]
        is_s, is_t = inside(me, s.sources), inside(me, s.targets)
        for own in (0, 1):
            mine = is_t if own else jnp.logical_not(is_t)
            if n_t - own > 0:

                @pl.when(jnp.logical_and(is_s, mine))
                def _():
                    view = s.many_src(ins[s.src], n_t - own) if s.many_src(ins[s.src], 1) is not None else outs[s.dst].at[pl.ds(0, n_t - own)]
                    pltpu.make_async_copy(view, view, send_sem.at[i]).wait()

            mine = is_s if own else jnp.logical_not(is_s)
            if n_s - own > 0:

                @pl.when(jnp.logical_and(is_t, mine))
                def _():
                    view = s.many_dst(outs[s.dst], n_s - own)
                    pltpu.make_async_copy(view, view, recv_sem.at[i]).wait()


def comm(collective, arrays, out_shapes, sends, nd, narrow):
    vmem = pl.BlockSpec(memory_space=pltpu.VMEM)
    n = len(sends)
    return pl.pallas_call(
        functools.partial(comm_body, sends, len(arrays), len(out_shapes), nd, narrow),
        out_shape=[jax.ShapeDtypeStruct(s, d) for s, d in out_shapes],
        in_specs=[vmem] * len(arrays),
        out_specs=[vmem] * len(out_shapes),
        scratch_shapes=[
            pltpu.SemaphoreType.DMA((n,)),
            pltpu.SemaphoreType.DMA((n,)),
            pltpu.SemaphoreType.DMA((n,)),
        ],
        compiler_params=pltpu.CompilerParams(collective_id=collective, has_side_effects=True),
    )(*arrays)


def send_all(src, dst, nd):
    return Send(
        src, dst,
        lambda ref, s, t: ref,
        lambda ref, s, t: ref.at[s],
        lambda ref, n: None, lambda ref, n: ref.at[pl.ds(0, n)],
        (0, nd), (0, nd),
    )


def send_blocks(src, dst, nd):
    return Send(
        src, dst,
        lambda ref, s, t: ref.at[t],
        lambda ref, s, t: ref.at[s],
        lambda ref, n: ref.at[pl.ds(0, n)], lambda ref, n: ref.at[pl.ds(0, n)],
        (0, nd), (0, nd),
    )


def stack_pairs(pieces, store):
    rows = pieces[0].shape[0]
    for i in range(0, len(pieces), 2):
        store(i * rows, jnp.concatenate(pieces[i : i + 2], axis=0))


def gather_body(rows, blocks, table_ref, ids_ref, out_ref, stacked):
    @pl.when(pl.program_id(0) == 0)
    def _():
        pieces = [
            table_ref[:, b * HASH : (b + 1) * HASH].astype(F32) for b in range(blocks)
        ]

        def store(row, value):
            stacked[row : row + value.shape[0], :] = value.astype(BF16)

        stack_pairs(pieces, store)

    ids = ids_ref[0]
    low = ids & (HASH - 1)
    high = ids >> (HASH.bit_length() - 1)
    width = ids.shape[1]
    hot = (lax.broadcasted_iota(jnp.int32, (HASH, width), 0) == low).astype(F32).astype(BF16)
    picked = jnp.dot(stacked[...], hot, preferred_element_type=F32)
    value = jnp.zeros((rows, width), F32)
    for b in range(blocks):
        value = jnp.where(high == b, picked[b * rows : (b + 1) * rows], value)
    out_ref[...] = value.astype(BF16)


def table_rows(table, ids):
    rows, total = table.shape
    tokens = ids.shape[0]
    tile = 512
    blocks = total // HASH
    return pl.pallas_call(
        functools.partial(gather_body, rows, blocks),
        grid=(tokens // tile,),
        out_shape=jax.ShapeDtypeStruct((rows, tokens), BF16),
        in_specs=[
            pl.BlockSpec((rows, total), lambda i: (0, 0)),
            pl.BlockSpec((1, 1, tile), lambda i: (i, 0, 0)),
        ],
        out_specs=pl.BlockSpec((rows, tile), lambda i: (0, i)),
        scratch_shapes=[pltpu.VMEM((blocks * rows, HASH), BF16)],
        name="table_rows",
    )(table, ids.reshape(tokens // tile, 1, tile))


def scatter_body(rows, blocks, values_ref, ids_ref, out_ref, spread, acc):
    step = pl.program_id(0)
    ids = ids_ref[0]
    low = ids & (HASH - 1)
    high = ids >> (HASH.bit_length() - 1)
    width = ids.shape[1]
    values = values_ref[...].astype(F32)
    pieces = [jnp.where(high == b, values, 0.0) for b in range(blocks)]

    def store(row, value):
        spread[row : row + value.shape[0], :] = value.astype(BF16)

    stack_pairs(pieces, store)
    hot = (lax.broadcasted_iota(jnp.int32, (HASH, width), 0) == low).astype(F32).astype(BF16)
    part = lax.dot_general(
        spread[...], hot, (((1,), (1,)), ((), ())), preferred_element_type=F32
    )

    @pl.when(step == 0)
    def _():
        acc[...] = part

    @pl.when(step > 0)
    def _():
        acc[...] += part

    @pl.when(step == pl.num_programs(0) - 1)
    def _():
        for b in range(blocks):
            out_ref[:, b * HASH : (b + 1) * HASH] = acc[b * rows : (b + 1) * rows, :]


def table_sums(values, ids, total):
    rows, tokens = values.shape
    tile = 1024
    blocks = total // HASH
    return pl.pallas_call(
        functools.partial(scatter_body, rows, blocks),
        grid=(tokens // tile,),
        out_shape=jax.ShapeDtypeStruct((rows, total), F32),
        in_specs=[
            pl.BlockSpec((rows, tile), lambda i: (0, i)),
            pl.BlockSpec((1, 1, tile), lambda i: (i, 0, 0)),
        ],
        out_specs=pl.BlockSpec((rows, total), lambda i: (0, 0)),
        scratch_shapes=[
            pltpu.VMEM((blocks * rows, tile), BF16),
            pltpu.VMEM((blocks * rows, HASH), F32),
        ],
        name="table_sums",
    )(values, ids.reshape(tokens // tile, 1, tile))


def head_mask(dtype):
    rows = lax.broadcasted_iota(jnp.int32, (H, D), 0)
    cols = lax.broadcasted_iota(jnp.int32, (H, D), 1)
    return (cols // HD == rows).astype(dtype)


def spread_heads(row):
    return row[None, :] * head_mask(row.dtype)


def encode_front(emb_t, w_in, w_out, gain, bias, length):
    width = emb_t.shape[1]
    center = emb_t - jnp.mean(emb_t, axis=0, keepdims=True)
    spread = jnp.mean(center * center, axis=0, keepdims=True)
    scale = lax.rsqrt(spread + NORM_EPS)
    hat = center * scale
    x0 = hat * gain[0][:, None] + bias[O_EMB : O_EMB + D][:, None]
    x_low = x0.astype(BF16)
    first_low = x_low[:, 0]
    q = (dot(first_low[None], w_in[:, :D], ((1,), (0,)))[0] + bias[O_Q : O_Q + D]).astype(BF16)
    k = dot(w_in[:, D : 2 * D], x_low, ((0,), (0,))).astype(BF16)
    v = (
        dot(w_in[:, 2 * D :], x_low, ((0,), (0,))) + bias[O_V : O_V + D][:, None]
    ).astype(BF16)
    q_heads = spread_heads(q)
    s = dot(q_heads, k, ((1,), (0,))) * 0.125
    if length < width:
        live = lax.broadcasted_iota(jnp.int32, (1, width), 1) < length
        s = jnp.where(live, s, -1e30)
    peak = jnp.max(s, axis=1, keepdims=True)
    e = jnp.exp(s - peak)
    p = e / jnp.sum(e, axis=1, keepdims=True)
    p_low = p.astype(BF16)
    mixed = dot(p_low, v, ((1,), (1,)))
    a = jnp.sum(mixed * head_mask(F32), axis=0).astype(BF16)
    o = dot(a[None], w_out, ((1,), (0,)))[0] + bias[O_O : O_O + D]
    return x0[:, 0] + o, (hat, scale, x_low, q, k, v, p, p_low, a)


def encode_back(kept, row_grad, w_in, w_out, gain):
    hat, scale, x_low, q, k, v, p, p_low, a = kept
    do = row_grad.astype(BF16)
    da = dot(do[None], w_out, ((1,), (1,)))[0].astype(BF16)
    da_heads = spread_heads(da)
    q_heads = spread_heads(q)
    dp = dot(da_heads, v, ((1,), (0,)))
    ds = (p * (dp - jnp.sum(dp * p, axis=1, keepdims=True))).astype(BF16)
    dq_heads = dot(ds, k, ((1,), (1,)))
    dq = (jnp.sum(dq_heads * head_mask(F32), axis=0) * 0.125).astype(BF16)
    t = dot(ds, x_low, ((1,), (1,))) * 0.125
    w = dot(p_low, x_low, ((1,), (1,)))
    gk = (dot(q_heads, w_in[:, D : 2 * D], ((1,), (1,))) * 0.125).astype(BF16)
    ev = dot(da_heads, w_in[:, 2 * D :], ((1,), (1,))).astype(BF16)
    gx = dot(gk, ds, ((0,), (0,))) + dot(ev, p_low, ((0,), (0,)))
    first = row_grad + dot(dq[None], w_in[:, :D], ((1,), (1,)))[0]
    is_first = lax.broadcasted_iota(jnp.int32, (1, gx.shape[1]), 1) == 0
    gx = gx + jnp.where(is_first, first[:, None], 0.0)
    p_sum = jnp.sum(p_low.astype(F32), axis=1)
    dbv = jnp.repeat(p_sum, HD) * da.astype(F32)
    g_gain = jnp.sum(gx * hat, axis=1)
    g_shift = jnp.sum(gx, axis=1)
    scaled = gx * gain[0][:, None]
    mean_one = jnp.mean(scaled, axis=0, keepdims=True)
    mean_two = jnp.mean(scaled * hat, axis=0, keepdims=True)
    g_emb = scale * (scaled - mean_one - hat * mean_two)
    return g_emb, (t.astype(BF16), w.astype(BF16), q, da, dq, dbv, g_gain, g_shift)


NN = (((1,), (0,)), ((), ()))
NT = (((1,), (1,)), ((), ()))
TN = (((0,), (0,)), ((), ()))
HIGH = lax.Precision.HIGHEST


def mm(left, right, dims, precision=None):
    return lax.dot_general(
        left, right, dims, preferred_element_type=F32, precision=precision
    )


def iota(shape, dim):
    return lax.broadcasted_iota(jnp.int32, shape, dim)


def as_bf16(mask):
    return mask.astype(F32).astype(BF16)


class Flow:
    def __init__(self, take, put, many, sources, targets):
        self.take, self.put, self.many = take, put, many
        self.sources, self.targets = sources, targets


class Net:
    def __init__(self, nd, narrow, send_sem, recv_sem, own_sem):
        self.nd, self.narrow = nd, narrow
        self.send_sem, self.recv_sem, self.own_sem = send_sem, recv_sem, own_sem
        self.me = lax.axis_index("wide") * narrow + lax.axis_index("narrow")
        self.used = 0

    def where(self, t):
        return (t // self.narrow, lax.rem(t, self.narrow))

    def barrier(self):
        sem = pltpu.get_barrier_semaphore()

        def greet(k, carry):
            t = lax.rem(self.me + k, self.nd)
            pl.semaphore_signal(sem, inc=1, device_id=self.where(t), device_id_type=MESH)
            return carry

        lax.fori_loop(1, self.nd, greet, 0)
        pl.semaphore_wait(sem, self.nd - 1)

    def start(self, flows):
        me, nd = self.me, self.nd
        base = self.used
        self.used += len(flows)

        def push(k, carry):
            t = lax.rem(me + k, nd)
            for i, f in enumerate(flows):

                @pl.when(jnp.logical_and(inside(me, f.sources), inside(t, f.targets)))
                def _():
                    pltpu.make_async_remote_copy(
                        src_ref=f.take(me, t),
                        dst_ref=f.put(me, t),
                        send_sem=self.send_sem.at[base + i],
                        recv_sem=self.recv_sem.at[base + i],
                        device_id=self.where(t),
                        device_id_type=MESH,
                    ).start()

            return carry

        for i, f in enumerate(flows):

            @pl.when(jnp.logical_and(inside(me, f.sources), inside(me, f.targets)))
            def _():
                pltpu.make_async_copy(
                    f.take(me, me), f.put(me, me), self.own_sem.at[base + i]
                ).start()

        lax.fori_loop(1, nd, push, 0)
        return base

    def finish(self, flows, base):
        me = self.me
        for i, f in enumerate(flows):
            n_t = f.targets[1] - f.targets[0]
            n_s = f.sources[1] - f.sources[0]
            is_s, is_t = inside(me, f.sources), inside(me, f.targets)

            @pl.when(jnp.logical_and(is_s, is_t))
            def _():
                pltpu.make_async_copy(
                    f.take(me, me), f.put(me, me), self.own_sem.at[base + i]
                ).wait()

            for own in (0, 1):
                mine = is_s if own else jnp.logical_not(is_s)
                if n_s - own > 0:

                    @pl.when(jnp.logical_and(is_t, mine))
                    def _():
                        view = f.many(n_s - own)
                        pltpu.make_async_copy(view, view, self.recv_sem.at[base + i]).wait()

            for own in (0, 1):
                mine = is_t if own else jnp.logical_not(is_t)
                if n_t - own > 0:

                    @pl.when(jnp.logical_and(is_s, mine))
                    def _():
                        view = f.many(n_t - own)
                        pltpu.make_async_copy(view, view, self.send_sem.at[base + i]).wait()


class Unit:
    def __init__(self, count, length):
        self.count, self.length = count, length
        self.tokens = count * length
        self.bits = count.bit_length() - 1
        self.rows = max(16, H * count)
        self.seqs = max(8, count)

    def pick(self):
        lane = iota((self.seqs, self.tokens), 1)
        seq = iota((self.seqs, self.tokens), 0)
        return lane == seq * self.length

    def spread(self):
        row, seq = iota((self.rows, self.seqs), 0), iota((self.rows, self.seqs), 1)
        return as_bf16((row & (self.count - 1)) == seq)

    def collect(self):
        row, seq = iota((self.seqs, self.rows), 1), iota((self.seqs, self.rows), 0)
        return as_bf16((row & (self.count - 1)) == seq)

    def heads(self):
        row, col = iota((self.rows, D), 0), iota((self.rows, D), 1)
        return ((row >> self.bits) == (col >> 6)).astype(F32)

    def live(self):
        row, lane = iota((self.rows, self.tokens), 0), iota((self.rows, self.tokens), 1)
        return (lane >> 5) == (row & (self.count - 1))


def unit_front(unit, emb, e, w, cv, rv, keep):
    center = emb - jnp.mean(emb, axis=0, keepdims=True)
    spread = jnp.mean(center * center, axis=0, keepdims=True)
    scale = lax.rsqrt(spread + NORM_EPS)
    hat = center * scale
    x0 = hat * cv[:, 3 * e : 3 * e + 1] + cv[:, 3 * e + 1 : 3 * e + 2]
    x_low = x0.astype(BF16)
    pick = unit.pick()
    x_first = mm(as_bf16(pick), x_low, NT).astype(BF16)
    x0_first = mm(pick.astype(F32), x0, NT, HIGH)
    q = (mm(x_first, w[:, 0:D], NN) + rv[8 * e : 8 * e + 1, :]).astype(BF16)
    k = mm(w[:, D : 2 * D], x_low, TN).astype(BF16)
    v = (mm(w[:, 2 * D : 3 * D], x_low, TN) + cv[:, 3 * e + 2 : 3 * e + 3]).astype(BF16)
    heads = unit.heads()
    q_heads = (mm(unit.spread(), q, NN) * heads).astype(BF16)
    s = mm(q_heads, k, NN) * 0.125
    if unit.count > 1:
        s = jnp.where(unit.live(), s, -1e30)
    peak = jnp.max(s, axis=1, keepdims=True)
    ex = jnp.exp(s - peak)
    p = ex / jnp.sum(ex, axis=1, keepdims=True)
    mixed = (mm(p.astype(BF16), v, NT) * heads).astype(BF16)
    a = mm(unit.collect(), mixed, NN).astype(BF16)
    o = mm(a, w[:, 3 * D : 4 * D], NN) + rv[8 * e + 1 : 8 * e + 2, :]
    keep(hat, scale, x_low, x_first, q, k, v, p, a)
    return x0_first + o


def unit_back(unit, row_grad, e, w, cv, kept):
    hat, scale, x_low, x_first, q, k, v, p, a = kept
    heads = unit.heads()
    spread, collect = unit.spread(), unit.collect()
    p_low = p.astype(BF16)
    do = row_grad.astype(BF16)
    da = mm(do, w[:, 3 * D : 4 * D], NT).astype(BF16)
    q_heads = (mm(spread, q, NN) * heads).astype(BF16)
    da_heads = (mm(spread, da, NN) * heads).astype(BF16)
    dp = mm(da_heads, v, NN)
    ds = (p * (dp - jnp.sum(dp * p, axis=1, keepdims=True))).astype(BF16)
    dq_heads = (mm(ds, k, NT) * heads * 0.125).astype(BF16)
    dq = mm(collect, dq_heads, NN).astype(BF16)
    t = mm(ds, x_low, NT) * 0.125
    wx = mm(p_low, x_low, NT)
    gk = (mm(q_heads, w[:, D : 2 * D], NT) * 0.125).astype(BF16)
    ev = mm(da_heads, w[:, 2 * D : 3 * D], NT).astype(BF16)
    first = row_grad + mm(dq, w[:, 0:D], NT)
    gx = mm(gk, ds, TN) + mm(ev, p_low, TN)
    gx = gx + mm(first, unit.pick().astype(F32), TN, HIGH)
    p_sum = jnp.sum(p_low.astype(F32), axis=1, keepdims=True)
    dbv = jnp.sum(p_sum * da_heads.astype(F32), axis=0, keepdims=True)
    g_gain = jnp.sum(gx * hat, axis=1, keepdims=True)
    g_shift = jnp.sum(gx, axis=1, keepdims=True)
    scaled = gx * cv[:, 3 * e : 3 * e + 1]
    mean_one = jnp.mean(scaled, axis=0, keepdims=True)
    mean_two = jnp.mean(scaled * hat, axis=0, keepdims=True)
    g_emb = scale * (scaled - mean_one - hat * mean_two)
    return g_emb, t, wx, da, dq, do, dbv, g_gain, g_shift


def load_rows(ref, count):
    return jnp.concatenate(
        [ref[pl.ds(j, count, stride=8), :] for j in range(D // LANE)], axis=1
    )


def store_rows(ref, value):
    for j in range(D // LANE):
        ref[pl.ds(j, value.shape[0], stride=8), :] = value[:, j * LANE : (j + 1) * LANE]


def middle_body(
    n_valid, nq, nd, narrow, cols, query_home, token_total,
    mine, mine_q, w_one, w_zero, up_mine, w_down, cv, rv, b_in, slots, ids,
    o_shrink, o_loss, g_table, g_in, g_out, g_up, g_bin, g_small, o_norm,
    hat_s, scale_s, xl_s, xf_s, q_s, k_s, v_s, p_s, a_s,
    hat_q, scale_q, xl_q, xf_q, q_q, k_q, v_q, p_q, a_q,
    r1_own, r1_ownq, r1_all, y_send, y_recv, y_sum, y_all, h_send, h_recv, h_recvq,
    du_own, du_f, gtok, gtok_q, fac, fac_q, line, line_q, f_s, slope_s, hlow_s, g_top_s, sums_s,
    size48, o_tok, o_fac, o_facq, o_line, o_lineq, o_du, o_h, up_got, w_up,
    t_all, w_all, q_exp, d_exp, spread_s, acc_s, norm_own, norm_all,
    send_sem, recv_sem, own_sem,
):
    cap = -(-n_valid // nd)
    rows = n_valid + nq
    net = Net(nd, narrow, send_sem, recv_sem, own_sem)
    me = net.me
    everyone = (0, nd)
    home = (query_home, query_home + 1)
    q_owner = nd - nq
    q_owners = (q_owner, nd)

    def span(c):
        return (0, min(nd, n_valid - c * nd))

    net.barrier()
    passage = Unit(1, LP)
    queries = Unit(nq, LQ)
    n_mine = jnp.where(me < n_valid - (cap - 1) * nd, cap, cap - 1)

    up_flows = [
        Flow(
            lambda s, t: up_mine.at[t], lambda s, t: up_got.at[s],
            lambda n: up_got.at[pl.ds(0, n)], everyone, everyone,
        )
    ]
    up_base = net.start(up_flows)

    def front(c, carry):
        at = pl.ds(pl.multiple_of(c * LP, LANE), LP)
        emb = mine[:, :, at].astype(F32).reshape(D, LP) + w_one[:, 4 * D :].astype(F32)

        def keep(hat, scale, x_low, x_first, q, k, v, p, a):
            hat_s[c], scale_s[c], xl_s[c], xf_s[c] = hat, scale, x_low, x_first
            q_s[c], k_s[c], v_s[c], p_s[c], a_s[c] = q, k, v, p, a

        r1 = unit_front(passage, emb, 1, w_one, cv, rv, keep)
        for j in range(D // LANE):
            r1_own[c, j : j + 1, :] = r1[0:1, j * LANE : (j + 1) * LANE]
        return carry

    lax.fori_loop(0, n_mine, front, 0)

    @pl.when(me == query_home)
    def _():
        parts = w_one[:, 4 * D : 4 * D + LANE].astype(F32)[:, 0:LQ]
        emb = mine_q[...].astype(F32).reshape(D, nq * LQ) + jnp.concatenate([parts] * nq, axis=1)

        def keep(hat, scale, x_low, x_first, q, k, v, p, a):
            hat_q[...], scale_q[...], xl_q[...], xf_q[...] = hat, scale, x_low, x_first
            q_q[...], k_q[...], v_q[...], p_q[...], a_q[...] = q, k, v, p, a

        store_rows(r1_ownq, unit_front(queries, emb, 0, w_zero, cv, rv, keep))

    flows = [
        Flow(
            lambda s, t, c=c: r1_own.at[c],
            lambda s, t, c=c: r1_all.at[pl.ds(pl.multiple_of(8 * (c * nd + s), 8), 8), :],
            lambda n: r1_all.at[pl.ds(0, 8 * n), :],
            span(c), everyone,
        )
        for c in range(cap)
    ] + [
        Flow(
            lambda s, t: r1_ownq,
            lambda s, t: r1_all.at[pl.ds(8 * n_valid, 8 * nq), :],
            lambda n: y_recv_q(n),
            home, everyone,
        )
    ]

    def y_recv_q(n):
        return h_recvq.at[pl.ds(0, n)]

    base = net.start(flows)
    net.finish(flows, base)

    net.finish(up_flows, up_base)
    for e in range(2):
        w_up[e] = up_got[:, e].astype(F32).reshape(D, LANE).astype(BF16)

    part = {1: (0, n_valid), 0: (n_valid, nq)}
    y_parts = []
    for e in (1, 0):
        at, n = part[e]
        r1 = load_rows(r1_all.at[pl.ds(8 * at, 8 * n), :], n)
        h, hat1, scale1 = norm_rows(r1, rv[8 * e + 5 : 8 * e + 6, :], rv[8 * e + 2 : 8 * e + 3, :])
        h_low = h.astype(BF16)
        hlow_s[at : at + n, :] = h
        o_h[at : at + n, :] = h_low.astype(F32)
        upper = mm(h_low, w_up[e], NN) + b_in[e : e + 1, :]
        active, slope = gelu_both(upper)
        f_low = active.astype(BF16)
        f_s[at : at + n, :] = f_low.astype(F32)
        slope_s[at : at + n, :] = slope
        y_parts.append(mm(f_low, w_down[e], NN))
    store_rows(y_send, jnp.concatenate(y_parts, axis=0))
    flows = [
        Flow(
            lambda s, t, c=c: y_send.at[pl.ds(pl.multiple_of(8 * (c * nd + t), 8), 8), :],
            lambda s, t, c=c: y_recv.at[s, c],
            lambda n, c=c: y_recv.at[pl.ds(0, n), c],
            everyone, span(c),
        )
        for c in range(cap)
    ] + [
        Flow(
            lambda s, t: y_send.at[pl.ds(pl.multiple_of(8 * (n_valid + t - q_owner), 8), 8), :],
            lambda s, t: y_recv.at[s, cap],
            lambda n: y_recv.at[pl.ds(0, n), cap],
            everyone, q_owners,
        )
    ]
    base = net.start(flows)
    net.finish(flows, base)
    y_sum[...] = jnp.sum(y_recv[...], axis=0)
    flows = [
        Flow(
            lambda s, t, c=c: y_sum.at[c],
            lambda s, t, c=c: y_all.at[pl.ds(pl.multiple_of(8 * (c * nd + s), 8), 8), :],
            lambda n: y_all.at[pl.ds(0, 8 * n), :],
            span(c), everyone,
        )
        for c in range(cap)
    ] + [
        Flow(
            lambda s, t: y_sum.at[cap],
            lambda s, t: y_all.at[pl.ds(pl.multiple_of(8 * (n_valid + s - q_owner), 8), 8), :],
            lambda n: y_all.at[pl.ds(0, 8 * n), :],
            q_owners, everyone,
        )
    ]
    base = net.start(flows)
    net.finish(flows, base)

    tops, vecs = {}, {}
    for e in (1, 0):
        at, n = part[e]
        y = load_rows(y_all.at[pl.ds(8 * at, 8 * n), :], n)
        top = hlow_s[at : at + n, :] + y + rv[8 * e + 3 : 8 * e + 4, :]
        z, hat2, scale2 = norm_rows(
            top, rv[8 * e + 6 : 8 * e + 7, :], rv[8 * e + 4 : 8 * e + 5, :]
        )
        tops[e] = (hat2, scale2)
        vecs[e] = z.astype(BF16)
    qvec, pvec = vecs[0], vecs[1]
    owner = slots[0:1, 0:n_valid]
    is_first = slots[1:2, 0:n_valid] == 1
    kept_slot = slots[2:3, 0:n_valid] == 1
    member = owner == iota((nq, n_valid), 0)
    valid = jnp.broadcast_to(owner >= 0, (nq, n_valid))
    positive = jnp.logical_and(member, is_first)
    negative = jnp.logical_and(member, jnp.logical_and(jnp.logical_not(is_first), kept_slot))
    counts = jnp.sum(member.astype(F32), axis=1, keepdims=True) - 1.0
    score_scale = 2.0 * D ** (-0.5)
    scores = mm(qvec, pvec, NT) * score_scale
    masked = jnp.where(valid, scores, -1e30)
    peak = jnp.max(masked, axis=1, keepdims=True)
    summed = jnp.sum(jnp.where(valid, jnp.exp(masked - peak), 0.0), axis=1, keepdims=True)
    logsum = peak + jnp.log(summed)
    pos_score = jnp.sum(jnp.where(positive, scores, 0.0), axis=1, keepdims=True)
    margins = MARGIN - pos_score + scores
    active = jnp.logical_and(negative, margins > 0)
    hinge = jnp.sum(jnp.where(active, margins, 0.0), axis=1, keepdims=True) / counts
    active_total = jnp.sum(active.astype(F32), axis=1, keepdims=True)
    loss = jnp.sum(logsum - pos_score + hinge, axis=0, keepdims=True)
    o_loss[...] = jnp.broadcast_to(loss, (8, LANE))
    score_grad = (
        jnp.where(valid, jnp.exp(scores - logsum), 0.0)
        - positive.astype(F32) * (1.0 + active_total / counts)
        + active.astype(F32) / counts
    )
    score_low = score_grad.astype(BF16)
    vec_grads = {
        0: (mm(score_low, pvec, NN) * score_scale).astype(BF16).astype(F32),
        1: (mm(score_low, qvec, TN) * score_scale).astype(BF16).astype(F32),
    }
    h_parts, out_rows = [], {}
    for e in (1, 0):
        at, n = part[e]
        hat2, scale2 = tops[e]
        grad = vec_grads[e]
        g_top = norm_rows_back(grad, rv[8 * e + 6 : 8 * e + 7, :], hat2, scale2)
        dy = g_top.astype(BF16)
        g_top_s[at : at + n, :] = g_top
        out_rows[e] = [
            jnp.sum(grad * hat2, axis=0, keepdims=True),
            jnp.sum(grad, axis=0, keepdims=True),
            jnp.sum(dy.astype(F32), axis=0, keepdims=True),
        ]
        f_low = f_s[at : at + n, :].astype(BF16)
        o_shrink[e] = mm(f_low, dy, TN)
        df = mm(dy, w_down[e], NT)
        du = (slope_s[at : at + n, :] * df).astype(BF16)
        du_f[at : at + n, :] = du.astype(F32)
        h_parts.append(mm(du, w_up[e], NT))
    du_own[...] = du_f[...].astype(BF16)
    store_rows(h_send, jnp.concatenate(h_parts, axis=0))
    flows = [
        Flow(
            lambda s, t, c=c: h_send.at[pl.ds(pl.multiple_of(8 * (c * nd + t), 8), 8), :],
            lambda s, t, c=c: h_recv.at[s, c],
            lambda n, c=c: h_recv.at[pl.ds(0, n), c],
            everyone, span(c),
        )
        for c in range(cap)
    ] + [
        Flow(
            lambda s, t: h_send.at[pl.ds(8 * n_valid, 8 * nq), :],
            lambda s, t: h_recvq.at[s],
            lambda n: h_recvq.at[pl.ds(0, n)],
            everyone, home,
        )
    ]
    du_flows = [
        Flow(
            lambda s, t: du_own,
            lambda s, t: o_du.at[:, pl.ds(pl.multiple_of(s * LANE, LANE), LANE)],
            lambda n: o_du.at[:, pl.ds(0, n * LANE)],
            everyone, everyone,
        )
    ]
    base = net.start(flows)
    du_base = net.start(du_flows)
    fac[...] = jnp.zeros_like(fac)
    line[...] = jnp.zeros_like(line)
    sums_s[...] = jnp.zeros_like(sums_s)
    o_tok[:, n_valid * LP + nq * LQ :] = jnp.zeros(
        (cols, token_total - n_valid * LP - nq * LQ), BF16
    )
    net.finish(flows, base)

    def load_rows_sum(ref, count):
        total = jnp.sum(ref[...], axis=0)
        h_send[0 : 8 * count, :] = total
        return load_rows(h_send.at[pl.ds(0, 8 * count), :], count)

    lane = iota((D, LANE), 1)

    def back(c, carry):
        slot = c * nd + me
        tile = jnp.sum(h_recv[:, c], axis=0)
        dh = jnp.concatenate([tile[j : j + 1, :] for j in range(D // LANE)], axis=1)
        top = g_top_s[pl.ds(slot, 1), :]
        g_h = top + dh
        r1 = jnp.concatenate([r1_own[c, j : j + 1, :] for j in range(D // LANE)], axis=1)
        gain1 = rv[8 + 5 : 8 + 6, :]
        _, hat1, scale1 = norm_rows(r1, gain1, gain1)
        g_mid = norm_rows_back(g_h, gain1, hat1, scale1)
        row_grad = jnp.where(iota((8, D), 0) == 0, jnp.broadcast_to(g_mid, (8, D)), 0.0)
        kept = (
            hat_s[c], scale_s[c], xl_s[c], xf_s[c], q_s[c], k_s[c], v_s[c], p_s[c], a_s[c]
        )
        g_emb, t, wx, da, dq, do, dbv, g_gain, g_shift = unit_back(
            passage, row_grad, 1, w_one, cv, kept
        )
        gtok[c] = g_emb.reshape(nd, cols, LP).astype(BF16)
        zero = jnp.zeros((16, D), F32)
        xa = jnp.concatenate(
            [xf_s[c].astype(F32)[0:1, :], jnp.zeros((15, D), F32), a_s[c].astype(F32)[0:1, :],
             jnp.zeros((31, D), F32)],
            axis=0,
        )
        tw = jnp.transpose(jnp.concatenate([t, zero, wx, zero, jnp.zeros((64, D), F32)], axis=0))
        xa = jnp.transpose(jnp.concatenate([jnp.zeros((64, D), F32), xa, zero], axis=0))
        placed = pltpu.roll(tw, 16 * c, 1) + pltpu.roll(xa, c, 1)
        fac[...] = (fac[...].astype(F32) + placed.reshape(nd, cols, LANE)).astype(BF16)
        which = iota((16, D), 0)
        new = jnp.zeros((16, D), F32)
        for j, row in enumerate((q_s[c], da, dq, do)):
            new = new + jnp.where(which == 2 * j + c, row.astype(F32)[0:1, :], 0.0)
        line[...] = line[...] + new
        columns = jnp.where(lane == 0, g_gain, jnp.where(lane == 1, g_shift, 0.0))
        flat = jnp.transpose(columns)[0:8, :]
        extra = (
            jnp.where(iota((8, D), 0) == 2, dbv, 0.0)
            + jnp.where(iota((8, D), 0) == 3, g_h * hat1, 0.0)
            + jnp.where(iota((8, D), 0) == 4, g_h, 0.0)
        )
        sums_s[...] = sums_s[...] + flat + extra
        return carry

    lax.fori_loop(0, n_mine, back, 0)
    line_q[0:16, :] = (line[...] + jnp.concatenate([jnp.zeros((8, D), F32), sums_s[...]], axis=0)).astype(BF16)

    @pl.when(me == query_home)
    def _():
        dh = load_rows_sum(h_recvq, nq)
        at, n = part[0]
        g_h = g_top_s[at : at + n, :] + dh
        r1 = load_rows(r1_ownq, nq)
        gain1 = rv[5:6, :]
        _, hat1, scale1 = norm_rows(r1, gain1, gain1)
        g_mid = norm_rows_back(g_h, gain1, hat1, scale1)
        kept = (
            hat_q[...], scale_q[...], xl_q[...], xf_q[...], q_q[...], k_q[...], v_q[...],
            p_q[...], a_q[...],
        )
        g_emb, t, w, da, dq, do, dbv, g_gain, g_shift = unit_back(
            queries, g_mid, 0, w_zero, cv, kept
        )
        gtok_q[...] = g_emb.reshape(nd, cols, nq * LQ).astype(BF16)
        tw = jnp.concatenate([t, w, xf_q[...].astype(F32), a_q[...].astype(F32)], axis=0)
        n_tw = tw.shape[0]
        tw = jnp.concatenate([tw, jnp.zeros((fac_q.shape[2] - n_tw, D), F32)], axis=0)
        fac_q[...] = jnp.transpose(tw).reshape(nd, cols, fac_q.shape[2]).astype(BF16)
        columns = jnp.where(lane == 0, g_gain, jnp.where(lane == 1, g_shift, 0.0))
        flat = jnp.transpose(columns)[0:8, :]
        extra = (
            jnp.where(iota((8, D), 0) == 2, dbv, 0.0)
            + jnp.where(iota((8, D), 0) == 3, jnp.sum(g_h * hat1, axis=0, keepdims=True), 0.0)
            + jnp.where(iota((8, D), 0) == 4, jnp.sum(g_h, axis=0, keepdims=True), 0.0)
        )
        block = jnp.concatenate(
            [q_q[...].astype(F32), da.astype(F32), dq.astype(F32), do.astype(F32), flat + extra,
             jnp.zeros((8, D), F32)],
            axis=0,
        )
        line_q[16:64, :] = block.astype(BF16)

    flows = [
        Flow(
            lambda s, t, c=c: gtok.at[c, t],
            lambda s, t, c=c: o_tok.at[:, pl.ds(pl.multiple_of((c * nd + s) * LP, LANE), LP)],
            lambda n: o_tok.at[:, pl.ds(0, n * LP)],
            span(c), everyone,
        )
        for c in range(cap)
    ] + [
        Flow(
            lambda s, t: gtok_q.at[t],
            lambda s, t: o_tok.at[:, pl.ds(n_valid * LP, nq * LQ)],
            lambda n: o_tok.at[:, pl.ds(0, n * nq * LQ)],
            home, everyone,
        ),
        Flow(
            lambda s, t: fac.at[t],
            lambda s, t: o_fac.at[s],
            lambda n: o_fac.at[pl.ds(0, n)],
            everyone, everyone,
        ),
        Flow(
            lambda s, t: fac_q.at[t],
            lambda s, t: o_facq,
            lambda n: fac_q.at[pl.ds(0, n)],
            home, everyone,
        ),
        Flow(
            lambda s, t: line_q.at[pl.ds(0, 16), :],
            lambda s, t: o_line.at[s],
            lambda n: o_line.at[pl.ds(0, n)],
            everyone, everyone,
        ),
        Flow(
            lambda s, t: line_q.at[pl.ds(16, 48), :],
            lambda s, t: o_lineq,
            lambda n: o_line48(n),
            home, everyone,
        ),
    ]

    def o_line48(n):
        return size48.at[pl.ds(0, n)]

    base = net.start(flows)

    net.finish(flows[cap + 1 :], base + cap + 1)
    net.finish(du_flows, du_base)
    lane1 = iota((cols, LANE), 1)
    for g in range(nd // 4):
        t_g = jnp.zeros((cols, LANE), F32)
        w_g = jnp.zeros((cols, LANE), F32)
        for j in range(4):
            block = o_fac[4 * g + j].astype(F32)
            t_part = jnp.where(lane1 < 32, block, 0.0)
            w_part = jnp.where(jnp.logical_and(lane1 >= 32, lane1 < 64), block, 0.0)
            t_g = t_g + (pltpu.roll(t_part, 32 * j, 1) if j else t_part)
            w_g = w_g + (pltpu.roll(w_part, (32 * j - 32) % LANE, 1) if j != 1 else w_part)
        t_all[:, g * LANE : (g + 1) * LANE] = t_g.astype(BF16)
        w_all[:, g * LANE : (g + 1) * LANE] = w_g.astype(BF16)
    x_all = jnp.zeros((cols, LANE), F32)
    a_all = jnp.zeros((cols, LANE), F32)
    for d in range(nd):
        block = o_fac[d].astype(F32)
        x_part = jnp.where(jnp.logical_and(lane1 >= 64, lane1 < 66), block, 0.0)
        a_part = jnp.where(jnp.logical_and(lane1 >= 80, lane1 < 82), block, 0.0)
        x_all = x_all + pltpu.roll(x_part, (2 * d - 64) % LANE, 1)
        a_all = a_all + pltpu.roll(a_part, (2 * d - 80) % LANE, 1)
    mask16 = ((iota((16, D), 0)) == (iota((16, D), 1) >> 6)).astype(F32)

    def expand(d, carry):
        for c in range(2):
            at = pl.ds(pl.multiple_of(32 * d + 16 * c, 16), 16)
            both = o_line[d].astype(F32)
            q_exp[at, :] = (both[c : c + 1, :] * mask16).astype(BF16)
            d_exp[at, :] = (both[2 + c : 3 + c, :] * mask16).astype(BF16)
        return carry

    lax.fori_loop(0, nd, expand, 0)
    everything = o_line[...].reshape(nd * 16, D)
    row, col = iota((272, nd * 16), 0), iota((272, nd * 16), 1)
    kind = col & 15
    pair = (col >> 4) * 2 + (col & 1)
    dq_rows = jnp.logical_and(row < 128, jnp.logical_and((kind >> 1) == 2, pair == row))
    do_rows = jnp.logical_and(
        jnp.logical_and(row >= 128, row < 256),
        jnp.logical_and((kind >> 1) == 3, pair == row - 128),
    )
    total_rows = jnp.logical_or(
        jnp.logical_and(jnp.logical_and(row >= 256, row < 261), kind == row - 248),
        jnp.logical_or(
            jnp.logical_and(row == 261, (kind >> 1) == 2),
            jnp.logical_and(row == 262, (kind >> 1) == 3),
        ),
    )
    select = as_bf16(jnp.logical_or(dq_rows, jnp.logical_or(do_rows, total_rows)))
    picked = mm(select, everything, NN)
    g_in[1, :, 0:D] = mm(x_all.astype(BF16), picked[0:128].astype(BF16), NN)
    g_in[1, :, D : 2 * D] = mm(t_all[...], q_exp[...], NN)
    g_in[1, :, 2 * D : 3 * D] = mm(w_all[...], d_exp[...], NN)
    g_out[1] = mm(a_all.astype(BF16), picked[128:256].astype(BF16), NN)
    sums1 = picked[256:272]

    fl = o_facq.shape[1]
    row, col = iota((fl, 48), 0), iota((fl, 48), 1)
    q_rows = H * nq
    rown = iota((fl, D), 0)
    headn = iota((fl, D), 1) >> 6

    def rhs(first_row, last_row, first_col, by_head):
        here = jnp.logical_and(row >= first_row, row < last_row)
        hit = jnp.logical_and(here, col == first_col + (row & (nq - 1)))
        out = mm(as_bf16(hit), o_lineq[...], NN)
        if by_head:
            out = jnp.where(((rown - first_row) >> (nq.bit_length() - 1)) == headn, out, 0.0)
        return out.astype(BF16)

    facq = o_facq[...]
    g_in[0, :, 0:D] = mm(facq, rhs(2 * q_rows, 2 * q_rows + nq, 2 * nq, False), NN)
    g_in[0, :, D : 2 * D] = mm(facq, rhs(0, q_rows, 0, True), NN)
    g_in[0, :, 2 * D : 3 * D] = mm(facq, rhs(q_rows, 2 * q_rows, nq, True), NN)
    g_out[0] = mm(facq, rhs(2 * q_rows + nq, 2 * q_rows + 2 * nq, 3 * nq, False), NN)
    line0 = o_lineq[...].astype(F32)
    sums0 = line0[4 * nq : 4 * nq + 8]
    dq0 = jnp.sum(line0[2 * nq : 3 * nq], axis=0, keepdims=True)
    do0 = jnp.sum(line0[3 * nq : 4 * nq], axis=0, keepdims=True)

    mine_at = as_bf16(iota((cols, D), 1) == iota((cols, D), 0) + me * cols)
    h_cols = mm(mine_at, o_h[...].astype(BF16), NT)
    both = jnp.concatenate([h_cols, h_cols], axis=0)
    r, c = iota((2 * cols, rows), 0), iota((2 * cols, rows), 1)
    both = jnp.where((r < cols) == (c >= n_valid), both, 0.0).astype(BF16)
    g_up[...] = mm(both, o_du[...], NN)
    ones = iota((8, rows), 0)
    which = iota((8, rows), 1)
    e_rows = as_bf16(
        jnp.logical_or(
            jnp.logical_and(ones == 0, which >= n_valid),
            jnp.logical_and(ones == 1, which < n_valid),
        )
    )
    db_in = mm(e_rows, o_du[...], NN)
    g_bin[...] = db_in
    small_rows = {
        0: (dq0, sums0[2:3], do0, sums0[4:5], out_rows[0][2], out_rows[0][1], sums0[1:2],
            sums0[0:1], sums0[3:4], out_rows[0][0]),
        1: (sums1[5:6], sums1[2:3], sums1[6:7], sums1[4:5], out_rows[1][2], out_rows[1][1],
            sums1[1:2], sums1[0:1], sums1[3:4], out_rows[1][0]),
    }
    small_squares = jnp.sum(db_in * db_in)
    for e in range(2):
        for j, value in enumerate(small_rows[e]):
            g_small[16 * e + j : 16 * e + j + 1, :] = value
            small_squares = small_squares + jnp.sum(value * value)
    squares = jnp.sum(g_in[...] * g_in[...]) + jnp.sum(g_out[...] * g_out[...])
    squares = squares + jnp.sum(g_up[...] * g_up[...]) + jnp.sum(o_shrink[...] * o_shrink[...])

    net.finish(flows[: cap + 1], base)
    blocks = g_table.shape[1] // HASH
    chunk = ids.shape[2]

    def add_chunk(i, carry):
        at = pl.ds(pl.multiple_of(i * chunk, LANE), chunk)
        now = ids[i]
        low = now & (HASH - 1)
        high = now >> (HASH.bit_length() - 1)
        values = o_tok[:, at].astype(F32)
        for b in range(0, blocks, 2):
            two = jnp.concatenate(
                [jnp.where(high == b, values, 0.0), jnp.where(high == b + 1, values, 0.0)], axis=0
            )
            spread_s[b * cols : (b + 2) * cols, :] = two.astype(BF16)
        hot = as_bf16(iota((HASH, chunk), 0) == low)
        part = mm(spread_s[...], hot, NT)

        @pl.when(i == 0)
        def _():
            acc_s[...] = part

        @pl.when(i > 0)
        def _():
            acc_s[...] += part

        return carry

    lax.fori_loop(0, ids.shape[0], add_chunk, 0)

    def add_slot(s, total):
        return total + o_tok[:, pl.ds(pl.multiple_of(s * LP, LANE), LP)].astype(F32)

    position = lax.fori_loop(0, n_valid, add_slot, jnp.zeros((cols, LP), F32))
    tq = nq * LQ
    q_tok = o_tok[:, n_valid * LP : n_valid * LP + tq].astype(F32)
    folded = q_tok[:, 0:LANE]
    for j in range(1, tq // LANE):
        folded = folded + q_tok[:, j * LANE : (j + 1) * LANE]
    around = folded
    for j in range(1, LANE // LQ):
        around = around + pltpu.roll(folded, LANE - LQ * j, 1)
    around = jnp.where(lane1 < LQ, around, 0.0)
    position = jnp.concatenate(
        [position[:, 0:LANE] + around, position[:, LANE:], jnp.zeros((cols, HASH - LP), F32)],
        axis=1,
    )
    shifted = pltpu.roll(position, V - (blocks - 1) * HASH, 1)
    for b in range(blocks):
        value = acc_s[b * cols : (b + 1) * cols, :]
        if b == blocks - 1:
            value = value + shifted
        g_table[:, b * HASH : (b + 1) * HASH] = value
        squares = squares + jnp.sum(value * value)

    norm_own[...] = jnp.broadcast_to(squares.reshape(1, 1), (8, LANE))
    flows = [
        Flow(
            lambda s, t: norm_own, lambda s, t: norm_all.at[s],
            lambda n: norm_all.at[pl.ds(0, n)], everyone, everyone,
        )
    ]
    base = net.start(flows)
    net.finish(flows, base)
    o_norm[...] = jnp.sqrt(jnp.sum(norm_all[...], axis=0) + small_squares)


def middle(n_valid, nq, nd, narrow, cols, query_home, token_total, arrays):
    cap = -(-n_valid // nd)
    rows = n_valid + nq
    tq = nq * LQ
    unit, unit_q = Unit(1, LP), Unit(nq, LQ)
    fac_lanes = -(-(2 * unit_q.rows + 2 * unit_q.seqs) // LANE) * LANE
    vmem = pl.BlockSpec(memory_space=pltpu.VMEM)

    def like(*shape, dtype=F32):
        return jax.ShapeDtypeStruct(shape, dtype)

    def kept(lead, u):
        return [
            pltpu.VMEM(lead + (D, u.tokens), F32),
            pltpu.VMEM(lead + (1, u.tokens), F32),
            pltpu.VMEM(lead + (D, u.tokens), BF16),
            pltpu.VMEM(lead + (u.seqs, D), BF16),
            pltpu.VMEM(lead + (u.seqs, D), BF16),
            pltpu.VMEM(lead + (D, u.tokens), BF16),
            pltpu.VMEM(lead + (D, u.tokens), BF16),
            pltpu.VMEM(lead + (u.rows, u.tokens), F32),
            pltpu.VMEM(lead + (u.seqs, D), BF16),
        ]

    flows = 5 * (cap + 1) + 7
    table_total = -(-(V + LP) // HASH) * HASH
    chunk = arrays[10].shape[2]
    return pl.pallas_call(
        functools.partial(
            middle_body, n_valid, nq, nd, narrow, cols, query_home, token_total
        ),
        out_shape=[
            like(2, LANE, D),
            like(8, LANE),
            like(cols, table_total),
            like(2, cols, 3 * D),
            like(2, cols, D),
            like(2 * cols, nd * LANE),
            like(8, nd * LANE),
            like(32, D),
            like(8, LANE),
        ],
        in_specs=[vmem] * len(arrays),
        out_specs=[vmem] * 9,
        scratch_shapes=kept((cap,), unit)
        + kept((), unit_q)
        + [
            pltpu.VMEM((cap, 8, LANE), F32),
            pltpu.VMEM((8 * nq, LANE), F32),
            pltpu.VMEM((8 * rows, LANE), F32),
            pltpu.VMEM((8 * rows, LANE), F32),
            pltpu.VMEM((nd, cap + 1, 8, LANE), F32),
            pltpu.VMEM((cap + 1, 8, LANE), F32),
            pltpu.VMEM((8 * rows, LANE), F32),
            pltpu.VMEM((8 * rows, LANE), F32),
            pltpu.VMEM((nd, cap, 8, LANE), F32),
            pltpu.VMEM((nd, 8 * nq, LANE), F32),
            pltpu.VMEM((rows, LANE), BF16),
            pltpu.VMEM((rows, LANE), F32),
            pltpu.VMEM((cap, nd, cols, LP), BF16),
            pltpu.VMEM((nd, cols, tq), BF16),
            pltpu.VMEM((nd, cols, LANE), BF16),
            pltpu.VMEM((nd, cols, fac_lanes), BF16),
            pltpu.VMEM((16, D), F32),
            pltpu.VMEM((64, D), BF16),
            pltpu.VMEM((rows, LANE), F32),
            pltpu.VMEM((rows, LANE), F32),
            pltpu.VMEM((rows, D), F32),
            pltpu.VMEM((rows, D), F32),
            pltpu.VMEM((8, D), F32),
            pltpu.VMEM((nd, 48, D), BF16),
            pltpu.VMEM((cols, token_total), BF16),
            pltpu.VMEM((nd, cols, LANE), BF16),
            pltpu.VMEM((cols, fac_lanes), BF16),
            pltpu.VMEM((nd, 16, D), BF16),
            pltpu.VMEM((48, D), BF16),
            pltpu.VMEM((rows, nd * LANE), BF16),
            pltpu.VMEM((rows, D), F32),
            pltpu.VMEM((nd, 2, cols, LANE), BF16),
            pltpu.VMEM((2, D, LANE), BF16),
            pltpu.VMEM((cols, nd * 32), BF16),
            pltpu.VMEM((cols, nd * 32), BF16),
            pltpu.VMEM((nd * 32, D), BF16),
            pltpu.VMEM((nd * 32, D), BF16),
            pltpu.VMEM((table_total // HASH * cols, chunk), BF16),
            pltpu.VMEM((table_total // HASH * cols, HASH), F32),
            pltpu.VMEM((8, LANE), F32),
            pltpu.VMEM((nd, 8, LANE), F32),
            pltpu.SemaphoreType.DMA((flows,)),
            pltpu.SemaphoreType.DMA((flows,)),
            pltpu.SemaphoreType.DMA((flows,)),
        ],
        compiler_params=pltpu.CompilerParams(
            collective_id=3, has_side_effects=True, vmem_limit_bytes=62 * 1024 * 1024
        ),
        name="middle",
    )(*arrays)


def stack_table(rows, blocks, table, stacked):
    last = (V - (blocks - 1) * HASH + LANE - 1) // LANE * LANE

    def piece(b):
        if b >= blocks:
            return []
        if b == blocks - 1:
            part = table[:, b * HASH : b * HASH + last].astype(F32)
            return [jnp.concatenate([part, jnp.zeros((rows, HASH - last), F32)], axis=1)]
        return [table[:, b * HASH : (b + 1) * HASH].astype(F32)]

    for b in range(0, blocks, 2):
        both = jnp.concatenate(piece(b) + piece(b + 1), axis=0)
        stacked[b * rows : b * rows + both.shape[0], :] = both.astype(BF16)


def pick_tokens(rows, blocks, stacked, ids):
    low = ids & (HASH - 1)
    high = ids >> (HASH.bit_length() - 1)
    width = ids.shape[1]
    hot = as_bf16(iota((HASH, width), 0) == low)
    picked = jnp.dot(stacked[...], hot, preferred_element_type=F32)
    value = jnp.zeros((rows, width), F32)
    for b in range(blocks):
        value = jnp.where(high == b, picked[b * rows : (b + 1) * rows], value)
    return value.astype(BF16)


def first_body(
    n_valid, nq, nd, narrow, cols, home_at, blocks, forward_from,
    ids_mine, small_mine, table, win, wout, pos_mine,
    ids_got, small_got, mine, mine_q, wall, w0,
    stacked, tokens, tokens_q, p0,
    send_sem, recv_sem, own_sem, wide_send, wide_recv, x_send, x_recv, c_send, c_recv,
):
    cap = -(-n_valid // nd)
    wide = nd // narrow
    tq = nq * LQ
    n_own = ids_mine.shape[0] - 1
    net = Net(nd, narrow, send_sem, recv_sem, own_sem)
    me = net.me
    w_at, n_at = lax.axis_index("wide"), lax.axis_index("narrow")
    x_at, c_at = n_at ^ 2, n_at ^ 1
    everyone = (0, nd)
    home = (home_at, home_at + 1)

    wall[w_at, n_at] = jnp.concatenate([win[1], wout[1], pos_mine[...]], axis=1).astype(BF16)
    p0[...] = jnp.concatenate([win[0], wout[0]], axis=1).astype(BF16)

    net.barrier()
    small = [
        Flow(
            lambda s, t: ids_mine, lambda s, t: ids_got.at[s],
            lambda n: ids_got.at[pl.ds(0, n)], everyone, everyone,
        ),
        Flow(
            lambda s, t: small_mine, lambda s, t: small_got.at[s],
            lambda n: small_got.at[pl.ds(0, n)], everyone, everyone,
        ),
    ]
    small_base = net.start(small)

    def wide_copy(k, carry):
        t = lax.rem(w_at + k, wide)
        pltpu.make_async_remote_copy(
            src_ref=wall.at[w_at, n_at], dst_ref=wall.at[w_at, n_at],
            send_sem=wide_send, recv_sem=wide_recv.at[w_at],
            device_id=(t, n_at), device_id_type=MESH,
        ).start()
        return carry

    lax.fori_loop(1, wide, wide_copy, 0)

    def to_x(row):
        return pltpu.make_async_remote_copy(
            src_ref=wall.at[row, n_at], dst_ref=wall.at[row, n_at],
            send_sem=x_send, recv_sem=x_recv.at[row],
            device_id=(w_at, x_at), device_id_type=MESH,
        )

    def to_core(row, col, which):
        return pltpu.make_async_remote_copy(
            src_ref=wall.at[row, col], dst_ref=wall.at[row, col],
            send_sem=c_send, recv_sem=c_recv.at[which, row],
            device_id=(w_at, c_at), device_id_type=MESH,
        )

    def forward(k):
        row = lax.rem(w_at - k + wide, wide)

        @pl.when(k > 0)
        def _():
            pltpu.make_async_copy(
                wall.at[row, n_at], wall.at[row, n_at], wide_recv.at[row]
            ).wait()

        to_x(row).start()
        to_core(row, n_at, 0).start()

    stack_table(cols, blocks, table, stacked)
    net.finish(small, small_base)

    pairs = n_valid // n_own
    moves = [
        Flow(
            lambda s, t, c=c: tokens.at[(c * nd + t) // n_own, lax.rem(c * nd + t, n_own)],
            lambda s, t, c=c: mine.at[s, :, pl.ds(c * LP, LP)],
            lambda n: mine.at[pl.ds(0, n), :, pl.ds(0, LP)],
            everyone, (0, min(nd, n_valid - c * nd)),
        )
        for c in range(cap)
    ]
    base = net.used
    net.used += cap

    def send_pair(at):
        for j in range(n_own):
            slot = at * n_own + j
            c = slot // nd
            t = lax.rem(slot, nd)
            dst = mine.at[me, :, pl.ds(pl.multiple_of(c * LP, LANE), LP)]

            @pl.when(t != me)
            def _():
                pltpu.make_async_remote_copy(
                    src_ref=tokens.at[at, j], dst_ref=dst,
                    send_sem=send_sem.at[base + c], recv_sem=recv_sem.at[base + c],
                    device_id=net.where(t), device_id_type=MESH,
                ).start()

            @pl.when(t == me)
            def _():
                pltpu.make_async_copy(tokens.at[at, j], dst, own_sem.at[base + c]).start()

    def gather(i, carry):
        at = lax.rem(i + me, pairs)
        ids = jnp.concatenate([ids_got[at, j : j + 1, 0:LP] for j in range(n_own)], axis=1)
        rows = pick_tokens(cols, blocks, stacked, ids)
        for j in range(n_own):
            tokens[at, j] = rows[:, j * LP : (j + 1) * LP]

        @pl.when(i > 0)
        def _():
            send_pair(lax.rem(i - 1 + me, pairs))

        @pl.when(jnp.logical_and(i >= forward_from, i < forward_from + wide))
        def _():
            forward(i - forward_from)

        return carry

    q_ids = jnp.zeros((1, tq), jnp.int32)
    for d in range(0, nd, narrow):
        q_ids = q_ids + ids_got[d, n_own : n_own + 1, 0:tq]
    tokens_q[...] = pick_tokens(cols, blocks, stacked, q_ids)
    q_moves = [
        Flow(
            lambda s, t: tokens_q, lambda s, t: mine_q.at[s],
            lambda n: mine_q.at[pl.ds(0, n)], everyone, home,
        ),
    ]
    home_moves = [
        Flow(
            lambda s, t: p0, lambda s, t: w0.at[s],
            lambda n: w0.at[pl.ds(0, n)], everyone, home,
        ),
    ]
    q_base = net.start(q_moves)
    home_base = net.start(home_moves)
    lax.fori_loop(0, pairs, gather, 0)
    send_pair(lax.rem(pairs - 1 + me, pairs))
    for k in range(wide):
        if forward_from + k >= pairs:
            forward(k)

    def second(k, carry):
        row = lax.rem(w_at - k + wide, wide)
        pltpu.make_async_copy(wall.at[row, x_at], wall.at[row, x_at], x_recv.at[row]).wait()
        to_core(row, x_at, 1).start()
        return carry

    lax.fori_loop(0, wide, second, 0)
    net.finish(moves, base)
    net.finish(q_moves, q_base)
    net.finish(home_moves, home_base)

    def last(row, carry):
        for which, col in ((0, c_at), (1, c_at ^ 2)):
            pltpu.make_async_copy(
                wall.at[row, col], wall.at[row, col], c_recv.at[which, row]
            ).wait()
        return carry

    lax.fori_loop(0, wide, last, 0)
    many = wall.at[pl.ds(0, wide - 1), 0]
    pltpu.make_async_copy(many, many, wide_send).wait()
    many = wall.at[:, 0]
    pltpu.make_async_copy(many, many, x_send).wait()
    many = wall.at[:, pl.ds(0, 2)]
    pltpu.make_async_copy(many, many, c_send).wait()


def first(n_valid, nq, nd, narrow, cols, home_at, arrays, forward_from):
    cap = -(-n_valid // nd)
    wide = nd // narrow
    tq = nq * LQ
    ids_mine, small_mine = arrays[0], arrays[1]
    n_own = ids_mine.shape[0] - 1
    blocks = -(-V // HASH)
    vmem = pl.BlockSpec(memory_space=pltpu.VMEM)
    flows = 4 + cap

    def like(*shape, dtype=BF16):
        return jax.ShapeDtypeStruct(shape, dtype)

    dma = pltpu.SemaphoreType.DMA
    return pl.pallas_call(
        functools.partial(
            first_body, n_valid, nq, nd, narrow, cols, home_at, blocks, forward_from
        ),
        out_shape=[
            like(nd, *ids_mine.shape, dtype=jnp.int32),
            like(nd, *small_mine.shape),
            like(nd, cols, cap * LP),
            like(nd, cols, tq),
            like(wide, narrow, cols, 4 * D + LP),
            like(nd, cols, 4 * D),
        ],
        in_specs=[vmem] * len(arrays),
        out_specs=[vmem] * 6,
        scratch_shapes=[
            pltpu.VMEM((blocks * cols, HASH), BF16),
            pltpu.VMEM((n_valid // n_own, n_own, cols, LP), BF16),
            pltpu.VMEM((cols, tq), BF16),
            pltpu.VMEM((cols, 4 * D), BF16),
            dma((flows,)), dma((flows,)), dma((flows,)),
            dma(()), dma((wide,)), dma(()), dma((wide,)), dma(()), dma((2, wide)),
        ],
        compiler_params=pltpu.CompilerParams(
            collective_id=2, has_side_effects=True, vmem_limit_bytes=62 * 1024 * 1024
        ),
        name="first",
    )(*arrays)


def on_device_rows(
    passage_ids, query_ids, passage_query, kept_mask, neg_count, step_count,
    embed_table, attend_in, attend_out, expand_weight, shrink_weight, norm_gains, bias_terms,
    embed_first, embed_second, attend_in_first, attend_in_second,
    attend_out_first, attend_out_second, expand_first, expand_second,
    shrink_first, shrink_second, gains_first, gains_second, bias_first, bias_second,
):
    narrow = lax.axis_size("narrow")
    nd = lax.axis_size("wide") * narrow
    me = lax.axis_index("wide") * narrow + lax.axis_index("narrow")
    cols = embed_table.shape[1]
    n_slots = passage_query.shape[0]
    nq = query_ids.shape[0] * lax.axis_size("wide")
    n_valid = VALID_PER_QUERY * nq
    cap = -(-n_valid // nd)
    rows_p = cap * nd
    ff_cols = FF // nd

    exch = functools.partial(comm, nd=nd, narrow=narrow)
    rows_c = -(-cols // 8) * 8
    n_ids = passage_ids.shape[0] + query_ids.shape[0]
    small_width = max(cols, bias_terms.shape[1], 1)
    small_width = -(-small_width // LANE) * LANE

    def widen(value, width):
        return jnp.pad(value, ((0, 0), (0, width - value.shape[1])))

    ids_mine = jnp.concatenate([passage_ids, widen(query_ids, LP)])
    small_mine = jnp.concatenate(
        [widen(norm_gains.reshape(6, cols), small_width), widen(bias_terms, small_width)]
    ).astype(BF16)
    ids_got, small_got = exch(
        1,
        [ids_mine, small_mine],
        [((nd, n_ids, LP), jnp.int32), ((nd, 8, small_width), BF16)],
        [send_all(0, 0, nd), send_all(1, 1, nd)],
    )
    n_own = passage_ids.shape[0]
    pid = ids_got[:, :n_own].reshape(n_slots, LP)[:n_valid]
    qid = ids_got.reshape(-1, narrow, n_ids, LP)[:, 0, n_own:, :LANE].reshape(nq, LANE)
    all_ids = jnp.concatenate([pid.reshape(-1), qid.reshape(-1)])
    gains = small_got[:, :6, :cols].transpose(1, 0, 2).reshape(2, 3, D).astype(F32)
    bias = small_got[:, 6:, : bias_terms.shape[1]].transpose(1, 0, 2).reshape(2, -1).astype(F32)

    table_t = embed_table.T
    table_low = table_t.astype(BF16)
    vocab = V + LP
    total = -(-vocab // HASH) * HASH
    table_pad = jnp.pad(table_low, ((0, rows_c - cols), (0, total - vocab)))
    got = table_rows(table_pad, all_ids)
    pos_mine = table_pad[:, V : V + LP]
    up_mine = expand_weight.astype(BF16).reshape(2 * cols, nd, ff_cols).transpose(1, 0, 2)
    q_from = n_valid * LP
    width = cap * LP + LANE

    def passage_move(c, forward):
        span = (0, min(nd, n_valid - c * nd))
        if forward:
            return Send(
                0, 0,
                lambda ref, s, t: ref.at[:, pl.ds(pl.multiple_of((c * nd + t) * LP, LANE), LP)],
                lambda ref, s, t: ref.at[s, :, pl.ds(c * LP, LP)],
                lambda ref, n: ref.at[:, pl.ds(0, n * LP)],
                lambda ref, n: ref.at[pl.ds(0, n), :, pl.ds(0, LP)],
                (0, nd), span,
            )
        return Send(
            0, 0,
            lambda ref, s, t: ref.at[t, :, pl.ds(c * LP, LP)],
            lambda ref, s, t: ref.at[:, pl.ds(pl.multiple_of((c * nd + s) * LP, LANE), LP)],
            lambda ref, n: ref.at[pl.ds(0, n), :, pl.ds(0, LP)],
            lambda ref, n: ref.at[:, pl.ds(0, n * LP)],
            span, (0, nd),
        )

    def query_move(forward):
        span = (nd - nq, nd)
        if forward:
            return Send(
                0, 0,
                lambda ref, s, t: ref.at[
                    :, pl.ds(pl.multiple_of(q_from + (t - (nd - nq)) * LANE, LANE), LANE)
                ],
                lambda ref, s, t: ref.at[s, :, pl.ds(cap * LP, LANE)],
                lambda ref, n: ref.at[:, pl.ds(0, n * LANE)],
                lambda ref, n: ref.at[pl.ds(0, n), :, pl.ds(0, LANE)],
                (0, nd), span,
            )
        return Send(
            0, 0,
            lambda ref, s, t: ref.at[t, :, pl.ds(cap * LP, LANE)],
            lambda ref, s, t: ref.at[
                :, pl.ds(pl.multiple_of(q_from + (s - (nd - nq)) * LANE, LANE), LANE)
            ],
            lambda ref, n: ref.at[pl.ds(0, n), :, pl.ds(0, LANE)],
            lambda ref, n: ref.at[:, pl.ds(0, n * LANE)],
            span, (0, nd),
        )

    mine, pos, w_up = exch(
        2,
        [got, pos_mine, up_mine],
        [((nd, rows_c, width), BF16), ((nd, rows_c, LP), BF16), ((nd, 2 * cols, ff_cols), BF16)],
        [passage_move(c, True) for c in range(cap)]
        + [query_move(True), send_all(1, 1, nd), send_blocks(2, 2, nd)],
    )
    live = jnp.concatenate(
        [jnp.broadcast_to(c * nd + me < n_valid, (LP,)) for c in range(cap)]
        + [jnp.broadcast_to(me >= nd - nq, (LANE,))]
    )
    mine = jnp.where(live, mine[:, :cols].reshape(D, width), 0)
    pos = pos[:, :cols].reshape(D, LP).astype(F32)
    w_up = w_up.reshape(nd, 2, cols, ff_cols).transpose(1, 0, 2, 3).reshape(2, D, ff_cols)
    w_down = shrink_weight.astype(BF16)
    w_in = lax.all_gather(attend_in.astype(BF16), AXES, axis=1, tiled=True)
    w_out = lax.all_gather(attend_out.astype(BF16), AXES, axis=1, tiled=True)

    fronts = []
    for c in range(cap):
        emb = mine[:, c * LP : (c + 1) * LP].astype(F32) + pos
        fronts.append(encode_front(emb, w_in[1], w_out[1], gains[1], bias[1], LP))
    emb = mine[:, cap * LP :].astype(F32) + pos[:, :LANE]
    fronts.append(encode_front(emb, w_in[0], w_out[0], gains[0], bias[0], LQ))
    (rows,) = exch(
        3, [jnp.stack([f[0] for f in fronts])], [((nd, cap + 1, D), F32)], [send_all(0, 0, nd)]
    )
    row_in = (rows[nd - nq :, cap], rows[:, :cap].transpose(1, 0, 2).reshape(rows_p, D))

    def by_owner(queries, passages):
        q_part = jnp.pad(queries, ((nd - nq, 0), (0, 0)))[:, None]
        return jnp.concatenate([passages.reshape(cap, nd, D).transpose(1, 0, 2), q_part], axis=1)

    def to_rows(blocks):
        return (
            blocks[nd - nq :, cap],
            blocks[:, :cap].transpose(1, 0, 2).reshape(rows_p, D),
        )


    mids, ups = [], []
    partial_y = []
    b_in_all = bias[:, O_IN : O_IN + FF].reshape(2, nd, ff_cols)
    b_in = lax.dynamic_index_in_dim(b_in_all, me, 1, False)
    for e in range(2):
        h, hat1, scale1 = norm_rows(row_in[e], gains[e, 1], bias[e, O_1 : O_1 + D])
        h_low = h.astype(BF16)
        upper = dot(h_low, w_up[e], ((1,), (0,))) + b_in[e]
        active, slope = gelu_both(upper)
        f_low = active.astype(BF16)
        partial_y.append(dot(f_low, w_down[e], ((1,), (0,))))
        mids.append((h, hat1, scale1, h_low))
        ups.append((f_low, slope))
    (y_parts,) = exch(
        4, [by_owner(*partial_y)], [((nd, cap + 1, D), F32)], [send_blocks(0, 0, nd)]
    )
    (y_all,) = exch(
        5, [jnp.sum(y_parts, axis=0)], [((nd, cap + 1, D), F32)], [send_all(0, 0, nd)]
    )
    y = to_rows(y_all)
    tops = []
    vecs = []
    for e in range(2):
        z, hat2, scale2 = norm_rows(
            mids[e][0] + y[e] + bias[e, O_OUT : O_OUT + D], gains[e, 2], bias[e, O_2 : O_2 + D]
        )
        tops.append((hat2, scale2))
        vecs.append(z.astype(BF16))
    qvec, pvec = vecs

    owner = passage_query[:rows_p]
    kept = kept_mask[:rows_p] == 1
    earlier = jnp.concatenate([jnp.full((1,), -1, jnp.int32), owner[:-1]])
    valid = owner >= 0
    first = valid & (owner != earlier)
    member = owner[None, :] == jnp.arange(nq, dtype=jnp.int32)[:, None]
    positive = member & first[None, :]
    negative = member & jnp.logical_not(first)[None, :] & kept[None, :]
    counts = jnp.sum(member.astype(F32), axis=1) - 1.0
    score_scale = 2.0 * D ** (-0.5)
    scores = dot(qvec, pvec, ((1,), (1,))) * score_scale
    masked = jnp.where(valid[None, :], scores, -1e30)
    peak = jnp.max(masked, axis=1)
    summed = jnp.sum(jnp.where(valid[None, :], jnp.exp(masked - peak[:, None]), 0.0), axis=1)
    logsum = peak + jnp.log(summed)
    pos_score = jnp.sum(jnp.where(positive, scores, 0.0), axis=1)
    margins = MARGIN - pos_score[:, None] + scores
    active_neg = negative & (margins > 0)
    hinge = jnp.sum(jnp.where(active_neg, margins, 0.0), axis=1) / counts
    active_total = jnp.sum(active_neg.astype(F32), axis=1)
    loss = jnp.sum(logsum - pos_score + hinge)
    score_grad = (
        jnp.where(valid[None, :], jnp.exp(scores - logsum[:, None]), 0.0)
        - positive.astype(F32) * (1.0 + active_total / counts)[:, None]
        + active_neg.astype(F32) / counts[:, None]
    )
    score_low = score_grad.astype(BF16)
    vec_grads = (
        (dot(score_low, pvec, ((1,), (0,))) * score_scale).astype(BF16).astype(F32),
        (dot(score_low, qvec, ((0,), (0,))) * score_scale).astype(BF16).astype(F32),
    )

    partial_h = []
    gain_grads = [[None] * 3 for _ in range(2)]
    shifts = [dict() for _ in range(2)]
    top_grads, shrink_grads, du_parts = [], [], []
    for e in range(2):
        hat2, scale2 = tops[e]
        gain_grads[e][2] = jnp.sum(vec_grads[e] * hat2, axis=0)
        shifts[e]["2"] = jnp.sum(vec_grads[e], axis=0)
        g_top = norm_rows_back(vec_grads[e], gains[e, 2], hat2, scale2)
        dy = g_top.astype(BF16)
        shifts[e]["out"] = jnp.sum(dy.astype(F32), axis=0)
        f_low, slope = ups[e]
        shrink_grads.append(dot(f_low, dy, ((0,), (0,))))
        df = dot(dy, w_down[e], ((1,), (1,)))
        du = (slope * df).astype(BF16)
        du_parts.append(du)
        partial_h.append(dot(du, w_up[e], ((1,), (1,))))
        top_grads.append(g_top)
    du_mine = jnp.concatenate(du_parts)
    h_parts, du_all = exch(
        6,
        [by_owner(*partial_h), du_mine],
        [((nd, cap + 1, D), F32), ((nd, nq + rows_p, ff_cols), BF16)],
        [send_blocks(0, 0, nd), send_all(1, 1, nd)],
    )
    h_mine = jnp.sum(h_parts, axis=0)
    top_mine = lax.dynamic_index_in_dim(by_owner(*top_grads), me, 0, False)
    rows_mine = lax.dynamic_index_in_dim(rows, me, 0, False)
    is_q = (me >= nd - nq).astype(F32)
    has = jnp.stack([(c * nd + me < n_valid).astype(F32) for c in range(cap)] + [is_q])
    g_h = (top_mine + h_mine) * has[:, None]
    gain_one = jnp.stack([gains[1, 1]] * cap + [gains[0, 1]])
    shift_one = jnp.stack([bias[1, O_1 : O_1 + D]] * cap + [bias[0, O_1 : O_1 + D]])
    _, hat_mine, scale_mine = norm_rows(rows_mine, gain_one, shift_one)
    g_mid = norm_rows_back(g_h, gain_one, hat_mine, scale_mine)
    gain_mid = g_h * hat_mine
    do_mine = g_mid.astype(BF16)
    backs = [
        encode_back(
            fronts[c][1], g_mid[c], w_in[1 if c < cap else 0], w_out[1 if c < cap else 0],
            gains[1 if c < cap else 0],
        )
        for c in range(cap + 1)
    ]

    def both_encoders(pick):
        return jnp.stack([pick(cap), sum(pick(c) for c in range(cap))])

    sums = jnp.concatenate(
        [both_encoders(lambda i, j=j: backs[i][1][j]) for j in (5, 6, 7)]
        + [both_encoders(lambda i: gain_mid[i]), both_encoders(lambda i: g_h[i])]
    )
    line = jnp.concatenate(
        [jnp.stack([b[1][j] for b in backs]) for j in (2, 3, 4)] + [do_mine, sums.astype(BF16)]
    )
    n_line = 4 * (cap + 1) + 10
    factor_t = jnp.concatenate(
        [b[1][0] for b in backs] + [b[1][1] for b in backs]
        + [f[1][2][:, 0][None] for f in fronts] + [f[1][8][None] for f in fronts]
    )
    n_factor = factor_t.shape[0]
    f_pad = -(-n_factor // LANE) * LANE
    factor_cols = jnp.pad(factor_t, ((0, f_pad - n_factor), (0, 0))).T

    def pad_rows(value):
        value = value.reshape(nd, cols, value.shape[1])
        return jnp.pad(value, ((0, 0), (0, rows_c - cols), (0, 0)))

    send = pad_rows(jnp.concatenate([b[0] for b in backs], axis=1).astype(BF16))
    token_grads, factors, lines = exch(
        7,
        [send, pad_rows(factor_cols), line],
        [
            ((rows_c, n_valid * LP + nq * LANE), BF16),
            ((nd, rows_c, f_pad), BF16),
            ((nd, n_line, D), BF16),
        ],
        [passage_move(c, False) for c in range(cap)]
        + [query_move(False), send_blocks(1, 1, nd), send_all(2, 2, nd)],
    )
    table_grad = table_sums(token_grads, all_ids, total)[:cols, :vocab]
    token_grads = token_grads[:cols].astype(F32)
    pos_grad = jnp.sum(token_grads[:, :q_from].reshape(cols, n_valid, LP), axis=1)
    pos_grad = pos_grad.at[:, :LANE].add(
        jnp.sum(token_grads[:, q_from:].reshape(cols, nq, LANE), axis=1)
    )
    table_grad = table_grad.at[:, V:].add(pos_grad)

    step_h = (cap + 1) * H
    factors = factors[:, :cols].transpose(0, 2, 1)
    t_all = factors[:, :step_h].reshape(nd, cap + 1, H, cols)
    w_all = factors[:, step_h : 2 * step_h].reshape(nd, cap + 1, H, cols)
    x_all = factors[:, 2 * step_h : 2 * step_h + cap + 1]
    a_all = factors[:, 2 * step_h + cap + 1 : 2 * step_h + 2 * (cap + 1)]
    q_all, da_all, dq_all, do_all = (
        lines[:, j * (cap + 1) : (j + 1) * (cap + 1)] for j in range(4)
    )
    sums = jnp.sum(lines[:, 4 * (cap + 1) :].astype(F32), axis=0).reshape(5, 2, D)

    def of_encoder(value, e):
        if e == 0:
            return value[nd - nq :, cap]
        return value[:, :cap].reshape((nd * cap,) + value.shape[2:])

    du_all = du_all.transpose(1, 0, 2).reshape(nq + rows_p, FF)
    in_grads, out_grads, expand_grads = [], [], []
    for e in range(2):
        du_full = du_all[:nq] if e == 0 else du_all[nq:]
        shifts[e]["in"] = jnp.sum(du_full.astype(F32), axis=0)
        h_cols = lax.dynamic_slice_in_dim(mids[e][3], me * cols, cols, 1)
        expand_grads.append(dot(h_cols, du_full, ((0,), (0,))))
        t, w, x, a = (of_encoder(u, e) for u in (t_all, w_all, x_all, a_all))
        q, da, dq, do = (of_encoder(u, e) for u in (q_all, da_all, dq_all, do_all))
        rows_e = q.shape[0]
        qh = q.reshape(rows_e, H, HD)
        dah = da.reshape(rows_e, H, HD)
        g_q = dot(x, dq, ((0,), (0,)))
        g_k = jnp.einsum("phi,phd->ihd", t, qh, preferred_element_type=F32).reshape(cols, D)
        g_v = jnp.einsum("phi,phd->ihd", w, dah, preferred_element_type=F32).reshape(cols, D)
        in_grads.append(jnp.concatenate([g_q, g_k, g_v], axis=1))
        out_grads.append(dot(a, do, ((0,), (0,))))
        shifts[e]["q"] = jnp.sum(dq.astype(F32), axis=0)
        shifts[e]["o"] = jnp.sum(do.astype(F32), axis=0)
    gain_grad = jnp.stack(
        [jnp.stack([sums[1, e], sums[3, e], gain_grads[e][2]]) for e in range(2)]
    )
    bias_grad = jnp.stack(
        [
            jnp.concatenate(
                [shifts[e]["q"], sums[0, e], shifts[e]["o"], sums[4, e], shifts[e]["in"],
                 shifts[e]["out"], shifts[e]["2"], sums[2, e]]
            )
            for e in range(2)
        ]
    )
    grads = (
        table_grad.T,
        jnp.stack(in_grads),
        jnp.stack(out_grads),
        jnp.stack(expand_grads),
        jnp.stack(shrink_grads),
        lax.dynamic_slice_in_dim(gain_grad, me * cols, cols, 2),
        lax.dynamic_slice_in_dim(bias_grad, me * bias_terms.shape[1], bias_terms.shape[1], 1),
    )
    local_squares = sum(jnp.sum(g * g) for g in grads)
    (squares,) = exch(
        8, [jnp.broadcast_to(local_squares, (8, LANE))], [((nd, 8, LANE), F32)],
        [send_all(0, 0, nd)],
    )
    grad_norm = jnp.sqrt(jnp.sum(squares[:, 0, 0]))
    factor = CLIP / jnp.maximum(grad_norm, CLIP)
    step = step_count[0].astype(F32)
    masters = (embed_table, attend_in, attend_out, expand_weight, shrink_weight, norm_gains, bias_terms)
    firsts = (embed_first, attend_in_first, attend_out_first, expand_first, shrink_first, gains_first, bias_first)
    seconds = (embed_second, attend_in_second, attend_out_second, expand_second, shrink_second, gains_second, bias_second)
    results = [loss, grad_norm]
    for index in range(7):
        results.extend(
            adam_update(masters[index], grads[index] * factor, firsts[index], seconds[index], step, LEARN_RATES[index])
        )
    return tuple(results)


def on_device(
    passage_ids, query_ids, passage_query, kept_mask, neg_count, step_count,
    embed_table, attend_in, attend_out, expand_weight, shrink_weight, norm_gains, bias_terms,
    embed_first, embed_second, attend_in_first, attend_in_second,
    attend_out_first, attend_out_second, expand_first, expand_second,
    shrink_first, shrink_second, gains_first, gains_second, bias_first, bias_second,
):
    if embed_table.shape[1] % 8 != 0 or lax.axis_size("narrow") != 4 or passage_ids.shape[0] != 2:
        return on_device_rows(
            passage_ids, query_ids, passage_query, kept_mask, neg_count, step_count,
            embed_table, attend_in, attend_out, expand_weight, shrink_weight, norm_gains,
            bias_terms, embed_first, embed_second, attend_in_first, attend_in_second,
            attend_out_first, attend_out_second, expand_first, expand_second,
            shrink_first, shrink_second, gains_first, gains_second, bias_first, bias_second,
        )
    narrow = lax.axis_size("narrow")
    nd = lax.axis_size("wide") * narrow
    me = lax.axis_index("wide") * narrow + lax.axis_index("narrow")
    cols = embed_table.shape[1]
    n_slots = passage_query.shape[0]
    per_wide = query_ids.shape[0]
    nq = per_wide * lax.axis_size("wide")
    n_valid = VALID_PER_QUERY * nq
    cap = -(-n_valid // nd)
    ff_cols = FF // nd
    rows = n_valid + nq
    tq = nq * LQ
    query_home = nd * 5 // 8 - 1
    exch = functools.partial(comm, nd=nd, narrow=narrow)
    small_width = -(-max(cols, bias_terms.shape[1]) // LANE) * LANE
    ids_width = max(LP, -(-tq // LANE) * LANE)

    def widen(value, width):
        return jnp.pad(value, ((0, 0), (0, width - value.shape[1])))

    spot = jnp.arange(tq) // (LQ * per_wide) == lax.axis_index("wide")
    spot = spot & (lax.axis_index("narrow") == 0)
    q_line = jnp.where(spot, jnp.tile(query_ids.reshape(-1), tq // (LQ * per_wide)), 0)
    ids_mine = jnp.concatenate([widen(passage_ids, ids_width), widen(q_line[None], ids_width)])
    small_mine = jnp.concatenate(
        [widen(norm_gains.reshape(6, cols), small_width), widen(bias_terms, small_width)]
    ).astype(BF16)
    n_own = passage_ids.shape[0]
    table_t = embed_table.T
    ids_got, small_got, mine, mine_q, w_one, w_zero = first(
        n_valid, nq, nd, narrow, cols, query_home,
        [ids_mine, small_mine, table_t, attend_in, attend_out, table_t[:, V : V + LP]],
        12,
    )
    w_one = w_one.reshape(D, 4 * D + LP)
    w_zero = w_zero.reshape(D, 4 * D)
    pid = ids_got[:, :n_own, :LP].reshape(n_slots, LP)[:n_valid]
    qid = jnp.sum(ids_got[:, n_own, :tq], axis=0)
    q_from = n_valid * LP
    token_total = -(-(q_from + tq) // 1024) * 1024
    all_ids = jnp.pad(jnp.concatenate([pid.reshape(-1), qid]), (0, token_total - q_from - tq))
    gains = small_got[:, :6, :cols].transpose(1, 0, 2).reshape(2, 3, D).astype(F32)
    bias = small_got[:, 6:, : bias_terms.shape[1]].transpose(1, 0, 2).reshape(2, -1).astype(F32)

    vocab = V + LP
    total = -(-vocab // HASH) * HASH
    up_mine = expand_weight.astype(BF16).reshape(2, cols, nd, ff_cols).transpose(2, 0, 1, 3)
    up_mine = jnp.pad(up_mine, ((0, 0), (0, 0), (0, 0), (0, LANE - ff_cols)))
    w_down = jnp.pad(shrink_weight.astype(BF16), ((0, 0), (0, LANE - ff_cols), (0, 0)))
    cv = jnp.stack(
        [v for e in range(2) for v in (
            gains[e, 0], bias[e, O_EMB : O_EMB + D], bias[e, O_V : O_V + D])]
        + [jnp.zeros((D,), F32)] * 2,
        axis=1,
    )
    rv = jnp.stack(
        [v for e in range(2) for v in (
            bias[e, O_Q : O_Q + D], bias[e, O_O : O_O + D], bias[e, O_1 : O_1 + D],
            bias[e, O_OUT : O_OUT + D], bias[e, O_2 : O_2 + D], gains[e, 1], gains[e, 2],
            jnp.zeros((D,), F32))]
    )
    b_in = lax.dynamic_index_in_dim(
        bias[:, O_IN : O_IN + FF].reshape(2, nd, ff_cols), me, 1, False
    )
    b_in = jnp.pad(b_in, ((0, 6), (0, LANE - ff_cols)))
    earlier = jnp.concatenate([jnp.full((1,), -1, jnp.int32), passage_query[:-1]])
    first_slot = ((passage_query >= 0) & (passage_query != earlier)).astype(jnp.int32)
    slots = jnp.pad(
        jnp.stack([passage_query, first_slot, kept_mask])[:, :n_valid],
        ((0, 5), (0, -(-n_valid // LANE) * LANE - n_valid)),
    )
    shrink_g, loss, g_table, g_in, g_out, g_up, g_bin, g_small, norm = middle(
        n_valid, nq, nd, narrow, cols, query_home, token_total,
        [mine, mine_q, w_one, w_zero, up_mine, w_down, cv, rv, b_in, slots,
         all_ids.reshape(-1, 1, 1024)],
    )
    loss = loss[0, 0]
    grad_norm = norm[0, 0]
    g_small = g_small.reshape(2, 16, D)
    g_bin = g_bin[:2].reshape(2, nd, LANE)[:, :, :ff_cols].reshape(2, FF)
    bias_grad = jnp.concatenate(
        [g_small[:, :4].reshape(2, 4 * D), g_bin, g_small[:, 4:7].reshape(2, 3 * D)], axis=1
    )
    grads = (
        g_table[:, : V + LP].T,
        g_in,
        g_out,
        g_up.reshape(2, cols, nd, LANE)[..., :ff_cols].reshape(2, cols, FF),
        shrink_g[:, :ff_cols],
        lax.dynamic_slice_in_dim(g_small[:, 7:10], me * cols, cols, 2),
        lax.dynamic_slice_in_dim(bias_grad, me * bias_terms.shape[1], bias_terms.shape[1], 1),
    )
    factor = CLIP / jnp.maximum(grad_norm, CLIP)
    step = step_count[0].astype(F32)
    masters = (embed_table, attend_in, attend_out, expand_weight, shrink_weight, norm_gains, bias_terms)
    firsts = (embed_first, attend_in_first, attend_out_first, expand_first, shrink_first, gains_first, bias_first)
    seconds = (embed_second, attend_in_second, attend_out_second, expand_second, shrink_second, gains_second, bias_second)
    results = [loss, grad_norm]
    for index in range(7):
        results.extend(
            adam_update(masters[index], grads[index] * factor, firsts[index], seconds[index], step, LEARN_RATES[index])
        )
    return tuple(results)


def solution(mesh):
    both = ("wide", "narrow")
    weight_specs = (P(None, both),) + (P(None, both, None),) * 4 + (P(None, None, both), P(None, both))
    pairs = tuple(s for spec in weight_specs for s in (spec, spec))
    in_specs = (P(both, None), P("wide", None), P(), P(), P("wide"), P()) + weight_specs + pairs
    out_specs = (P(), P()) + tuple(s for spec in weight_specs for s in (spec, spec, spec))
    return jax.shard_map(on_device, mesh=mesh, in_specs=in_specs, out_specs=out_specs, check_vma=False)
```

```python
import functools

import jax
import jax.numpy as jnp
from jax import lax
from jax.experimental import pallas as pl
from jax.experimental.pallas import tpu as pltpu
from jax.sharding import PartitionSpec as P

D = 768
H = 12
HD = 64
FF = 3072
V = 18000
LP = 384
LQ = 32
LANE = 128
VALID_PER_QUERY = 5

MARGIN = 1.0
CLIP = 1.0
BETA_ONE = 0.9
BETA_TWO = 0.999
LEARN_RATES = (1.0, 0.02, 0.08, 0.02, 0.02, 1.0, 0.1)
WEIGHT_DECAY = 0.01
ADAM_EPS = 1e-08
NORM_EPS = 1e-05
AXES = ("wide", "narrow")
F32 = jnp.float32
BF16 = jnp.bfloat16
O_Q, O_V, O_O, O_1, O_IN, O_OUT, O_2, O_EMB = (
    0, D, 2 * D, 3 * D, 4 * D, 4 * D + FF, 5 * D + FF, 6 * D + FF
)


def dot(left, right, dims):
    return lax.dot_general(left, right, (dims, ((), ())), preferred_element_type=F32)


def norm_rows(values, gain, shift):
    center = values - jnp.mean(values, axis=-1, keepdims=True)
    spread = jnp.mean(center * center, axis=-1, keepdims=True)
    scale = lax.rsqrt(spread + NORM_EPS)
    hat = center * scale
    return hat * gain + shift, hat, scale


def norm_rows_back(grad, gain, hat, scale):
    scaled = grad * gain
    mean_one = jnp.mean(scaled, axis=-1, keepdims=True)
    mean_two = jnp.mean(scaled * hat, axis=-1, keepdims=True)
    return scale * (scaled - mean_one - hat * mean_two)


def gelu_both(upper):
    cdf = 0.5 * (1.0 + lax.erf(upper * 0.7071067811865476))
    pdf = jnp.exp(-0.5 * upper * upper) * 0.3989422804014327
    return upper * cdf, cdf + upper * pdf


def adam_update(weight, grad, first, second, step, rate):
    first_new = BETA_ONE * first + (1.0 - BETA_ONE) * grad
    second_new = BETA_TWO * second + (1.0 - BETA_TWO) * grad * grad
    first_hat = first_new / (1.0 - BETA_ONE**step)
    second_hat = second_new / (1.0 - BETA_TWO**step)
    weight_new = weight - rate * (
        first_hat / (jnp.sqrt(second_hat) + ADAM_EPS) + WEIGHT_DECAY * weight
    )
    return (weight_new, first_new, second_new)


MESH = pl.DeviceIdType.MESH
HASH = 512
FORWARD_PLAN = (0, 4, 7, 10, 12, 13, 14, 15) + (99,) * 8


class Send:
    def __init__(self, src, dst, take, put, many_src, many_dst, sources, targets):
        self.src, self.dst, self.take, self.put = src, dst, take, put
        self.many_src, self.many_dst = many_src, many_dst
        self.sources, self.targets = sources, targets


def inside(index, span):
    return jnp.logical_and(index >= span[0], index < span[1])


def comm_body(sends, n_in, n_out, nd, narrow, *refs):
    ins, outs = refs[:n_in], refs[n_in : n_in + n_out]
    send_sem, recv_sem, own_sem = refs[n_in + n_out :]
    me = lax.axis_index("wide") * narrow + lax.axis_index("narrow")
    barrier = pltpu.get_barrier_semaphore()

    def greet(k, carry):
        t = lax.rem(me + k, nd)
        pl.semaphore_signal(
            barrier, inc=1, device_id=(t // narrow, lax.rem(t, narrow)), device_id_type=MESH
        )
        return carry

    lax.fori_loop(1, nd, greet, 0)
    pl.semaphore_wait(barrier, nd - 1)

    def push(k, carry):
        t = lax.rem(me + k, nd)
        for i, s in enumerate(sends):

            @pl.when(jnp.logical_and(inside(me, s.sources), inside(t, s.targets)))
            def _():
                pltpu.make_async_remote_copy(
                    src_ref=s.take(ins[s.src], me, t),
                    dst_ref=s.put(outs[s.dst], me, t),
                    send_sem=send_sem.at[i],
                    recv_sem=recv_sem.at[i],
                    device_id=(t // narrow, lax.rem(t, narrow)),
                    device_id_type=MESH,
                ).start()

        return carry

    lax.fori_loop(1, nd, push, 0)
    for i, s in enumerate(sends):
        both = jnp.logical_and(inside(me, s.sources), inside(me, s.targets))

        @pl.when(both)
        def _():
            own = pltpu.make_async_copy(
                s.take(ins[s.src], me, me), s.put(outs[s.dst], me, me), own_sem.at[i]
            )
            own.start()
            own.wait()

    for i, s in enumerate(sends):
        n_t = s.targets[1] - s.targets[0]
        n_s = s.sources[1] - s.sources[0]
        is_s, is_t = inside(me, s.sources), inside(me, s.targets)
        for own in (0, 1):
            mine = is_t if own else jnp.logical_not(is_t)
            if n_t - own > 0:

                @pl.when(jnp.logical_and(is_s, mine))
                def _():
                    view = s.many_src(ins[s.src], n_t - own) if s.many_src(ins[s.src], 1) is not None else outs[s.dst].at[pl.ds(0, n_t - own)]
                    pltpu.make_async_copy(view, view, send_sem.at[i]).wait()

            mine = is_s if own else jnp.logical_not(is_s)
            if n_s - own > 0:

                @pl.when(jnp.logical_and(is_t, mine))
                def _():
                    view = s.many_dst(outs[s.dst], n_s - own)
                    pltpu.make_async_copy(view, view, recv_sem.at[i]).wait()


def comm(collective, arrays, out_shapes, sends, nd, narrow):
    vmem = pl.BlockSpec(memory_space=pltpu.VMEM)
    n = len(sends)
    return pl.pallas_call(
        functools.partial(comm_body, sends, len(arrays), len(out_shapes), nd, narrow),
        out_shape=[jax.ShapeDtypeStruct(s, d) for s, d in out_shapes],
        in_specs=[vmem] * len(arrays),
        out_specs=[vmem] * len(out_shapes),
        scratch_shapes=[
            pltpu.SemaphoreType.DMA((n,)),
            pltpu.SemaphoreType.DMA((n,)),
            pltpu.SemaphoreType.DMA((n,)),
        ],
        compiler_params=pltpu.CompilerParams(collective_id=collective, has_side_effects=True),
    )(*arrays)


def send_all(src, dst, nd):
    return Send(
        src, dst,
        lambda ref, s, t: ref,
        lambda ref, s, t: ref.at[s],
        lambda ref, n: None, lambda ref, n: ref.at[pl.ds(0, n)],
        (0, nd), (0, nd),
    )


def send_blocks(src, dst, nd):
    return Send(
        src, dst,
        lambda ref, s, t: ref.at[t],
        lambda ref, s, t: ref.at[s],
        lambda ref, n: ref.at[pl.ds(0, n)], lambda ref, n: ref.at[pl.ds(0, n)],
        (0, nd), (0, nd),
    )


def stack_pairs(pieces, store):
    rows = pieces[0].shape[0]
    for i in range(0, len(pieces), 2):
        store(i * rows, jnp.concatenate(pieces[i : i + 2], axis=0))


def gather_body(rows, blocks, table_ref, ids_ref, out_ref, stacked):
    @pl.when(pl.program_id(0) == 0)
    def _():
        pieces = [
            table_ref[:, b * HASH : (b + 1) * HASH].astype(F32) for b in range(blocks)
        ]

        def store(row, value):
            stacked[row : row + value.shape[0], :] = value.astype(BF16)

        stack_pairs(pieces, store)

    ids = ids_ref[0]
    low = ids & (HASH - 1)
    high = ids >> (HASH.bit_length() - 1)
    width = ids.shape[1]
    hot = (lax.broadcasted_iota(jnp.int32, (HASH, width), 0) == low).astype(F32).astype(BF16)
    picked = jnp.dot(stacked[...], hot, preferred_element_type=F32)
    value = jnp.zeros((rows, width), F32)
    for b in range(blocks):
        value = jnp.where(high == b, picked[b * rows : (b + 1) * rows], value)
    out_ref[...] = value.astype(BF16)


def table_rows(table, ids):
    rows, total = table.shape
    tokens = ids.shape[0]
    tile = 512
    blocks = total // HASH
    return pl.pallas_call(
        functools.partial(gather_body, rows, blocks),
        grid=(tokens // tile,),
        out_shape=jax.ShapeDtypeStruct((rows, tokens), BF16),
        in_specs=[
            pl.BlockSpec((rows, total), lambda i: (0, 0)),
            pl.BlockSpec((1, 1, tile), lambda i: (i, 0, 0)),
        ],
        out_specs=pl.BlockSpec((rows, tile), lambda i: (0, i)),
        scratch_shapes=[pltpu.VMEM((blocks * rows, HASH), BF16)],
        name="table_rows",
    )(table, ids.reshape(tokens // tile, 1, tile))


def scatter_body(rows, blocks, values_ref, ids_ref, out_ref, spread, acc):
    step = pl.program_id(0)
    ids = ids_ref[0]
    low = ids & (HASH - 1)
    high = ids >> (HASH.bit_length() - 1)
    width = ids.shape[1]
    values = values_ref[...].astype(F32)
    pieces = [jnp.where(high == b, values, 0.0) for b in range(blocks)]

    def store(row, value):
        spread[row : row + value.shape[0], :] = value.astype(BF16)

    stack_pairs(pieces, store)
    hot = (lax.broadcasted_iota(jnp.int32, (HASH, width), 0) == low).astype(F32).astype(BF16)
    part = lax.dot_general(
        spread[...], hot, (((1,), (1,)), ((), ())), preferred_element_type=F32
    )

    @pl.when(step == 0)
    def _():
        acc[...] = part

    @pl.when(step > 0)
    def _():
        acc[...] += part

    @pl.when(step == pl.num_programs(0) - 1)
    def _():
        for b in range(blocks):
            out_ref[:, b * HASH : (b + 1) * HASH] = acc[b * rows : (b + 1) * rows, :]


def table_sums(values, ids, total):
    rows, tokens = values.shape
    tile = 1024
    blocks = total // HASH
    return pl.pallas_call(
        functools.partial(scatter_body, rows, blocks),
        grid=(tokens // tile,),
        out_shape=jax.ShapeDtypeStruct((rows, total), F32),
        in_specs=[
            pl.BlockSpec((rows, tile), lambda i: (0, i)),
            pl.BlockSpec((1, 1, tile), lambda i: (i, 0, 0)),
        ],
        out_specs=pl.BlockSpec((rows, total), lambda i: (0, 0)),
        scratch_shapes=[
            pltpu.VMEM((blocks * rows, tile), BF16),
            pltpu.VMEM((blocks * rows, HASH), F32),
        ],
        name="table_sums",
    )(values, ids.reshape(tokens // tile, 1, tile))


def head_mask(dtype):
    rows = lax.broadcasted_iota(jnp.int32, (H, D), 0)
    cols = lax.broadcasted_iota(jnp.int32, (H, D), 1)
    return (cols // HD == rows).astype(dtype)


def spread_heads(row):
    return row[None, :] * head_mask(row.dtype)


def encode_front(emb_t, w_in, w_out, gain, bias, length):
    width = emb_t.shape[1]
    center = emb_t - jnp.mean(emb_t, axis=0, keepdims=True)
    spread = jnp.mean(center * center, axis=0, keepdims=True)
    scale = lax.rsqrt(spread + NORM_EPS)
    hat = center * scale
    x0 = hat * gain[0][:, None] + bias[O_EMB : O_EMB + D][:, None]
    x_low = x0.astype(BF16)
    first_low = x_low[:, 0]
    q = (dot(first_low[None], w_in[:, :D], ((1,), (0,)))[0] + bias[O_Q : O_Q + D]).astype(BF16)
    k = dot(w_in[:, D : 2 * D], x_low, ((0,), (0,))).astype(BF16)
    v = (
        dot(w_in[:, 2 * D :], x_low, ((0,), (0,))) + bias[O_V : O_V + D][:, None]
    ).astype(BF16)
    q_heads = spread_heads(q)
    s = dot(q_heads, k, ((1,), (0,))) * 0.125
    if length < width:
        live = lax.broadcasted_iota(jnp.int32, (1, width), 1) < length
        s = jnp.where(live, s, -1e30)
    peak = jnp.max(s, axis=1, keepdims=True)
    e = jnp.exp(s - peak)
    p = e / jnp.sum(e, axis=1, keepdims=True)
    p_low = p.astype(BF16)
    mixed = dot(p_low, v, ((1,), (1,)))
    a = jnp.sum(mixed * head_mask(F32), axis=0).astype(BF16)
    o = dot(a[None], w_out, ((1,), (0,)))[0] + bias[O_O : O_O + D]
    return x0[:, 0] + o, (hat, scale, x_low, q, k, v, p, p_low, a)


def encode_back(kept, row_grad, w_in, w_out, gain):
    hat, scale, x_low, q, k, v, p, p_low, a = kept
    do = row_grad.astype(BF16)
    da = dot(do[None], w_out, ((1,), (1,)))[0].astype(BF16)
    da_heads = spread_heads(da)
    q_heads = spread_heads(q)
    dp = dot(da_heads, v, ((1,), (0,)))
    ds = (p * (dp - jnp.sum(dp * p, axis=1, keepdims=True))).astype(BF16)
    dq_heads = dot(ds, k, ((1,), (1,)))
    dq = (jnp.sum(dq_heads * head_mask(F32), axis=0) * 0.125).astype(BF16)
    t = dot(ds, x_low, ((1,), (1,))) * 0.125
    w = dot(p_low, x_low, ((1,), (1,)))
    gk = (dot(q_heads, w_in[:, D : 2 * D], ((1,), (1,))) * 0.125).astype(BF16)
    ev = dot(da_heads, w_in[:, 2 * D :], ((1,), (1,))).astype(BF16)
    gx = dot(gk, ds, ((0,), (0,))) + dot(ev, p_low, ((0,), (0,)))
    first = row_grad + dot(dq[None], w_in[:, :D], ((1,), (1,)))[0]
    is_first = lax.broadcasted_iota(jnp.int32, (1, gx.shape[1]), 1) == 0
    gx = gx + jnp.where(is_first, first[:, None], 0.0)
    p_sum = jnp.sum(p_low.astype(F32), axis=1)
    dbv = jnp.repeat(p_sum, HD) * da.astype(F32)
    g_gain = jnp.sum(gx * hat, axis=1)
    g_shift = jnp.sum(gx, axis=1)
    scaled = gx * gain[0][:, None]
    mean_one = jnp.mean(scaled, axis=0, keepdims=True)
    mean_two = jnp.mean(scaled * hat, axis=0, keepdims=True)
    g_emb = scale * (scaled - mean_one - hat * mean_two)
    return g_emb, (t.astype(BF16), w.astype(BF16), q, da, dq, dbv, g_gain, g_shift)


NN = (((1,), (0,)), ((), ()))
NT = (((1,), (1,)), ((), ()))
TN = (((0,), (0,)), ((), ()))
HIGH = lax.Precision.HIGHEST


def mm(left, right, dims, precision=None):
    return lax.dot_general(
        left, right, dims, preferred_element_type=F32, precision=precision
    )


def iota(shape, dim):
    return lax.broadcasted_iota(jnp.int32, shape, dim)


def as_bf16(mask):
    return mask.astype(F32).astype(BF16)


def group(count, nd, first=0):
    return (first, nd // count, count)


def within(index, span):
    first, stride, count = span
    if count == 0:
        return index < 0
    if stride == 1:
        return jnp.logical_and(index >= first, index < first + count)
    return ((index - first) & (stride - 1)) == 0


def place(index, span):
    return (index - span[0]) // span[1]


class Flow:
    def __init__(self, take, put, many, sources, targets):
        self.take, self.put, self.many = take, put, many
        self.sources, self.targets = sources, targets


class Net:
    def __init__(self, nd, narrow, send_sem, recv_sem, own_sem):
        self.nd, self.narrow = nd, narrow
        self.send_sem, self.recv_sem, self.own_sem = send_sem, recv_sem, own_sem
        self.me = lax.axis_index("wide") * narrow + lax.axis_index("narrow")
        self.used = 0

    def where(self, t):
        return (t // self.narrow, lax.rem(t, self.narrow))

    def barrier(self):
        sem = pltpu.get_barrier_semaphore()

        def greet(k, carry):
            t = lax.rem(self.me + k, self.nd)
            pl.semaphore_signal(sem, inc=1, device_id=self.where(t), device_id_type=MESH)
            return carry

        lax.fori_loop(1, self.nd, greet, 0)
        pl.semaphore_wait(sem, self.nd - 1)

    def start(self, flows):
        me, nd = self.me, self.nd
        base = self.used
        self.used += len(flows)

        def push(k, carry):
            t = lax.rem(me + k, nd)
            for i, f in enumerate(flows):

                @pl.when(jnp.logical_and(within(me, f.sources), within(t, f.targets)))
                def _():
                    pltpu.make_async_remote_copy(
                        src_ref=f.take(me, t),
                        dst_ref=f.put(me, t),
                        send_sem=self.send_sem.at[base + i],
                        recv_sem=self.recv_sem.at[base + i],
                        device_id=self.where(t),
                        device_id_type=MESH,
                    ).start()

            return carry

        for i, f in enumerate(flows):

            @pl.when(jnp.logical_and(within(me, f.sources), within(me, f.targets)))
            def _():
                pltpu.make_async_copy(
                    f.take(me, me), f.put(me, me), self.own_sem.at[base + i]
                ).start()

        lax.fori_loop(1, nd, push, 0)
        return base

    def finish(self, flows, base):
        me = self.me
        for i, f in enumerate(flows):
            n_t, n_s = f.targets[2], f.sources[2]
            is_s, is_t = within(me, f.sources), within(me, f.targets)

            @pl.when(jnp.logical_and(is_s, is_t))
            def _():
                pltpu.make_async_copy(
                    f.take(me, me), f.put(me, me), self.own_sem.at[base + i]
                ).wait()

            for own in (0, 1):
                mine = is_s if own else jnp.logical_not(is_s)
                if n_s - own > 0:

                    @pl.when(jnp.logical_and(is_t, mine))
                    def _():
                        view = f.many(n_s - own)
                        pltpu.make_async_copy(view, view, self.recv_sem.at[base + i]).wait()

            for own in (0, 1):
                mine = is_t if own else jnp.logical_not(is_t)
                if n_t - own > 0:

                    @pl.when(jnp.logical_and(is_s, mine))
                    def _():
                        view = f.many(n_t - own)
                        pltpu.make_async_copy(view, view, self.send_sem.at[base + i]).wait()


class Unit:
    def __init__(self, count, length):
        self.count, self.length = count, length
        self.tokens = count * length
        self.bits = count.bit_length() - 1
        self.rows = max(16, H * count)
        self.seqs = max(8, count)

    def pick(self):
        lane = iota((self.seqs, self.tokens), 1)
        seq = iota((self.seqs, self.tokens), 0)
        return lane == seq * self.length

    def spread(self):
        row, seq = iota((self.rows, self.seqs), 0), iota((self.rows, self.seqs), 1)
        return as_bf16((row & (self.count - 1)) == seq)

    def collect(self):
        row, seq = iota((self.seqs, self.rows), 1), iota((self.seqs, self.rows), 0)
        return as_bf16((row & (self.count - 1)) == seq)

    def heads(self):
        row, col = iota((self.rows, D), 0), iota((self.rows, D), 1)
        return ((row >> self.bits) == (col >> 6)).astype(F32)

    def live(self):
        row, lane = iota((self.rows, self.tokens), 0), iota((self.rows, self.tokens), 1)
        return (lane >> 5) == (row & (self.count - 1))


def unit_front(unit, emb, e, w, cv, rv, keep):
    center = emb - jnp.mean(emb, axis=0, keepdims=True)
    spread = jnp.mean(center * center, axis=0, keepdims=True)
    scale = lax.rsqrt(spread + NORM_EPS)
    hat = center * scale
    x0 = hat * cv[:, 3 * e : 3 * e + 1] + cv[:, 3 * e + 1 : 3 * e + 2]
    x_low = x0.astype(BF16)
    pick = unit.pick()
    x_first = mm(as_bf16(pick), x_low, NT).astype(BF16)
    x0_first = mm(pick.astype(F32), x0, NT, HIGH)
    q = (mm(x_first, w[:, 0:D], NN) + rv[8 * e : 8 * e + 1, :]).astype(BF16)
    k = mm(w[:, D : 2 * D], x_low, TN).astype(BF16)
    v = (mm(w[:, 2 * D : 3 * D], x_low, TN) + cv[:, 3 * e + 2 : 3 * e + 3]).astype(BF16)
    heads = unit.heads()
    q_heads = (mm(unit.spread(), q, NN) * heads).astype(BF16)
    s = mm(q_heads, k, NN) * 0.125
    if unit.count > 1:
        s = jnp.where(unit.live(), s, -1e30)
    peak = jnp.max(s, axis=1, keepdims=True)
    ex = jnp.exp(s - peak)
    p = ex / jnp.sum(ex, axis=1, keepdims=True)
    mixed = (mm(p.astype(BF16), v, NT) * heads).astype(BF16)
    a = mm(unit.collect(), mixed, NN).astype(BF16)
    o = mm(a, w[:, 3 * D : 4 * D], NN) + rv[8 * e + 1 : 8 * e + 2, :]
    keep(hat, scale, x_low, x_first, q, k, v, p, a)
    return x0_first + o


def unit_back(unit, row_grad, e, w, cv, kept):
    hat, scale, x_low, x_first, q, k, v, p, a = kept
    heads = unit.heads()
    spread, collect = unit.spread(), unit.collect()
    p_low = p.astype(BF16)
    do = row_grad.astype(BF16)
    da = mm(do, w[:, 3 * D : 4 * D], NT).astype(BF16)
    q_heads = (mm(spread, q, NN) * heads).astype(BF16)
    da_heads = (mm(spread, da, NN) * heads).astype(BF16)
    dp = mm(da_heads, v, NN)
    ds = (p * (dp - jnp.sum(dp * p, axis=1, keepdims=True))).astype(BF16)
    dq_heads = (mm(ds, k, NT) * heads * 0.125).astype(BF16)
    dq = mm(collect, dq_heads, NN).astype(BF16)
    t = mm(ds, x_low, NT) * 0.125
    wx = mm(p_low, x_low, NT)
    gk = (mm(q_heads, w[:, D : 2 * D], NT) * 0.125).astype(BF16)
    ev = mm(da_heads, w[:, 2 * D : 3 * D], NT).astype(BF16)
    first = row_grad + mm(dq, w[:, 0:D], NT)
    gx = mm(gk, ds, TN) + mm(ev, p_low, TN)
    gx = gx + mm(first, unit.pick().astype(F32), TN, HIGH)
    p_sum = jnp.sum(p_low.astype(F32), axis=1, keepdims=True)
    dbv = jnp.sum(p_sum * da_heads.astype(F32), axis=0, keepdims=True)
    g_gain = jnp.sum(gx * hat, axis=1, keepdims=True)
    g_shift = jnp.sum(gx, axis=1, keepdims=True)
    scaled = gx * cv[:, 3 * e : 3 * e + 1]
    mean_one = jnp.mean(scaled, axis=0, keepdims=True)
    mean_two = jnp.mean(scaled * hat, axis=0, keepdims=True)
    g_emb = scale * (scaled - mean_one - hat * mean_two)
    return g_emb, t, wx, da, dq, do, dbv, g_gain, g_shift


def load_rows(ref, count):
    return jnp.concatenate(
        [ref[pl.ds(j, count, stride=8), :] for j in range(D // LANE)], axis=1
    )


def store_rows(ref, value):
    for j in range(D // LANE):
        ref[pl.ds(j, value.shape[0], stride=8), :] = value[:, j * LANE : (j + 1) * LANE]


def middle_body(
    n_valid, nq, nd, narrow, cols, query_home,
    mine, mine_q, w_one, w_zero, up_mine, w_down, cv, rv, b_in, slots, ids, ids_q,
    o_shrink, o_loss, g_table, g_in, g_out, g_up, g_bin, g_small, o_norm,
    hat_s, scale_s, xl_s, xf_s, q_s, k_s, v_s, p_s, a_s,
    hat_q, scale_q, xl_q, xf_q, q_q, k_q, v_q, p_q, a_q,
    r1_own, r1_ownq, r1_all, y_send, y_recv, y_sum, y_all, h_send, h_recv, h_recvq,
    du_own, du_f, gtok, gtok_q, fac, fac_q, line, line_q, f_s, slope_s, hlow_s, g_top_s, sums_s,
    o_tok, o_fac, o_facq, o_line, o_lineq, o_du, o_h, up_got, w_up,
    t_all, w_all, q_exp, d_exp, spread_s, acc_s, norm_own, norm_all,
    tok_send, tok_recv, twin_send, twin_recv, chain_send, chain_recv,
    send_sem, recv_sem, own_sem,
):
    cap = -(-n_valid // nd)
    rows = n_valid + nq
    net = Net(nd, narrow, send_sem, recv_sem, own_sem)
    me = net.me
    everyone = group(nd, nd)
    home = (query_home, 1, 1)
    q_owners = group(nq, nd, 2)
    core = me & 1
    alike = (core, 2, nd // 2)

    def span(c):
        return group(nd, nd) if c == 0 else group(n_valid - nd, nd, 1)

    def slot_of(c, d):
        return c * nd + place(d, span(c))

    net.barrier()
    passage = Unit(1, LP)
    queries = Unit(nq, LQ)
    n_mine = jnp.where(within(me, span(1)), 2, 1)

    up_flows = [
        Flow(
            lambda s, t: up_mine.at[t], lambda s, t: up_got.at[s],
            lambda n: up_got.at[pl.ds(0, n)], everyone, everyone,
        )
    ]
    up_base = net.start(up_flows)

    def front(c, carry):
        at = pl.ds(pl.multiple_of(c * LP, LANE), LP)
        emb = mine[:, :, at].astype(F32).reshape(D, LP) + w_one[:, 4 * D :].astype(F32)

        def keep(hat, scale, x_low, x_first, q, k, v, p, a):
            hat_s[c], scale_s[c], xl_s[c], xf_s[c] = hat, scale, x_low, x_first
            q_s[c], k_s[c], v_s[c], p_s[c], a_s[c] = q, k, v, p, a

        r1 = unit_front(passage, emb, 1, w_one, cv, rv, keep)
        for j in range(D // LANE):
            r1_own[c, j : j + 1, :] = r1[0:1, j * LANE : (j + 1) * LANE]
        return carry

    lax.fori_loop(0, n_mine, front, 0)

    @pl.when(me == query_home)
    def _():
        parts = w_one[:, 4 * D : 4 * D + LANE].astype(F32)[:, 0:LQ]
        emb = mine_q[...].astype(F32).reshape(D, nq * LQ) + jnp.concatenate([parts] * nq, axis=1)

        def keep(hat, scale, x_low, x_first, q, k, v, p, a):
            hat_q[...], scale_q[...], xl_q[...], xf_q[...] = hat, scale, x_low, x_first
            q_q[...], k_q[...], v_q[...], p_q[...], a_q[...] = q, k, v, p, a

        store_rows(r1_ownq, unit_front(queries, emb, 0, w_zero, cv, rv, keep))

    flows = [
        Flow(
            lambda s, t, c=c: r1_own.at[c],
            lambda s, t, c=c: r1_all.at[pl.ds(pl.multiple_of(8 * slot_of(c, s), 8), 8), :],
            lambda n: r1_all.at[pl.ds(0, 8 * n), :],
            span(c), everyone,
        )
        for c in range(cap)
    ] + [
        Flow(
            lambda s, t: r1_ownq,
            lambda s, t: r1_all.at[pl.ds(8 * n_valid, 8 * nq), :],
            lambda n: y_recv_q(n),
            home, everyone,
        )
    ]

    def y_recv_q(n):
        return h_recvq.at[pl.ds(0, n)]

    base = net.start(flows)
    net.finish(flows, base)

    net.finish(up_flows, up_base)
    for e in range(2):
        w_up[e] = up_got[:, e].astype(F32).reshape(D, LANE).astype(BF16)

    part = {1: (0, n_valid), 0: (n_valid, nq)}
    y_parts = []
    for e in (1, 0):
        at, n = part[e]
        r1 = load_rows(r1_all.at[pl.ds(8 * at, 8 * n), :], n)
        h, hat1, scale1 = norm_rows(r1, rv[8 * e + 5 : 8 * e + 6, :], rv[8 * e + 2 : 8 * e + 3, :])
        h_low = h.astype(BF16)
        hlow_s[at : at + n, :] = h
        o_h[at : at + n, :] = h_low.astype(F32)
        upper = mm(h_low, w_up[e], NN) + b_in[e : e + 1, :]
        active, slope = gelu_both(upper)
        f_low = active.astype(BF16)
        f_s[at : at + n, :] = f_low.astype(F32)
        slope_s[at : at + n, :] = slope
        y_parts.append(mm(f_low, w_down[e], NN))
    store_rows(y_send, jnp.concatenate(y_parts, axis=0))
    flows = [
        Flow(
            lambda s, t, c=c: y_send.at[pl.ds(pl.multiple_of(8 * slot_of(c, t), 8), 8), :],
            lambda s, t, c=c: y_recv.at[s, c],
            lambda n, c=c: y_recv.at[pl.ds(0, n), c],
            everyone, span(c),
        )
        for c in range(cap)
    ] + [
        Flow(
            lambda s, t: y_send.at[pl.ds(pl.multiple_of(8 * (n_valid + place(t, q_owners)), 8), 8), :],
            lambda s, t: y_recv.at[s, cap],
            lambda n: y_recv.at[pl.ds(0, n), cap],
            everyone, q_owners,
        )
    ]
    base = net.start(flows)
    net.finish(flows, base)
    y_sum[...] = jnp.sum(y_recv[...], axis=0)
    flows = [
        Flow(
            lambda s, t, c=c: y_sum.at[c],
            lambda s, t, c=c: y_all.at[pl.ds(pl.multiple_of(8 * slot_of(c, s), 8), 8), :],
            lambda n: y_all.at[pl.ds(0, 8 * n), :],
            span(c), everyone,
        )
        for c in range(cap)
    ] + [
        Flow(
            lambda s, t: y_sum.at[cap],
            lambda s, t: y_all.at[pl.ds(pl.multiple_of(8 * (n_valid + place(s, q_owners)), 8), 8), :],
            lambda n: y_all.at[pl.ds(0, 8 * n), :],
            q_owners, everyone,
        )
    ]
    base = net.start(flows)
    net.finish(flows, base)

    tops, vecs = {}, {}
    for e in (1, 0):
        at, n = part[e]
        y = load_rows(y_all.at[pl.ds(8 * at, 8 * n), :], n)
        top = hlow_s[at : at + n, :] + y + rv[8 * e + 3 : 8 * e + 4, :]
        z, hat2, scale2 = norm_rows(
            top, rv[8 * e + 6 : 8 * e + 7, :], rv[8 * e + 4 : 8 * e + 5, :]
        )
        tops[e] = (hat2, scale2)
        vecs[e] = z.astype(BF16)
    qvec, pvec = vecs[0], vecs[1]
    owner = slots[0:1, 0:n_valid]
    is_first = slots[1:2, 0:n_valid] == 1
    kept_slot = slots[2:3, 0:n_valid] == 1
    member = owner == iota((nq, n_valid), 0)
    valid = jnp.broadcast_to(owner >= 0, (nq, n_valid))
    positive = jnp.logical_and(member, is_first)
    negative = jnp.logical_and(member, jnp.logical_and(jnp.logical_not(is_first), kept_slot))
    counts = jnp.sum(member.astype(F32), axis=1, keepdims=True) - 1.0
    score_scale = 2.0 * D ** (-0.5)
    scores = mm(qvec, pvec, NT) * score_scale
    masked = jnp.where(valid, scores, -1e30)
    peak = jnp.max(masked, axis=1, keepdims=True)
    summed = jnp.sum(jnp.where(valid, jnp.exp(masked - peak), 0.0), axis=1, keepdims=True)
    logsum = peak + jnp.log(summed)
    pos_score = jnp.sum(jnp.where(positive, scores, 0.0), axis=1, keepdims=True)
    margins = MARGIN - pos_score + scores
    active = jnp.logical_and(negative, margins > 0)
    hinge = jnp.sum(jnp.where(active, margins, 0.0), axis=1, keepdims=True) / counts
    active_total = jnp.sum(active.astype(F32), axis=1, keepdims=True)
    loss = jnp.sum(logsum - pos_score + hinge, axis=0, keepdims=True)
    o_loss[...] = jnp.broadcast_to(loss, (8, LANE))
    score_grad = (
        jnp.where(valid, jnp.exp(scores - logsum), 0.0)
        - positive.astype(F32) * (1.0 + active_total / counts)
        + active.astype(F32) / counts
    )
    score_low = score_grad.astype(BF16)
    vec_grads = {
        0: (mm(score_low, pvec, NN) * score_scale).astype(BF16).astype(F32),
        1: (mm(score_low, qvec, TN) * score_scale).astype(BF16).astype(F32),
    }
    h_parts, out_rows = [], {}
    for e in (1, 0):
        at, n = part[e]
        hat2, scale2 = tops[e]
        grad = vec_grads[e]
        g_top = norm_rows_back(grad, rv[8 * e + 6 : 8 * e + 7, :], hat2, scale2)
        dy = g_top.astype(BF16)
        g_top_s[at : at + n, :] = g_top
        out_rows[e] = [
            jnp.sum(grad * hat2, axis=0, keepdims=True),
            jnp.sum(grad, axis=0, keepdims=True),
            jnp.sum(dy.astype(F32), axis=0, keepdims=True),
        ]
        f_low = f_s[at : at + n, :].astype(BF16)
        o_shrink[e] = mm(f_low, dy, TN)
        df = mm(dy, w_down[e], NT)
        du = (slope_s[at : at + n, :] * df).astype(BF16)
        du_f[at : at + n, :] = du.astype(F32)
        h_parts.append(mm(du, w_up[e], NT))
    du_own[...] = du_f[...].astype(BF16)
    store_rows(h_send, jnp.concatenate(h_parts, axis=0))
    flows = [
        Flow(
            lambda s, t, c=c: h_send.at[pl.ds(pl.multiple_of(8 * slot_of(c, t), 8), 8), :],
            lambda s, t, c=c: h_recv.at[s, c],
            lambda n, c=c: h_recv.at[pl.ds(0, n), c],
            everyone, span(c),
        )
        for c in range(cap)
    ] + [
        Flow(
            lambda s, t: h_send.at[pl.ds(8 * n_valid, 8 * nq), :],
            lambda s, t: h_recvq.at[s],
            lambda n: h_recvq.at[pl.ds(0, n)],
            everyone, home,
        )
    ]
    du_flows = [
        Flow(
            lambda s, t: du_own,
            lambda s, t: o_du.at[
                :, pl.ds(pl.multiple_of(((s & 1) * (nd // 2) + s // 2) * LANE, LANE), LANE)
            ],
            lambda n: o_du.at[:, pl.ds(0, n * LANE)],
            alike, alike,
        )
    ]
    base = net.start(flows)
    du_base = net.start(du_flows)
    fac[...] = jnp.zeros_like(fac)
    line[...] = jnp.zeros_like(line)
    sums_s[...] = jnp.zeros_like(sums_s)
    net.finish(flows, base)

    def load_rows_sum(ref, count):
        total = jnp.sum(ref[...], axis=0)
        h_send[0 : 8 * count, :] = total
        return load_rows(h_send.at[pl.ds(0, 8 * count), :], count)

    lane = iota((D, LANE), 1)

    def back(c, carry):
        slot = jnp.where(c == 0, me, slot_of(1, me))
        tile = jnp.sum(h_recv[:, c], axis=0)
        dh = jnp.concatenate([tile[j : j + 1, :] for j in range(D // LANE)], axis=1)
        top = g_top_s[pl.ds(slot, 1), :]
        g_h = top + dh
        r1 = jnp.concatenate([r1_own[c, j : j + 1, :] for j in range(D // LANE)], axis=1)
        gain1 = rv[8 + 5 : 8 + 6, :]
        _, hat1, scale1 = norm_rows(r1, gain1, gain1)
        g_mid = norm_rows_back(g_h, gain1, hat1, scale1)
        row_grad = jnp.where(iota((8, D), 0) == 0, jnp.broadcast_to(g_mid, (8, D)), 0.0)
        kept = (
            hat_s[c], scale_s[c], xl_s[c], xf_s[c], q_s[c], k_s[c], v_s[c], p_s[c], a_s[c]
        )
        g_emb, t, wx, da, dq, do, dbv, g_gain, g_shift = unit_back(
            passage, row_grad, 1, w_one, cv, kept
        )
        gtok[c] = g_emb.reshape(nd, cols, LP).astype(BF16)
        zero = jnp.zeros((16, D), F32)
        xa = jnp.concatenate(
            [xf_s[c].astype(F32)[0:1, :], jnp.zeros((15, D), F32), a_s[c].astype(F32)[0:1, :],
             jnp.zeros((31, D), F32)],
            axis=0,
        )
        tw = jnp.transpose(jnp.concatenate([t, zero, wx, zero, jnp.zeros((64, D), F32)], axis=0))
        xa = jnp.transpose(jnp.concatenate([jnp.zeros((64, D), F32), xa, zero], axis=0))
        placed = pltpu.roll(tw, 16 * c, 1) + pltpu.roll(xa, c, 1)
        fac[...] = (fac[...].astype(F32) + placed.reshape(nd, cols, LANE)).astype(BF16)
        which = iota((16, D), 0)
        new = jnp.zeros((16, D), F32)
        for j, row in enumerate((q_s[c], da, dq, do)):
            new = new + jnp.where(which == 2 * j + c, row.astype(F32)[0:1, :], 0.0)
        line[...] = line[...] + new
        columns = jnp.where(lane == 0, g_gain, jnp.where(lane == 1, g_shift, 0.0))
        flat = jnp.transpose(columns)[0:8, :]
        extra = (
            jnp.where(iota((8, D), 0) == 2, dbv, 0.0)
            + jnp.where(iota((8, D), 0) == 3, g_h * hat1, 0.0)
            + jnp.where(iota((8, D), 0) == 4, g_h, 0.0)
        )
        sums_s[...] = sums_s[...] + flat + extra
        return carry

    lax.fori_loop(0, n_mine, back, 0)
    line_q[0:16, :] = (line[...] + jnp.concatenate([jnp.zeros((8, D), F32), sums_s[...]], axis=0)).astype(BF16)

    @pl.when(me == query_home)
    def _():
        dh = load_rows_sum(h_recvq, nq)
        at, n = part[0]
        g_h = g_top_s[at : at + n, :] + dh
        r1 = load_rows(r1_ownq, nq)
        gain1 = rv[5:6, :]
        _, hat1, scale1 = norm_rows(r1, gain1, gain1)
        g_mid = norm_rows_back(g_h, gain1, hat1, scale1)
        kept = (
            hat_q[...], scale_q[...], xl_q[...], xf_q[...], q_q[...], k_q[...], v_q[...],
            p_q[...], a_q[...],
        )
        g_emb, t, w, da, dq, do, dbv, g_gain, g_shift = unit_back(
            queries, g_mid, 0, w_zero, cv, kept
        )
        gtok_q[...] = g_emb.reshape(nd, cols, nq * LQ).astype(BF16)
        tw = jnp.concatenate([t, w, xf_q[...].astype(F32), a_q[...].astype(F32)], axis=0)
        n_tw = tw.shape[0]
        tw = jnp.concatenate([tw, jnp.zeros((fac_q.shape[2] - n_tw, D), F32)], axis=0)
        fac_q[...] = jnp.transpose(tw).reshape(nd, cols, fac_q.shape[2]).astype(BF16)
        columns = jnp.where(lane == 0, g_gain, jnp.where(lane == 1, g_shift, 0.0))
        flat = jnp.transpose(columns)[0:8, :]
        extra = (
            jnp.where(iota((8, D), 0) == 2, dbv, 0.0)
            + jnp.where(iota((8, D), 0) == 3, jnp.sum(g_h * hat1, axis=0, keepdims=True), 0.0)
            + jnp.where(iota((8, D), 0) == 4, jnp.sum(g_h, axis=0, keepdims=True), 0.0)
        )
        block = jnp.concatenate(
            [q_q[...].astype(F32), da.astype(F32), dq.astype(F32), do.astype(F32), flat + extra,
             jnp.zeros((8, D), F32)],
            axis=0,
        )
        line_q[16:64, :] = block.astype(BF16)

    half = nd // 2

    def to_twin(src, sem):
        return pltpu.make_async_remote_copy(
            src_ref=src, dst_ref=src, send_sem=twin_send.at[sem], recv_sem=twin_recv.at[sem],
            device_id=net.where(me ^ 1), device_id_type=MESH,
        )

    row_flows = [
        Flow(
            lambda s, t: line_q.at[pl.ds(0, 16), :],
            lambda s, t: o_line.at[s & 1, s // 2],
            lambda n: o_line.at[0, pl.ds(0, n)],
            alike, alike,
        ),
    ]
    plane, home_core = query_home // 8, query_home % 2
    z_at = me // 8
    on_core = core == home_core
    query_rows = line_q.at[pl.ds(16, 48), :]

    def pass_rows(src, t, sem):
        pltpu.make_async_remote_copy(
            src_ref=src, dst_ref=o_lineq, send_sem=chain_send.at[sem], recv_sem=chain_recv,
            device_id=net.where(t), device_id_type=MESH,
        ).start()

    def rows_sent(sem):
        pltpu.make_async_copy(o_lineq, o_lineq, chain_send.at[sem]).wait()

    at_home = me == query_home
    in_plane = jnp.logical_and(z_at == plane, on_core)
    goes_up = jnp.logical_and(on_core, jnp.logical_and(z_at >= plane, z_at < nd // 8 - 1))
    goes_down = jnp.logical_and(on_core, jnp.logical_and(z_at <= plane, z_at > 0))

    @pl.when(at_home)
    def _():
        own = pltpu.make_async_copy(query_rows, o_lineq, own_sem.at[own_sem.shape[0] - 1])
        own.start()
        for j in range(1, 4):
            pass_rows(query_rows, me ^ (2 * j), j)
        own.wait()

    row_base = net.start(row_flows)
    flows = [
        Flow(
            lambda s, t: gtok_q.at[t],
            lambda s, t: o_tok.at[:, pl.ds(n_valid * LP, nq * LQ)],
            lambda n: o_tok.at[:, pl.ds(0, n * nq * LQ)],
            home, everyone,
        ),
        Flow(
            lambda s, t: fac.at[t],
            lambda s, t: o_fac.at[s],
            lambda n: o_fac.at[pl.ds(0, n)],
            everyone, everyone,
        ),
        Flow(
            lambda s, t: fac_q.at[t],
            lambda s, t: o_facq,
            lambda n: fac_q.at[pl.ds(0, n)],
            home, everyone,
        ),
    ]
    base = net.start(flows)

    def tok_view(slot):
        return o_tok.at[:, pl.ds(pl.multiple_of(slot * LP, LANE), LP)]

    def push_tokens(k, carry):
        t = lax.rem(me + k, nd)
        for c in range(cap):

            @pl.when(within(me, span(c)))
            def _():
                slot = slot_of(c, me)
                pltpu.make_async_remote_copy(
                    src_ref=gtok.at[c, t], dst_ref=tok_view(slot),
                    send_sem=tok_send.at[c], recv_sem=tok_recv.at[slot],
                    device_id=net.where(t), device_id_type=MESH,
                ).start()

        return carry

    for c in range(cap):

        @pl.when(within(me, span(c)))
        def _():
            slot = slot_of(c, me)
            pltpu.make_async_copy(gtok.at[c, me], tok_view(slot), tok_recv.at[slot]).start()

    lax.fori_loop(1, nd, push_tokens, 0)

    @pl.when(jnp.logical_not(at_home))
    def _():
        pltpu.make_async_copy(o_lineq, o_lineq, chain_recv).wait()

    @pl.when(goes_up)
    def _():
        pass_rows(o_lineq, me + 8, 4)

    @pl.when(goes_down)
    def _():
        pass_rows(o_lineq, me - 8, 5)

    @pl.when(on_core)
    def _():
        pass_rows(o_lineq, me ^ 1, 6)

    net.finish(du_flows, du_base)
    du_half = o_du.at[:, pl.ds(pl.multiple_of(core * (half * LANE), LANE), half * LANE)]
    to_twin(du_half, 0).start()
    net.finish(row_flows, row_base)
    to_twin(o_line.at[core], 1).start()

    net.finish(flows[1:], base + 1)
    lane1 = iota((cols, LANE), 1)
    for g in range(nd // 4):
        t_g = jnp.zeros((cols, LANE), F32)
        w_g = jnp.zeros((cols, LANE), F32)
        for j in range(4):
            block = o_fac[4 * g + j].astype(F32)
            t_part = jnp.where(lane1 < 32, block, 0.0)
            w_part = jnp.where(jnp.logical_and(lane1 >= 32, lane1 < 64), block, 0.0)
            t_g = t_g + (pltpu.roll(t_part, 32 * j, 1) if j else t_part)
            w_g = w_g + (pltpu.roll(w_part, (32 * j - 32) % LANE, 1) if j != 1 else w_part)
        t_all[:, g * LANE : (g + 1) * LANE] = t_g.astype(BF16)
        w_all[:, g * LANE : (g + 1) * LANE] = w_g.astype(BF16)
    x_all = jnp.zeros((cols, LANE), F32)
    a_all = jnp.zeros((cols, LANE), F32)
    for d in range(nd):
        block = o_fac[d].astype(F32)
        x_part = jnp.where(jnp.logical_and(lane1 >= 64, lane1 < 66), block, 0.0)
        a_part = jnp.where(jnp.logical_and(lane1 >= 80, lane1 < 82), block, 0.0)
        x_all = x_all + pltpu.roll(x_part, (2 * d - 64) % LANE, 1)
        a_all = a_all + pltpu.roll(a_part, (2 * d - 80) % LANE, 1)
    mask16 = ((iota((16, D), 0)) == (iota((16, D), 1) >> 6)).astype(F32)

    to_twin(du_half, 0).wait()
    to_twin(o_line.at[core], 1).wait()

    def expand(d, carry):
        both = o_line[d & 1, d // 2].astype(F32)
        for c in range(2):
            at = pl.ds(pl.multiple_of(32 * d + 16 * c, 16), 16)
            q_exp[at, :] = (both[c : c + 1, :] * mask16).astype(BF16)
            d_exp[at, :] = (both[2 + c : 3 + c, :] * mask16).astype(BF16)
        return carry

    lax.fori_loop(0, nd, expand, 0)
    everything = o_line[...].reshape(nd * 16, D)
    row, col = iota((272, nd * 16), 0), iota((272, nd * 16), 1)
    kind = col & 15
    at_block = col >> 4
    device = (at_block & (half - 1)) * 2 + (at_block // half)
    pair = device * 2 + (col & 1)
    dq_rows = jnp.logical_and(row < 128, jnp.logical_and((kind >> 1) == 2, pair == row))
    do_rows = jnp.logical_and(
        jnp.logical_and(row >= 128, row < 256),
        jnp.logical_and((kind >> 1) == 3, pair == row - 128),
    )
    total_rows = jnp.logical_or(
        jnp.logical_and(jnp.logical_and(row >= 256, row < 261), kind == row - 248),
        jnp.logical_or(
            jnp.logical_and(row == 261, (kind >> 1) == 2),
            jnp.logical_and(row == 262, (kind >> 1) == 3),
        ),
    )
    select = as_bf16(jnp.logical_or(dq_rows, jnp.logical_or(do_rows, total_rows)))
    picked = mm(select, everything, NN)
    g_in[1, :, 0:D] = mm(x_all.astype(BF16), picked[0:128].astype(BF16), NN)
    g_in[1, :, D : 2 * D] = mm(t_all[...], q_exp[...], NN)
    g_in[1, :, 2 * D : 3 * D] = mm(w_all[...], d_exp[...], NN)
    g_out[1] = mm(a_all.astype(BF16), picked[128:256].astype(BF16), NN)
    sums1 = picked[256:272]

    fl = o_facq.shape[1]
    row, col = iota((fl, 48), 0), iota((fl, 48), 1)
    q_rows = H * nq
    rown = iota((fl, D), 0)
    headn = iota((fl, D), 1) >> 6

    def rhs(first_row, last_row, first_col, by_head):
        here = jnp.logical_and(row >= first_row, row < last_row)
        hit = jnp.logical_and(here, col == first_col + (row & (nq - 1)))
        out = mm(as_bf16(hit), o_lineq[...], NN)
        if by_head:
            out = jnp.where(((rown - first_row) >> (nq.bit_length() - 1)) == headn, out, 0.0)
        return out.astype(BF16)

    facq = o_facq[...]
    g_in[0, :, 0:D] = mm(facq, rhs(2 * q_rows, 2 * q_rows + nq, 2 * nq, False), NN)
    g_in[0, :, D : 2 * D] = mm(facq, rhs(0, q_rows, 0, True), NN)
    g_in[0, :, 2 * D : 3 * D] = mm(facq, rhs(q_rows, 2 * q_rows, nq, True), NN)
    g_out[0] = mm(facq, rhs(2 * q_rows + nq, 2 * q_rows + 2 * nq, 3 * nq, False), NN)
    line0 = o_lineq[...].astype(F32)
    sums0 = line0[4 * nq : 4 * nq + 8]
    dq0 = jnp.sum(line0[2 * nq : 3 * nq], axis=0, keepdims=True)
    do0 = jnp.sum(line0[3 * nq : 4 * nq], axis=0, keepdims=True)

    mine_at = as_bf16(iota((cols, D), 1) == iota((cols, D), 0) + me * cols)
    h_cols = mm(mine_at, o_h[...].astype(BF16), NT)
    both = jnp.concatenate([h_cols, h_cols], axis=0)
    r, c = iota((2 * cols, rows), 0), iota((2 * cols, rows), 1)
    both = jnp.where((r < cols) == (c >= n_valid), both, 0.0).astype(BF16)
    g_up[...] = mm(both, o_du[...], NN)
    ones = iota((8, rows), 0)
    which = iota((8, rows), 1)
    e_rows = as_bf16(
        jnp.logical_or(
            jnp.logical_and(ones == 0, which >= n_valid),
            jnp.logical_and(ones == 1, which < n_valid),
        )
    )
    db_in = mm(e_rows, o_du[...], NN)
    g_bin[...] = db_in
    small_rows = {
        0: (dq0, sums0[2:3], do0, sums0[4:5], out_rows[0][2], out_rows[0][1], sums0[1:2],
            sums0[0:1], sums0[3:4], out_rows[0][0]),
        1: (sums1[5:6], sums1[2:3], sums1[6:7], sums1[4:5], out_rows[1][2], out_rows[1][1],
            sums1[1:2], sums1[0:1], sums1[3:4], out_rows[1][0]),
    }
    small_squares = jnp.sum(db_in * db_in)
    for e in range(2):
        for j, value in enumerate(small_rows[e]):
            g_small[16 * e + j : 16 * e + j + 1, :] = value
            small_squares = small_squares + jnp.sum(value * value)
    squares = jnp.sum(g_in[...] * g_in[...]) + jnp.sum(g_out[...] * g_out[...])
    squares = squares + jnp.sum(g_up[...] * g_up[...]) + jnp.sum(o_shrink[...] * o_shrink[...])

    blocks = g_table.shape[1] // HASH
    acc_s[...] = jnp.zeros_like(acc_s)

    def add_tokens(now, values):
        low = now & (HASH - 1)
        high = now >> (HASH.bit_length() - 1)
        width = now.shape[1]
        for b in range(0, blocks, 2):
            two = jnp.concatenate(
                [jnp.where(high == b, values, 0.0), jnp.where(high == b + 1, values, 0.0)], axis=0
            )
            spread_s[b * cols : (b + 2) * cols, 0:width] = two.astype(BF16)
        hot = as_bf16(iota((HASH, width), 0) == low)
        acc_s[...] += mm(spread_s[:, 0:width], hot, NT)

    def add_slots(slots_now):
        for slot in slots_now:
            pltpu.make_async_copy(tok_view(slot), tok_view(slot), tok_recv.at[slot]).wait()
        values = [tok_view(slot)[...].astype(F32) for slot in slots_now]
        add_tokens(
            jnp.concatenate([ids[slot] for slot in slots_now], axis=1),
            jnp.concatenate(values, axis=1),
        )

    def add_near(k, carry):
        add_slots([lax.rem(me - 2 * k - j + nd, nd) for j in range(2)])
        return carry

    def add_far(k, carry):
        extra = n_valid - nd
        first = me // (nd // extra)
        add_slots([nd + lax.rem(first - 2 * k - j + 2 * extra, extra) for j in range(2)])
        return carry

    lax.fori_loop(0, nd // 2, add_near, 0)
    lax.fori_loop(0, (n_valid - nd) // 2, add_far, 0)
    net.finish(flows[:1], base)
    add_tokens(ids_q[...], o_tok[:, n_valid * LP : n_valid * LP + nq * LQ].astype(F32))
    for c in range(cap):

        @pl.when(within(me, span(c)))
        def _():
            sent = o_tok.at[:, pl.ds(0, (nd - 1) * LP)]
            pltpu.make_async_copy(sent, sent, tok_send.at[c]).wait()

    @pl.when(at_home)
    def _():
        for j in range(1, 4):
            rows_sent(j)

    for ok, sem in ((goes_up, 4), (goes_down, 5), (on_core, 6)):

        @pl.when(ok)
        def _():
            rows_sent(sem)

    def add_slot(s, total):
        return total + o_tok[:, pl.ds(pl.multiple_of(s * LP, LANE), LP)].astype(F32)

    position = lax.fori_loop(0, n_valid, add_slot, jnp.zeros((cols, LP), F32))
    tq = nq * LQ
    q_tok = o_tok[:, n_valid * LP : n_valid * LP + tq].astype(F32)
    folded = q_tok[:, 0:LANE]
    for j in range(1, tq // LANE):
        folded = folded + q_tok[:, j * LANE : (j + 1) * LANE]
    around = folded
    for j in range(1, LANE // LQ):
        around = around + pltpu.roll(folded, LANE - LQ * j, 1)
    around = jnp.where(lane1 < LQ, around, 0.0)
    position = jnp.concatenate(
        [position[:, 0:LANE] + around, position[:, LANE:], jnp.zeros((cols, HASH - LP), F32)],
        axis=1,
    )
    shifted = pltpu.roll(position, V - (blocks - 1) * HASH, 1)
    for b in range(blocks):
        value = acc_s[b * cols : (b + 1) * cols, :]
        if b == blocks - 1:
            value = value + shifted
        g_table[:, b * HASH : (b + 1) * HASH] = value
        squares = squares + jnp.sum(value * value)

    norm_own[...] = jnp.broadcast_to(squares.reshape(1, 1), (8, LANE))
    flows = [
        Flow(
            lambda s, t: norm_own, lambda s, t: norm_all.at[s],
            lambda n: norm_all.at[pl.ds(0, n)], everyone, everyone,
        )
    ]
    base = net.start(flows)
    net.finish(flows, base)
    o_norm[...] = jnp.sqrt(jnp.sum(norm_all[...], axis=0) + small_squares)


def middle(n_valid, nq, nd, narrow, cols, query_home, arrays):
    cap = -(-n_valid // nd)
    rows = n_valid + nq
    tq = nq * LQ
    unit, unit_q = Unit(1, LP), Unit(nq, LQ)
    fac_lanes = -(-(2 * unit_q.rows + 2 * unit_q.seqs) // LANE) * LANE
    vmem = pl.BlockSpec(memory_space=pltpu.VMEM)

    def like(*shape, dtype=F32):
        return jax.ShapeDtypeStruct(shape, dtype)

    def kept(lead, u):
        return [
            pltpu.VMEM(lead + (D, u.tokens), F32),
            pltpu.VMEM(lead + (1, u.tokens), F32),
            pltpu.VMEM(lead + (D, u.tokens), BF16),
            pltpu.VMEM(lead + (u.seqs, D), BF16),
            pltpu.VMEM(lead + (u.seqs, D), BF16),
            pltpu.VMEM(lead + (D, u.tokens), BF16),
            pltpu.VMEM(lead + (D, u.tokens), BF16),
            pltpu.VMEM(lead + (u.rows, u.tokens), F32),
            pltpu.VMEM(lead + (u.seqs, D), BF16),
        ]

    flows = 5 * (cap + 1) + 7
    table_total = -(-(V + LP) // HASH) * HASH
    chunk = 2 * LP
    return pl.pallas_call(
        functools.partial(
            middle_body, n_valid, nq, nd, narrow, cols, query_home
        ),
        out_shape=[
            like(2, LANE, D),
            like(8, LANE),
            like(cols, table_total),
            like(2, cols, 3 * D),
            like(2, cols, D),
            like(2 * cols, nd * LANE),
            like(8, nd * LANE),
            like(32, D),
            like(8, LANE),
        ],
        in_specs=[vmem] * len(arrays),
        out_specs=[vmem] * 9,
        scratch_shapes=kept((cap,), unit)
        + kept((), unit_q)
        + [
            pltpu.VMEM((cap, 8, LANE), F32),
            pltpu.VMEM((8 * nq, LANE), F32),
            pltpu.VMEM((8 * rows, LANE), F32),
            pltpu.VMEM((8 * rows, LANE), F32),
            pltpu.VMEM((nd, cap + 1, 8, LANE), F32),
            pltpu.VMEM((cap + 1, 8, LANE), F32),
            pltpu.VMEM((8 * rows, LANE), F32),
            pltpu.VMEM((8 * rows, LANE), F32),
            pltpu.VMEM((nd, cap, 8, LANE), F32),
            pltpu.VMEM((nd, 8 * nq, LANE), F32),
            pltpu.VMEM((rows, LANE), BF16),
            pltpu.VMEM((rows, LANE), F32),
            pltpu.VMEM((cap, nd, cols, LP), BF16),
            pltpu.VMEM((nd, cols, tq), BF16),
            pltpu.VMEM((nd, cols, LANE), BF16),
            pltpu.VMEM((nd, cols, fac_lanes), BF16),
            pltpu.VMEM((16, D), F32),
            pltpu.VMEM((64, D), BF16),
            pltpu.VMEM((rows, LANE), F32),
            pltpu.VMEM((rows, LANE), F32),
            pltpu.VMEM((rows, D), F32),
            pltpu.VMEM((rows, D), F32),
            pltpu.VMEM((8, D), F32),
            pltpu.VMEM((cols, n_valid * LP + tq), BF16),
            pltpu.VMEM((nd, cols, LANE), BF16),
            pltpu.VMEM((cols, fac_lanes), BF16),
            pltpu.VMEM((2, nd // 2, 16, D), BF16),
            pltpu.VMEM((48, D), BF16),
            pltpu.VMEM((rows, nd * LANE), BF16),
            pltpu.VMEM((rows, D), F32),
            pltpu.VMEM((nd, 2, cols, LANE), BF16),
            pltpu.VMEM((2, D, LANE), BF16),
            pltpu.VMEM((cols, nd * 32), BF16),
            pltpu.VMEM((cols, nd * 32), BF16),
            pltpu.VMEM((nd * 32, D), BF16),
            pltpu.VMEM((nd * 32, D), BF16),
            pltpu.VMEM((table_total // HASH * cols, chunk), BF16),
            pltpu.VMEM((table_total // HASH * cols, HASH), F32),
            pltpu.VMEM((8, LANE), F32),
            pltpu.VMEM((nd, 8, LANE), F32),
            pltpu.SemaphoreType.DMA((cap,)),
            pltpu.SemaphoreType.DMA((n_valid,)),
            pltpu.SemaphoreType.DMA((2,)),
            pltpu.SemaphoreType.DMA((2,)),
            pltpu.SemaphoreType.DMA((7,)),
            pltpu.SemaphoreType.DMA(()),
            pltpu.SemaphoreType.DMA((flows,)),
            pltpu.SemaphoreType.DMA((flows,)),
            pltpu.SemaphoreType.DMA((flows,)),
        ],
        compiler_params=pltpu.CompilerParams(
            collective_id=3, has_side_effects=True, vmem_limit_bytes=62 * 1024 * 1024
        ),
        name="middle",
    )(*arrays)


def stack_table(rows, blocks, table, stacked):
    last = (V - (blocks - 1) * HASH + LANE - 1) // LANE * LANE

    def piece(b):
        if b >= blocks:
            return []
        if b == blocks - 1:
            part = table[:, b * HASH : b * HASH + last].astype(F32)
            return [jnp.concatenate([part, jnp.zeros((rows, HASH - last), F32)], axis=1)]
        return [table[:, b * HASH : (b + 1) * HASH].astype(F32)]

    for b in range(0, blocks, 2):
        both = jnp.concatenate(piece(b) + piece(b + 1), axis=0)
        stacked[b * rows : b * rows + both.shape[0], :] = both.astype(BF16)


def pick_tokens(rows, blocks, stacked, ids):
    low = ids & (HASH - 1)
    high = ids >> (HASH.bit_length() - 1)
    width = ids.shape[1]
    hot = as_bf16(iota((HASH, width), 0) == low)
    picked = jnp.dot(stacked[...], hot, preferred_element_type=F32)
    value = jnp.zeros((rows, width), F32)
    for b in range(blocks):
        value = jnp.where(high == b, picked[b * rows : (b + 1) * rows], value)
    return value.astype(BF16)


def first_body(
    n_valid, nq, nd, narrow, cols, home_at, blocks, plan,
    ids_mine, small_mine, table, win, wout, pos_mine,
    ids_got, small_got, mine, mine_q, wall, w0,
    stacked, tokens, tokens_q, p0,
    send_sem, recv_sem, own_sem, up_send, down_send, z_recv, y_send, y_recv, x_send, x_recv,
    c_send, c_recv,
):
    cap = -(-n_valid // nd)
    wide = nd // narrow
    tq = nq * LQ
    n_own = ids_mine.shape[0] - 1
    net = Net(nd, narrow, send_sem, recv_sem, own_sem)
    me = net.me
    w_at, n_at = lax.axis_index("wide"), lax.axis_index("narrow")
    x_at, c_at = n_at ^ 2, n_at ^ 1
    everyone = group(nd, nd)
    home = (home_at, 1, 1)

    def span(c):
        return group(nd, nd) if c == 0 else group(n_valid - nd, nd, 1)

    def slot_of(c, d):
        return c * nd + place(d, span(c))

    wall[w_at, n_at] = jnp.concatenate([win[1], wout[1], pos_mine[...]], axis=1).astype(BF16)
    p0[...] = jnp.concatenate([win[0], wout[0]], axis=1).astype(BF16)

    net.barrier()
    small = [
        Flow(
            lambda s, t: ids_mine, lambda s, t: ids_got.at[s],
            lambda n: ids_got.at[pl.ds(0, n)], everyone, everyone,
        ),
        Flow(
            lambda s, t: small_mine, lambda s, t: small_got.at[s],
            lambda n: small_got.at[pl.ds(0, n)], everyone, everyone,
        ),
    ]
    small_base = net.start(small)

    tall = wide // 2
    z_at, y_at = w_at // 2, lax.rem(w_at, 2)

    def pass_on(row, col, w_to, n_to, sent, got):
        pltpu.make_async_remote_copy(
            src_ref=wall.at[row, col], dst_ref=wall.at[row, col], send_sem=sent, recv_sem=got,
            device_id=(w_to, n_to), device_id_type=MESH,
        ).start()

    def await_piece(row, col, sem):
        pltpu.make_async_copy(wall.at[row, col], wall.at[row, col], sem).wait()

    def up(z):
        @pl.when(z_at < tall - 1)
        def _():
            pass_on(2 * z + y_at, n_at, w_at + 2, n_at, up_send.at[z], z_recv.at[z])

    def down(z):
        @pl.when(z_at > 0)
        def _():
            pass_on(2 * z + y_at, n_at, w_at - 2, n_at, down_send.at[z], z_recv.at[z])

    def across(row):
        pass_on(row, n_at, w_at, x_at, x_send, x_recv.at[row])
        pass_on(row, n_at, w_at, c_at, c_send, c_recv.at[0, row])

    def around(z):
        pass_on(2 * z + y_at, n_at, w_at ^ 1, n_at, y_send, y_recv.at[z])
        across(2 * z + y_at)

    def z_step(k):
        for z, onward in ((z_at - k, up), (z_at + k, down)):

            @pl.when(jnp.logical_and(z >= 0, z < tall))
            def _():
                await_piece(2 * z + y_at, n_at, z_recv.at[z])
                onward(z)
                around(z)

    def y_step(z):
        row = 2 * z + (y_at ^ 1)
        await_piece(row, n_at, y_recv.at[z])
        across(row)

    def x_step(row):
        await_piece(row, x_at, x_recv.at[row])
        pass_on(row, x_at, w_at, c_at, c_send, c_recv.at[1, row])

    def forward(step):
        if step < tall:
            z_step(step)
        elif step < 2 * tall:
            y_step(lax.rem(z_at + step - tall, tall))
        else:
            k = step - 2 * tall
            row = 2 * lax.rem(z_at + k, tall) + y_at if k < tall else (
                2 * lax.rem(z_at + k, tall) + (y_at ^ 1)
            )
            x_step(row)

    up(z_at)
    down(z_at)
    around(z_at)

    stack_table(cols, blocks, table, stacked)
    net.finish(small, small_base)

    pairs = n_valid // n_own
    moves = [
        Flow(
            lambda s, t, c=c: tokens.at[slot_of(c, t) // n_own, lax.rem(slot_of(c, t), n_own)],
            lambda s, t, c=c: mine.at[s, :, pl.ds(c * LP, LP)],
            lambda n: mine.at[pl.ds(0, n), :, pl.ds(0, LP)],
            everyone, span(c),
        )
        for c in range(cap)
    ]
    base = net.used
    net.used += cap

    def send_pair(at):
        for j in range(n_own):
            slot = at * n_own + j
            c = slot // nd
            far = span(1)
            t = jnp.where(c == 0, slot, far[0] + far[1] * (slot - nd))
            dst = mine.at[me, :, pl.ds(pl.multiple_of(c * LP, LANE), LP)]

            @pl.when(t != me)
            def _():
                pltpu.make_async_remote_copy(
                    src_ref=tokens.at[at, j], dst_ref=dst,
                    send_sem=send_sem.at[base + c], recv_sem=recv_sem.at[base + c],
                    device_id=net.where(t), device_id_type=MESH,
                ).start()

            @pl.when(t == me)
            def _():
                pltpu.make_async_copy(tokens.at[at, j], dst, own_sem.at[base + c]).start()

    def gather(i, carry):
        at = lax.rem(i + me, pairs)
        ids = jnp.concatenate([ids_got[at, j : j + 1, 0:LP] for j in range(n_own)], axis=1)
        rows = pick_tokens(cols, blocks, stacked, ids)
        for j in range(n_own):
            tokens[at, j] = rows[:, j * LP : (j + 1) * LP]

        @pl.when(i > 0)
        def _():
            send_pair(lax.rem(i - 1 + me, pairs))

        for step, turn in enumerate(plan):
            if 0 < step and turn < pairs:

                @pl.when(i == turn)
                def _():
                    forward(step)

        return carry

    q_ids = jnp.zeros((1, tq), jnp.int32)
    for d in range(0, nd, narrow):
        q_ids = q_ids + ids_got[d, n_own : n_own + 1, 0:tq]
    tokens_q[...] = pick_tokens(cols, blocks, stacked, q_ids)
    q_moves = [
        Flow(
            lambda s, t: tokens_q, lambda s, t: mine_q.at[s],
            lambda n: mine_q.at[pl.ds(0, n)], everyone, home,
        ),
    ]
    home_moves = [
        Flow(
            lambda s, t: p0, lambda s, t: w0.at[s],
            lambda n: w0.at[pl.ds(0, n)], everyone, home,
        ),
    ]
    q_base = net.start(q_moves)
    home_base = net.start(home_moves)
    lax.fori_loop(0, pairs, gather, 0)
    send_pair(lax.rem(pairs - 1 + me, pairs))
    for step, turn in enumerate(plan):
        if 0 < step and turn >= pairs:
            forward(step)
    net.finish(moves, base)
    net.finish(q_moves, q_base)
    net.finish(home_moves, home_base)

    def last(row, carry):
        for which, col in ((0, c_at), (1, c_at ^ 2)):
            pltpu.make_async_copy(
                wall.at[row, col], wall.at[row, col], c_recv.at[which, row]
            ).wait()
        return carry

    lax.fori_loop(0, wide, last, 0)
    for z in range(tall):
        for hop, ok in (
            (up_send, jnp.logical_and(z_at < tall - 1, z <= z_at)),
            (down_send, jnp.logical_and(z_at > 0, z >= z_at)),
        ):

            @pl.when(ok)
            def _():
                await_piece(0, 0, hop.at[z])

    many = wall.at[pl.ds(0, tall), 0]
    pltpu.make_async_copy(many, many, y_send).wait()
    many = wall.at[:, 0]
    pltpu.make_async_copy(many, many, x_send).wait()
    many = wall.at[:, pl.ds(0, 2)]
    pltpu.make_async_copy(many, many, c_send).wait()


def first(n_valid, nq, nd, narrow, cols, home_at, arrays, plan):
    cap = -(-n_valid // nd)
    wide = nd // narrow
    tq = nq * LQ
    ids_mine, small_mine = arrays[0], arrays[1]
    n_own = ids_mine.shape[0] - 1
    blocks = -(-V // HASH)
    vmem = pl.BlockSpec(memory_space=pltpu.VMEM)
    flows = 4 + cap

    def like(*shape, dtype=BF16):
        return jax.ShapeDtypeStruct(shape, dtype)

    dma = pltpu.SemaphoreType.DMA
    return pl.pallas_call(
        functools.partial(
            first_body, n_valid, nq, nd, narrow, cols, home_at, blocks, plan
        ),
        out_shape=[
            like(nd, *ids_mine.shape, dtype=jnp.int32),
            like(nd, *small_mine.shape),
            like(nd, cols, cap * LP),
            like(nd, cols, tq),
            like(wide, narrow, cols, 4 * D + LP),
            like(nd, cols, 4 * D),
        ],
        in_specs=[vmem] * len(arrays),
        out_specs=[vmem] * 6,
        scratch_shapes=[
            pltpu.VMEM((blocks * cols, HASH), BF16),
            pltpu.VMEM((n_valid // n_own, n_own, cols, LP), BF16),
            pltpu.VMEM((cols, tq), BF16),
            pltpu.VMEM((cols, 4 * D), BF16),
            dma((flows,)), dma((flows,)), dma((flows,)),
            dma((wide // 2,)), dma((wide // 2,)), dma((wide // 2,)), dma(()), dma((wide // 2,)),
            dma(()), dma((wide,)), dma(()), dma((2, wide)),
        ],
        compiler_params=pltpu.CompilerParams(
            collective_id=2, has_side_effects=True, vmem_limit_bytes=62 * 1024 * 1024
        ),
        name="first",
    )(*arrays)


def on_device_rows(
    passage_ids, query_ids, passage_query, kept_mask, neg_count, step_count,
    embed_table, attend_in, attend_out, expand_weight, shrink_weight, norm_gains, bias_terms,
    embed_first, embed_second, attend_in_first, attend_in_second,
    attend_out_first, attend_out_second, expand_first, expand_second,
    shrink_first, shrink_second, gains_first, gains_second, bias_first, bias_second,
):
    narrow = lax.axis_size("narrow")
    nd = lax.axis_size("wide") * narrow
    me = lax.axis_index("wide") * narrow + lax.axis_index("narrow")
    cols = embed_table.shape[1]
    n_slots = passage_query.shape[0]
    nq = query_ids.shape[0] * lax.axis_size("wide")
    n_valid = VALID_PER_QUERY * nq
    cap = -(-n_valid // nd)
    rows_p = cap * nd
    ff_cols = FF // nd

    exch = functools.partial(comm, nd=nd, narrow=narrow)
    rows_c = -(-cols // 8) * 8
    n_ids = passage_ids.shape[0] + query_ids.shape[0]
    small_width = max(cols, bias_terms.shape[1], 1)
    small_width = -(-small_width // LANE) * LANE

    def widen(value, width):
        return jnp.pad(value, ((0, 0), (0, width - value.shape[1])))

    ids_mine = jnp.concatenate([passage_ids, widen(query_ids, LP)])
    small_mine = jnp.concatenate(
        [widen(norm_gains.reshape(6, cols), small_width), widen(bias_terms, small_width)]
    ).astype(BF16)
    ids_got, small_got = exch(
        1,
        [ids_mine, small_mine],
        [((nd, n_ids, LP), jnp.int32), ((nd, 8, small_width), BF16)],
        [send_all(0, 0, nd), send_all(1, 1, nd)],
    )
    n_own = passage_ids.shape[0]
    pid = ids_got[:, :n_own].reshape(n_slots, LP)[:n_valid]
    qid = ids_got.reshape(-1, narrow, n_ids, LP)[:, 0, n_own:, :LANE].reshape(nq, LANE)
    all_ids = jnp.concatenate([pid.reshape(-1), qid.reshape(-1)])
    gains = small_got[:, :6, :cols].transpose(1, 0, 2).reshape(2, 3, D).astype(F32)
    bias = small_got[:, 6:, : bias_terms.shape[1]].transpose(1, 0, 2).reshape(2, -1).astype(F32)

    table_t = embed_table.T
    table_low = table_t.astype(BF16)
    vocab = V + LP
    total = -(-vocab // HASH) * HASH
    table_pad = jnp.pad(table_low, ((0, rows_c - cols), (0, total - vocab)))
    got = table_rows(table_pad, all_ids)
    pos_mine = table_pad[:, V : V + LP]
    up_mine = expand_weight.astype(BF16).reshape(2 * cols, nd, ff_cols).transpose(1, 0, 2)
    q_from = n_valid * LP
    width = cap * LP + LANE

    def passage_move(c, forward):
        span = (0, min(nd, n_valid - c * nd))
        if forward:
            return Send(
                0, 0,
                lambda ref, s, t: ref.at[:, pl.ds(pl.multiple_of((c * nd + t) * LP, LANE), LP)],
                lambda ref, s, t: ref.at[s, :, pl.ds(c * LP, LP)],
                lambda ref, n: ref.at[:, pl.ds(0, n * LP)],
                lambda ref, n: ref.at[pl.ds(0, n), :, pl.ds(0, LP)],
                (0, nd), span,
            )
        return Send(
            0, 0,
            lambda ref, s, t: ref.at[t, :, pl.ds(c * LP, LP)],
            lambda ref, s, t: ref.at[:, pl.ds(pl.multiple_of((c * nd + s) * LP, LANE), LP)],
            lambda ref, n: ref.at[pl.ds(0, n), :, pl.ds(0, LP)],
            lambda ref, n: ref.at[:, pl.ds(0, n * LP)],
            span, (0, nd),
        )

    def query_move(forward):
        span = (nd - nq, nd)
        if forward:
            return Send(
                0, 0,
                lambda ref, s, t: ref.at[
                    :, pl.ds(pl.multiple_of(q_from + (t - (nd - nq)) * LANE, LANE), LANE)
                ],
                lambda ref, s, t: ref.at[s, :, pl.ds(cap * LP, LANE)],
                lambda ref, n: ref.at[:, pl.ds(0, n * LANE)],
                lambda ref, n: ref.at[pl.ds(0, n), :, pl.ds(0, LANE)],
                (0, nd), span,
            )
        return Send(
            0, 0,
            lambda ref, s, t: ref.at[t, :, pl.ds(cap * LP, LANE)],
            lambda ref, s, t: ref.at[
                :, pl.ds(pl.multiple_of(q_from + (s - (nd - nq)) * LANE, LANE), LANE)
            ],
            lambda ref, n: ref.at[pl.ds(0, n), :, pl.ds(0, LANE)],
            lambda ref, n: ref.at[:, pl.ds(0, n * LANE)],
            span, (0, nd),
        )

    mine, pos, w_up = exch(
        2,
        [got, pos_mine, up_mine],
        [((nd, rows_c, width), BF16), ((nd, rows_c, LP), BF16), ((nd, 2 * cols, ff_cols), BF16)],
        [passage_move(c, True) for c in range(cap)]
        + [query_move(True), send_all(1, 1, nd), send_blocks(2, 2, nd)],
    )
    live = jnp.concatenate(
        [jnp.broadcast_to(c * nd + me < n_valid, (LP,)) for c in range(cap)]
        + [jnp.broadcast_to(me >= nd - nq, (LANE,))]
    )
    mine = jnp.where(live, mine[:, :cols].reshape(D, width), 0)
    pos = pos[:, :cols].reshape(D, LP).astype(F32)
    w_up = w_up.reshape(nd, 2, cols, ff_cols).transpose(1, 0, 2, 3).reshape(2, D, ff_cols)
    w_down = shrink_weight.astype(BF16)
    w_in = lax.all_gather(attend_in.astype(BF16), AXES, axis=1, tiled=True)
    w_out = lax.all_gather(attend_out.astype(BF16), AXES, axis=1, tiled=True)

    fronts = []
    for c in range(cap):
        emb = mine[:, c * LP : (c + 1) * LP].astype(F32) + pos
        fronts.append(encode_front(emb, w_in[1], w_out[1], gains[1], bias[1], LP))
    emb = mine[:, cap * LP :].astype(F32) + pos[:, :LANE]
    fronts.append(encode_front(emb, w_in[0], w_out[0], gains[0], bias[0], LQ))
    (rows,) = exch(
        3, [jnp.stack([f[0] for f in fronts])], [((nd, cap + 1, D), F32)], [send_all(0, 0, nd)]
    )
    row_in = (rows[nd - nq :, cap], rows[:, :cap].transpose(1, 0, 2).reshape(rows_p, D))

    def by_owner(queries, passages):
        q_part = jnp.pad(queries, ((nd - nq, 0), (0, 0)))[:, None]
        return jnp.concatenate([passages.reshape(cap, nd, D).transpose(1, 0, 2), q_part], axis=1)

    def to_rows(blocks):
        return (
            blocks[nd - nq :, cap],
            blocks[:, :cap].transpose(1, 0, 2).reshape(rows_p, D),
        )


    mids, ups = [], []
    partial_y = []
    b_in_all = bias[:, O_IN : O_IN + FF].reshape(2, nd, ff_cols)
    b_in = lax.dynamic_index_in_dim(b_in_all, me, 1, False)
    for e in range(2):
        h, hat1, scale1 = norm_rows(row_in[e], gains[e, 1], bias[e, O_1 : O_1 + D])
        h_low = h.astype(BF16)
        upper = dot(h_low, w_up[e], ((1,), (0,))) + b_in[e]
        active, slope = gelu_both(upper)
        f_low = active.astype(BF16)
        partial_y.append(dot(f_low, w_down[e], ((1,), (0,))))
        mids.append((h, hat1, scale1, h_low))
        ups.append((f_low, slope))
    (y_parts,) = exch(
        4, [by_owner(*partial_y)], [((nd, cap + 1, D), F32)], [send_blocks(0, 0, nd)]
    )
    (y_all,) = exch(
        5, [jnp.sum(y_parts, axis=0)], [((nd, cap + 1, D), F32)], [send_all(0, 0, nd)]
    )
    y = to_rows(y_all)
    tops = []
    vecs = []
    for e in range(2):
        z, hat2, scale2 = norm_rows(
            mids[e][0] + y[e] + bias[e, O_OUT : O_OUT + D], gains[e, 2], bias[e, O_2 : O_2 + D]
        )
        tops.append((hat2, scale2))
        vecs.append(z.astype(BF16))
    qvec, pvec = vecs

    owner = passage_query[:rows_p]
    kept = kept_mask[:rows_p] == 1
    earlier = jnp.concatenate([jnp.full((1,), -1, jnp.int32), owner[:-1]])
    valid = owner >= 0
    first = valid & (owner != earlier)
    member = owner[None, :] == jnp.arange(nq, dtype=jnp.int32)[:, None]
    positive = member & first[None, :]
    negative = member & jnp.logical_not(first)[None, :] & kept[None, :]
    counts = jnp.sum(member.astype(F32), axis=1) - 1.0
    score_scale = 2.0 * D ** (-0.5)
    scores = dot(qvec, pvec, ((1,), (1,))) * score_scale
    masked = jnp.where(valid[None, :], scores, -1e30)
    peak = jnp.max(masked, axis=1)
    summed = jnp.sum(jnp.where(valid[None, :], jnp.exp(masked - peak[:, None]), 0.0), axis=1)
    logsum = peak + jnp.log(summed)
    pos_score = jnp.sum(jnp.where(positive, scores, 0.0), axis=1)
    margins = MARGIN - pos_score[:, None] + scores
    active_neg = negative & (margins > 0)
    hinge = jnp.sum(jnp.where(active_neg, margins, 0.0), axis=1) / counts
    active_total = jnp.sum(active_neg.astype(F32), axis=1)
    loss = jnp.sum(logsum - pos_score + hinge)
    score_grad = (
        jnp.where(valid[None, :], jnp.exp(scores - logsum[:, None]), 0.0)
        - positive.astype(F32) * (1.0 + active_total / counts)[:, None]
        + active_neg.astype(F32) / counts[:, None]
    )
    score_low = score_grad.astype(BF16)
    vec_grads = (
        (dot(score_low, pvec, ((1,), (0,))) * score_scale).astype(BF16).astype(F32),
        (dot(score_low, qvec, ((0,), (0,))) * score_scale).astype(BF16).astype(F32),
    )

    partial_h = []
    gain_grads = [[None] * 3 for _ in range(2)]
    shifts = [dict() for _ in range(2)]
    top_grads, shrink_grads, du_parts = [], [], []
    for e in range(2):
        hat2, scale2 = tops[e]
        gain_grads[e][2] = jnp.sum(vec_grads[e] * hat2, axis=0)
        shifts[e]["2"] = jnp.sum(vec_grads[e], axis=0)
        g_top = norm_rows_back(vec_grads[e], gains[e, 2], hat2, scale2)
        dy = g_top.astype(BF16)
        shifts[e]["out"] = jnp.sum(dy.astype(F32), axis=0)
        f_low, slope = ups[e]
        shrink_grads.append(dot(f_low, dy, ((0,), (0,))))
        df = dot(dy, w_down[e], ((1,), (1,)))
        du = (slope * df).astype(BF16)
        du_parts.append(du)
        partial_h.append(dot(du, w_up[e], ((1,), (1,))))
        top_grads.append(g_top)
    du_mine = jnp.concatenate(du_parts)
    h_parts, du_all = exch(
        6,
        [by_owner(*partial_h), du_mine],
        [((nd, cap + 1, D), F32), ((nd, nq + rows_p, ff_cols), BF16)],
        [send_blocks(0, 0, nd), send_all(1, 1, nd)],
    )
    h_mine = jnp.sum(h_parts, axis=0)
    top_mine = lax.dynamic_index_in_dim(by_owner(*top_grads), me, 0, False)
    rows_mine = lax.dynamic_index_in_dim(rows, me, 0, False)
    is_q = (me >= nd - nq).astype(F32)
    has = jnp.stack([(c * nd + me < n_valid).astype(F32) for c in range(cap)] + [is_q])
    g_h = (top_mine + h_mine) * has[:, None]
    gain_one = jnp.stack([gains[1, 1]] * cap + [gains[0, 1]])
    shift_one = jnp.stack([bias[1, O_1 : O_1 + D]] * cap + [bias[0, O_1 : O_1 + D]])
    _, hat_mine, scale_mine = norm_rows(rows_mine, gain_one, shift_one)
    g_mid = norm_rows_back(g_h, gain_one, hat_mine, scale_mine)
    gain_mid = g_h * hat_mine
    do_mine = g_mid.astype(BF16)
    backs = [
        encode_back(
            fronts[c][1], g_mid[c], w_in[1 if c < cap else 0], w_out[1 if c < cap else 0],
            gains[1 if c < cap else 0],
        )
        for c in range(cap + 1)
    ]

    def both_encoders(pick):
        return jnp.stack([pick(cap), sum(pick(c) for c in range(cap))])

    sums = jnp.concatenate(
        [both_encoders(lambda i, j=j: backs[i][1][j]) for j in (5, 6, 7)]
        + [both_encoders(lambda i: gain_mid[i]), both_encoders(lambda i: g_h[i])]
    )
    line = jnp.concatenate(
        [jnp.stack([b[1][j] for b in backs]) for j in (2, 3, 4)] + [do_mine, sums.astype(BF16)]
    )
    n_line = 4 * (cap + 1) + 10
    factor_t = jnp.concatenate(
        [b[1][0] for b in backs] + [b[1][1] for b in backs]
        + [f[1][2][:, 0][None] for f in fronts] + [f[1][8][None] for f in fronts]
    )
    n_factor = factor_t.shape[0]
    f_pad = -(-n_factor // LANE) * LANE
    factor_cols = jnp.pad(factor_t, ((0, f_pad - n_factor), (0, 0))).T

    def pad_rows(value):
        value = value.reshape(nd, cols, value.shape[1])
        return jnp.pad(value, ((0, 0), (0, rows_c - cols), (0, 0)))

    send = pad_rows(jnp.concatenate([b[0] for b in backs], axis=1).astype(BF16))
    token_grads, factors, lines = exch(
        7,
        [send, pad_rows(factor_cols), line],
        [
            ((rows_c, n_valid * LP + nq * LANE), BF16),
            ((nd, rows_c, f_pad), BF16),
            ((nd, n_line, D), BF16),
        ],
        [passage_move(c, False) for c in range(cap)]
        + [query_move(False), send_blocks(1, 1, nd), send_all(2, 2, nd)],
    )
    table_grad = table_sums(token_grads, all_ids, total)[:cols, :vocab]
    token_grads = token_grads[:cols].astype(F32)
    pos_grad = jnp.sum(token_grads[:, :q_from].reshape(cols, n_valid, LP), axis=1)
    pos_grad = pos_grad.at[:, :LANE].add(
        jnp.sum(token_grads[:, q_from:].reshape(cols, nq, LANE), axis=1)
    )
    table_grad = table_grad.at[:, V:].add(pos_grad)

    step_h = (cap + 1) * H
    factors = factors[:, :cols].transpose(0, 2, 1)
    t_all = factors[:, :step_h].reshape(nd, cap + 1, H, cols)
    w_all = factors[:, step_h : 2 * step_h].reshape(nd, cap + 1, H, cols)
    x_all = factors[:, 2 * step_h : 2 * step_h + cap + 1]
    a_all = factors[:, 2 * step_h + cap + 1 : 2 * step_h + 2 * (cap + 1)]
    q_all, da_all, dq_all, do_all = (
        lines[:, j * (cap + 1) : (j + 1) * (cap + 1)] for j in range(4)
    )
    sums = jnp.sum(lines[:, 4 * (cap + 1) :].astype(F32), axis=0).reshape(5, 2, D)

    def of_encoder(value, e):
        if e == 0:
            return value[nd - nq :, cap]
        return value[:, :cap].reshape((nd * cap,) + value.shape[2:])

    du_all = du_all.transpose(1, 0, 2).reshape(nq + rows_p, FF)
    in_grads, out_grads, expand_grads = [], [], []
    for e in range(2):
        du_full = du_all[:nq] if e == 0 else du_all[nq:]
        shifts[e]["in"] = jnp.sum(du_full.astype(F32), axis=0)
        h_cols = lax.dynamic_slice_in_dim(mids[e][3], me * cols, cols, 1)
        expand_grads.append(dot(h_cols, du_full, ((0,), (0,))))
        t, w, x, a = (of_encoder(u, e) for u in (t_all, w_all, x_all, a_all))
        q, da, dq, do = (of_encoder(u, e) for u in (q_all, da_all, dq_all, do_all))
        rows_e = q.shape[0]
        qh = q.reshape(rows_e, H, HD)
        dah = da.reshape(rows_e, H, HD)
        g_q = dot(x, dq, ((0,), (0,)))
        g_k = jnp.einsum("phi,phd->ihd", t, qh, preferred_element_type=F32).reshape(cols, D)
        g_v = jnp.einsum("phi,phd->ihd", w, dah, preferred_element_type=F32).reshape(cols, D)
        in_grads.append(jnp.concatenate([g_q, g_k, g_v], axis=1))
        out_grads.append(dot(a, do, ((0,), (0,))))
        shifts[e]["q"] = jnp.sum(dq.astype(F32), axis=0)
        shifts[e]["o"] = jnp.sum(do.astype(F32), axis=0)
    gain_grad = jnp.stack(
        [jnp.stack([sums[1, e], sums[3, e], gain_grads[e][2]]) for e in range(2)]
    )
    bias_grad = jnp.stack(
        [
            jnp.concatenate(
                [shifts[e]["q"], sums[0, e], shifts[e]["o"], sums[4, e], shifts[e]["in"],
                 shifts[e]["out"], shifts[e]["2"], sums[2, e]]
            )
            for e in range(2)
        ]
    )
    grads = (
        table_grad.T,
        jnp.stack(in_grads),
        jnp.stack(out_grads),
        jnp.stack(expand_grads),
        jnp.stack(shrink_grads),
        lax.dynamic_slice_in_dim(gain_grad, me * cols, cols, 2),
        lax.dynamic_slice_in_dim(bias_grad, me * bias_terms.shape[1], bias_terms.shape[1], 1),
    )
    local_squares = sum(jnp.sum(g * g) for g in grads)
    (squares,) = exch(
        8, [jnp.broadcast_to(local_squares, (8, LANE))], [((nd, 8, LANE), F32)],
        [send_all(0, 0, nd)],
    )
    grad_norm = jnp.sqrt(jnp.sum(squares[:, 0, 0]))
    factor = CLIP / jnp.maximum(grad_norm, CLIP)
    step = step_count[0].astype(F32)
    masters = (embed_table, attend_in, attend_out, expand_weight, shrink_weight, norm_gains, bias_terms)
    firsts = (embed_first, attend_in_first, attend_out_first, expand_first, shrink_first, gains_first, bias_first)
    seconds = (embed_second, attend_in_second, attend_out_second, expand_second, shrink_second, gains_second, bias_second)
    results = [loss, grad_norm]
    for index in range(7):
        results.extend(
            adam_update(masters[index], grads[index] * factor, firsts[index], seconds[index], step, LEARN_RATES[index])
        )
    return tuple(results)


def on_device(
    passage_ids, query_ids, passage_query, kept_mask, neg_count, step_count,
    embed_table, attend_in, attend_out, expand_weight, shrink_weight, norm_gains, bias_terms,
    embed_first, embed_second, attend_in_first, attend_in_second,
    attend_out_first, attend_out_second, expand_first, expand_second,
    shrink_first, shrink_second, gains_first, gains_second, bias_first, bias_second,
):
    if embed_table.shape[1] % 8 != 0 or lax.axis_size("narrow") != 4 or lax.axis_size("wide") != 8 or passage_ids.shape[0] != 2:
        return on_device_rows(
            passage_ids, query_ids, passage_query, kept_mask, neg_count, step_count,
            embed_table, attend_in, attend_out, expand_weight, shrink_weight, norm_gains,
            bias_terms, embed_first, embed_second, attend_in_first, attend_in_second,
            attend_out_first, attend_out_second, expand_first, expand_second,
            shrink_first, shrink_second, gains_first, gains_second, bias_first, bias_second,
        )
    narrow = lax.axis_size("narrow")
    nd = lax.axis_size("wide") * narrow
    me = lax.axis_index("wide") * narrow + lax.axis_index("narrow")
    cols = embed_table.shape[1]
    n_slots = passage_query.shape[0]
    per_wide = query_ids.shape[0]
    nq = per_wide * lax.axis_size("wide")
    n_valid = VALID_PER_QUERY * nq
    cap = -(-n_valid // nd)
    ff_cols = FF // nd
    rows = n_valid + nq
    tq = nq * LQ
    query_home = nd * 5 // 8 - 1
    exch = functools.partial(comm, nd=nd, narrow=narrow)
    small_width = -(-max(cols, bias_terms.shape[1]) // LANE) * LANE
    ids_width = max(LP, -(-tq // LANE) * LANE)

    def widen(value, width):
        return jnp.pad(value, ((0, 0), (0, width - value.shape[1])))

    spot = jnp.arange(tq) // (LQ * per_wide) == lax.axis_index("wide")
    spot = spot & (lax.axis_index("narrow") == 0)
    q_line = jnp.where(spot, jnp.tile(query_ids.reshape(-1), tq // (LQ * per_wide)), 0)
    ids_mine = jnp.concatenate([widen(passage_ids, ids_width), widen(q_line[None], ids_width)])
    small_mine = jnp.concatenate(
        [widen(norm_gains.reshape(6, cols), small_width), widen(bias_terms, small_width)]
    ).astype(BF16)
    n_own = passage_ids.shape[0]
    table_t = embed_table.T
    ids_got, small_got, mine, mine_q, w_one, w_zero = first(
        n_valid, nq, nd, narrow, cols, query_home,
        [ids_mine, small_mine, table_t, attend_in, attend_out, table_t[:, V : V + LP]],
        FORWARD_PLAN,
    )
    w_one = w_one.reshape(D, 4 * D + LP)
    w_zero = w_zero.reshape(D, 4 * D)
    pid = ids_got[:, :n_own, :LP].reshape(n_slots, LP)[:n_valid]
    qid = jnp.sum(ids_got[:, n_own, :tq], axis=0)
    gains = small_got[:, :6, :cols].transpose(1, 0, 2).reshape(2, 3, D).astype(F32)
    bias = small_got[:, 6:, : bias_terms.shape[1]].transpose(1, 0, 2).reshape(2, -1).astype(F32)

    vocab = V + LP
    total = -(-vocab // HASH) * HASH
    up_mine = expand_weight.astype(BF16).reshape(2, cols, nd, ff_cols).transpose(2, 0, 1, 3)
    up_mine = jnp.pad(up_mine, ((0, 0), (0, 0), (0, 0), (0, LANE - ff_cols)))
    w_down = jnp.pad(shrink_weight.astype(BF16), ((0, 0), (0, LANE - ff_cols), (0, 0)))
    cv = jnp.stack(
        [v for e in range(2) for v in (
            gains[e, 0], bias[e, O_EMB : O_EMB + D], bias[e, O_V : O_V + D])]
        + [jnp.zeros((D,), F32)] * 2,
        axis=1,
    )
    rv = jnp.stack(
        [v for e in range(2) for v in (
            bias[e, O_Q : O_Q + D], bias[e, O_O : O_O + D], bias[e, O_1 : O_1 + D],
            bias[e, O_OUT : O_OUT + D], bias[e, O_2 : O_2 + D], gains[e, 1], gains[e, 2],
            jnp.zeros((D,), F32))]
    )
    b_in = lax.dynamic_index_in_dim(
        bias[:, O_IN : O_IN + FF].reshape(2, nd, ff_cols), me, 1, False
    )
    b_in = jnp.pad(b_in, ((0, 6), (0, LANE - ff_cols)))
    earlier = jnp.concatenate([jnp.full((1,), -1, jnp.int32), passage_query[:-1]])
    first_slot = ((passage_query >= 0) & (passage_query != earlier)).astype(jnp.int32)
    slots = jnp.pad(
        jnp.stack([passage_query, first_slot, kept_mask])[:, :n_valid],
        ((0, 5), (0, -(-n_valid // LANE) * LANE - n_valid)),
    )
    shrink_g, loss, g_table, g_in, g_out, g_up, g_bin, g_small, norm = middle(
        n_valid, nq, nd, narrow, cols, query_home,
        [mine, mine_q, w_one, w_zero, up_mine, w_down, cv, rv, b_in, slots,
         pid.reshape(n_valid, 1, LP), qid.reshape(1, tq)],
    )
    loss = loss[0, 0]
    grad_norm = norm[0, 0]
    g_small = g_small.reshape(2, 16, D)
    g_bin = g_bin[:2].reshape(2, 2, nd // 2, LANE)[..., :ff_cols]
    g_bin = g_bin.transpose(0, 2, 1, 3).reshape(2, FF)
    g_up = g_up.reshape(2, cols, 2, nd // 2, LANE)[..., :ff_cols].transpose(0, 1, 3, 2, 4)
    bias_grad = jnp.concatenate(
        [g_small[:, :4].reshape(2, 4 * D), g_bin, g_small[:, 4:7].reshape(2, 3 * D)], axis=1
    )
    grads = (
        g_table[:, : V + LP].T,
        g_in,
        g_out,
        g_up.reshape(2, cols, FF),
        shrink_g[:, :ff_cols],
        lax.dynamic_slice_in_dim(g_small[:, 7:10], me * cols, cols, 2),
        lax.dynamic_slice_in_dim(bias_grad, me * bias_terms.shape[1], bias_terms.shape[1], 1),
    )
    factor = CLIP / jnp.maximum(grad_norm, CLIP)
    step = step_count[0].astype(F32)
    masters = (embed_table, attend_in, attend_out, expand_weight, shrink_weight, norm_gains, bias_terms)
    firsts = (embed_first, attend_in_first, attend_out_first, expand_first, shrink_first, gains_first, bias_first)
    seconds = (embed_second, attend_in_second, attend_out_second, expand_second, shrink_second, gains_second, bias_second)
    results = [loss, grad_norm]
    for index in range(7):
        results.extend(
            adam_update(masters[index], grads[index] * factor, firsts[index], seconds[index], step, LEARN_RATES[index])
        )
    return tuple(results)


def solution(mesh):
    both = ("wide", "narrow")
    weight_specs = (P(None, both),) + (P(None, both, None),) * 4 + (P(None, None, both), P(None, both))
    pairs = tuple(s for spec in weight_specs for s in (spec, spec))
    in_specs = (P(both, None), P("wide", None), P(), P(), P("wide"), P()) + weight_specs + pairs
    out_specs = (P(), P()) + tuple(s for spec in weight_specs for s in (spec, spec, spec))
    return jax.shard_map(on_device, mesh=mesh, in_specs=in_specs, out_specs=out_specs, check_vma=False)
```

```python
import functools

import jax
import jax.numpy as jnp
from jax import lax
from jax.experimental import pallas as pl
from jax.experimental.pallas import tpu as pltpu
from jax.sharding import PartitionSpec as P

D = 768
H = 12
HD = 64
FF = 3072
V = 18000
LP = 384
LQ = 32
LANE = 128
VALID_PER_QUERY = 5

MARGIN = 1.0
CLIP = 1.0
BETA_ONE = 0.9
BETA_TWO = 0.999
LEARN_RATES = (1.0, 0.02, 0.08, 0.02, 0.02, 1.0, 0.1)
WEIGHT_DECAY = 0.01
ADAM_EPS = 1e-08
NORM_EPS = 1e-05
AXES = ("wide", "narrow")
F32 = jnp.float32
BF16 = jnp.bfloat16
O_Q, O_V, O_O, O_1, O_IN, O_OUT, O_2, O_EMB = (
    0, D, 2 * D, 3 * D, 4 * D, 4 * D + FF, 5 * D + FF, 6 * D + FF
)


def dot(left, right, dims):
    return lax.dot_general(left, right, (dims, ((), ())), preferred_element_type=F32)


def norm_rows(values, gain, shift):
    center = values - jnp.mean(values, axis=-1, keepdims=True)
    spread = jnp.mean(center * center, axis=-1, keepdims=True)
    scale = lax.rsqrt(spread + NORM_EPS)
    hat = center * scale
    return hat * gain + shift, hat, scale


def norm_rows_back(grad, gain, hat, scale):
    scaled = grad * gain
    mean_one = jnp.mean(scaled, axis=-1, keepdims=True)
    mean_two = jnp.mean(scaled * hat, axis=-1, keepdims=True)
    return scale * (scaled - mean_one - hat * mean_two)


def gelu_both(upper):
    cdf = 0.5 * (1.0 + lax.erf(upper * 0.7071067811865476))
    pdf = jnp.exp(-0.5 * upper * upper) * 0.3989422804014327
    return upper * cdf, cdf + upper * pdf


def adam_update(weight, grad, first, second, step, rate):
    first_new = BETA_ONE * first + (1.0 - BETA_ONE) * grad
    second_new = BETA_TWO * second + (1.0 - BETA_TWO) * grad * grad
    first_hat = first_new / (1.0 - BETA_ONE**step)
    second_hat = second_new / (1.0 - BETA_TWO**step)
    weight_new = weight - rate * (
        first_hat / (jnp.sqrt(second_hat) + ADAM_EPS) + WEIGHT_DECAY * weight
    )
    return (weight_new, first_new, second_new)


MESH = pl.DeviceIdType.MESH
HASH = 512
FORWARD_PLAN = (0, 4, 7, 10, 12, 13, 14, 15) + (99,) * 8


class Send:
    def __init__(self, src, dst, take, put, many_src, many_dst, sources, targets):
        self.src, self.dst, self.take, self.put = src, dst, take, put
        self.many_src, self.many_dst = many_src, many_dst
        self.sources, self.targets = sources, targets


def inside(index, span):
    return jnp.logical_and(index >= span[0], index < span[1])


def comm_body(sends, n_in, n_out, nd, narrow, *refs):
    ins, outs = refs[:n_in], refs[n_in : n_in + n_out]
    send_sem, recv_sem, own_sem = refs[n_in + n_out :]
    me = lax.axis_index("wide") * narrow + lax.axis_index("narrow")
    barrier = pltpu.get_barrier_semaphore()

    def greet(k, carry):
        t = lax.rem(me + k, nd)
        pl.semaphore_signal(
            barrier, inc=1, device_id=(t // narrow, lax.rem(t, narrow)), device_id_type=MESH
        )
        return carry

    lax.fori_loop(1, nd, greet, 0)
    pl.semaphore_wait(barrier, nd - 1)

    def push(k, carry):
        t = lax.rem(me + k, nd)
        for i, s in enumerate(sends):

            @pl.when(jnp.logical_and(inside(me, s.sources), inside(t, s.targets)))
            def _():
                pltpu.make_async_remote_copy(
                    src_ref=s.take(ins[s.src], me, t),
                    dst_ref=s.put(outs[s.dst], me, t),
                    send_sem=send_sem.at[i],
                    recv_sem=recv_sem.at[i],
                    device_id=(t // narrow, lax.rem(t, narrow)),
                    device_id_type=MESH,
                ).start()

        return carry

    lax.fori_loop(1, nd, push, 0)
    for i, s in enumerate(sends):
        both = jnp.logical_and(inside(me, s.sources), inside(me, s.targets))

        @pl.when(both)
        def _():
            own = pltpu.make_async_copy(
                s.take(ins[s.src], me, me), s.put(outs[s.dst], me, me), own_sem.at[i]
            )
            own.start()
            own.wait()

    for i, s in enumerate(sends):
        n_t = s.targets[1] - s.targets[0]
        n_s = s.sources[1] - s.sources[0]
        is_s, is_t = inside(me, s.sources), inside(me, s.targets)
        for own in (0, 1):
            mine = is_t if own else jnp.logical_not(is_t)
            if n_t - own > 0:

                @pl.when(jnp.logical_and(is_s, mine))
                def _():
                    view = s.many_src(ins[s.src], n_t - own) if s.many_src(ins[s.src], 1) is not None else outs[s.dst].at[pl.ds(0, n_t - own)]
                    pltpu.make_async_copy(view, view, send_sem.at[i]).wait()

            mine = is_s if own else jnp.logical_not(is_s)
            if n_s - own > 0:

                @pl.when(jnp.logical_and(is_t, mine))
                def _():
                    view = s.many_dst(outs[s.dst], n_s - own)
                    pltpu.make_async_copy(view, view, recv_sem.at[i]).wait()


def comm(collective, arrays, out_shapes, sends, nd, narrow):
    vmem = pl.BlockSpec(memory_space=pltpu.VMEM)
    n = len(sends)
    return pl.pallas_call(
        functools.partial(comm_body, sends, len(arrays), len(out_shapes), nd, narrow),
        out_shape=[jax.ShapeDtypeStruct(s, d) for s, d in out_shapes],
        in_specs=[vmem] * len(arrays),
        out_specs=[vmem] * len(out_shapes),
        scratch_shapes=[
            pltpu.SemaphoreType.DMA((n,)),
            pltpu.SemaphoreType.DMA((n,)),
            pltpu.SemaphoreType.DMA((n,)),
        ],
        compiler_params=pltpu.CompilerParams(collective_id=collective, has_side_effects=True),
    )(*arrays)


def send_all(src, dst, nd):
    return Send(
        src, dst,
        lambda ref, s, t: ref,
        lambda ref, s, t: ref.at[s],
        lambda ref, n: None, lambda ref, n: ref.at[pl.ds(0, n)],
        (0, nd), (0, nd),
    )


def send_blocks(src, dst, nd):
    return Send(
        src, dst,
        lambda ref, s, t: ref.at[t],
        lambda ref, s, t: ref.at[s],
        lambda ref, n: ref.at[pl.ds(0, n)], lambda ref, n: ref.at[pl.ds(0, n)],
        (0, nd), (0, nd),
    )


def stack_pairs(pieces, store):
    rows = pieces[0].shape[0]
    for i in range(0, len(pieces), 2):
        store(i * rows, jnp.concatenate(pieces[i : i + 2], axis=0))


def gather_body(rows, blocks, table_ref, ids_ref, out_ref, stacked):
    @pl.when(pl.program_id(0) == 0)
    def _():
        pieces = [
            table_ref[:, b * HASH : (b + 1) * HASH].astype(F32) for b in range(blocks)
        ]

        def store(row, value):
            stacked[row : row + value.shape[0], :] = value.astype(BF16)

        stack_pairs(pieces, store)

    ids = ids_ref[0]
    low = ids & (HASH - 1)
    high = ids >> (HASH.bit_length() - 1)
    width = ids.shape[1]
    hot = (lax.broadcasted_iota(jnp.int32, (HASH, width), 0) == low).astype(F32).astype(BF16)
    picked = jnp.dot(stacked[...], hot, preferred_element_type=F32)
    value = jnp.zeros((rows, width), F32)
    for b in range(blocks):
        value = jnp.where(high == b, picked[b * rows : (b + 1) * rows], value)
    out_ref[...] = value.astype(BF16)


def table_rows(table, ids):
    rows, total = table.shape
    tokens = ids.shape[0]
    tile = 512
    blocks = total // HASH
    return pl.pallas_call(
        functools.partial(gather_body, rows, blocks),
        grid=(tokens // tile,),
        out_shape=jax.ShapeDtypeStruct((rows, tokens), BF16),
        in_specs=[
            pl.BlockSpec((rows, total), lambda i: (0, 0)),
            pl.BlockSpec((1, 1, tile), lambda i: (i, 0, 0)),
        ],
        out_specs=pl.BlockSpec((rows, tile), lambda i: (0, i)),
        scratch_shapes=[pltpu.VMEM((blocks * rows, HASH), BF16)],
        name="table_rows",
    )(table, ids.reshape(tokens // tile, 1, tile))


def scatter_body(rows, blocks, values_ref, ids_ref, out_ref, spread, acc):
    step = pl.program_id(0)
    ids = ids_ref[0]
    low = ids & (HASH - 1)
    high = ids >> (HASH.bit_length() - 1)
    width = ids.shape[1]
    values = values_ref[...].astype(F32)
    pieces = [jnp.where(high == b, values, 0.0) for b in range(blocks)]

    def store(row, value):
        spread[row : row + value.shape[0], :] = value.astype(BF16)

    stack_pairs(pieces, store)
    hot = (lax.broadcasted_iota(jnp.int32, (HASH, width), 0) == low).astype(F32).astype(BF16)
    part = lax.dot_general(
        spread[...], hot, (((1,), (1,)), ((), ())), preferred_element_type=F32
    )

    @pl.when(step == 0)
    def _():
        acc[...] = part

    @pl.when(step > 0)
    def _():
        acc[...] += part

    @pl.when(step == pl.num_programs(0) - 1)
    def _():
        for b in range(blocks):
            out_ref[:, b * HASH : (b + 1) * HASH] = acc[b * rows : (b + 1) * rows, :]


def table_sums(values, ids, total):
    rows, tokens = values.shape
    tile = 1024
    blocks = total // HASH
    return pl.pallas_call(
        functools.partial(scatter_body, rows, blocks),
        grid=(tokens // tile,),
        out_shape=jax.ShapeDtypeStruct((rows, total), F32),
        in_specs=[
            pl.BlockSpec((rows, tile), lambda i: (0, i)),
            pl.BlockSpec((1, 1, tile), lambda i: (i, 0, 0)),
        ],
        out_specs=pl.BlockSpec((rows, total), lambda i: (0, 0)),
        scratch_shapes=[
            pltpu.VMEM((blocks * rows, tile), BF16),
            pltpu.VMEM((blocks * rows, HASH), F32),
        ],
        name="table_sums",
    )(values, ids.reshape(tokens // tile, 1, tile))


def head_mask(dtype):
    rows = lax.broadcasted_iota(jnp.int32, (H, D), 0)
    cols = lax.broadcasted_iota(jnp.int32, (H, D), 1)
    return (cols // HD == rows).astype(dtype)


def spread_heads(row):
    return row[None, :] * head_mask(row.dtype)


def encode_front(emb_t, w_in, w_out, gain, bias, length):
    width = emb_t.shape[1]
    center = emb_t - jnp.mean(emb_t, axis=0, keepdims=True)
    spread = jnp.mean(center * center, axis=0, keepdims=True)
    scale = lax.rsqrt(spread + NORM_EPS)
    hat = center * scale
    x0 = hat * gain[0][:, None] + bias[O_EMB : O_EMB + D][:, None]
    x_low = x0.astype(BF16)
    first_low = x_low[:, 0]
    q = (dot(first_low[None], w_in[:, :D], ((1,), (0,)))[0] + bias[O_Q : O_Q + D]).astype(BF16)
    k = dot(w_in[:, D : 2 * D], x_low, ((0,), (0,))).astype(BF16)
    v = (
        dot(w_in[:, 2 * D :], x_low, ((0,), (0,))) + bias[O_V : O_V + D][:, None]
    ).astype(BF16)
    q_heads = spread_heads(q)
    s = dot(q_heads, k, ((1,), (0,))) * 0.125
    if length < width:
        live = lax.broadcasted_iota(jnp.int32, (1, width), 1) < length
        s = jnp.where(live, s, -1e30)
    peak = jnp.max(s, axis=1, keepdims=True)
    e = jnp.exp(s - peak)
    p = e / jnp.sum(e, axis=1, keepdims=True)
    p_low = p.astype(BF16)
    mixed = dot(p_low, v, ((1,), (1,)))
    a = jnp.sum(mixed * head_mask(F32), axis=0).astype(BF16)
    o = dot(a[None], w_out, ((1,), (0,)))[0] + bias[O_O : O_O + D]
    return x0[:, 0] + o, (hat, scale, x_low, q, k, v, p, p_low, a)


def encode_back(kept, row_grad, w_in, w_out, gain):
    hat, scale, x_low, q, k, v, p, p_low, a = kept
    do = row_grad.astype(BF16)
    da = dot(do[None], w_out, ((1,), (1,)))[0].astype(BF16)
    da_heads = spread_heads(da)
    q_heads = spread_heads(q)
    dp = dot(da_heads, v, ((1,), (0,)))
    ds = (p * (dp - jnp.sum(dp * p, axis=1, keepdims=True))).astype(BF16)
    dq_heads = dot(ds, k, ((1,), (1,)))
    dq = (jnp.sum(dq_heads * head_mask(F32), axis=0) * 0.125).astype(BF16)
    t = dot(ds, x_low, ((1,), (1,))) * 0.125
    w = dot(p_low, x_low, ((1,), (1,)))
    gk = (dot(q_heads, w_in[:, D : 2 * D], ((1,), (1,))) * 0.125).astype(BF16)
    ev = dot(da_heads, w_in[:, 2 * D :], ((1,), (1,))).astype(BF16)
    gx = dot(gk, ds, ((0,), (0,))) + dot(ev, p_low, ((0,), (0,)))
    first = row_grad + dot(dq[None], w_in[:, :D], ((1,), (1,)))[0]
    is_first = lax.broadcasted_iota(jnp.int32, (1, gx.shape[1]), 1) == 0
    gx = gx + jnp.where(is_first, first[:, None], 0.0)
    p_sum = jnp.sum(p_low.astype(F32), axis=1)
    dbv = jnp.repeat(p_sum, HD) * da.astype(F32)
    g_gain = jnp.sum(gx * hat, axis=1)
    g_shift = jnp.sum(gx, axis=1)
    scaled = gx * gain[0][:, None]
    mean_one = jnp.mean(scaled, axis=0, keepdims=True)
    mean_two = jnp.mean(scaled * hat, axis=0, keepdims=True)
    g_emb = scale * (scaled - mean_one - hat * mean_two)
    return g_emb, (t.astype(BF16), w.astype(BF16), q, da, dq, dbv, g_gain, g_shift)


NN = (((1,), (0,)), ((), ()))
NT = (((1,), (1,)), ((), ()))
TN = (((0,), (0,)), ((), ()))
HIGH = lax.Precision.HIGHEST


def mm(left, right, dims, precision=None):
    return lax.dot_general(
        left, right, dims, preferred_element_type=F32, precision=precision
    )


def iota(shape, dim):
    return lax.broadcasted_iota(jnp.int32, shape, dim)


def as_bf16(mask):
    return mask.astype(F32).astype(BF16)


def group(count, nd, first=0):
    return (first, nd // count, count)


def within(index, span):
    first, stride, count = span
    if count == 0:
        return index < 0
    if stride == 1:
        return jnp.logical_and(index >= first, index < first + count)
    return ((index - first) & (stride - 1)) == 0


def place(index, span):
    return (index - span[0]) >> (span[1].bit_length() - 1)


class Flow:
    def __init__(self, take, put, many, sources, targets):
        self.take, self.put, self.many = take, put, many
        self.sources, self.targets = sources, targets


class Net:
    def __init__(self, nd, narrow, send_sem, recv_sem, own_sem):
        self.nd, self.narrow = nd, narrow
        self.send_sem, self.recv_sem, self.own_sem = send_sem, recv_sem, own_sem
        self.me = lax.axis_index("wide") * narrow + lax.axis_index("narrow")
        self.used = 0

    def where(self, t):
        return (t >> (self.narrow.bit_length() - 1), t & (self.narrow - 1))

    def barrier(self):
        sem = pltpu.get_barrier_semaphore()

        def greet(k, carry):
            t = (self.me + k) & (self.nd - 1)
            pl.semaphore_signal(sem, inc=1, device_id=self.where(t), device_id_type=MESH)
            return carry

        lax.fori_loop(1, self.nd, greet, 0)
        pl.semaphore_wait(sem, self.nd - 1)

    def start(self, flows):
        me, nd = self.me, self.nd
        base = self.used
        self.used += len(flows)

        def push(k, carry):
            t = (me + k) & (nd - 1)
            for i, f in enumerate(flows):

                @pl.when(jnp.logical_and(within(me, f.sources), within(t, f.targets)))
                def _():
                    pltpu.make_async_remote_copy(
                        src_ref=f.take(me, t),
                        dst_ref=f.put(me, t),
                        send_sem=self.send_sem.at[base + i],
                        recv_sem=self.recv_sem.at[base + i],
                        device_id=self.where(t),
                        device_id_type=MESH,
                    ).start()

            return carry

        for i, f in enumerate(flows):

            @pl.when(jnp.logical_and(within(me, f.sources), within(me, f.targets)))
            def _():
                pltpu.make_async_copy(
                    f.take(me, me), f.put(me, me), self.own_sem.at[base + i]
                ).start()

        lax.fori_loop(1, nd, push, 0)
        return base

    def finish(self, flows, base):
        me = self.me
        for i, f in enumerate(flows):
            n_t, n_s = f.targets[2], f.sources[2]
            is_s, is_t = within(me, f.sources), within(me, f.targets)

            @pl.when(jnp.logical_and(is_s, is_t))
            def _():
                pltpu.make_async_copy(
                    f.take(me, me), f.put(me, me), self.own_sem.at[base + i]
                ).wait()

            for own in (0, 1):
                mine = is_s if own else jnp.logical_not(is_s)
                if n_s - own > 0:

                    @pl.when(jnp.logical_and(is_t, mine))
                    def _():
                        view = f.many(n_s - own)
                        pltpu.make_async_copy(view, view, self.recv_sem.at[base + i]).wait()

            for own in (0, 1):
                mine = is_t if own else jnp.logical_not(is_t)
                if n_t - own > 0:

                    @pl.when(jnp.logical_and(is_s, mine))
                    def _():
                        view = f.many(n_t - own)
                        pltpu.make_async_copy(view, view, self.send_sem.at[base + i]).wait()


class Unit:
    def __init__(self, count, length):
        self.count, self.length = count, length
        self.tokens = count * length
        self.bits = count.bit_length() - 1
        self.rows = max(16, H * count)
        self.seqs = max(8, count)

    def pick(self):
        lane = iota((self.seqs, self.tokens), 1)
        seq = iota((self.seqs, self.tokens), 0)
        return lane == seq * self.length

    def spread(self):
        row, seq = iota((self.rows, self.seqs), 0), iota((self.rows, self.seqs), 1)
        return as_bf16((row & (self.count - 1)) == seq)

    def collect(self):
        row, seq = iota((self.seqs, self.rows), 1), iota((self.seqs, self.rows), 0)
        return as_bf16((row & (self.count - 1)) == seq)

    def heads(self):
        row, col = iota((self.rows, D), 0), iota((self.rows, D), 1)
        return ((row >> self.bits) == (col >> 6)).astype(F32)

    def live(self):
        row, lane = iota((self.rows, self.tokens), 0), iota((self.rows, self.tokens), 1)
        return (lane >> 5) == (row & (self.count - 1))


def unit_front(unit, emb, e, w, cv, rv, keep):
    center = emb - jnp.mean(emb, axis=0, keepdims=True)
    spread = jnp.mean(center * center, axis=0, keepdims=True)
    scale = lax.rsqrt(spread + NORM_EPS)
    hat = center * scale
    x0 = hat * cv[:, 3 * e : 3 * e + 1] + cv[:, 3 * e + 1 : 3 * e + 2]
    x_low = x0.astype(BF16)
    pick = unit.pick()
    x_first = mm(as_bf16(pick), x_low, NT).astype(BF16)
    x0_first = mm(pick.astype(F32), x0, NT, HIGH)
    q = (mm(x_first, w[:, 0:D], NN) + rv[8 * e : 8 * e + 1, :]).astype(BF16)
    k = mm(w[:, D : 2 * D], x_low, TN).astype(BF16)
    v = (mm(w[:, 2 * D : 3 * D], x_low, TN) + cv[:, 3 * e + 2 : 3 * e + 3]).astype(BF16)
    heads = unit.heads()
    q_heads = (mm(unit.spread(), q, NN) * heads).astype(BF16)
    s = mm(q_heads, k, NN) * 0.125
    if unit.count > 1:
        s = jnp.where(unit.live(), s, -1e30)
    peak = jnp.max(s, axis=1, keepdims=True)
    ex = jnp.exp(s - peak)
    p = ex / jnp.sum(ex, axis=1, keepdims=True)
    mixed = (mm(p.astype(BF16), v, NT) * heads).astype(BF16)
    a = mm(unit.collect(), mixed, NN).astype(BF16)
    o = mm(a, w[:, 3 * D : 4 * D], NN) + rv[8 * e + 1 : 8 * e + 2, :]
    keep(hat, scale, x_low, x_first, q, k, v, p, a)
    return x0_first + o


def unit_back(unit, row_grad, e, w, cv, kept):
    hat, scale, x_low, x_first, q, k, v, p, a = kept
    heads = unit.heads()
    spread, collect = unit.spread(), unit.collect()
    p_low = p.astype(BF16)
    do = row_grad.astype(BF16)
    da = mm(do, w[:, 3 * D : 4 * D], NT).astype(BF16)
    q_heads = (mm(spread, q, NN) * heads).astype(BF16)
    da_heads = (mm(spread, da, NN) * heads).astype(BF16)
    dp = mm(da_heads, v, NN)
    ds = (p * (dp - jnp.sum(dp * p, axis=1, keepdims=True))).astype(BF16)
    dq_heads = (mm(ds, k, NT) * heads * 0.125).astype(BF16)
    dq = mm(collect, dq_heads, NN).astype(BF16)
    t = mm(ds, x_low, NT) * 0.125
    wx = mm(p_low, x_low, NT)
    gk = (mm(q_heads, w[:, D : 2 * D], NT) * 0.125).astype(BF16)
    ev = mm(da_heads, w[:, 2 * D : 3 * D], NT).astype(BF16)
    first = row_grad + mm(dq, w[:, 0:D], NT)
    gx = mm(gk, ds, TN) + mm(ev, p_low, TN)
    gx = gx + mm(first, unit.pick().astype(F32), TN, HIGH)
    p_sum = jnp.sum(p_low.astype(F32), axis=1, keepdims=True)
    dbv = jnp.sum(p_sum * da_heads.astype(F32), axis=0, keepdims=True)
    g_gain = jnp.sum(gx * hat, axis=1, keepdims=True)
    g_shift = jnp.sum(gx, axis=1, keepdims=True)
    scaled = gx * cv[:, 3 * e : 3 * e + 1]
    mean_one = jnp.mean(scaled, axis=0, keepdims=True)
    mean_two = jnp.mean(scaled * hat, axis=0, keepdims=True)
    g_emb = scale * (scaled - mean_one - hat * mean_two)
    return g_emb, t, wx, da, dq, do, dbv, g_gain, g_shift


def load_rows(ref, count):
    return jnp.concatenate(
        [ref[pl.ds(j, count, stride=8), :] for j in range(D // LANE)], axis=1
    )


def store_rows(ref, value):
    for j in range(D // LANE):
        ref[pl.ds(j, value.shape[0], stride=8), :] = value[:, j * LANE : (j + 1) * LANE]


def middle_body(
    n_valid, nq, nd, narrow, cols, query_home,
    mine, mine_q, w_one, w_zero, up_mine, shrink, small, slots, ids,
    o_shrink, o_loss, g_table, g_in, g_out, g_up, g_bin, g_small, o_norm,
    hat_s, scale_s, xl_s, xf_s, q_s, k_s, v_s, p_s, a_s,
    hat_q, scale_q, xl_q, xf_q, q_q, k_q, v_q, p_q, a_q,
    r1_own, r1_ownq, r1_all, y_send, y_recv, y_sum, y_all, h_send, h_recv, h_recvq,
    du_own, du_f, gtok, gtok_q, fac, fac_q, line, line_q, f_s, slope_s, hlow_s, g_top_s, sums_s,
    o_tok, o_fac, o_facq, o_line, o_lineq, o_du, o_h, up_got, w_up,
    t_all, w_all, q_exp, d_exp, spread_s, acc_s, norm_own, norm_all,
    w_down, bias_s, gain_s, rows_s, cv, rv, b_in,
    tok_send, tok_recv, twin_send, twin_recv, chain_send, chain_recv,
    send_sem, recv_sem, own_sem,
):
    cap = -(-n_valid // nd)
    rows = n_valid + nq
    net = Net(nd, narrow, send_sem, recv_sem, own_sem)
    me = net.me
    everyone = group(nd, nd)
    home = (query_home, 1, 1)
    q_owners = group(nq, nd, 2)
    core = me & 1
    alike = (core, 2, nd // 2)

    def span(c):
        return group(nd, nd) if c == 0 else group(n_valid - nd, nd, 1)

    def slot_of(c, d):
        return c * nd + place(d, span(c))

    net.barrier()
    passage = Unit(1, LP)
    queries = Unit(nq, LQ)
    n_mine = jnp.where(within(me, span(1)), 2, 1)

    up_flows = [
        Flow(
            lambda s, t: up_mine.at[t], lambda s, t: up_got.at[s],
            lambda n: up_got.at[pl.ds(0, n)], everyone, everyone,
        )
    ]
    up_base = net.start(up_flows)

    ff_cols = shrink.shape[1]
    bias_cols = (5 * D + FF + 2 * D) // nd
    bias_s[...] = jnp.zeros_like(bias_s)
    gain_s[...] = jnp.zeros_like(gain_s)
    span_b, span_g = small.shape[2] + LANE, 2 * LANE
    for d in range(nd):
        block = small[d].astype(F32)
        wide_block = jnp.concatenate([block, jnp.zeros((8, LANE), F32)], axis=1)
        at, turn = bias_cols * d // LANE * LANE, bias_cols * d % LANE
        bias_s[:, at : at + span_b] += pltpu.roll(wide_block, turn, 1) if turn else wide_block
        at, turn = cols * d // LANE * LANE, cols * d % LANE
        near = block[:, 0:span_g]
        gain_s[:, at : at + span_g] += pltpu.roll(near, turn, 1) if turn else near
    rows_s[...] = jnp.zeros_like(rows_s)
    w_down[...] = jnp.zeros_like(w_down)
    inner = pltpu.roll(bias_s[:, O_IN : O_IN + FF], jnp.where(me == 0, 0, FF - ff_cols * me), 1)
    inner = jnp.where(iota((8, LANE), 1) < ff_cols, inner[:, 0:LANE], 0.0)
    for e in range(2):
        for j, at in enumerate((O_Q, O_O, O_1, O_OUT, O_2)):
            rv[8 * e + j : 8 * e + j + 1, :] = bias_s[6 + e : 7 + e, at : at + D]
        for j in (1, 2):
            rv[8 * e + 4 + j : 8 * e + 5 + j, :] = gain_s[3 * e + j : 3 * e + j + 1, 0:D]
        rows_s[3 * e : 3 * e + 1, :] = gain_s[3 * e : 3 * e + 1, 0:D]
        rows_s[3 * e + 1 : 3 * e + 2, :] = bias_s[6 + e : 7 + e, O_EMB : O_EMB + D]
        rows_s[3 * e + 2 : 3 * e + 3, :] = bias_s[6 + e : 7 + e, O_V : O_V + D]
        b_in[e : e + 1, :] = inner[6 + e : 7 + e, :]
        w_down[e, 0:ff_cols, :] = shrink[e].astype(BF16)
    cv[...] = jnp.transpose(rows_s[...])

    def front(c, carry):
        at = pl.ds(pl.multiple_of(c * LP, LANE), LP)
        emb = mine[:, :, at].astype(F32).reshape(D, LP) + w_one[:, 4 * D :].astype(F32)

        def keep(hat, scale, x_low, x_first, q, k, v, p, a):
            hat_s[c], scale_s[c], xl_s[c], xf_s[c] = hat, scale, x_low, x_first
            q_s[c], k_s[c], v_s[c], p_s[c], a_s[c] = q, k, v, p, a

        r1 = unit_front(passage, emb, 1, w_one, cv, rv, keep)
        for j in range(D // LANE):
            r1_own[c, j : j + 1, :] = r1[0:1, j * LANE : (j + 1) * LANE]
        return carry

    lax.fori_loop(0, n_mine, front, 0)

    @pl.when(me == query_home)
    def _():
        parts = w_one[:, 4 * D : 4 * D + LANE].astype(F32)[:, 0:LQ]
        emb = mine_q[...].astype(F32).reshape(D, nq * LQ) + jnp.concatenate([parts] * nq, axis=1)

        def keep(hat, scale, x_low, x_first, q, k, v, p, a):
            hat_q[...], scale_q[...], xl_q[...], xf_q[...] = hat, scale, x_low, x_first
            q_q[...], k_q[...], v_q[...], p_q[...], a_q[...] = q, k, v, p, a

        store_rows(r1_ownq, unit_front(queries, emb, 0, w_zero, cv, rv, keep))

    flows = [
        Flow(
            lambda s, t, c=c: r1_own.at[c],
            lambda s, t, c=c: r1_all.at[pl.ds(pl.multiple_of(8 * slot_of(c, s), 8), 8), :],
            lambda n: r1_all.at[pl.ds(0, 8 * n), :],
            span(c), everyone,
        )
        for c in range(cap)
    ] + [
        Flow(
            lambda s, t: r1_ownq,
            lambda s, t: r1_all.at[pl.ds(8 * n_valid, 8 * nq), :],
            lambda n: y_recv_q(n),
            home, everyone,
        )
    ]

    def y_recv_q(n):
        return h_recvq.at[pl.ds(0, n)]

    base = net.start(flows)
    net.finish(flows, base)

    net.finish(up_flows, up_base)
    for e in range(2):
        w_up[e] = up_got[:, e].astype(F32).reshape(D, LANE).astype(BF16)

    part = {1: (0, n_valid), 0: (n_valid, nq)}
    y_parts = []
    for e in (1, 0):
        at, n = part[e]
        r1 = load_rows(r1_all.at[pl.ds(8 * at, 8 * n), :], n)
        h, hat1, scale1 = norm_rows(r1, rv[8 * e + 5 : 8 * e + 6, :], rv[8 * e + 2 : 8 * e + 3, :])
        h_low = h.astype(BF16)
        hlow_s[at : at + n, :] = h
        o_h[at : at + n, :] = h_low.astype(F32)
        upper = mm(h_low, w_up[e], NN) + b_in[e : e + 1, :]
        active, slope = gelu_both(upper)
        f_low = active.astype(BF16)
        f_s[at : at + n, :] = f_low.astype(F32)
        slope_s[at : at + n, :] = slope
        y_parts.append(mm(f_low, w_down[e], NN))
    store_rows(y_send, jnp.concatenate(y_parts, axis=0))
    flows = [
        Flow(
            lambda s, t, c=c: y_send.at[pl.ds(pl.multiple_of(8 * slot_of(c, t), 8), 8), :],
            lambda s, t, c=c: y_recv.at[s, c],
            lambda n, c=c: y_recv.at[pl.ds(0, n), c],
            everyone, span(c),
        )
        for c in range(cap)
    ] + [
        Flow(
            lambda s, t: y_send.at[pl.ds(pl.multiple_of(8 * (n_valid + place(t, q_owners)), 8), 8), :],
            lambda s, t: y_recv.at[s, cap],
            lambda n: y_recv.at[pl.ds(0, n), cap],
            everyone, q_owners,
        )
    ]
    base = net.start(flows)
    net.finish(flows, base)
    y_sum[...] = jnp.sum(y_recv[...], axis=0)
    flows = [
        Flow(
            lambda s, t, c=c: y_sum.at[c],
            lambda s, t, c=c: y_all.at[pl.ds(pl.multiple_of(8 * slot_of(c, s), 8), 8), :],
            lambda n: y_all.at[pl.ds(0, 8 * n), :],
            span(c), everyone,
        )
        for c in range(cap)
    ] + [
        Flow(
            lambda s, t: y_sum.at[cap],
            lambda s, t: y_all.at[pl.ds(pl.multiple_of(8 * (n_valid + place(s, q_owners)), 8), 8), :],
            lambda n: y_all.at[pl.ds(0, 8 * n), :],
            q_owners, everyone,
        )
    ]
    base = net.start(flows)
    net.finish(flows, base)

    tops, vecs = {}, {}
    for e in (1, 0):
        at, n = part[e]
        y = load_rows(y_all.at[pl.ds(8 * at, 8 * n), :], n)
        top = hlow_s[at : at + n, :] + y + rv[8 * e + 3 : 8 * e + 4, :]
        z, hat2, scale2 = norm_rows(
            top, rv[8 * e + 6 : 8 * e + 7, :], rv[8 * e + 4 : 8 * e + 5, :]
        )
        tops[e] = (hat2, scale2)
        vecs[e] = z.astype(BF16)
    qvec, pvec = vecs[0], vecs[1]
    owner = slots[0:1, 0:n_valid]
    is_first = slots[1:2, 0:n_valid] == 1
    kept_slot = slots[2:3, 0:n_valid] == 1
    member = owner == iota((nq, n_valid), 0)
    valid = jnp.broadcast_to(owner >= 0, (nq, n_valid))
    positive = jnp.logical_and(member, is_first)
    negative = jnp.logical_and(member, jnp.logical_and(jnp.logical_not(is_first), kept_slot))
    counts = jnp.sum(member.astype(F32), axis=1, keepdims=True) - 1.0
    score_scale = 2.0 * D ** (-0.5)
    scores = mm(qvec, pvec, NT) * score_scale
    masked = jnp.where(valid, scores, -1e30)
    peak = jnp.max(masked, axis=1, keepdims=True)
    summed = jnp.sum(jnp.where(valid, jnp.exp(masked - peak), 0.0), axis=1, keepdims=True)
    logsum = peak + jnp.log(summed)
    pos_score = jnp.sum(jnp.where(positive, scores, 0.0), axis=1, keepdims=True)
    margins = MARGIN - pos_score + scores
    active = jnp.logical_and(negative, margins > 0)
    hinge = jnp.sum(jnp.where(active, margins, 0.0), axis=1, keepdims=True) / counts
    active_total = jnp.sum(active.astype(F32), axis=1, keepdims=True)
    loss = jnp.sum(logsum - pos_score + hinge, axis=0, keepdims=True)
    o_loss[...] = jnp.broadcast_to(loss, (8, LANE))
    score_grad = (
        jnp.where(valid, jnp.exp(scores - logsum), 0.0)
        - positive.astype(F32) * (1.0 + active_total / counts)
        + active.astype(F32) / counts
    )
    score_low = score_grad.astype(BF16)
    vec_grads = {
        0: (mm(score_low, pvec, NN) * score_scale).astype(BF16).astype(F32),
        1: (mm(score_low, qvec, TN) * score_scale).astype(BF16).astype(F32),
    }
    h_parts, out_rows = [], {}
    for e in (1, 0):
        at, n = part[e]
        hat2, scale2 = tops[e]
        grad = vec_grads[e]
        g_top = norm_rows_back(grad, rv[8 * e + 6 : 8 * e + 7, :], hat2, scale2)
        dy = g_top.astype(BF16)
        g_top_s[at : at + n, :] = g_top
        out_rows[e] = [
            jnp.sum(grad * hat2, axis=0, keepdims=True),
            jnp.sum(grad, axis=0, keepdims=True),
            jnp.sum(dy.astype(F32), axis=0, keepdims=True),
        ]
        f_low = f_s[at : at + n, :].astype(BF16)
        o_shrink[e] = mm(f_low, dy, TN)
        df = mm(dy, w_down[e], NT)
        du = (slope_s[at : at + n, :] * df).astype(BF16)
        du_f[at : at + n, :] = du.astype(F32)
        h_parts.append(mm(du, w_up[e], NT))
    du_own[...] = du_f[...].astype(BF16)
    store_rows(h_send, jnp.concatenate(h_parts, axis=0))
    flows = [
        Flow(
            lambda s, t, c=c: h_send.at[pl.ds(pl.multiple_of(8 * slot_of(c, t), 8), 8), :],
            lambda s, t, c=c: h_recv.at[s, c],
            lambda n, c=c: h_recv.at[pl.ds(0, n), c],
            everyone, span(c),
        )
        for c in range(cap)
    ] + [
        Flow(
            lambda s, t: h_send.at[pl.ds(8 * n_valid, 8 * nq), :],
            lambda s, t: h_recvq.at[s],
            lambda n: h_recvq.at[pl.ds(0, n)],
            everyone, home,
        )
    ]
    du_flows = [
        Flow(
            lambda s, t: du_own,
            lambda s, t: o_du.at[
                :, pl.ds(pl.multiple_of(((s & 1) * (nd // 2) + (s >> 1)) * LANE, LANE), LANE)
            ],
            lambda n: o_du.at[:, pl.ds(0, n * LANE)],
            alike, alike,
        )
    ]
    base = net.start(flows)
    du_base = net.start(du_flows)
    fac[...] = jnp.zeros_like(fac)
    line[...] = jnp.zeros_like(line)
    sums_s[...] = jnp.zeros_like(sums_s)
    net.finish(flows, base)

    def load_rows_sum(ref, count):
        total = jnp.sum(ref[...], axis=0)
        h_send[0 : 8 * count, :] = total
        return load_rows(h_send.at[pl.ds(0, 8 * count), :], count)

    lane = iota((D, LANE), 1)

    def back(c, carry):
        slot = jnp.where(c == 0, me, slot_of(1, me))
        tile = jnp.sum(h_recv[:, c], axis=0)
        dh = jnp.concatenate([tile[j : j + 1, :] for j in range(D // LANE)], axis=1)
        top = g_top_s[pl.ds(slot, 1), :]
        g_h = top + dh
        r1 = jnp.concatenate([r1_own[c, j : j + 1, :] for j in range(D // LANE)], axis=1)
        gain1 = rv[8 + 5 : 8 + 6, :]
        _, hat1, scale1 = norm_rows(r1, gain1, gain1)
        g_mid = norm_rows_back(g_h, gain1, hat1, scale1)
        row_grad = jnp.where(iota((8, D), 0) == 0, jnp.broadcast_to(g_mid, (8, D)), 0.0)
        kept = (
            hat_s[c], scale_s[c], xl_s[c], xf_s[c], q_s[c], k_s[c], v_s[c], p_s[c], a_s[c]
        )
        g_emb, t, wx, da, dq, do, dbv, g_gain, g_shift = unit_back(
            passage, row_grad, 1, w_one, cv, kept
        )
        gtok[c] = g_emb.reshape(nd, cols, LP).astype(BF16)
        zero = jnp.zeros((16, D), F32)
        xa = jnp.concatenate(
            [xf_s[c].astype(F32)[0:1, :], jnp.zeros((15, D), F32), a_s[c].astype(F32)[0:1, :],
             jnp.zeros((31, D), F32)],
            axis=0,
        )
        tw = jnp.transpose(jnp.concatenate([t, zero, wx, zero, jnp.zeros((64, D), F32)], axis=0))
        xa = jnp.transpose(jnp.concatenate([jnp.zeros((64, D), F32), xa, zero], axis=0))
        placed = pltpu.roll(tw, 16 * c, 1) + pltpu.roll(xa, c, 1)
        fac[...] = (fac[...].astype(F32) + placed.reshape(nd, cols, LANE)).astype(BF16)
        which = iota((16, D), 0)
        new = jnp.zeros((16, D), F32)
        for j, row in enumerate((q_s[c], da, dq, do)):
            new = new + jnp.where(which == 2 * j + c, row.astype(F32)[0:1, :], 0.0)
        line[...] = line[...] + new
        columns = jnp.where(lane == 0, g_gain, jnp.where(lane == 1, g_shift, 0.0))
        flat = jnp.transpose(columns)[0:8, :]
        extra = (
            jnp.where(iota((8, D), 0) == 2, dbv, 0.0)
            + jnp.where(iota((8, D), 0) == 3, g_h * hat1, 0.0)
            + jnp.where(iota((8, D), 0) == 4, g_h, 0.0)
        )
        sums_s[...] = sums_s[...] + flat + extra
        return carry

    lax.fori_loop(0, n_mine, back, 0)
    line_q[0:16, :] = (line[...] + jnp.concatenate([jnp.zeros((8, D), F32), sums_s[...]], axis=0)).astype(BF16)

    @pl.when(me == query_home)
    def _():
        dh = load_rows_sum(h_recvq, nq)
        at, n = part[0]
        g_h = g_top_s[at : at + n, :] + dh
        r1 = load_rows(r1_ownq, nq)
        gain1 = rv[5:6, :]
        _, hat1, scale1 = norm_rows(r1, gain1, gain1)
        g_mid = norm_rows_back(g_h, gain1, hat1, scale1)
        kept = (
            hat_q[...], scale_q[...], xl_q[...], xf_q[...], q_q[...], k_q[...], v_q[...],
            p_q[...], a_q[...],
        )
        g_emb, t, w, da, dq, do, dbv, g_gain, g_shift = unit_back(
            queries, g_mid, 0, w_zero, cv, kept
        )
        gtok_q[...] = g_emb.reshape(nd, cols, nq * LQ).astype(BF16)
        tw = jnp.concatenate([t, w, xf_q[...].astype(F32), a_q[...].astype(F32)], axis=0)
        n_tw = tw.shape[0]
        tw = jnp.concatenate([tw, jnp.zeros((fac_q.shape[2] - n_tw, D), F32)], axis=0)
        fac_q[...] = jnp.transpose(tw).reshape(nd, cols, fac_q.shape[2]).astype(BF16)
        columns = jnp.where(lane == 0, g_gain, jnp.where(lane == 1, g_shift, 0.0))
        flat = jnp.transpose(columns)[0:8, :]
        extra = (
            jnp.where(iota((8, D), 0) == 2, dbv, 0.0)
            + jnp.where(iota((8, D), 0) == 3, jnp.sum(g_h * hat1, axis=0, keepdims=True), 0.0)
            + jnp.where(iota((8, D), 0) == 4, jnp.sum(g_h, axis=0, keepdims=True), 0.0)
        )
        block = jnp.concatenate(
            [q_q[...].astype(F32), da.astype(F32), dq.astype(F32), do.astype(F32), flat + extra,
             jnp.zeros((8, D), F32)],
            axis=0,
        )
        line_q[16:64, :] = block.astype(BF16)

    half = nd // 2

    def to_twin(src, sem):
        return pltpu.make_async_remote_copy(
            src_ref=src, dst_ref=src, send_sem=twin_send.at[sem], recv_sem=twin_recv.at[sem],
            device_id=net.where(me ^ 1), device_id_type=MESH,
        )

    row_flows = [
        Flow(
            lambda s, t: line_q.at[pl.ds(0, 16), :],
            lambda s, t: o_line.at[s & 1, s >> 1],
            lambda n: o_line.at[0, pl.ds(0, n)],
            alike, alike,
        ),
    ]
    plane, home_core = query_home // 8, query_home % 2
    z_at = me >> 3
    on_core = core == home_core
    query_rows = line_q.at[pl.ds(16, 48), :]

    def pass_rows(src, t, sem):
        pltpu.make_async_remote_copy(
            src_ref=src, dst_ref=o_lineq, send_sem=chain_send.at[sem], recv_sem=chain_recv,
            device_id=net.where(t), device_id_type=MESH,
        ).start()

    def rows_sent(sem):
        pltpu.make_async_copy(o_lineq, o_lineq, chain_send.at[sem]).wait()

    at_home = me == query_home
    in_plane = jnp.logical_and(z_at == plane, on_core)
    goes_up = jnp.logical_and(on_core, jnp.logical_and(z_at >= plane, z_at < nd // 8 - 1))
    goes_down = jnp.logical_and(on_core, jnp.logical_and(z_at <= plane, z_at > 0))

    @pl.when(at_home)
    def _():
        own = pltpu.make_async_copy(query_rows, o_lineq, own_sem.at[own_sem.shape[0] - 1])
        own.start()
        for j in range(1, 4):
            pass_rows(query_rows, me ^ (2 * j), j)
        own.wait()

    row_base = net.start(row_flows)
    flows = [
        Flow(
            lambda s, t: gtok_q.at[t],
            lambda s, t: o_tok.at[:, pl.ds(n_valid * LP, nq * LQ)],
            lambda n: o_tok.at[:, pl.ds(0, n * nq * LQ)],
            home, everyone,
        ),
        Flow(
            lambda s, t: fac.at[t],
            lambda s, t: o_fac.at[s],
            lambda n: o_fac.at[pl.ds(0, n)],
            everyone, everyone,
        ),
        Flow(
            lambda s, t: fac_q.at[t],
            lambda s, t: o_facq,
            lambda n: fac_q.at[pl.ds(0, n)],
            home, everyone,
        ),
    ]
    base = net.start(flows)

    def tok_view(slot):
        return o_tok.at[:, pl.ds(pl.multiple_of(slot * LP, LANE), LP)]

    def push_tokens(k, carry):
        t = (me + k) & (nd - 1)
        for c in range(cap):

            @pl.when(within(me, span(c)))
            def _():
                slot = slot_of(c, me)
                pltpu.make_async_remote_copy(
                    src_ref=gtok.at[c, t], dst_ref=tok_view(slot),
                    send_sem=tok_send.at[c], recv_sem=tok_recv.at[slot],
                    device_id=net.where(t), device_id_type=MESH,
                ).start()

        return carry

    for c in range(cap):

        @pl.when(within(me, span(c)))
        def _():
            slot = slot_of(c, me)
            pltpu.make_async_copy(gtok.at[c, me], tok_view(slot), tok_recv.at[slot]).start()

    lax.fori_loop(1, nd, push_tokens, 0)

    @pl.when(jnp.logical_not(at_home))
    def _():
        pltpu.make_async_copy(o_lineq, o_lineq, chain_recv).wait()

    @pl.when(goes_up)
    def _():
        pass_rows(o_lineq, me + 8, 4)

    @pl.when(goes_down)
    def _():
        pass_rows(o_lineq, me - 8, 5)

    @pl.when(on_core)
    def _():
        pass_rows(o_lineq, me ^ 1, 6)

    net.finish(du_flows, du_base)
    du_half = o_du.at[:, pl.ds(pl.multiple_of(core * (half * LANE), LANE), half * LANE)]
    to_twin(du_half, 0).start()
    net.finish(row_flows, row_base)
    to_twin(o_line.at[core], 1).start()

    net.finish(flows[1:], base + 1)
    lane1 = iota((cols, LANE), 1)
    for g in range(nd // 4):
        t_g = jnp.zeros((cols, LANE), F32)
        w_g = jnp.zeros((cols, LANE), F32)
        for j in range(4):
            block = o_fac[4 * g + j].astype(F32)
            t_part = jnp.where(lane1 < 32, block, 0.0)
            w_part = jnp.where(jnp.logical_and(lane1 >= 32, lane1 < 64), block, 0.0)
            t_g = t_g + (pltpu.roll(t_part, 32 * j, 1) if j else t_part)
            w_g = w_g + (pltpu.roll(w_part, (32 * j - 32) % LANE, 1) if j != 1 else w_part)
        t_all[:, g * LANE : (g + 1) * LANE] = t_g.astype(BF16)
        w_all[:, g * LANE : (g + 1) * LANE] = w_g.astype(BF16)
    x_all = jnp.zeros((cols, LANE), F32)
    a_all = jnp.zeros((cols, LANE), F32)
    for d in range(nd):
        block = o_fac[d].astype(F32)
        x_part = jnp.where(jnp.logical_and(lane1 >= 64, lane1 < 66), block, 0.0)
        a_part = jnp.where(jnp.logical_and(lane1 >= 80, lane1 < 82), block, 0.0)
        x_all = x_all + pltpu.roll(x_part, (2 * d - 64) % LANE, 1)
        a_all = a_all + pltpu.roll(a_part, (2 * d - 80) % LANE, 1)
    mask16 = ((iota((16, D), 0)) == (iota((16, D), 1) >> 6)).astype(F32)

    to_twin(du_half, 0).wait()
    to_twin(o_line.at[core], 1).wait()

    def expand(d, carry):
        both = o_line[d & 1, d >> 1].astype(F32)
        for c in range(2):
            at = pl.ds(pl.multiple_of(32 * d + 16 * c, 16), 16)
            q_exp[at, :] = (both[c : c + 1, :] * mask16).astype(BF16)
            d_exp[at, :] = (both[2 + c : 3 + c, :] * mask16).astype(BF16)
        return carry

    lax.fori_loop(0, nd, expand, 0)
    everything = o_line[...].reshape(nd * 16, D)
    row, col = iota((272, nd * 16), 0), iota((272, nd * 16), 1)
    kind = col & 15
    at_block = col >> 4
    device = (at_block & (half - 1)) * 2 + (at_block >> (half.bit_length() - 1))
    pair = device * 2 + (col & 1)
    dq_rows = jnp.logical_and(row < 128, jnp.logical_and((kind >> 1) == 2, pair == row))
    do_rows = jnp.logical_and(
        jnp.logical_and(row >= 128, row < 256),
        jnp.logical_and((kind >> 1) == 3, pair == row - 128),
    )
    total_rows = jnp.logical_or(
        jnp.logical_and(jnp.logical_and(row >= 256, row < 261), kind == row - 248),
        jnp.logical_or(
            jnp.logical_and(row == 261, (kind >> 1) == 2),
            jnp.logical_and(row == 262, (kind >> 1) == 3),
        ),
    )
    select = as_bf16(jnp.logical_or(dq_rows, jnp.logical_or(do_rows, total_rows)))
    picked = mm(select, everything, NN)
    g_in[1, :, 0:D] = mm(x_all.astype(BF16), picked[0:128].astype(BF16), NN)
    g_in[1, :, D : 2 * D] = mm(t_all[...], q_exp[...], NN)
    g_in[1, :, 2 * D : 3 * D] = mm(w_all[...], d_exp[...], NN)
    g_out[1] = mm(a_all.astype(BF16), picked[128:256].astype(BF16), NN)
    sums1 = picked[256:272]

    fl = o_facq.shape[1]
    row, col = iota((fl, 48), 0), iota((fl, 48), 1)
    q_rows = H * nq
    rown = iota((fl, D), 0)
    headn = iota((fl, D), 1) >> 6

    def rhs(first_row, last_row, first_col, by_head):
        here = jnp.logical_and(row >= first_row, row < last_row)
        hit = jnp.logical_and(here, col == first_col + (row & (nq - 1)))
        out = mm(as_bf16(hit), o_lineq[...], NN)
        if by_head:
            out = jnp.where(((rown - first_row) >> (nq.bit_length() - 1)) == headn, out, 0.0)
        return out.astype(BF16)

    facq = o_facq[...]
    g_in[0, :, 0:D] = mm(facq, rhs(2 * q_rows, 2 * q_rows + nq, 2 * nq, False), NN)
    g_in[0, :, D : 2 * D] = mm(facq, rhs(0, q_rows, 0, True), NN)
    g_in[0, :, 2 * D : 3 * D] = mm(facq, rhs(q_rows, 2 * q_rows, nq, True), NN)
    g_out[0] = mm(facq, rhs(2 * q_rows + nq, 2 * q_rows + 2 * nq, 3 * nq, False), NN)
    line0 = o_lineq[...].astype(F32)
    sums0 = line0[4 * nq : 4 * nq + 8]
    dq0 = jnp.sum(line0[2 * nq : 3 * nq], axis=0, keepdims=True)
    do0 = jnp.sum(line0[3 * nq : 4 * nq], axis=0, keepdims=True)

    mine_at = as_bf16(iota((cols, D), 1) == iota((cols, D), 0) + me * cols)
    h_cols = mm(mine_at, o_h[...].astype(BF16), NT)
    both = jnp.concatenate([h_cols, h_cols], axis=0)
    r, c = iota((2 * cols, rows), 0), iota((2 * cols, rows), 1)
    both = jnp.where((r < cols) == (c >= n_valid), both, 0.0).astype(BF16)
    g_up[...] = mm(both, o_du[...], NN)
    ones = iota((8, rows), 0)
    which = iota((8, rows), 1)
    e_rows = as_bf16(
        jnp.logical_or(
            jnp.logical_and(ones == 0, which >= n_valid),
            jnp.logical_and(ones == 1, which < n_valid),
        )
    )
    db_in = mm(e_rows, o_du[...], NN)
    g_bin[...] = db_in
    small_rows = {
        0: (dq0, sums0[2:3], do0, sums0[4:5], out_rows[0][2], out_rows[0][1], sums0[1:2],
            sums0[0:1], sums0[3:4], out_rows[0][0]),
        1: (sums1[5:6], sums1[2:3], sums1[6:7], sums1[4:5], out_rows[1][2], out_rows[1][1],
            sums1[1:2], sums1[0:1], sums1[3:4], out_rows[1][0]),
    }
    small_squares = jnp.sum(db_in * db_in)
    for e in range(2):
        for j, value in enumerate(small_rows[e]):
            g_small[16 * e + j : 16 * e + j + 1, :] = value
            small_squares = small_squares + jnp.sum(value * value)
    squares = jnp.sum(g_in[...] * g_in[...]) + jnp.sum(g_out[...] * g_out[...])
    squares = squares + jnp.sum(g_up[...] * g_up[...]) + jnp.sum(o_shrink[...] * o_shrink[...])

    blocks = g_table.shape[1] // HASH
    acc_s[...] = jnp.zeros_like(acc_s)

    def add_tokens(now, values):
        low = now & (HASH - 1)
        high = now >> (HASH.bit_length() - 1)
        width = now.shape[1]
        for b in range(0, blocks, 2):
            two = jnp.concatenate(
                [jnp.where(high == b, values, 0.0), jnp.where(high == b + 1, values, 0.0)], axis=0
            )
            spread_s[b * cols : (b + 2) * cols, 0:width] = two.astype(BF16)
        hot = as_bf16(iota((HASH, width), 0) == low)
        acc_s[...] += mm(spread_s[:, 0:width], hot, NT)

    def add_slots(slots_now):
        for slot in slots_now:
            pltpu.make_async_copy(tok_view(slot), tok_view(slot), tok_recv.at[slot]).wait()
        values = [tok_view(slot)[...].astype(F32) for slot in slots_now]
        add_tokens(
            jnp.concatenate(
                [ids[slot >> 1, pl.ds(slot & 1, 1), 0:LP] for slot in slots_now], axis=1
            ),
            jnp.concatenate(values, axis=1),
        )

    def add_near(k, carry):
        add_slots([(me - 2 * k - j) & (nd - 1) for j in range(2)])
        return carry

    def add_far(k, carry):
        extra = n_valid - nd
        first = me >> 2
        add_slots([nd + ((first - 2 * k - j) & (extra - 1)) for j in range(2)])
        return carry

    lax.fori_loop(0, nd // 2, add_near, 0)
    lax.fori_loop(0, (n_valid - nd) // 2, add_far, 0)
    net.finish(flows[:1], base)
    tq = nq * LQ
    ids_q = jnp.zeros((1, tq), jnp.int32)
    for d in range(0, nd, narrow):
        ids_q = ids_q + ids[d, 2:3, 0:tq]
    add_tokens(ids_q, o_tok[:, n_valid * LP : n_valid * LP + nq * LQ].astype(F32))
    for c in range(cap):

        @pl.when(within(me, span(c)))
        def _():
            sent = o_tok.at[:, pl.ds(0, (nd - 1) * LP)]
            pltpu.make_async_copy(sent, sent, tok_send.at[c]).wait()

    @pl.when(at_home)
    def _():
        for j in range(1, 4):
            rows_sent(j)

    for ok, sem in ((goes_up, 4), (goes_down, 5), (on_core, 6)):

        @pl.when(ok)
        def _():
            rows_sent(sem)

    def add_slot(s, total):
        return total + o_tok[:, pl.ds(pl.multiple_of(s * LP, LANE), LP)].astype(F32)

    position = lax.fori_loop(0, n_valid, add_slot, jnp.zeros((cols, LP), F32))
    tq = nq * LQ
    q_tok = o_tok[:, n_valid * LP : n_valid * LP + tq].astype(F32)
    folded = q_tok[:, 0:LANE]
    for j in range(1, tq // LANE):
        folded = folded + q_tok[:, j * LANE : (j + 1) * LANE]
    around = folded
    for j in range(1, LANE // LQ):
        around = around + pltpu.roll(folded, LANE - LQ * j, 1)
    around = jnp.where(lane1 < LQ, around, 0.0)
    position = jnp.concatenate(
        [position[:, 0:LANE] + around, position[:, LANE:], jnp.zeros((cols, HASH - LP), F32)],
        axis=1,
    )
    shifted = pltpu.roll(position, V - (blocks - 1) * HASH, 1)
    for b in range(blocks):
        value = acc_s[b * cols : (b + 1) * cols, :]
        if b == blocks - 1:
            value = value + shifted
        g_table[:, b * HASH : (b + 1) * HASH] = value
        squares = squares + jnp.sum(value * value)

    norm_own[...] = jnp.broadcast_to(squares.reshape(1, 1), (8, LANE))
    flows = [
        Flow(
            lambda s, t: norm_own, lambda s, t: norm_all.at[s],
            lambda n: norm_all.at[pl.ds(0, n)], everyone, everyone,
        )
    ]
    base = net.start(flows)
    net.finish(flows, base)
    o_norm[...] = jnp.sqrt(jnp.sum(norm_all[...], axis=0) + small_squares)


def middle(n_valid, nq, nd, narrow, cols, query_home, arrays):
    cap = -(-n_valid // nd)
    rows = n_valid + nq
    tq = nq * LQ
    unit, unit_q = Unit(1, LP), Unit(nq, LQ)
    fac_lanes = -(-(2 * unit_q.rows + 2 * unit_q.seqs) // LANE) * LANE
    vmem = pl.BlockSpec(memory_space=pltpu.VMEM)

    def like(*shape, dtype=F32):
        return jax.ShapeDtypeStruct(shape, dtype)

    def kept(lead, u):
        return [
            pltpu.VMEM(lead + (D, u.tokens), F32),
            pltpu.VMEM(lead + (1, u.tokens), F32),
            pltpu.VMEM(lead + (D, u.tokens), BF16),
            pltpu.VMEM(lead + (u.seqs, D), BF16),
            pltpu.VMEM(lead + (u.seqs, D), BF16),
            pltpu.VMEM(lead + (D, u.tokens), BF16),
            pltpu.VMEM(lead + (D, u.tokens), BF16),
            pltpu.VMEM(lead + (u.rows, u.tokens), F32),
            pltpu.VMEM(lead + (u.seqs, D), BF16),
        ]

    flows = 5 * (cap + 1) + 7
    table_total = -(-(V + LP) // HASH) * HASH
    chunk = 2 * LP
    return pl.pallas_call(
        functools.partial(
            middle_body, n_valid, nq, nd, narrow, cols, query_home
        ),
        out_shape=[
            like(2, LANE, D),
            like(8, LANE),
            like(cols, table_total),
            like(2, cols, 3 * D),
            like(2, cols, D),
            like(2 * cols, nd * LANE),
            like(8, nd * LANE),
            like(32, D),
            like(8, LANE),
        ],
        in_specs=[vmem] * len(arrays),
        out_specs=[vmem] * 9,
        scratch_shapes=kept((cap,), unit)
        + kept((), unit_q)
        + [
            pltpu.VMEM((cap, 8, LANE), F32),
            pltpu.VMEM((8 * nq, LANE), F32),
            pltpu.VMEM((8 * rows, LANE), F32),
            pltpu.VMEM((8 * rows, LANE), F32),
            pltpu.VMEM((nd, cap + 1, 8, LANE), F32),
            pltpu.VMEM((cap + 1, 8, LANE), F32),
            pltpu.VMEM((8 * rows, LANE), F32),
            pltpu.VMEM((8 * rows, LANE), F32),
            pltpu.VMEM((nd, cap, 8, LANE), F32),
            pltpu.VMEM((nd, 8 * nq, LANE), F32),
            pltpu.VMEM((rows, LANE), BF16),
            pltpu.VMEM((rows, LANE), F32),
            pltpu.VMEM((cap, nd, cols, LP), BF16),
            pltpu.VMEM((nd, cols, tq), BF16),
            pltpu.VMEM((nd, cols, LANE), BF16),
            pltpu.VMEM((nd, cols, fac_lanes), BF16),
            pltpu.VMEM((16, D), F32),
            pltpu.VMEM((64, D), BF16),
            pltpu.VMEM((rows, LANE), F32),
            pltpu.VMEM((rows, LANE), F32),
            pltpu.VMEM((rows, D), F32),
            pltpu.VMEM((rows, D), F32),
            pltpu.VMEM((8, D), F32),
            pltpu.VMEM((cols, n_valid * LP + tq), BF16),
            pltpu.VMEM((nd, cols, LANE), BF16),
            pltpu.VMEM((cols, fac_lanes), BF16),
            pltpu.VMEM((2, nd // 2, 16, D), BF16),
            pltpu.VMEM((48, D), BF16),
            pltpu.VMEM((rows, nd * LANE), BF16),
            pltpu.VMEM((rows, D), F32),
            pltpu.VMEM((nd, 2, cols, LANE), BF16),
            pltpu.VMEM((2, D, LANE), BF16),
            pltpu.VMEM((cols, nd * 32), BF16),
            pltpu.VMEM((cols, nd * 32), BF16),
            pltpu.VMEM((nd * 32, D), BF16),
            pltpu.VMEM((nd * 32, D), BF16),
            pltpu.VMEM((table_total // HASH * cols, chunk), BF16),
            pltpu.VMEM((table_total // HASH * cols, HASH), F32),
            pltpu.VMEM((8, LANE), F32),
            pltpu.VMEM((nd, 8, LANE), F32),
            pltpu.VMEM((2, LANE, D), BF16),
            pltpu.VMEM((8, 7 * D + FF + 4 * LANE), F32),
            pltpu.VMEM((8, D + 2 * LANE), F32),
            pltpu.VMEM((LANE, D), F32),
            pltpu.VMEM((D, LANE), F32),
            pltpu.VMEM((16, D), F32),
            pltpu.VMEM((8, LANE), F32),
            pltpu.SemaphoreType.DMA((cap,)),
            pltpu.SemaphoreType.DMA((n_valid,)),
            pltpu.SemaphoreType.DMA((2,)),
            pltpu.SemaphoreType.DMA((2,)),
            pltpu.SemaphoreType.DMA((7,)),
            pltpu.SemaphoreType.DMA(()),
            pltpu.SemaphoreType.DMA((flows,)),
            pltpu.SemaphoreType.DMA((flows,)),
            pltpu.SemaphoreType.DMA((flows,)),
        ],
        compiler_params=pltpu.CompilerParams(
            collective_id=3, has_side_effects=True, vmem_limit_bytes=62 * 1024 * 1024
        ),
        name="middle",
    )(*arrays)


def stack_table(rows, blocks, table, stacked):
    last = (V - (blocks - 1) * HASH + LANE - 1) // LANE * LANE

    def piece(b):
        if b >= blocks:
            return []
        if b == blocks - 1:
            part = table[:, b * HASH : b * HASH + last].astype(F32)
            return [jnp.concatenate([part, jnp.zeros((rows, HASH - last), F32)], axis=1)]
        return [table[:, b * HASH : (b + 1) * HASH].astype(F32)]

    for b in range(0, blocks, 2):
        both = jnp.concatenate(piece(b) + piece(b + 1), axis=0)
        stacked[b * rows : b * rows + both.shape[0], :] = both.astype(BF16)


def pick_tokens(rows, blocks, stacked, ids):
    low = ids & (HASH - 1)
    high = ids >> (HASH.bit_length() - 1)
    width = ids.shape[1]
    hot = as_bf16(iota((HASH, width), 0) == low)
    picked = jnp.dot(stacked[...], hot, preferred_element_type=F32)
    value = jnp.zeros((rows, width), F32)
    for b in range(blocks):
        value = jnp.where(high == b, picked[b * rows : (b + 1) * rows], value)
    return value.astype(BF16)


def first_body(
    n_valid, nq, nd, narrow, cols, home_at, blocks, plan,
    ids_mine, small_mine, table, win, wout, pos_mine,
    ids_got, small_got, mine, mine_q, wall, w0,
    stacked, tokens, tokens_q, p0,
    send_sem, recv_sem, own_sem, up_send, down_send, z_recv, y_send, y_recv, x_send, x_recv,
    c_send, c_recv,
):
    cap = -(-n_valid // nd)
    wide = nd // narrow
    tq = nq * LQ
    n_own = ids_mine.shape[0] - 1
    net = Net(nd, narrow, send_sem, recv_sem, own_sem)
    me = net.me
    w_at, n_at = lax.axis_index("wide"), lax.axis_index("narrow")
    x_at, c_at = n_at ^ 2, n_at ^ 1
    everyone = group(nd, nd)
    home = (home_at, 1, 1)

    def span(c):
        return group(nd, nd) if c == 0 else group(n_valid - nd, nd, 1)

    def slot_of(c, d):
        return c * nd + place(d, span(c))

    wall[w_at, n_at] = jnp.concatenate([win[1], wout[1], pos_mine[...]], axis=1).astype(BF16)
    p0[...] = jnp.concatenate([win[0], wout[0]], axis=1).astype(BF16)

    net.barrier()
    small = [
        Flow(
            lambda s, t: ids_mine, lambda s, t: ids_got.at[s],
            lambda n: ids_got.at[pl.ds(0, n)], everyone, everyone,
        ),
        Flow(
            lambda s, t: small_mine, lambda s, t: small_got.at[s],
            lambda n: small_got.at[pl.ds(0, n)], everyone, everyone,
        ),
    ]
    small_base = net.start(small)

    tall = wide // 2
    z_at, y_at = w_at >> 1, w_at & 1

    def pass_on(row, col, w_to, n_to, sent, got):
        pltpu.make_async_remote_copy(
            src_ref=wall.at[row, col], dst_ref=wall.at[row, col], send_sem=sent, recv_sem=got,
            device_id=(w_to, n_to), device_id_type=MESH,
        ).start()

    def await_piece(row, col, sem):
        pltpu.make_async_copy(wall.at[row, col], wall.at[row, col], sem).wait()

    def up(z):
        @pl.when(z_at < tall - 1)
        def _():
            pass_on(2 * z + y_at, n_at, w_at + 2, n_at, up_send.at[z], z_recv.at[z])

    def down(z):
        @pl.when(z_at > 0)
        def _():
            pass_on(2 * z + y_at, n_at, w_at - 2, n_at, down_send.at[z], z_recv.at[z])

    def across(row):
        pass_on(row, n_at, w_at, x_at, x_send, x_recv.at[row])
        pass_on(row, n_at, w_at, c_at, c_send, c_recv.at[0, row])

    def around(z):
        pass_on(2 * z + y_at, n_at, w_at ^ 1, n_at, y_send, y_recv.at[z])
        across(2 * z + y_at)

    def z_step(k):
        for z, onward in ((z_at - k, up), (z_at + k, down)):

            @pl.when(jnp.logical_and(z >= 0, z < tall))
            def _():
                await_piece(2 * z + y_at, n_at, z_recv.at[z])
                onward(z)
                around(z)

    def y_step(z):
        row = 2 * z + (y_at ^ 1)
        await_piece(row, n_at, y_recv.at[z])
        across(row)

    def x_step(row):
        await_piece(row, x_at, x_recv.at[row])
        pass_on(row, x_at, w_at, c_at, c_send, c_recv.at[1, row])

    def forward(step):
        if step < tall:
            z_step(step)
        elif step < 2 * tall:
            y_step((z_at + step - tall) & (tall - 1))
        else:
            k = step - 2 * tall
            row = 2 * ((z_at + k) & (tall - 1)) + y_at if k < tall else (
                2 * ((z_at + k) & (tall - 1)) + (y_at ^ 1)
            )
            x_step(row)

    up(z_at)
    down(z_at)
    around(z_at)
    home_moves = [
        Flow(
            lambda s, t: p0, lambda s, t: w0.at[s],
            lambda n: w0.at[pl.ds(0, n)], everyone, home,
        ),
    ]
    home_base = net.start(home_moves)

    stack_table(cols, blocks, table, stacked)
    net.finish(small, small_base)

    pairs = n_valid // n_own
    moves = [
        Flow(
            lambda s, t, c=c: tokens.at[slot_of(c, t) >> 1, slot_of(c, t) & 1],
            lambda s, t, c=c: mine.at[s, :, pl.ds(c * LP, LP)],
            lambda n: mine.at[pl.ds(0, n), :, pl.ds(0, LP)],
            everyone, span(c),
        )
        for c in range(cap)
    ]
    base = net.used
    net.used += cap

    def send_pair(at):
        for j in range(n_own):
            slot = at * n_own + j
            c = (slot >= nd).astype(jnp.int32)
            far = span(1)
            t = jnp.where(c == 0, slot, far[0] + far[1] * (slot - nd))
            dst = mine.at[me, :, pl.ds(pl.multiple_of(c * LP, LANE), LP)]

            @pl.when(t != me)
            def _():
                pltpu.make_async_remote_copy(
                    src_ref=tokens.at[at, j], dst_ref=dst,
                    send_sem=send_sem.at[base + c], recv_sem=recv_sem.at[base + c],
                    device_id=net.where(t), device_id_type=MESH,
                ).start()

            @pl.when(t == me)
            def _():
                pltpu.make_async_copy(tokens.at[at, j], dst, own_sem.at[base + c]).start()

    def turn_of(i):
        at = i + me
        for _ in range((pairs + nd - 2) // pairs):
            at = jnp.where(at >= pairs, at - pairs, at)
        return at

    def gather(i, carry):
        at = turn_of(i)
        ids = jnp.concatenate([ids_got[at, j : j + 1, 0:LP] for j in range(n_own)], axis=1)
        rows = pick_tokens(cols, blocks, stacked, ids)
        for j in range(n_own):
            tokens[at, j] = rows[:, j * LP : (j + 1) * LP]

        @pl.when(i > 0)
        def _():
            send_pair(turn_of(i - 1))

        for step, turn in enumerate(plan):
            if 0 < step and turn < pairs:

                @pl.when(i == turn)
                def _():
                    forward(step)

        return carry

    q_ids = jnp.zeros((1, tq), jnp.int32)
    for d in range(0, nd, narrow):
        q_ids = q_ids + ids_got[d, n_own : n_own + 1, 0:tq]
    tokens_q[...] = pick_tokens(cols, blocks, stacked, q_ids)
    q_moves = [
        Flow(
            lambda s, t: tokens_q, lambda s, t: mine_q.at[s],
            lambda n: mine_q.at[pl.ds(0, n)], everyone, home,
        ),
    ]
    q_base = net.start(q_moves)
    lax.fori_loop(0, pairs, gather, 0)
    send_pair(turn_of(pairs - 1))
    for step, turn in enumerate(plan):
        if 0 < step and turn >= pairs:
            forward(step)
    net.finish(moves, base)
    net.finish(q_moves, q_base)
    net.finish(home_moves, home_base)

    def last(row, carry):
        for which, col in ((0, c_at), (1, c_at ^ 2)):
            pltpu.make_async_copy(
                wall.at[row, col], wall.at[row, col], c_recv.at[which, row]
            ).wait()
        return carry

    lax.fori_loop(0, wide, last, 0)
    for z in range(tall):
        for hop, ok in (
            (up_send, jnp.logical_and(z_at < tall - 1, z <= z_at)),
            (down_send, jnp.logical_and(z_at > 0, z >= z_at)),
        ):

            @pl.when(ok)
            def _():
                await_piece(0, 0, hop.at[z])

    many = wall.at[pl.ds(0, tall), 0]
    pltpu.make_async_copy(many, many, y_send).wait()
    many = wall.at[:, 0]
    pltpu.make_async_copy(many, many, x_send).wait()
    many = wall.at[:, pl.ds(0, 2)]
    pltpu.make_async_copy(many, many, c_send).wait()


def first(n_valid, nq, nd, narrow, cols, home_at, arrays, plan):
    cap = -(-n_valid // nd)
    wide = nd // narrow
    tq = nq * LQ
    ids_mine, small_mine = arrays[0], arrays[1]
    n_own = ids_mine.shape[0] - 1
    blocks = -(-V // HASH)
    vmem = pl.BlockSpec(memory_space=pltpu.VMEM)
    flows = 4 + cap

    def like(*shape, dtype=BF16):
        return jax.ShapeDtypeStruct(shape, dtype)

    dma = pltpu.SemaphoreType.DMA
    return pl.pallas_call(
        functools.partial(
            first_body, n_valid, nq, nd, narrow, cols, home_at, blocks, plan
        ),
        out_shape=[
            like(nd, *ids_mine.shape, dtype=jnp.int32),
            like(nd, *small_mine.shape),
            like(nd, cols, cap * LP),
            like(nd, cols, tq),
            like(wide, narrow, cols, 4 * D + LP),
            like(nd, cols, 4 * D),
        ],
        in_specs=[vmem] * len(arrays),
        out_specs=[vmem] * 6,
        scratch_shapes=[
            pltpu.VMEM((blocks * cols, HASH), BF16),
            pltpu.VMEM((n_valid // n_own, n_own, cols, LP), BF16),
            pltpu.VMEM((cols, tq), BF16),
            pltpu.VMEM((cols, 4 * D), BF16),
            dma((flows,)), dma((flows,)), dma((flows,)),
            dma((wide // 2,)), dma((wide // 2,)), dma((wide // 2,)), dma(()), dma((wide // 2,)),
            dma(()), dma((wide,)), dma(()), dma((2, wide)),
        ],
        compiler_params=pltpu.CompilerParams(
            collective_id=2, has_side_effects=True, vmem_limit_bytes=62 * 1024 * 1024
        ),
        name="first",
    )(*arrays)


def on_device_rows(
    passage_ids, query_ids, passage_query, kept_mask, neg_count, step_count,
    embed_table, attend_in, attend_out, expand_weight, shrink_weight, norm_gains, bias_terms,
    embed_first, embed_second, attend_in_first, attend_in_second,
    attend_out_first, attend_out_second, expand_first, expand_second,
    shrink_first, shrink_second, gains_first, gains_second, bias_first, bias_second,
):
    narrow = lax.axis_size("narrow")
    nd = lax.axis_size("wide") * narrow
    me = lax.axis_index("wide") * narrow + lax.axis_index("narrow")
    cols = embed_table.shape[1]
    n_slots = passage_query.shape[0]
    nq = query_ids.shape[0] * lax.axis_size("wide")
    n_valid = VALID_PER_QUERY * nq
    cap = -(-n_valid // nd)
    rows_p = cap * nd
    ff_cols = FF // nd

    exch = functools.partial(comm, nd=nd, narrow=narrow)
    rows_c = -(-cols // 8) * 8
    n_ids = passage_ids.shape[0] + query_ids.shape[0]
    small_width = max(cols, bias_terms.shape[1], 1)
    small_width = -(-small_width // LANE) * LANE

    def widen(value, width):
        return jnp.pad(value, ((0, 0), (0, width - value.shape[1])))

    ids_mine = jnp.concatenate([passage_ids, widen(query_ids, LP)])
    small_mine = jnp.concatenate(
        [widen(norm_gains.reshape(6, cols), small_width), widen(bias_terms, small_width)]
    ).astype(BF16)
    ids_got, small_got = exch(
        1,
        [ids_mine, small_mine],
        [((nd, n_ids, LP), jnp.int32), ((nd, 8, small_width), BF16)],
        [send_all(0, 0, nd), send_all(1, 1, nd)],
    )
    n_own = passage_ids.shape[0]
    pid = ids_got[:, :n_own].reshape(n_slots, LP)[:n_valid]
    qid = ids_got.reshape(-1, narrow, n_ids, LP)[:, 0, n_own:, :LANE].reshape(nq, LANE)
    all_ids = jnp.concatenate([pid.reshape(-1), qid.reshape(-1)])
    gains = small_got[:, :6, :cols].transpose(1, 0, 2).reshape(2, 3, D).astype(F32)
    bias = small_got[:, 6:, : bias_terms.shape[1]].transpose(1, 0, 2).reshape(2, -1).astype(F32)

    table_t = embed_table.T
    table_low = table_t.astype(BF16)
    vocab = V + LP
    total = -(-vocab // HASH) * HASH
    table_pad = jnp.pad(table_low, ((0, rows_c - cols), (0, total - vocab)))
    got = table_rows(table_pad, all_ids)
    pos_mine = table_pad[:, V : V + LP]
    up_mine = expand_weight.astype(BF16).reshape(2 * cols, nd, ff_cols).transpose(1, 0, 2)
    q_from = n_valid * LP
    width = cap * LP + LANE

    def passage_move(c, forward):
        span = (0, min(nd, n_valid - c * nd))
        if forward:
            return Send(
                0, 0,
                lambda ref, s, t: ref.at[:, pl.ds(pl.multiple_of((c * nd + t) * LP, LANE), LP)],
                lambda ref, s, t: ref.at[s, :, pl.ds(c * LP, LP)],
                lambda ref, n: ref.at[:, pl.ds(0, n * LP)],
                lambda ref, n: ref.at[pl.ds(0, n), :, pl.ds(0, LP)],
                (0, nd), span,
            )
        return Send(
            0, 0,
            lambda ref, s, t: ref.at[t, :, pl.ds(c * LP, LP)],
            lambda ref, s, t: ref.at[:, pl.ds(pl.multiple_of((c * nd + s) * LP, LANE), LP)],
            lambda ref, n: ref.at[pl.ds(0, n), :, pl.ds(0, LP)],
            lambda ref, n: ref.at[:, pl.ds(0, n * LP)],
            span, (0, nd),
        )

    def query_move(forward):
        span = (nd - nq, nd)
        if forward:
            return Send(
                0, 0,
                lambda ref, s, t: ref.at[
                    :, pl.ds(pl.multiple_of(q_from + (t - (nd - nq)) * LANE, LANE), LANE)
                ],
                lambda ref, s, t: ref.at[s, :, pl.ds(cap * LP, LANE)],
                lambda ref, n: ref.at[:, pl.ds(0, n * LANE)],
                lambda ref, n: ref.at[pl.ds(0, n), :, pl.ds(0, LANE)],
                (0, nd), span,
            )
        return Send(
            0, 0,
            lambda ref, s, t: ref.at[t, :, pl.ds(cap * LP, LANE)],
            lambda ref, s, t: ref.at[
                :, pl.ds(pl.multiple_of(q_from + (s - (nd - nq)) * LANE, LANE), LANE)
            ],
            lambda ref, n: ref.at[pl.ds(0, n), :, pl.ds(0, LANE)],
            lambda ref, n: ref.at[:, pl.ds(0, n * LANE)],
            span, (0, nd),
        )

    mine, pos, w_up = exch(
        2,
        [got, pos_mine, up_mine],
        [((nd, rows_c, width), BF16), ((nd, rows_c, LP), BF16), ((nd, 2 * cols, ff_cols), BF16)],
        [passage_move(c, True) for c in range(cap)]
        + [query_move(True), send_all(1, 1, nd), send_blocks(2, 2, nd)],
    )
    live = jnp.concatenate(
        [jnp.broadcast_to(c * nd + me < n_valid, (LP,)) for c in range(cap)]
        + [jnp.broadcast_to(me >= nd - nq, (LANE,))]
    )
    mine = jnp.where(live, mine[:, :cols].reshape(D, width), 0)
    pos = pos[:, :cols].reshape(D, LP).astype(F32)
    w_up = w_up.reshape(nd, 2, cols, ff_cols).transpose(1, 0, 2, 3).reshape(2, D, ff_cols)
    w_down = shrink_weight.astype(BF16)
    w_in = lax.all_gather(attend_in.astype(BF16), AXES, axis=1, tiled=True)
    w_out = lax.all_gather(attend_out.astype(BF16), AXES, axis=1, tiled=True)

    fronts = []
    for c in range(cap):
        emb = mine[:, c * LP : (c + 1) * LP].astype(F32) + pos
        fronts.append(encode_front(emb, w_in[1], w_out[1], gains[1], bias[1], LP))
    emb = mine[:, cap * LP :].astype(F32) + pos[:, :LANE]
    fronts.append(encode_front(emb, w_in[0], w_out[0], gains[0], bias[0], LQ))
    (rows,) = exch(
        3, [jnp.stack([f[0] for f in fronts])], [((nd, cap + 1, D), F32)], [send_all(0, 0, nd)]
    )
    row_in = (rows[nd - nq :, cap], rows[:, :cap].transpose(1, 0, 2).reshape(rows_p, D))

    def by_owner(queries, passages):
        q_part = jnp.pad(queries, ((nd - nq, 0), (0, 0)))[:, None]
        return jnp.concatenate([passages.reshape(cap, nd, D).transpose(1, 0, 2), q_part], axis=1)

    def to_rows(blocks):
        return (
            blocks[nd - nq :, cap],
            blocks[:, :cap].transpose(1, 0, 2).reshape(rows_p, D),
        )


    mids, ups = [], []
    partial_y = []
    b_in_all = bias[:, O_IN : O_IN + FF].reshape(2, nd, ff_cols)
    b_in = lax.dynamic_index_in_dim(b_in_all, me, 1, False)
    for e in range(2):
        h, hat1, scale1 = norm_rows(row_in[e], gains[e, 1], bias[e, O_1 : O_1 + D])
        h_low = h.astype(BF16)
        upper = dot(h_low, w_up[e], ((1,), (0,))) + b_in[e]
        active, slope = gelu_both(upper)
        f_low = active.astype(BF16)
        partial_y.append(dot(f_low, w_down[e], ((1,), (0,))))
        mids.append((h, hat1, scale1, h_low))
        ups.append((f_low, slope))
    (y_parts,) = exch(
        4, [by_owner(*partial_y)], [((nd, cap + 1, D), F32)], [send_blocks(0, 0, nd)]
    )
    (y_all,) = exch(
        5, [jnp.sum(y_parts, axis=0)], [((nd, cap + 1, D), F32)], [send_all(0, 0, nd)]
    )
    y = to_rows(y_all)
    tops = []
    vecs = []
    for e in range(2):
        z, hat2, scale2 = norm_rows(
            mids[e][0] + y[e] + bias[e, O_OUT : O_OUT + D], gains[e, 2], bias[e, O_2 : O_2 + D]
        )
        tops.append((hat2, scale2))
        vecs.append(z.astype(BF16))
    qvec, pvec = vecs

    owner = passage_query[:rows_p]
    kept = kept_mask[:rows_p] == 1
    earlier = jnp.concatenate([jnp.full((1,), -1, jnp.int32), owner[:-1]])
    valid = owner >= 0
    first = valid & (owner != earlier)
    member = owner[None, :] == jnp.arange(nq, dtype=jnp.int32)[:, None]
    positive = member & first[None, :]
    negative = member & jnp.logical_not(first)[None, :] & kept[None, :]
    counts = jnp.sum(member.astype(F32), axis=1) - 1.0
    score_scale = 2.0 * D ** (-0.5)
    scores = dot(qvec, pvec, ((1,), (1,))) * score_scale
    masked = jnp.where(valid[None, :], scores, -1e30)
    peak = jnp.max(masked, axis=1)
    summed = jnp.sum(jnp.where(valid[None, :], jnp.exp(masked - peak[:, None]), 0.0), axis=1)
    logsum = peak + jnp.log(summed)
    pos_score = jnp.sum(jnp.where(positive, scores, 0.0), axis=1)
    margins = MARGIN - pos_score[:, None] + scores
    active_neg = negative & (margins > 0)
    hinge = jnp.sum(jnp.where(active_neg, margins, 0.0), axis=1) / counts
    active_total = jnp.sum(active_neg.astype(F32), axis=1)
    loss = jnp.sum(logsum - pos_score + hinge)
    score_grad = (
        jnp.where(valid[None, :], jnp.exp(scores - logsum[:, None]), 0.0)
        - positive.astype(F32) * (1.0 + active_total / counts)[:, None]
        + active_neg.astype(F32) / counts[:, None]
    )
    score_low = score_grad.astype(BF16)
    vec_grads = (
        (dot(score_low, pvec, ((1,), (0,))) * score_scale).astype(BF16).astype(F32),
        (dot(score_low, qvec, ((0,), (0,))) * score_scale).astype(BF16).astype(F32),
    )

    partial_h = []
    gain_grads = [[None] * 3 for _ in range(2)]
    shifts = [dict() for _ in range(2)]
    top_grads, shrink_grads, du_parts = [], [], []
    for e in range(2):
        hat2, scale2 = tops[e]
        gain_grads[e][2] = jnp.sum(vec_grads[e] * hat2, axis=0)
        shifts[e]["2"] = jnp.sum(vec_grads[e], axis=0)
        g_top = norm_rows_back(vec_grads[e], gains[e, 2], hat2, scale2)
        dy = g_top.astype(BF16)
        shifts[e]["out"] = jnp.sum(dy.astype(F32), axis=0)
        f_low, slope = ups[e]
        shrink_grads.append(dot(f_low, dy, ((0,), (0,))))
        df = dot(dy, w_down[e], ((1,), (1,)))
        du = (slope * df).astype(BF16)
        du_parts.append(du)
        partial_h.append(dot(du, w_up[e], ((1,), (1,))))
        top_grads.append(g_top)
    du_mine = jnp.concatenate(du_parts)
    h_parts, du_all = exch(
        6,
        [by_owner(*partial_h), du_mine],
        [((nd, cap + 1, D), F32), ((nd, nq + rows_p, ff_cols), BF16)],
        [send_blocks(0, 0, nd), send_all(1, 1, nd)],
    )
    h_mine = jnp.sum(h_parts, axis=0)
    top_mine = lax.dynamic_index_in_dim(by_owner(*top_grads), me, 0, False)
    rows_mine = lax.dynamic_index_in_dim(rows, me, 0, False)
    is_q = (me >= nd - nq).astype(F32)
    has = jnp.stack([(c * nd + me < n_valid).astype(F32) for c in range(cap)] + [is_q])
    g_h = (top_mine + h_mine) * has[:, None]
    gain_one = jnp.stack([gains[1, 1]] * cap + [gains[0, 1]])
    shift_one = jnp.stack([bias[1, O_1 : O_1 + D]] * cap + [bias[0, O_1 : O_1 + D]])
    _, hat_mine, scale_mine = norm_rows(rows_mine, gain_one, shift_one)
    g_mid = norm_rows_back(g_h, gain_one, hat_mine, scale_mine)
    gain_mid = g_h * hat_mine
    do_mine = g_mid.astype(BF16)
    backs = [
        encode_back(
            fronts[c][1], g_mid[c], w_in[1 if c < cap else 0], w_out[1 if c < cap else 0],
            gains[1 if c < cap else 0],
        )
        for c in range(cap + 1)
    ]

    def both_encoders(pick):
        return jnp.stack([pick(cap), sum(pick(c) for c in range(cap))])

    sums = jnp.concatenate(
        [both_encoders(lambda i, j=j: backs[i][1][j]) for j in (5, 6, 7)]
        + [both_encoders(lambda i: gain_mid[i]), both_encoders(lambda i: g_h[i])]
    )
    line = jnp.concatenate(
        [jnp.stack([b[1][j] for b in backs]) for j in (2, 3, 4)] + [do_mine, sums.astype(BF16)]
    )
    n_line = 4 * (cap + 1) + 10
    factor_t = jnp.concatenate(
        [b[1][0] for b in backs] + [b[1][1] for b in backs]
        + [f[1][2][:, 0][None] for f in fronts] + [f[1][8][None] for f in fronts]
    )
    n_factor = factor_t.shape[0]
    f_pad = -(-n_factor // LANE) * LANE
    factor_cols = jnp.pad(factor_t, ((0, f_pad - n_factor), (0, 0))).T

    def pad_rows(value):
        value = value.reshape(nd, cols, value.shape[1])
        return jnp.pad(value, ((0, 0), (0, rows_c - cols), (0, 0)))

    send = pad_rows(jnp.concatenate([b[0] for b in backs], axis=1).astype(BF16))
    token_grads, factors, lines = exch(
        7,
        [send, pad_rows(factor_cols), line],
        [
            ((rows_c, n_valid * LP + nq * LANE), BF16),
            ((nd, rows_c, f_pad), BF16),
            ((nd, n_line, D), BF16),
        ],
        [passage_move(c, False) for c in range(cap)]
        + [query_move(False), send_blocks(1, 1, nd), send_all(2, 2, nd)],
    )
    table_grad = table_sums(token_grads, all_ids, total)[:cols, :vocab]
    token_grads = token_grads[:cols].astype(F32)
    pos_grad = jnp.sum(token_grads[:, :q_from].reshape(cols, n_valid, LP), axis=1)
    pos_grad = pos_grad.at[:, :LANE].add(
        jnp.sum(token_grads[:, q_from:].reshape(cols, nq, LANE), axis=1)
    )
    table_grad = table_grad.at[:, V:].add(pos_grad)

    step_h = (cap + 1) * H
    factors = factors[:, :cols].transpose(0, 2, 1)
    t_all = factors[:, :step_h].reshape(nd, cap + 1, H, cols)
    w_all = factors[:, step_h : 2 * step_h].reshape(nd, cap + 1, H, cols)
    x_all = factors[:, 2 * step_h : 2 * step_h + cap + 1]
    a_all = factors[:, 2 * step_h + cap + 1 : 2 * step_h + 2 * (cap + 1)]
    q_all, da_all, dq_all, do_all = (
        lines[:, j * (cap + 1) : (j + 1) * (cap + 1)] for j in range(4)
    )
    sums = jnp.sum(lines[:, 4 * (cap + 1) :].astype(F32), axis=0).reshape(5, 2, D)

    def of_encoder(value, e):
        if e == 0:
            return value[nd - nq :, cap]
        return value[:, :cap].reshape((nd * cap,) + value.shape[2:])

    du_all = du_all.transpose(1, 0, 2).reshape(nq + rows_p, FF)
    in_grads, out_grads, expand_grads = [], [], []
    for e in range(2):
        du_full = du_all[:nq] if e == 0 else du_all[nq:]
        shifts[e]["in"] = jnp.sum(du_full.astype(F32), axis=0)
        h_cols = lax.dynamic_slice_in_dim(mids[e][3], me * cols, cols, 1)
        expand_grads.append(dot(h_cols, du_full, ((0,), (0,))))
        t, w, x, a = (of_encoder(u, e) for u in (t_all, w_all, x_all, a_all))
        q, da, dq, do = (of_encoder(u, e) for u in (q_all, da_all, dq_all, do_all))
        rows_e = q.shape[0]
        qh = q.reshape(rows_e, H, HD)
        dah = da.reshape(rows_e, H, HD)
        g_q = dot(x, dq, ((0,), (0,)))
        g_k = jnp.einsum("phi,phd->ihd", t, qh, preferred_element_type=F32).reshape(cols, D)
        g_v = jnp.einsum("phi,phd->ihd", w, dah, preferred_element_type=F32).reshape(cols, D)
        in_grads.append(jnp.concatenate([g_q, g_k, g_v], axis=1))
        out_grads.append(dot(a, do, ((0,), (0,))))
        shifts[e]["q"] = jnp.sum(dq.astype(F32), axis=0)
        shifts[e]["o"] = jnp.sum(do.astype(F32), axis=0)
    gain_grad = jnp.stack(
        [jnp.stack([sums[1, e], sums[3, e], gain_grads[e][2]]) for e in range(2)]
    )
    bias_grad = jnp.stack(
        [
            jnp.concatenate(
                [shifts[e]["q"], sums[0, e], shifts[e]["o"], sums[4, e], shifts[e]["in"],
                 shifts[e]["out"], shifts[e]["2"], sums[2, e]]
            )
            for e in range(2)
        ]
    )
    grads = (
        table_grad.T,
        jnp.stack(in_grads),
        jnp.stack(out_grads),
        jnp.stack(expand_grads),
        jnp.stack(shrink_grads),
        lax.dynamic_slice_in_dim(gain_grad, me * cols, cols, 2),
        lax.dynamic_slice_in_dim(bias_grad, me * bias_terms.shape[1], bias_terms.shape[1], 1),
    )
    local_squares = sum(jnp.sum(g * g) for g in grads)
    (squares,) = exch(
        8, [jnp.broadcast_to(local_squares, (8, LANE))], [((nd, 8, LANE), F32)],
        [send_all(0, 0, nd)],
    )
    grad_norm = jnp.sqrt(jnp.sum(squares[:, 0, 0]))
    factor = CLIP / jnp.maximum(grad_norm, CLIP)
    step = step_count[0].astype(F32)
    masters = (embed_table, attend_in, attend_out, expand_weight, shrink_weight, norm_gains, bias_terms)
    firsts = (embed_first, attend_in_first, attend_out_first, expand_first, shrink_first, gains_first, bias_first)
    seconds = (embed_second, attend_in_second, attend_out_second, expand_second, shrink_second, gains_second, bias_second)
    results = [loss, grad_norm]
    for index in range(7):
        results.extend(
            adam_update(masters[index], grads[index] * factor, firsts[index], seconds[index], step, LEARN_RATES[index])
        )
    return tuple(results)


def on_device(
    passage_ids, query_ids, passage_query, kept_mask, neg_count, step_count,
    embed_table, attend_in, attend_out, expand_weight, shrink_weight, norm_gains, bias_terms,
    embed_first, embed_second, attend_in_first, attend_in_second,
    attend_out_first, attend_out_second, expand_first, expand_second,
    shrink_first, shrink_second, gains_first, gains_second, bias_first, bias_second,
):
    if embed_table.shape[1] % 8 != 0 or lax.axis_size("narrow") != 4 or lax.axis_size("wide") != 8 or passage_ids.shape[0] != 2:
        return on_device_rows(
            passage_ids, query_ids, passage_query, kept_mask, neg_count, step_count,
            embed_table, attend_in, attend_out, expand_weight, shrink_weight, norm_gains,
            bias_terms, embed_first, embed_second, attend_in_first, attend_in_second,
            attend_out_first, attend_out_second, expand_first, expand_second,
            shrink_first, shrink_second, gains_first, gains_second, bias_first, bias_second,
        )
    narrow = lax.axis_size("narrow")
    nd = lax.axis_size("wide") * narrow
    me = lax.axis_index("wide") * narrow + lax.axis_index("narrow")
    cols = embed_table.shape[1]
    n_slots = passage_query.shape[0]
    per_wide = query_ids.shape[0]
    nq = per_wide * lax.axis_size("wide")
    n_valid = VALID_PER_QUERY * nq
    cap = -(-n_valid // nd)
    ff_cols = FF // nd
    rows = n_valid + nq
    tq = nq * LQ
    query_home = nd * 5 // 8 - 1
    exch = functools.partial(comm, nd=nd, narrow=narrow)
    small_width = -(-max(cols, bias_terms.shape[1]) // LANE) * LANE
    ids_width = max(LP, -(-tq // LANE) * LANE)

    def widen(value, width):
        return jnp.pad(value, ((0, 0), (0, width - value.shape[1])))

    spot = jnp.arange(tq) // (LQ * per_wide) == lax.axis_index("wide")
    spot = spot & (lax.axis_index("narrow") == 0)
    q_line = jnp.where(spot, jnp.tile(query_ids.reshape(-1), tq // (LQ * per_wide)), 0)
    ids_mine = jnp.concatenate([widen(passage_ids, ids_width), widen(q_line[None], ids_width)])
    small_mine = jnp.concatenate(
        [widen(norm_gains.reshape(6, cols), small_width), widen(bias_terms, small_width)]
    ).astype(BF16)
    n_own = passage_ids.shape[0]
    table_t = embed_table.T
    ids_got, small_got, mine, mine_q, w_one, w_zero = first(
        n_valid, nq, nd, narrow, cols, query_home,
        [ids_mine, small_mine, table_t, attend_in, attend_out, table_t[:, V : V + LP]],
        FORWARD_PLAN,
    )
    w_one = w_one.reshape(D, 4 * D + LP)
    w_zero = w_zero.reshape(D, 4 * D)
    up_mine = expand_weight.astype(BF16).reshape(2, cols, nd, ff_cols).transpose(2, 0, 1, 3)
    up_mine = jnp.pad(up_mine, ((0, 0), (0, 0), (0, 0), (0, LANE - ff_cols)))
    earlier = jnp.concatenate([jnp.full((1,), -1, jnp.int32), passage_query[:-1]])
    first_slot = ((passage_query >= 0) & (passage_query != earlier)).astype(jnp.int32)
    slots = jnp.pad(
        jnp.stack([passage_query, first_slot, kept_mask])[:, :n_valid],
        ((0, 5), (0, -(-n_valid // LANE) * LANE - n_valid)),
    )
    shrink_g, loss, g_table, g_in, g_out, g_up, g_bin, g_small, norm = middle(
        n_valid, nq, nd, narrow, cols, query_home,
        [mine, mine_q, w_one, w_zero, up_mine, shrink_weight, small_got, slots, ids_got],
    )
    loss = loss[0, 0]
    grad_norm = norm[0, 0]
    g_small = g_small.reshape(2, 16, D)
    g_bin = g_bin[:2].reshape(2, 2, nd // 2, LANE)[..., :ff_cols]
    g_bin = g_bin.transpose(0, 2, 1, 3).reshape(2, FF)
    g_up = g_up.reshape(2, cols, 2, nd // 2, LANE)[..., :ff_cols].transpose(0, 1, 3, 2, 4)
    bias_grad = jnp.concatenate(
        [g_small[:, :4].reshape(2, 4 * D), g_bin, g_small[:, 4:7].reshape(2, 3 * D)], axis=1
    )
    grads = (
        g_table[:, : V + LP].T,
        g_in,
        g_out,
        g_up.reshape(2, cols, FF),
        shrink_g[:, :ff_cols],
        lax.dynamic_slice_in_dim(g_small[:, 7:10], me * cols, cols, 2),
        lax.dynamic_slice_in_dim(bias_grad, me * bias_terms.shape[1], bias_terms.shape[1], 1),
    )
    factor = CLIP / jnp.maximum(grad_norm, CLIP)
    step = step_count[0].astype(F32)
    masters = (embed_table, attend_in, attend_out, expand_weight, shrink_weight, norm_gains, bias_terms)
    firsts = (embed_first, attend_in_first, attend_out_first, expand_first, shrink_first, gains_first, bias_first)
    seconds = (embed_second, attend_in_second, attend_out_second, expand_second, shrink_second, gains_second, bias_second)
    results = [loss, grad_norm]
    for index in range(7):
        results.extend(
            adam_update(masters[index], grads[index] * factor, firsts[index], seconds[index], step, LEARN_RATES[index])
        )
    return tuple(results)


def solution(mesh):
    both = ("wide", "narrow")
    weight_specs = (P(None, both),) + (P(None, both, None),) * 4 + (P(None, None, both), P(None, both))
    pairs = tuple(s for spec in weight_specs for s in (spec, spec))
    in_specs = (P(both, None), P("wide", None), P(), P(), P("wide"), P()) + weight_specs + pairs
    out_specs = (P(), P()) + tuple(s for spec in weight_specs for s in (spec, spec, spec))
    return jax.shard_map(on_device, mesh=mesh, in_specs=in_specs, out_specs=out_specs, check_vma=False)
```
